32 devices in a mesh: dp: 16 (over z, y, core), tensor: 2 (over x).
Axes of the slice: x: 2, y: 2, z: 4, core: 2. Of those that a mesh axis runs over, the one named last changes fastest.
Arguments:
- tokens: bfloat16 [2048, 16, 1024], P('tensor', 'dp'), may hold values from -6 to 6
- lengths: int32 [16], P('dp'), may hold values from 512 to 2048, as said below
- cotangent: bfloat16 [2048, 16, 1024], P('tensor', 'dp'), may hold values from -16 to 16
- w_query: bfloat16 [1024, 1024], P(None, 'tensor'), may hold values from -0.1875 to 0.1875
- w_key: bfloat16 [1024, 1024], P(None, 'tensor'), may hold values from -0.1875 to 0.1875
- w_value: bfloat16 [1024, 1024], P(None, 'tensor'), may hold values from -0.1875 to 0.1875
- w_out: bfloat16 [1024, 1024], P('tensor'), may hold values from -0.1875 to 0.1875
- up_weight: bfloat16 [1024, 4096], P(None, 'tensor'), may hold values from -0.1875 to 0.1875
- bias_up: bfloat16 [4096], P('tensor'), may hold values from -3 to 3
- down_weight: bfloat16 [4096, 1024], P('tensor'), may hold values from -0.09375 to 0.09375
- bias_down: bfloat16 [1024], replicated, may hold values from -3 to 3
- norm_gains: float32 [4, 1024], replicated, may hold values from 0.1 to 1.9
- norm_shifts: float32 [4, 1024], replicated, may hold values from -3 to 3
Outputs:
- layer_out: bfloat16 [2048, 16, 1024], P('tensor', 'dp')
- grad_tokens: bfloat16 [2048, 16, 1024], P('tensor', 'dp')
- grad_query: float32 [1024, 1024], P(None, 'tensor')
- grad_key: float32 [1024, 1024], P(None, 'tensor')
- grad_value: float32 [1024, 1024], P(None, 'tensor')
- grad_out: float32 [1024, 1024], P('tensor')
- grad_up: float32 [1024, 4096], P(None, 'tensor')
- grad_bias_up: float32 [4096], P('tensor')
- down_weight_gradient: float32 [4096, 1024], P('tensor')
- grad_bias_down: float32 [1024], replicated
- grad_gains: float32 [4, 1024], replicated
- grad_shifts: float32 [4, 1024], replicated
The draws below stay inside these ranges and needn't reach their ends.
Inputs may be any that keep to these rules, and one draw needn't show every extreme that they name: Row b's valid tokens are its first lengths[b] slots; in every draw some row has exactly 2048 and some row exactly 512.
All inputs are finite; a program needn't handle non-finite values.
Results may differ from the reference program's by a relative error of at most 0.02.
Values may be sent and summed in bfloat16 or wider, within the bound.
A program may use at most 320 MiB of HBM per device.

```python
from functools import partial
import jax
import jax.numpy as jnp
from jax import lax

D = 1024
H = 16
HD = 64
FF = 4096
SEQ = 2048
BATCH = 16
MINLEN = 512
N_TENSOR = 2


def draw_lengths(key, part):
    key_one, key_two, key_three = jax.random.split(key, 3)
    values = jax.random.randint(key_one, (BATCH,), MINLEN, SEQ + 1)
    longest = jax.random.randint(key_two, (), 0, BATCH)
    shortest = (longest + 1 + jax.random.randint(key_three, (), 0, BATCH - 1)) % BATCH
    values = values.at[longest].set(SEQ).at[shortest].set(MINLEN)
    return values.astype(jnp.int32)


def draw_cotangent(key, part):
    key_one = jax.random.fold_in(key, 7)
    row_pos = jnp.arange(BATCH).astype(jnp.float32) / max(BATCH - 1, 1)
    slot_pos = jnp.arange(SEQ).astype(jnp.float32) / max(SEQ - 1, 1)
    scaling = 0.5 * (3.0 ** row_pos)[None, :, None] * (2.0 ** slot_pos)[:, None, None]
    base = jnp.clip(jax.random.normal(key_one, (SEQ, BATCH, D), jnp.float32), -4.0, 4.0)
    return (base * scaling).astype(jnp.bfloat16)


def block_levels(own_key, extent, shards, low, high):
    level = 1.0
    for position, blocks in shards:
        heights = jax.random.uniform(jax.random.fold_in(jax.random.fold_in(own_key, 6), position), (blocks,), jnp.float32, low / len(shards), high / len(shards))
        level = level * jnp.repeat(jnp.exp(heights), extent[position] // blocks).reshape((-1,) + (1,) * (len(extent) - 1 - position))
    return level


def noise(rng, extent, deviation, limit, shards=(), kind=jnp.bfloat16):
    values = deviation * jax.random.normal(rng, extent, jnp.float32)
    if shards:
        values = values * block_levels(rng, extent, shards, -0.22, 0.18)
    return jnp.clip(values, -limit, limit).astype(kind)


def setup_inputs(seed: int = 0) -> dict:
    seeds = jax.random.split(jax.random.key(seed), 14)
    return {
        "tokens": noise(seeds[0], (SEQ, BATCH, D), 1.0, 6.0, ((0, 2), (1, 16))),
        "lengths": draw_lengths(jax.random.fold_in(seeds[13], 71), 0),
        "cotangent": draw_cotangent(jax.random.fold_in(seeds[13], 71), 0),
        "w_query": noise(seeds[3], (D, H * HD), D ** -0.5, 0.1875, ((1, 2),)),
        "w_key": noise(seeds[4], (D, H * HD), D ** -0.5, 0.1875, ((1, 2),)),
        "w_value": noise(seeds[5], (D, H * HD), D ** -0.5, 0.1875, ((1, 2),)),
        "w_out": noise(seeds[6], (H * HD, D), (H * HD) ** -0.5, 0.1875, ((0, 2),)),
        "up_weight": noise(seeds[7], (D, FF), D ** -0.5, 0.1875, ((1, 2),)),
        "bias_up": noise(seeds[8], (FF,), 0.5, 3.0, ((0, 2),)),
        "down_weight": noise(seeds[9], (FF, D), FF ** -0.5, 0.09375, ((0, 2),)),
        "bias_down": noise(seeds[10], (D,), 0.5, 3.0),
        "norm_gains": jnp.clip(1.0 + 0.18 * jax.random.normal(seeds[11], (4, D), jnp.float32), 0.1, 1.9),
        "norm_shifts": noise(seeds[12], (4, D), 0.5, 3.0, (), jnp.float32),
    }


@jax.custom_vjp
def low(v):
    return lax.optimization_barrier(v.astype(jnp.bfloat16)).astype(jnp.float32)

@jax.custom_vjp
def low_back(v):
    return v

def low_keep(v):
    return (low(v), None)

def low_pass(kept, grad):
    return (grad,)

def back_keep(v):
    return (v, None)

def back_low(kept, grad):
    return (low(grad),)
low.defvjp(low_keep, low_pass)
low_back.defvjp(back_keep, back_low)
HIGHEST = lax.Precision.HIGHEST
EPSILON = 1e-05

def layer_norm(values, gain, shift):
    average = lax.optimization_barrier(jnp.mean(values, axis=-1, keepdims=True))
    centred = values - average
    spread = lax.optimization_barrier(jnp.mean(centred * centred, axis=-1, keepdims=True))
    return centred * lax.rsqrt(spread + EPSILON) * gain + shift

def rotate(values, cosine, sine):
    half_size = values.shape[-1] // 2
    first_half = values[..., :half_size]
    second_half = values[..., half_size:]
    return jnp.concatenate([first_half * cosine - second_half * sine, second_half * cosine + first_half * sine], axis=-1)

def head_attention(length, inputs):
    query, keys, values = inputs
    scores = low_back(jnp.dot(query, keys.T, precision=HIGHEST) * HD ** (-0.5))
    query_index = jnp.arange(SEQ)[:, None]
    key_index = jnp.arange(SEQ)[None, :]
    allowed = (key_index <= query_index) & (key_index < length)
    masked = jnp.where(allowed, scores, -1e+30)
    highest = lax.optimization_barrier(jnp.max(masked, axis=-1, keepdims=True))
    expo = jnp.exp(masked - highest)
    probs = low(expo / lax.optimization_barrier(jnp.sum(expo, axis=-1, keepdims=True)))
    return jnp.dot(probs, values, precision=HIGHEST)

def row_forward(params, row, length):
    w_query, w_key, w_value, w_out, up_weight, bias_up, down_weight, bias_down, norm_gains, norm_shifts = params
    positions = jnp.arange(SEQ).astype(jnp.float32)
    freqs = 10000.0 ** (-jnp.arange(HD // 2).astype(jnp.float32) * 2.0 / HD)
    angles = positions[:, None] * freqs[None, :]
    cosine = jnp.cos(angles)[:, None, :]
    sine = jnp.sin(angles)[:, None, :]
    heads_local = H // N_TENSOR
    width = heads_local * HD
    ff_local = FF // N_TENSOR
    normed_one = low(layer_norm(row, norm_gains[0], norm_shifts[0]))
    attn_total = jnp.zeros((SEQ, D), jnp.float32)
    for group in range(N_TENSOR):
        lo_col = group * width
        shared = low_back(normed_one)
        query = low_back(jnp.dot(shared, w_query[:, lo_col:lo_col + width], precision=HIGHEST))
        keyed = low_back(jnp.dot(shared, w_key[:, lo_col:lo_col + width], precision=HIGHEST))
        valued = low(low_back(jnp.dot(shared, w_value[:, lo_col:lo_col + width], precision=HIGHEST)))
        query = low(rotate(query.reshape(SEQ, heads_local, HD), cosine, sine))
        keyed = low(rotate(keyed.reshape(SEQ, heads_local, HD), cosine, sine))
        valued = valued.reshape(SEQ, heads_local, HD)
        stacked = (jnp.swapaxes(query, 0, 1), jnp.swapaxes(keyed, 0, 1), jnp.swapaxes(valued, 0, 1))
        outputs = lax.map(jax.checkpoint(partial(head_attention, length)), stacked)
        mixed = low(low_back(jnp.swapaxes(outputs, 0, 1).reshape(SEQ, width)))
        attn_total = attn_total + low(jnp.dot(mixed, w_out[lo_col:lo_col + width, :], precision=HIGHEST))
    attn_total = low_back(attn_total)
    resid = row + layer_norm(attn_total, norm_gains[1], norm_shifts[1])
    normed_two = low(layer_norm(resid, norm_gains[2], norm_shifts[2]))
    mlp_total = jnp.zeros((SEQ, D), jnp.float32)
    for group in range(N_TENSOR):
        lo_col = group * ff_local
        shared_two = low_back(normed_two)
        pre_up = low_back(jnp.dot(shared_two, up_weight[:, lo_col:lo_col + ff_local], precision=HIGHEST) + bias_up[lo_col:lo_col + ff_local])
        activation_value = low(jax.nn.gelu(pre_up, approximate=True))
        mlp_total = mlp_total + low(jnp.dot(activation_value, down_weight[lo_col:lo_col + ff_local, :], precision=HIGHEST))
    branch = low_back(mlp_total + bias_down)
    result = resid + layer_norm(branch, norm_gains[3], norm_shifts[3])
    valid = (jnp.arange(SEQ) < length).astype(jnp.float32)[:, None]
    return result * valid

def reference(tokens, lengths, cotangent, w_query, w_key, w_value, w_out, up_weight, bias_up, down_weight, bias_down, norm_gains, norm_shifts):
    params = tuple((weight.astype(jnp.float32) for weight in (w_query, w_key, w_value, w_out, up_weight, bias_up, down_weight, bias_down, norm_gains, norm_shifts)))
    rows = jnp.swapaxes(tokens.astype(jnp.float32), 0, 1)
    cot_rows = jnp.swapaxes(cotangent.astype(jnp.float32), 0, 1)
    zero_grads = tuple((jnp.zeros_like(weight) for weight in params))

    def one_row(carry, inputs):
        row, cot_row, length = inputs
        output, pullback = jax.vjp(lambda param_set, row_in: row_forward(param_set, row_in, length), params, row)
        grad_params, grad_row = pullback(cot_row)
        carry = jax.tree.map(lambda first_sum, second_sum: first_sum + second_sum, carry, grad_params)
        return (carry, (output.astype(jnp.bfloat16), grad_row.astype(jnp.bfloat16)))
    grads, (outputs, grad_rows) = lax.scan(one_row, zero_grads, (rows, cot_rows, lengths))
    return (jnp.swapaxes(outputs, 0, 1), jnp.swapaxes(grad_rows, 0, 1), grads[0], grads[1], grads[2], grads[3], grads[4], grads[5], grads[6], grads[7], grads[8], grads[9])
```

```python
import functools
import jax
import jax.numpy as jnp
from jax import lax
from jax.experimental import pallas as pl
from jax.experimental.pallas import tpu as pltpu
from jax.sharding import PartitionSpec as P

HD = 64
BF = jnp.bfloat16
F32 = jnp.float32
NT = (((1,), (1,)), ((), ()))
NN = (((1,), (0,)), ((), ()))


def dotg(a,b,dn): return lax.dot_general(a,b,dn,preferred_element_type=F32)

def fwd_kernel(len_ref, q_ref, k_ref, v_ref, o_ref, lse_ref, vt, *, blk):
    i = pl.program_id(1)
    @pl.when(i == 0)
    def _(): vt[...] = jnp.transpose(v_ref[...])
    length = len_ref[0]
    lane = lax.broadcasted_iota(jnp.int32,(blk,128),1)
    q = q_ref[...] * jnp.asarray(0.125, BF)
    zero = jnp.zeros_like(q)
    qs = (jnp.where(lane<64,q,zero), jnp.where(lane<64,zero,q))
    def step(j, carry, diag):
        start = pl.multiple_of(j*blk, blk)
        kb = k_ref[pl.ds(start,blk),:]
        out=[]
        for h in range(2):
            m,l,acc = carry[h]
            s = dotg(kb, qs[h], NT)
            if diag:
                key = lax.broadcasted_iota(jnp.int32,(blk,blk),0)
                qry = lax.broadcasted_iota(jnp.int32,(blk,blk),1)
                s = jnp.where((key<=qry)&(key+start<length), s, -1e30)
            mn = jnp.maximum(m, jnp.max(s,axis=0,keepdims=True))
            p = jnp.exp(s-mn)
            al = jnp.exp(m-mn)
            l = l*al + jnp.sum(p,axis=0,keepdims=True)
            vb = vt[64*h:64*h+64, pl.ds(start,blk)]
            acc = acc*al + dotg(vb, p.astype(BF), NN)
            out.append((m*0+mn,l,acc))
        return tuple(out)
    init = tuple((jnp.full((1,blk),-1e30,F32), jnp.zeros((1,blk),F32), jnp.zeros((64,blk),F32)) for _ in range(2))
    c = lax.fori_loop(0, i, lambda j,c: step(j,c,False), init)
    c = step(i, c, True)
    ot = jnp.concatenate([c[h][2]/c[h][1] for h in range(2)],axis=0)
    o_ref[...] = jnp.transpose(ot).astype(BF)
    lse_ref[0] = jnp.concatenate([c[h][0]+jnp.log(c[h][1]) for h in range(2)],axis=0)

def flash_fwd(length, joint, width, blk=256):
    T=joint.shape[0]; np_=width//128; nb=T//blk
    return pl.pallas_call(functools.partial(fwd_kernel,blk=blk),
        grid_spec=pltpu.PrefetchScalarGridSpec(num_scalar_prefetch=1, grid=(np_,nb),
          in_specs=[pl.BlockSpec((blk,128),lambda p,i,*_:(i,p)),
                    pl.BlockSpec((T,128),lambda p,i,*_:(0,np_+p)),
                    pl.BlockSpec((T,128),lambda p,i,*_:(0,2*np_+p))],
          out_specs=[pl.BlockSpec((blk,128),lambda p,i,*_:(i,p)),
                     pl.BlockSpec((1,2,blk),lambda p,i,*_:(p,0,i))],
          scratch_shapes=[pltpu.VMEM((128,T),BF)]),
        out_shape=[jax.ShapeDtypeStruct((T,width),BF), jax.ShapeDtypeStruct((np_,2,T),F32)],
        compiler_params=pltpu.CompilerParams(vmem_limit_bytes=40<<20),
        name="attend",
    )(length, joint, joint, joint)

def bwd_kernel(len_ref, q_ref, k_ref, v_ref, o_ref, do_ref, lse_ref, dq_ref, dk_ref, dv_ref, kt, dlt, dqt, *, blk, nb):
    T=q_ref.shape[0]
    j = pl.program_id(1)
    length = len_ref[0]
    @pl.when(j == 0)
    def _():
        kt[...] = jnp.transpose(k_ref[...])
        dqt[...] = jnp.zeros_like(dqt)
        def body(i,_):
            st=pl.multiple_of(i*blk,blk)
            pr = jnp.transpose(do_ref[pl.ds(st,blk),:].astype(F32)*o_ref[pl.ds(st,blk),:].astype(F32))
            for h in range(2):
                dlt[h:h+1,pl.ds(st,blk)] = jnp.sum(pr[64*h:64*h+64],axis=0,keepdims=True)
            return 0
        lax.fori_loop(0,nb,body,0)
    js = pl.multiple_of(j*blk,blk)
    lane = lax.broadcasted_iota(jnp.int32,(blk,128),1)
    kb = k_ref[pl.ds(js,blk),:]*jnp.asarray(0.125,BF); vb=v_ref[pl.ds(js,blk),:]
    zero = jnp.zeros_like(kb)
    ks = (jnp.where(lane<64,kb,zero), jnp.where(lane<64,zero,kb))
    vs = (jnp.where(lane<64,vb,zero), jnp.where(lane<64,zero,vb))
    def step(i, carry, diag):
        st = pl.multiple_of(i*blk,blk)
        qb = q_ref[pl.ds(st,blk),:]; dob = do_ref[pl.ds(st,blk),:]
        out=[]
        for h in range(2):
            dk,dv = carry[h]
            s = dotg(ks[h], qb, NT)
            if diag:
                key = lax.broadcasted_iota(jnp.int32,(blk,blk),0)
                qry = lax.broadcasted_iota(jnp.int32,(blk,blk),1)
                s = jnp.where((key<=qry)&(key+js<length), s, -1e30)
            p = jnp.exp(s - lse_ref[0,h:h+1,pl.ds(st,blk)])
            dp = dotg(vs[h], dob, NT)
            ds = (p*(dp - dlt[h:h+1,pl.ds(st,blk)])).astype(BF)
            dv = dv + dotg(p.astype(BF), dob, NN)
            dk = dk + dotg(ds, qb, NN)
            dqt[64*h:64*h+64,pl.ds(st,blk)] += dotg(kt[64*h:64*h+64,pl.ds(js,blk)], ds, NN)
            out.append((dk,dv))
        return tuple(out)
    z=jnp.zeros((blk,128),F32)
    c = step(j, ((z,z),(z,z)), True)
    c = lax.fori_loop(j+1, nb, lambda i,c: step(i,c,False), c)
    dk_ref[...] = jnp.where(lane<64,c[0][0],c[1][0])*0.125
    dv_ref[...] = jnp.where(lane<64,c[0][1],c[1][1]).astype(dv_ref.dtype)
    @pl.when(j == nb-1)
    def _():
        def body(i,_):
            st=pl.multiple_of(i*blk,blk)
            dq_ref[pl.ds(st,blk),:] = jnp.transpose(dqt[:,pl.ds(st,blk)])*0.125
            return 0
        lax.fori_loop(0,nb,body,0)

def flash_bwd(length, joint, mixed, dmixed, lse, width, blk=256):
    T=joint.shape[0]; np_=width//128; nb=T//blk
    full=lambda off: pl.BlockSpec((T,128),lambda p,j,*_:(0,off*np_+p))
    return pl.pallas_call(functools.partial(bwd_kernel,blk=blk,nb=nb),
        grid_spec=pltpu.PrefetchScalarGridSpec(num_scalar_prefetch=1, grid=(np_,nb),
          in_specs=[full(0),full(1),full(2),full(0),full(0),pl.BlockSpec((1,2,T),lambda p,j,*_:(p,0,0))],
          out_specs=[full(0), pl.BlockSpec((blk,128),lambda p,j,*_:(j,p)), pl.BlockSpec((blk,128),lambda p,j,*_:(j,p))],
          scratch_shapes=[pltpu.VMEM((128,T),BF),pltpu.VMEM((2,T),F32),pltpu.VMEM((128,T),F32)]),
        out_shape=[jax.ShapeDtypeStruct((T,width),F32), jax.ShapeDtypeStruct((T,width),F32), jax.ShapeDtypeStruct((T,width),BF)],
        compiler_params=pltpu.CompilerParams(vmem_limit_bytes=48<<20),
        name="attend_back",
    )(length, joint, joint, joint, mixed, dmixed, lse)


EPSILON = 1e-05


def layer_norm(values, gain, shift):
    average = jnp.mean(values, axis=-1, keepdims=True)
    centred = values - average
    spread = jnp.mean(centred * centred, axis=-1, keepdims=True)
    return centred * lax.rsqrt(spread + EPSILON) * gain + shift


def rotate(values, cosine, sine):
    half_size = values.shape[-1] // 2
    first_half = values[..., :half_size]
    second_half = values[..., half_size:]
    return jnp.concatenate(
        [first_half * cosine - second_half * sine, second_half * cosine + first_half * sine],
        axis=-1,
    )


def gelu_tanh(values):
    return jax.nn.gelu(values, approximate=True)


def shards(
    tokens,
    lengths,
    cotangent,
    w_query,
    w_key,
    w_value,
    w_out,
    up_weight,
    bias_up,
    down_weight,
    bias_down,
    norm_gains,
    norm_shifts,
):
    shard_rows, batch_rows, model_width = tokens.shape
    seq_len = shard_rows * lax.axis_size("tensor")
    local_width = w_query.shape[1]
    heads_local = local_width // HD
    positions = lax.axis_index("tensor") * shard_rows + jnp.arange(shard_rows)
    valid_local = (positions[:, None] < lengths[None, :]).astype(jnp.float32)[:, :, None]
    inputs = tokens.astype(jnp.float32)
    normed_one = layer_norm(inputs, norm_gains[0], norm_shifts[0])
    lowered_one = normed_one.astype(jnp.bfloat16)
    w_joint = jnp.concatenate([w_query, w_key, w_value], axis=1)
    joint = jnp.einsum(
        "trd,dc->trc",
        lax.all_gather(lowered_one, "tensor", axis=0, tiled=True),
        w_joint,
        preferred_element_type=jnp.float32,
    )
    slot_float = jnp.arange(seq_len).astype(jnp.float32)
    freqs = 10000.0 ** (-jnp.arange(HD // 2).astype(jnp.float32) * 2.0 / HD)
    angles = slot_float[:, None] * freqs[None, :]
    cosine = jnp.cos(angles)[:, None, None, :]
    sine = jnp.sin(angles)[:, None, None, :]
    shaped = joint.reshape(seq_len, batch_rows, 3, heads_local, HD)
    query_rot = rotate(shaped[:, :, 0], cosine, sine).astype(jnp.bfloat16)
    key_rot = rotate(shaped[:, :, 1], cosine, sine).astype(jnp.bfloat16)
    value_low = shaped[:, :, 2].astype(jnp.bfloat16)
    packed = jnp.concatenate(
        [t.reshape(seq_len, local_width) for t in (query_rot, key_rot, value_low)], axis=1
    )
    mixed_flat, log_totals = flash_fwd(lengths, packed, local_width, 512)
    mixed_low = mixed_flat.reshape(seq_len, batch_rows, local_width)
    partial_row_set = mixed_low
    attn_sum = lax.psum_scatter(
        jnp.einsum(
            "trc,cd->trd", partial_row_set, w_out, preferred_element_type=jnp.float32
        ).astype(jnp.bfloat16),
        "tensor",
        scatter_dimension=0,
        tiled=True,
    ).astype(jnp.float32)
    resid = inputs + layer_norm(attn_sum, norm_gains[1], norm_shifts[1])
    normed_two = layer_norm(resid, norm_gains[2], norm_shifts[2])
    lowered_two = normed_two.astype(jnp.bfloat16)
    bias_up_f = bias_up.astype(jnp.float32)
    pre_up = (
        jnp.einsum(
            "pvl,ls->pvs",
            lax.all_gather(lowered_two, "tensor", axis=0, tiled=True),
            up_weight,
            preferred_element_type=jnp.float32,
        )
        + bias_up_f
    )
    activation_value = gelu_tanh(pre_up).astype(jnp.bfloat16)
    partial_row_set = activation_value
    branch = lax.psum_scatter(
        jnp.einsum(
            "xew,wq->xeq", partial_row_set, down_weight, preferred_element_type=jnp.float32
        ).astype(jnp.bfloat16),
        "tensor",
        scatter_dimension=0,
        tiled=True,
    ).astype(jnp.float32) + bias_down.astype(jnp.float32)
    result = resid + layer_norm(branch, norm_gains[3], norm_shifts[3])
    layer_out = (result * valid_local).astype(jnp.bfloat16)
    grad_result = cotangent.astype(jnp.float32) * valid_local
    ignored, pull_three = jax.vjp(layer_norm, branch, norm_gains[3], norm_shifts[3])
    grad_branch, gain_three, shift_three = pull_three(grad_result)
    grad_branch_low = grad_branch.astype(jnp.bfloat16)
    grad_bias_down = jnp.sum(grad_branch_low.astype(jnp.float32), axis=(0, 1))
    row_segment = lax.all_gather(grad_branch_low, "tensor", axis=0, tiled=True)
    down_weight_gradient = jnp.einsum(
        "pwy,pwq->yq", activation_value, row_segment, preferred_element_type=jnp.float32
    )
    row_gradient_block = jnp.einsum(
        "yvz,az->yva", row_segment, down_weight, preferred_element_type=jnp.float32
    )
    grad_act = row_gradient_block
    grad_act, down_weight_gradient = (grad_act, down_weight_gradient)
    ignored, pull_gelu = jax.vjp(gelu_tanh, pre_up)
    grad_pre_low = pull_gelu(grad_act)[0].astype(jnp.bfloat16)
    grad_bias_up = jnp.sum(grad_pre_low.astype(jnp.float32), axis=(0, 1))
    preactivation_rows = grad_pre_low
    grad_up = jnp.einsum(
        "now,nov->wv",
        lax.all_gather(lowered_two, "tensor", axis=0, tiled=True),
        preactivation_rows,
        preferred_element_type=jnp.float32,
    )
    preactivation_rows = grad_pre_low
    grad_normed_two = lax.psum_scatter(
        jnp.einsum(
            "vuk,gk->vug", preactivation_rows, up_weight, preferred_element_type=jnp.float32
        ).astype(jnp.bfloat16),
        "tensor",
        scatter_dimension=0,
        tiled=True,
    ).astype(jnp.float32)
    ignored, pull_two = jax.vjp(layer_norm, resid, norm_gains[2], norm_shifts[2])
    grad_resid_part, gain_two, shift_two = pull_two(grad_normed_two)
    grad_resid = grad_result + grad_resid_part
    ignored, pull_one = jax.vjp(layer_norm, attn_sum, norm_gains[1], norm_shifts[1])
    grad_attn, gain_one, shift_one = pull_one(grad_resid)
    grad_attn_low = grad_attn.astype(jnp.bfloat16)
    row_segment = lax.all_gather(grad_attn_low, "tensor", axis=0, tiled=True)
    grad_out = jnp.einsum("trc,trd->cd", mixed_low, row_segment, preferred_element_type=jnp.float32)
    row_gradient_block = jnp.einsum(
        "trd,cd->trc", row_segment, w_out, preferred_element_type=jnp.float32
    )
    grad_mixed = row_gradient_block
    grad_mixed, grad_out = (grad_mixed, grad_out)
    grad_mixed_low = grad_mixed.astype(jnp.bfloat16).reshape(seq_len, local_width)
    grad_queries, grad_keys, grad_values = flash_bwd(
        lengths, packed, mixed_flat, grad_mixed_low, log_totals, local_width, 512
    )
    grad_keys = grad_keys.reshape(seq_len, batch_rows, heads_local, HD)
    grad_queries = rotate(grad_queries.reshape(seq_len, batch_rows, heads_local, HD), cosine, -sine)
    grad_keys = rotate(grad_keys, cosine, -sine)
    grad_joint_low = jnp.concatenate(
        [
            grad_queries.reshape(seq_len, batch_rows, local_width),
            grad_keys.reshape(seq_len, batch_rows, local_width),
            grad_values.reshape(seq_len, batch_rows, local_width).astype(jnp.float32),
        ],
        axis=-1,
    ).astype(jnp.bfloat16)
    joint_rows = grad_joint_low
    grad_joint = jnp.einsum(
        "trd,trc->dc",
        lax.all_gather(lowered_one, "tensor", axis=0, tiled=True),
        joint_rows,
        preferred_element_type=jnp.float32,
    )
    joint_rows = grad_joint_low
    grad_normed_one = lax.psum_scatter(
        jnp.einsum("trc,dc->trd", joint_rows, w_joint, preferred_element_type=jnp.float32).astype(
            jnp.bfloat16
        ),
        "tensor",
        scatter_dimension=0,
        tiled=True,
    ).astype(jnp.float32)
    ignored, pull_zero = jax.vjp(layer_norm, inputs, norm_gains[0], norm_shifts[0])
    grad_inputs, gain_zero, shift_zero = pull_zero(grad_normed_one)
    grad_tokens = (grad_resid + grad_inputs).astype(jnp.bfloat16)
    summed = (
        lax.psum(grad_joint[:, :local_width].astype(jnp.bfloat16), "dp").astype(jnp.float32),
        lax.psum(grad_joint[:, local_width : 2 * local_width].astype(jnp.bfloat16), "dp").astype(
            jnp.float32
        ),
        lax.psum(grad_joint[:, 2 * local_width :].astype(jnp.bfloat16), "dp").astype(jnp.float32),
        lax.psum(grad_out.astype(jnp.bfloat16), "dp").astype(jnp.float32),
        lax.psum(grad_up.astype(jnp.bfloat16), "dp").astype(jnp.float32),
        lax.psum(grad_bias_up.astype(jnp.bfloat16), "dp").astype(jnp.float32),
        lax.psum(down_weight_gradient.astype(jnp.bfloat16), "dp").astype(jnp.float32),
    )
    norm_sums = lax.psum(
        (
            jnp.stack([gain_zero, gain_one, gain_two, gain_three]),
            jnp.stack([shift_zero, shift_one, shift_two, shift_three]),
            grad_bias_down,
        ),
        ("dp", "tensor"),
    )
    return (
        layer_out,
        grad_tokens,
        summed[0],
        summed[1],
        summed[2],
        summed[3],
        summed[4],
        summed[5],
        summed[6],
        norm_sums[2],
        norm_sums[0],
        norm_sums[1],
    )


def solution(mesh):
    placed = (
        P("tensor", "dp", None),
        P("dp"),
        P("tensor", "dp", None),
        P(None, "tensor"),
        P(None, "tensor"),
        P(None, "tensor"),
        P("tensor", None),
        P(None, "tensor"),
        P("tensor"),
        P("tensor", None),
        P(),
        P(),
        P(),
    )
    return jax.shard_map(
        shards,
        mesh=mesh,
        in_specs=placed,
        out_specs=(
            P("tensor", "dp", None),
            P("tensor", "dp", None),
            P(None, "tensor"),
            P(None, "tensor"),
            P(None, "tensor"),
            P("tensor", None),
            P(None, "tensor"),
            P("tensor"),
            P("tensor", None),
            P(),
            P(),
            P(),
        ),
        check_vma=False,
    )
```

```python
import functools
import jax
import jax.numpy as jnp
from jax import lax
from jax.experimental import pallas as pl
from jax.experimental.pallas import tpu as pltpu
from jax.sharding import PartitionSpec as P

HD = 64
EPSILON = 1e-05
BF = jnp.bfloat16
F32 = jnp.float32
NT = (((1,), (1,)), ((), ()))
NN = (((1,), (0,)), ((), ()))
TN = (((0,), (0,)), ((), ()))
MIB = 1 << 20


def dotg(a, b, dims=NN):
    return lax.dot_general(a, b, dims, preferred_element_type=F32)


def rotate(x, cos, sin):
    first = lax.broadcasted_iota(jnp.int32, (x.shape[0], 128), 1) % HD < HD // 2
    parts = []
    for a in range(0, x.shape[1], 128):
        v = x[:, a : a + 128]
        swapped = jnp.where(first, pltpu.roll(v, 96, 1), pltpu.roll(v, 32, 1))
        parts.append(v * cos + swapped * sin)
    return jnp.concatenate(parts, axis=1) if len(parts) > 1 else parts[0]


def qkv_kernel(x_ref, wq_ref, wk_ref, wv_ref, cos_ref, sin_ref, o_ref):
    width = wq_ref.shape[1]
    x, cos, sin = x_ref[...], cos_ref[...], sin_ref[...]
    o_ref[:, :width] = rotate(dotg(x, wq_ref[...]), cos, sin).astype(BF)
    o_ref[:, width : 2 * width] = rotate(dotg(x, wk_ref[...]), cos, sin).astype(BF)
    o_ref[:, 2 * width :] = dotg(x, wv_ref[...]).astype(BF)


def project(x, w_query, w_key, w_value, cos, sin, blk=256):
    rows, depth = x.shape
    width = w_query.shape[1]
    weight = pl.BlockSpec((depth, width), lambda i: (0, 0))
    angle = pl.BlockSpec((blk, 128), lambda i: (i, 0))
    return pl.pallas_call(
        qkv_kernel,
        grid=(rows // blk,),
        in_specs=[pl.BlockSpec((blk, depth), lambda i: (i, 0)), weight, weight, weight, angle, angle],
        out_specs=pl.BlockSpec((blk, 3 * width), lambda i: (i, 0)),
        out_shape=jax.ShapeDtypeStruct((rows, 3 * width), BF),
        compiler_params=pltpu.CompilerParams(vmem_limit_bytes=40 * MIB),
        cost_estimate=pl.CostEstimate(
            flops=6 * rows * depth * width, bytes_accessed=8 * rows * depth, transcendentals=0
        ),
        name="project",
    )(x, w_query, w_key, w_value, cos, sin)


def attend_kernel(len_ref, q_ref, k_ref, v_ref, o_ref, lse_ref, vt, *, blk):
    i = pl.program_id(1)

    @pl.when(i == 0)
    def _():
        vt[...] = jnp.transpose(v_ref[...])

    length = len_ref[0]
    lane = lax.broadcasted_iota(jnp.int32, (blk, 128), 1)
    q = q_ref[...] * jnp.asarray(0.125, BF)
    zero = jnp.zeros_like(q)
    qs = (jnp.where(lane < HD, q, zero), jnp.where(lane < HD, zero, q))

    def step(j, carry, diag):
        start = pl.multiple_of(j * blk, blk)
        kb = k_ref[pl.ds(start, blk), :]
        out = []
        for h in range(2):
            m, l, acc = carry[h]
            s = dotg(kb, qs[h], NT)
            if diag:
                key = lax.broadcasted_iota(jnp.int32, (blk, blk), 0)
                qry = lax.broadcasted_iota(jnp.int32, (blk, blk), 1)
                s = jnp.where((key <= qry) & (key + start < length), s, -1e30)
            mn = jnp.maximum(m, jnp.max(s, axis=0, keepdims=True))
            p = jnp.exp(s - mn)
            al = jnp.exp(m - mn)
            l = l * al + jnp.sum(p, axis=0, keepdims=True)
            vb = vt[HD * h : HD * h + HD, pl.ds(start, blk)]
            acc = acc * al + dotg(vb, p.astype(BF))
            out.append((mn, l, acc))
        return tuple(out)

    init = tuple(
        (jnp.full((1, blk), -1e30, F32), jnp.zeros((1, blk), F32), jnp.zeros((HD, blk), F32))
        for _ in range(2)
    )
    c = lax.fori_loop(0, i, lambda j, c: step(j, c, False), init)
    c = step(i, c, True)
    ot = jnp.concatenate([c[h][2] / c[h][1] for h in range(2)], axis=0)
    o_ref[...] = jnp.transpose(ot).astype(BF)
    lse_ref[0] = jnp.concatenate([c[h][0] + jnp.log(c[h][1]) for h in range(2)], axis=0)


def attend(length, joint, width, blk=512):
    rows = joint.shape[0]
    pairs, blocks = width // 128, rows // blk
    return pl.pallas_call(
        functools.partial(attend_kernel, blk=blk),
        grid_spec=pltpu.PrefetchScalarGridSpec(
            num_scalar_prefetch=1,
            grid=(pairs, blocks),
            in_specs=[
                pl.BlockSpec((blk, 128), lambda p, i, *_: (i, p)),
                pl.BlockSpec((rows, 128), lambda p, i, *_: (0, pairs + p)),
                pl.BlockSpec((rows, 128), lambda p, i, *_: (0, 2 * pairs + p)),
            ],
            out_specs=[
                pl.BlockSpec((blk, 128), lambda p, i, *_: (i, p)),
                pl.BlockSpec((1, 2, blk), lambda p, i, *_: (p, 0, i)),
            ],
            scratch_shapes=[pltpu.VMEM((128, rows), BF)],
        ),
        out_shape=[
            jax.ShapeDtypeStruct((rows, width), BF),
            jax.ShapeDtypeStruct((pairs, 2, rows), F32),
        ],
        compiler_params=pltpu.CompilerParams(vmem_limit_bytes=40 * MIB),
        cost_estimate=pl.CostEstimate(
            flops=16 * rows * rows * width, bytes_accessed=8 * rows * width, transcendentals=0
        ),
        name="attend",
    )(length, joint, joint, joint)


def attend_back_kernel(
    len_ref, q_ref, k_ref, v_ref, o_ref, do_ref, lse_ref, cos_ref, sin_ref,
    dq_ref, dk_ref, dv_ref, kt, dlt, dqt, *, blk, blocks,
):
    j = pl.program_id(1)
    length = len_ref[0]

    @pl.when(j == 0)
    def _():
        kt[...] = jnp.transpose(k_ref[...])
        dqt[...] = jnp.zeros_like(dqt)

        def body(i, _):
            at = pl.ds(pl.multiple_of(i * blk, blk), blk)
            both = jnp.transpose(do_ref[at, :].astype(F32) * o_ref[at, :].astype(F32))
            for h in range(2):
                dlt[h : h + 1, at] = jnp.sum(both[HD * h : HD * h + HD], axis=0, keepdims=True)
            return 0

        lax.fori_loop(0, blocks, body, 0)

    js = pl.multiple_of(j * blk, blk)
    lane = lax.broadcasted_iota(jnp.int32, (blk, 128), 1)
    kb = k_ref[pl.ds(js, blk), :] * jnp.asarray(0.125, BF)
    vb = v_ref[pl.ds(js, blk), :]
    zero = jnp.zeros_like(kb)
    ks = (jnp.where(lane < HD, kb, zero), jnp.where(lane < HD, zero, kb))
    vs = (jnp.where(lane < HD, vb, zero), jnp.where(lane < HD, zero, vb))

    def step(i, carry, diag):
        at = pl.ds(pl.multiple_of(i * blk, blk), blk)
        qb, dob = q_ref[at, :], do_ref[at, :]
        out = []
        for h in range(2):
            dk, dv = carry[h]
            s = dotg(ks[h], qb, NT)
            if diag:
                key = lax.broadcasted_iota(jnp.int32, (blk, blk), 0)
                qry = lax.broadcasted_iota(jnp.int32, (blk, blk), 1)
                s = jnp.where((key <= qry) & (key + js < length), s, -1e30)
            p = jnp.exp(s - lse_ref[0, h : h + 1, at])
            dp = dotg(vs[h], dob, NT)
            ds = (p * (dp - dlt[h : h + 1, at])).astype(BF)
            dv = dv + dotg(p.astype(BF), dob)
            dk = dk + dotg(ds, qb)
            dqt[HD * h : HD * h + HD, at] += dotg(kt[HD * h : HD * h + HD, pl.ds(js, blk)], ds)
            out.append((dk, dv))
        return tuple(out)

    z = jnp.zeros((blk, 128), F32)
    c = step(j, ((z, z), (z, z)), True)
    c = lax.fori_loop(j + 1, blocks, lambda i, c: step(i, c, False), c)
    grad = jnp.where(lane < HD, c[0][0], c[1][0]) * 0.125
    dk_ref[...] = rotate(grad, cos_ref[pl.ds(js, blk), :], -sin_ref[pl.ds(js, blk), :]).astype(BF)
    dv_ref[...] = jnp.where(lane < HD, c[0][1], c[1][1]).astype(BF)

    @pl.when(j == blocks - 1)
    def _():
        def body(i, _):
            at = pl.ds(pl.multiple_of(i * blk, blk), blk)
            grad = jnp.transpose(dqt[:, at]) * 0.125
            dq_ref[at, :] = rotate(grad, cos_ref[at, :], -sin_ref[at, :]).astype(BF)
            return 0

        lax.fori_loop(0, blocks, body, 0)


def attend_back(length, joint, mixed, dmixed, lse, cos, sin, width, blk=512):
    rows = joint.shape[0]
    pairs, blocks = width // 128, rows // blk
    full = lambda off: pl.BlockSpec((rows, 128), lambda p, j, *_: (0, off * pairs + p))
    angle = pl.BlockSpec((rows, 128), lambda p, j, *_: (0, 0))
    block = pl.BlockSpec((blk, 128), lambda p, j, *_: (j, p))
    return pl.pallas_call(
        functools.partial(attend_back_kernel, blk=blk, blocks=blocks),
        grid_spec=pltpu.PrefetchScalarGridSpec(
            num_scalar_prefetch=1,
            grid=(pairs, blocks),
            in_specs=[full(0), full(1), full(2), full(0), full(0)]
            + [pl.BlockSpec((1, 2, rows), lambda p, j, *_: (p, 0, 0)), angle, angle],
            out_specs=[full(0), block, block],
            scratch_shapes=[
                pltpu.VMEM((128, rows), BF),
                pltpu.VMEM((2, rows), F32),
                pltpu.VMEM((128, rows), F32),
            ],
        ),
        out_shape=[jax.ShapeDtypeStruct((rows, width), BF)] * 3,
        compiler_params=pltpu.CompilerParams(vmem_limit_bytes=48 * MIB),
        cost_estimate=pl.CostEstimate(
            flops=30 * rows * rows * width, bytes_accessed=16 * rows * width, transcendentals=0
        ),
        name="attend_back",
    )(length, joint, joint, joint, mixed, dmixed, lse, cos, sin)


def norm_parts(values):
    average = jnp.mean(values, axis=-1, keepdims=True)
    centred = values - average
    scale = lax.rsqrt(jnp.mean(centred * centred, axis=-1, keepdims=True) + EPSILON)
    return centred * scale, scale


def norm_back(grad, hat, scale, gain):
    g = grad * gain
    back = scale * (
        g - jnp.mean(g, axis=-1, keepdims=True) - hat * jnp.mean(g * hat, axis=-1, keepdims=True)
    )
    return back, jnp.sum(grad * hat, axis=0), jnp.sum(grad, axis=0)


def gelu(v):
    return jax.nn.gelu(v, approximate=True)


def gelu_slope(v):
    c = 0.7978845608028654
    t = jnp.tanh(c * (v + 0.044715 * v * v * v))
    return 0.5 * (1.0 + t) + 0.5 * v * (1.0 - t * t) * c * (1.0 + 3 * 0.044715 * v * v)


def shift(x, axis, count, step):
    return lax.ppermute(x, axis, [((i + step) % count, i) for i in range(count)])


def bit_of(axis, bit):
    return (lax.axis_index(axis) >> bit) & 1


def flip(x, axis, bit):
    return lax.ppermute(x, axis, [(i, i ^ (1 << bit)) for i in range(lax.axis_size(axis))])


def halve(x, bit):
    b, half = bit_of("dp", bit), x.shape[0] // 2
    xs = x.reshape((2, half) + x.shape[1:])
    send = lax.dynamic_index_in_dim(xs, 1 - b, 0, False)
    keep = lax.dynamic_index_in_dim(xs, b, 0, False)
    return (keep.astype(F32) + flip(send, "dp", bit).astype(F32)).astype(BF)


def double(x, bit):
    b, other = bit_of("dp", bit), flip(x, "dp", bit)
    return jnp.where(b == 0, jnp.concatenate([x, other]), jnp.concatenate([other, x]))


def rows_sum(x):
    bits = (lax.axis_size("dp") - 1).bit_length()
    x = halve(x, 0)
    half = x.shape[0] // 2
    parts = [x[:half], x[half:]]
    outer = tuple(range(1, bits))
    orders = [outer, outer[1:] + outer[:1]]
    for i in range(len(outer)):
        parts = [halve(p, o[i]) for p, o in zip(parts, orders)]
    for i in reversed(range(len(outer))):
        parts = [double(p, o[i]) for p, o in zip(parts, orders)]
    return double(jnp.concatenate(parts), 0)


def small_sum(x):
    for axis in ("tensor", "dp"):
        for bit in range((lax.axis_size(axis) - 1).bit_length()):
            x = x + flip(x, axis, bit)
    return x


def shards(
    tokens,
    lengths,
    cotangent,
    w_query,
    w_key,
    w_value,
    w_out,
    up_weight,
    bias_up,
    down_weight,
    bias_down,
    norm_gains,
    norm_shifts,
):
    rows, _, depth = tokens.shape
    groups, replicas = lax.axis_size("tensor"), lax.axis_size("dp")
    me, replica = lax.axis_index("tensor"), lax.axis_index("dp")
    slots = rows * groups
    width = w_query.shape[1]
    hidden = up_weight.shape[1]
    x = tokens.reshape(rows, depth).astype(F32)
    positions = me * rows + jnp.arange(rows)
    valid = (positions < lengths[0]).astype(F32)[:, None]

    def others(v):
        return [shift(v, "tensor", groups, r) for r in range(1, groups)]

    def in_order(own, rest):
        if groups == 2:
            a, b = jnp.concatenate([own, rest[0]]), jnp.concatenate([rest[0], own])
            return jnp.where(me == 0, a, b)
        stacked = jnp.stack([own] + rest)
        return jnp.roll(stacked, me, axis=0).reshape((-1,) + own.shape[1:])

    def shared_sum(part):
        total = part(0)
        for r in range(1, groups):
            total = total + shift(part(r).astype(BF), "tensor", groups, groups - r).astype(F32)
        return total

    def rows_of(v, r):
        return lax.dynamic_slice_in_dim(v, (me + r) % groups * rows, rows, 0)

    hat0, scale0 = norm_parts(x)
    normed_one = (hat0 * norm_gains[0] + norm_shifts[0]).astype(BF)
    normed_one_all = in_order(normed_one, others(normed_one))
    up_piece = lax.dynamic_slice_in_dim(up_weight, replica * (depth // replicas), depth // replicas, 0)
    down_piece = lax.dynamic_slice_in_dim(
        down_weight, replica * (hidden // replicas), hidden // replicas, 0
    )
    ups = [up_weight] + [lax.all_gather(p, "dp", axis=0, tiled=True) for p in others(up_piece)]
    downs = [down_weight] + [lax.all_gather(p, "dp", axis=0, tiled=True) for p in others(down_piece)]
    biases = [b.astype(F32) for b in [bias_up] + others(bias_up)]

    freqs = 10000.0 ** (-jnp.arange(HD // 2).astype(F32) * 2.0 / HD)
    angles = jnp.arange(slots).astype(F32)[:, None] * freqs[None, :]
    cosine, sine = jnp.cos(angles), jnp.sin(angles)
    cosine = jnp.concatenate([cosine] * 4, axis=1)
    sine = jnp.concatenate([-sine, sine] * 2, axis=1)
    joint = project(normed_one_all, w_query, w_key, w_value, cosine, sine)
    mixed, lse = attend(lengths, joint, width)
    attn_sum = shared_sum(lambda r: dotg(rows_of(mixed, r), w_out))

    hat1, scale1 = norm_parts(attn_sum)
    resid = x + hat1 * norm_gains[1] + norm_shifts[1]
    hat2, scale2 = norm_parts(resid)
    normed_two = (hat2 * norm_gains[2] + norm_shifts[2]).astype(BF)
    normed_two_rest = others(normed_two)
    pres = [dotg(normed_two, up) + b for up, b in zip(ups, biases)]
    acts = [gelu(p).astype(BF) for p in pres]
    branch = bias_down.astype(F32)
    for a, down in zip(acts, downs):
        branch = branch + dotg(a, down)
    hat3, scale3 = norm_parts(branch)
    layer_out = (valid * (resid + hat3 * norm_gains[3] + norm_shifts[3])).astype(BF)

    g_out = cotangent.reshape(rows, depth).astype(F32) * valid
    g_branch, gain3, shift3 = norm_back(g_out, hat3, scale3, norm_gains[3])
    g_branch_low = g_branch.astype(BF)
    g_branch_rest = others(g_branch_low)
    bias_down_sum = jnp.sum(g_branch_low.astype(F32), axis=0)
    g_pres = [
        (dotg(g_branch_low, down, NT) * gelu_slope(p)).astype(BF) for p, down in zip(pres, downs)
    ]
    g_normed_two = sum(dotg(g, up, NT) for g, up in zip(g_pres, ups))
    back2, gain2, shift2 = norm_back(g_normed_two, hat2, scale2, norm_gains[2])
    g_resid = g_out + back2
    g_attn, gain1, shift1 = norm_back(g_resid, hat1, scale1, norm_gains[1])
    g_attn_low = g_attn.astype(BF)
    g_attn_all = in_order(g_attn_low, others(g_attn_low))

    bias_own = biases[0]
    g_pre_own, act_own = [g_pres[0]], [acts[0]]
    for n2, gb in zip(normed_two_rest, g_branch_rest):
        pre = dotg(n2, up_weight) + bias_own
        act_own.append(gelu(pre).astype(BF))
        g_pre_own.append((dotg(gb, down_weight, NT) * gelu_slope(pre)).astype(BF))
    grad_down = sum(dotg(a, g, TN) for a, g in zip(act_own, [g_branch_low] + g_branch_rest))
    grad_up = sum(dotg(n, g, TN) for n, g in zip([normed_two] + normed_two_rest, g_pre_own))
    bias_up_sum = sum(jnp.sum(g.astype(F32), axis=0) for g in g_pre_own)
    grad_up, grad_down = (lax.psum(g.astype(BF), "dp").astype(F32) for g in (grad_up, grad_down))

    g_mixed = dotg(g_attn_all, w_out, NT).astype(BF)
    grad_out = dotg(mixed, g_attn_all, TN)
    g_query, g_key, g_value = attend_back(
        lengths, joint, mixed, g_mixed, lse, cosine, sine, width
    )
    grads = [dotg(normed_one_all, g, TN).astype(BF) for g in (g_query, g_key, g_value)]
    packed = rows_sum(
        jnp.concatenate(grads + [grad_out.astype(BF).reshape(depth, width)])
    )
    grad_query, grad_key, grad_value = (packed[i * depth : (i + 1) * depth].astype(F32) for i in range(3))
    grad_out = packed[3 * depth :].reshape(width, depth).astype(F32)

    def share(r):
        return (
            dotg(rows_of(g_query, r), w_query, NT)
            + dotg(rows_of(g_key, r), w_key, NT)
            + dotg(rows_of(g_value, r), w_value, NT)
        )

    g_normed_one = shared_sum(share)
    back0, gain0, shift0 = norm_back(g_normed_one, hat0, scale0, norm_gains[0])
    grad_tokens = (g_resid + back0).astype(BF)

    placed = lax.dynamic_update_slice(
        jnp.zeros((groups * hidden,), F32), bias_up_sum, (me * hidden,)
    ).reshape(-1, depth)
    early = small_sum(
        jnp.concatenate(
            [jnp.stack([gain1, gain2, gain3, shift1, shift2, shift3, bias_down_sum]), placed]
        )
    )
    late = small_sum(jnp.stack([gain0, shift0]))
    grad_gains = jnp.concatenate([late[:1], early[:3]])
    grad_shifts = jnp.concatenate([late[1:], early[3:6]])
    grad_bias_up = lax.dynamic_slice_in_dim(early[7:].reshape(-1), me * hidden, hidden, 0)
    whole = (rows, 1, depth)
    return (
        layer_out.reshape(whole),
        grad_tokens.reshape(whole),
        grad_query,
        grad_key,
        grad_value,
        grad_out,
        grad_up,
        grad_bias_up,
        grad_down,
        early[6],
        grad_gains,
        grad_shifts,
    )


def solution(mesh):
    wide, tall = P(None, "tensor"), P("tensor", None)
    acts = P("tensor", "dp", None)
    return jax.shard_map(
        shards,
        mesh=mesh,
        in_specs=(acts, P("dp"), acts, wide, wide, wide, tall, wide, P("tensor"), tall, P(), P(), P()),
        out_specs=(acts, acts, wide, wide, wide, tall, wide, P("tensor"), tall, P(), P(), P()),
        check_vma=False,
    )
```

```python
import functools
import jax
import jax.numpy as jnp
from jax import lax
from jax.experimental import pallas as pl
from jax.experimental.pallas import tpu as pltpu
from jax.sharding import PartitionSpec as P

HD = 64
EPSILON = 1e-05
BF = jnp.bfloat16
F32 = jnp.float32
NT = (((1,), (1,)), ((), ()))
NN = (((1,), (0,)), ((), ()))
TN = (((0,), (0,)), ((), ()))
MIB = 1 << 20


def dotg(a, b, dims=NN):
    return lax.dot_general(a, b, dims, preferred_element_type=F32)


def rotate(x, cos, sin):
    first = lax.broadcasted_iota(jnp.int32, (x.shape[0], 128), 1) % HD < HD // 2
    parts = []
    for a in range(0, x.shape[1], 128):
        v = x[:, a : a + 128]
        swapped = jnp.where(first, pltpu.roll(v, 96, 1), pltpu.roll(v, 32, 1))
        parts.append(v * cos + swapped * sin)
    return jnp.concatenate(parts, axis=1) if len(parts) > 1 else parts[0]


def qkv_kernel(x_ref, wq_ref, wk_ref, wv_ref, cos_ref, sin_ref, o_ref):
    width = wq_ref.shape[1]
    x, cos, sin = x_ref[...], cos_ref[...], sin_ref[...]
    o_ref[:, :width] = rotate(dotg(x, wq_ref[...]), cos, sin).astype(BF)
    o_ref[:, width : 2 * width] = rotate(dotg(x, wk_ref[...]), cos, sin).astype(BF)
    o_ref[:, 2 * width :] = dotg(x, wv_ref[...]).astype(BF)


def project(x, w_query, w_key, w_value, cos, sin, blk=256):
    rows, depth = x.shape
    width = w_query.shape[1]
    weight = pl.BlockSpec((depth, width), lambda i: (0, 0))
    angle = pl.BlockSpec((blk, 128), lambda i: (i, 0))
    return pl.pallas_call(
        qkv_kernel,
        grid=(rows // blk,),
        in_specs=[pl.BlockSpec((blk, depth), lambda i: (i, 0)), weight, weight, weight, angle, angle],
        out_specs=pl.BlockSpec((blk, 3 * width), lambda i: (i, 0)),
        out_shape=jax.ShapeDtypeStruct((rows, 3 * width), BF),
        compiler_params=pltpu.CompilerParams(vmem_limit_bytes=40 * MIB),
        cost_estimate=pl.CostEstimate(
            flops=6 * rows * depth * width, bytes_accessed=8 * rows * depth, transcendentals=0
        ),
        name="project",
    )(x, w_query, w_key, w_value, cos, sin)


def attend_kernel(len_ref, q_ref, k_ref, v_ref, o_ref, lse_ref, vt, *, blk):
    i = pl.program_id(1)

    @pl.when(i == 0)
    def _():
        vt[...] = jnp.transpose(v_ref[...])

    length = len_ref[0]
    lane = lax.broadcasted_iota(jnp.int32, (blk, 128), 1)
    q = q_ref[...] * jnp.asarray(0.125, BF)
    zero = jnp.zeros_like(q)
    qs = (jnp.where(lane < HD, q, zero), jnp.where(lane < HD, zero, q))

    def step(j, carry, diag):
        start = pl.multiple_of(j * blk, blk)
        kb = k_ref[pl.ds(start, blk), :]
        out = []
        for h in range(2):
            m, l, acc = carry[h]
            s = dotg(kb, qs[h], NT)
            if diag:
                key = lax.broadcasted_iota(jnp.int32, (blk, blk), 0)
                qry = lax.broadcasted_iota(jnp.int32, (blk, blk), 1)
                s = jnp.where((key <= qry) & (key + start < length), s, -1e30)
            mn = jnp.maximum(m, jnp.max(s, axis=0, keepdims=True))
            p = jnp.exp(s - mn)
            al = jnp.exp(m - mn)
            l = l * al + jnp.sum(p, axis=0, keepdims=True)
            vb = vt[HD * h : HD * h + HD, pl.ds(start, blk)]
            acc = acc * al + dotg(vb, p.astype(BF))
            out.append((mn, l, acc))
        return tuple(out)

    init = tuple(
        (jnp.full((1, blk), -1e30, F32), jnp.zeros((1, blk), F32), jnp.zeros((HD, blk), F32))
        for _ in range(2)
    )
    c = lax.fori_loop(0, i, lambda j, c: step(j, c, False), init)
    c = step(i, c, True)
    ot = jnp.concatenate([c[h][2] / c[h][1] for h in range(2)], axis=0)
    o_ref[...] = jnp.transpose(ot).astype(BF)
    lse_ref[0] = jnp.concatenate([c[h][0] + jnp.log(c[h][1]) for h in range(2)], axis=0)


def attend(length, joint, width, blk=512):
    rows = joint.shape[0]
    pairs, blocks = width // 128, rows // blk
    return pl.pallas_call(
        functools.partial(attend_kernel, blk=blk),
        grid_spec=pltpu.PrefetchScalarGridSpec(
            num_scalar_prefetch=1,
            grid=(pairs, blocks),
            in_specs=[
                pl.BlockSpec((blk, 128), lambda p, i, *_: (i, p)),
                pl.BlockSpec((rows, 128), lambda p, i, *_: (0, pairs + p)),
                pl.BlockSpec((rows, 128), lambda p, i, *_: (0, 2 * pairs + p)),
            ],
            out_specs=[
                pl.BlockSpec((blk, 128), lambda p, i, *_: (i, p)),
                pl.BlockSpec((1, 2, blk), lambda p, i, *_: (p, 0, i)),
            ],
            scratch_shapes=[pltpu.VMEM((128, rows), BF)],
        ),
        out_shape=[
            jax.ShapeDtypeStruct((rows, width), BF),
            jax.ShapeDtypeStruct((pairs, 2, rows), F32),
        ],
        compiler_params=pltpu.CompilerParams(vmem_limit_bytes=40 * MIB),
        cost_estimate=pl.CostEstimate(
            flops=rows * width, bytes_accessed=rows * width, transcendentals=0
        ),
        name="attend",
    )(length, joint, joint, joint)


def attend_back_kernel(
    len_ref, q_ref, k_ref, v_ref, o_ref, do_ref, lse_ref, cos_ref, sin_ref,
    dq_ref, dk_ref, dv_ref, kt, dlt, dqt, *, blk, blocks,
):
    j = pl.program_id(1)
    length = len_ref[0]

    @pl.when(j == 0)
    def _():
        kt[...] = jnp.transpose(k_ref[...])
        dqt[...] = jnp.zeros_like(dqt)

        def body(i, _):
            at = pl.ds(pl.multiple_of(i * blk, blk), blk)
            both = jnp.transpose(do_ref[at, :].astype(F32) * o_ref[at, :].astype(F32))
            for h in range(2):
                dlt[h : h + 1, at] = jnp.sum(both[HD * h : HD * h + HD], axis=0, keepdims=True)
            return 0

        lax.fori_loop(0, blocks, body, 0)

    js = pl.multiple_of(j * blk, blk)
    lane = lax.broadcasted_iota(jnp.int32, (blk, 128), 1)
    kb = k_ref[pl.ds(js, blk), :] * jnp.asarray(0.125, BF)
    vb = v_ref[pl.ds(js, blk), :]
    zero = jnp.zeros_like(kb)
    ks = (jnp.where(lane < HD, kb, zero), jnp.where(lane < HD, zero, kb))
    vs = (jnp.where(lane < HD, vb, zero), jnp.where(lane < HD, zero, vb))

    def step(i, carry, diag):
        at = pl.ds(pl.multiple_of(i * blk, blk), blk)
        qb, dob = q_ref[at, :], do_ref[at, :]
        out = []
        for h in range(2):
            dk, dv = carry[h]
            s = dotg(ks[h], qb, NT)
            if diag:
                key = lax.broadcasted_iota(jnp.int32, (blk, blk), 0)
                qry = lax.broadcasted_iota(jnp.int32, (blk, blk), 1)
                s = jnp.where((key <= qry) & (key + js < length), s, -1e30)
            p = jnp.exp(s - lse_ref[0, h : h + 1, at])
            dp = dotg(vs[h], dob, NT)
            ds = (p * (dp - dlt[h : h + 1, at])).astype(BF)
            dv = dv + dotg(p.astype(BF), dob)
            dk = dk + dotg(ds, qb)
            dqt[HD * h : HD * h + HD, at] += dotg(kt[HD * h : HD * h + HD, pl.ds(js, blk)], ds)
            out.append((dk, dv))
        return tuple(out)

    z = jnp.zeros((blk, 128), F32)
    c = step(j, ((z, z), (z, z)), True)
    c = lax.fori_loop(j + 1, blocks, lambda i, c: step(i, c, False), c)
    grad = jnp.where(lane < HD, c[0][0], c[1][0]) * 0.125
    dk_ref[...] = rotate(grad, cos_ref[pl.ds(js, blk), :], -sin_ref[pl.ds(js, blk), :]).astype(BF)
    dv_ref[...] = jnp.where(lane < HD, c[0][1], c[1][1]).astype(BF)

    @pl.when(j == blocks - 1)
    def _():
        def body(i, _):
            at = pl.ds(pl.multiple_of(i * blk, blk), blk)
            grad = jnp.transpose(dqt[:, at]) * 0.125
            dq_ref[at, :] = rotate(grad, cos_ref[at, :], -sin_ref[at, :]).astype(BF)
            return 0

        lax.fori_loop(0, blocks, body, 0)


def attend_back(length, joint, mixed, dmixed, lse, cos, sin, width, blk=512):
    rows = joint.shape[0]
    pairs, blocks = width // 128, rows // blk
    full = lambda off: pl.BlockSpec((rows, 128), lambda p, j, *_: (0, off * pairs + p))
    angle = pl.BlockSpec((rows, 128), lambda p, j, *_: (0, 0))
    block = pl.BlockSpec((blk, 128), lambda p, j, *_: (j, p))
    return pl.pallas_call(
        functools.partial(attend_back_kernel, blk=blk, blocks=blocks),
        grid_spec=pltpu.PrefetchScalarGridSpec(
            num_scalar_prefetch=1,
            grid=(pairs, blocks),
            in_specs=[full(0), full(1), full(2), full(0), full(0)]
            + [pl.BlockSpec((1, 2, rows), lambda p, j, *_: (p, 0, 0)), angle, angle],
            out_specs=[full(0), block, block],
            scratch_shapes=[
                pltpu.VMEM((128, rows), BF),
                pltpu.VMEM((2, rows), F32),
                pltpu.VMEM((128, rows), F32),
            ],
        ),
        out_shape=[jax.ShapeDtypeStruct((rows, width), BF)] * 3,
        compiler_params=pltpu.CompilerParams(vmem_limit_bytes=48 * MIB),
        cost_estimate=pl.CostEstimate(
            flops=rows * width, bytes_accessed=rows * width, transcendentals=0
        ),
        name="attend_back",
    )(length, joint, joint, joint, mixed, dmixed, lse, cos, sin)


def gelu_parts(v):
    c = 0.7978845608028654
    return c, jnp.tanh(c * (v + 0.044715 * v * v * v))


def gelu(v):
    return 0.5 * v * (1.0 + gelu_parts(v)[1])


def gelu_both(v):
    c, t = gelu_parts(v)
    half = 0.5 * (1.0 + t)
    return v * half, half + 0.5 * v * (1.0 - t * t) * c * (1.0 + 3 * 0.044715 * v * v)


def norm_parts(values):
    average = jnp.mean(values, axis=-1, keepdims=True)
    centred = values - average
    scale = lax.rsqrt(jnp.mean(centred * centred, axis=-1, keepdims=True) + EPSILON)
    return centred * scale, scale


def norm_back(grad, hat, scale, gain):
    g = grad * gain
    return scale * (
        g - jnp.mean(g, axis=-1, keepdims=True) - hat * jnp.mean(g * hat, axis=-1, keepdims=True)
    )


def column_sum(v):
    return jnp.sum(v, axis=0, keepdims=True)


def valid_rows(info_ref, start, count):
    at = info_ref[1] + start + lax.broadcasted_iota(jnp.int32, (count, 1), 0)
    return (at < info_ref[0]).astype(F32)


def loop_rows(rows, blk, body):
    def step(i, _):
        body(pl.multiple_of(i * blk, blk))
        return 0

    lax.fori_loop(0, rows // blk, step, 0)


def feed_kernel(info_ref, *refs, groups, chunks, sub):
    x_ref, bias_ref, resid_ref, cot_ref, bd_ref, gain_ref, shift_ref = refs[:7]
    ups, downs = refs[7 : 7 + groups], refs[7 + groups : 7 + 2 * groups]
    pre_ref, act_ref, out_ref, gb_ref, sums_ref, acc = refs[7 + 2 * groups :]
    step = pl.program_id(0)
    rows = x_ref.shape[0]

    @pl.when(step == 0)
    def _():
        acc[...] = jnp.zeros_like(acc) + bd_ref[...].astype(F32)

    for g in range(groups):

        @pl.when(step // chunks == g)
        def _():
            for r in range(0, rows, sub):
                pre = dotg(x_ref[r : r + sub], ups[g][...]) + bias_ref[0]
                pre_ref[r : r + sub] = pre
                act = gelu(pre).astype(BF)
                if g == 0:
                    act_ref[r : r + sub] = act
                acc[r : r + sub] += dotg(act, downs[g][...])

    @pl.when(step == groups * chunks - 1)
    def _():
        sums_ref[...] = jnp.zeros_like(sums_ref)
        gain, shift = gain_ref[3:4], shift_ref[3:4]

        def body(r):
            at = pl.ds(r, 64)
            valid = valid_rows(info_ref, r, 64)
            hat, scale = norm_parts(acc[at])
            out_ref[at] = (valid * (resid_ref[at] + hat * gain + shift)).astype(BF)
            g_out = valid * cot_ref[at].astype(F32)
            low = norm_back(g_out, hat, scale, gain).astype(BF)
            gb_ref[at] = low
            sums_ref[0:1] += column_sum(g_out * hat)
            sums_ref[1:2] += column_sum(g_out)
            sums_ref[2:3] += column_sum(low.astype(F32))

        loop_rows(rows, 64, body)


def feed(info, x, biases, ups, downs, resid, cot, bias_down, gains, shifts, cols=512):
    rows, depth = x.shape
    groups, hidden = len(ups), ups[0].shape[1]
    chunks = hidden // cols
    once = lambda shape: pl.BlockSpec(shape, lambda s, *_: (0, 0), pipeline_mode=pl.Buffered(1))
    own = lambda g: (lambda s, *_: (0, jnp.clip(s - g * chunks, 0, chunks - 1)))
    own_t = lambda g: (lambda s, *_: (jnp.clip(s - g * chunks, 0, chunks - 1), 0))
    return pl.pallas_call(
        functools.partial(feed_kernel, groups=groups, chunks=chunks, sub=min(512, rows)),
        grid_spec=pltpu.PrefetchScalarGridSpec(
            num_scalar_prefetch=1,
            grid=(groups * chunks,),
            in_specs=[
                once((rows, depth)),
                pl.BlockSpec((1, 1, cols), lambda s, *_: (s, 0, 0)),
                once((rows, depth)),
                once((rows, depth)),
                once((1, depth)),
                once(gains.shape),
                once(gains.shape),
            ]
            + [pl.BlockSpec((depth, cols), own(g)) for g in range(groups)]
            + [pl.BlockSpec((cols, depth), own_t(g)) for g in range(groups)],
            out_specs=[
                pl.BlockSpec((rows, cols), lambda s, *_: (0, s)),
                pl.BlockSpec((rows, cols), own(0)),
                once((rows, depth)),
                once((rows, depth)),
                once((8, depth)),
            ],
            scratch_shapes=[pltpu.VMEM((rows, depth), F32)],
        ),
        out_shape=[
            jax.ShapeDtypeStruct((rows, groups * hidden), F32),
            jax.ShapeDtypeStruct((rows, hidden), BF),
            jax.ShapeDtypeStruct((rows, depth), BF),
            jax.ShapeDtypeStruct((rows, depth), BF),
            jax.ShapeDtypeStruct((8, depth), F32),
        ],
        compiler_params=pltpu.CompilerParams(vmem_limit_bytes=56 * MIB),
        cost_estimate=pl.CostEstimate(
            flops=rows * depth, bytes_accessed=rows * depth, transcendentals=0
        ),
        name="feed",
    )(info, x, biases.reshape(-1, 1, cols), resid, cot, bias_down, gains, shifts, *ups, *downs)


def feed_back_kernel(info_ref, *refs, groups, chunks, sub):
    gb_ref, pre_ref, resid_ref, attn_ref, cot_ref, gain_ref = refs[:6]
    ups, downs = refs[6 : 6 + groups], refs[6 + groups : 6 + 2 * groups]
    gp_ref, gr_ref, ga_ref, sums_ref, acc = refs[6 + 2 * groups :]
    step = pl.program_id(0)
    rows = gb_ref.shape[0]

    @pl.when(step == 0)
    def _():
        acc[...] = jnp.zeros_like(acc)

    for g in range(groups):

        @pl.when(step // chunks == g)
        def _():
            for r in range(0, rows, sub):
                grad = dotg(gb_ref[r : r + sub], downs[g][...], NT)
                low = (grad * gelu_both(pre_ref[r : r + sub])[1]).astype(BF)
                if g == 0:
                    gp_ref[r : r + sub] = low
                acc[r : r + sub] += dotg(low, ups[g][...], NT)

    @pl.when(step == groups * chunks - 1)
    def _():
        sums_ref[...] = jnp.zeros_like(sums_ref)

        def body(r):
            at = pl.ds(r, 64)
            g_out = valid_rows(info_ref, r, 64) * cot_ref[at].astype(F32)
            hat, scale = norm_parts(resid_ref[at])
            g_two = acc[at]
            g_resid = g_out + norm_back(g_two, hat, scale, gain_ref[2:3])
            gr_ref[at] = g_resid
            sums_ref[0:1] += column_sum(g_two * hat)
            sums_ref[1:2] += column_sum(g_two)
            hat, scale = norm_parts(attn_ref[at])
            ga_ref[at] = norm_back(g_resid, hat, scale, gain_ref[1:2]).astype(BF)
            sums_ref[2:3] += column_sum(g_resid * hat)
            sums_ref[3:4] += column_sum(g_resid)

        loop_rows(rows, 64, body)


def feed_back(info, gb, pre, ups, downs, resid, attn_sum, cot, gains, cols=512):
    rows, depth = gb.shape
    groups, hidden = len(ups), ups[0].shape[1]
    chunks = hidden // cols
    once = lambda shape: pl.BlockSpec(shape, lambda s, *_: (0, 0), pipeline_mode=pl.Buffered(1))
    own = lambda g: (lambda s, *_: (0, jnp.clip(s - g * chunks, 0, chunks - 1)))
    own_t = lambda g: (lambda s, *_: (jnp.clip(s - g * chunks, 0, chunks - 1), 0))
    return pl.pallas_call(
        functools.partial(feed_back_kernel, groups=groups, chunks=chunks, sub=min(512, rows)),
        grid_spec=pltpu.PrefetchScalarGridSpec(
            num_scalar_prefetch=1,
            grid=(groups * chunks,),
            in_specs=[
                once((rows, depth)),
                pl.BlockSpec((rows, cols), lambda s, *_: (0, s)),
                once((rows, depth)),
                once((rows, depth)),
                once((rows, depth)),
                once(gains.shape),
            ]
            + [pl.BlockSpec((depth, cols), own(g)) for g in range(groups)]
            + [pl.BlockSpec((cols, depth), own_t(g)) for g in range(groups)],
            out_specs=[
                pl.BlockSpec((rows, cols), own(0)),
                once((rows, depth)),
                once((rows, depth)),
                once((8, depth)),
            ],
            scratch_shapes=[pltpu.VMEM((rows, depth), F32)],
        ),
        out_shape=[
            jax.ShapeDtypeStruct((rows, hidden), BF),
            jax.ShapeDtypeStruct((rows, depth), F32),
            jax.ShapeDtypeStruct((rows, depth), BF),
            jax.ShapeDtypeStruct((8, depth), F32),
        ],
        compiler_params=pltpu.CompilerParams(vmem_limit_bytes=56 * MIB),
        cost_estimate=pl.CostEstimate(
            flops=rows * depth, bytes_accessed=rows * depth, transcendentals=0
        ),
        name="feed_back",
    )(info, gb, pre, resid, attn_sum, cot, gains, *ups, *downs)


def feed_grad_kernel(*refs, groups):
    up_ref, down_ref, bias_ref, act_ref, gp_ref = refs[:5]
    n2s, gbs = refs[5 : 5 + groups], refs[5 + groups : 5 + 2 * groups]
    grad_ref, sum_ref = refs[5 + 2 * groups :]
    act, gp = act_ref[...], gp_ref[...]
    dup = dotg(gp, n2s[0][...], TN)
    ddown = dotg(act, gbs[0][...], TN)
    sums = column_sum(gp.astype(F32))
    for g in range(1, groups):
        pre = dotg(n2s[g][...], up_ref[...]) + bias_ref[0]
        act, slope = gelu_both(pre)
        act = act.astype(BF)
        gp = (dotg(gbs[g][...], down_ref[...], NT) * slope).astype(BF)
        dup += dotg(gp, n2s[g][...], TN)
        ddown += dotg(act, gbs[g][...], TN)
        sums += column_sum(gp.astype(F32))
    grad_ref[0] = dup.astype(BF)
    grad_ref[1] = ddown.astype(BF)
    sum_ref[0] = sums


def feed_grad(up, down, bias, act, gp, n2s, gbs, cols=256):
    rows, depth = n2s[0].shape
    groups, hidden = len(n2s), up.shape[1]
    once = lambda shape: pl.BlockSpec(shape, lambda s: (0, 0), pipeline_mode=pl.Buffered(1))
    wide = lambda count: pl.BlockSpec((count, cols), lambda s: (0, s))
    tall = pl.BlockSpec((cols, depth), lambda s: (s, 0))
    flat = pl.BlockSpec((1, 1, cols), lambda s: (s, 0, 0))
    return pl.pallas_call(
        functools.partial(feed_grad_kernel, groups=groups),
        grid=(hidden // cols,),
        in_specs=[wide(depth), tall, flat, wide(rows), wide(rows)] + [once((rows, depth))] * (2 * groups),
        out_specs=[pl.BlockSpec((2, cols, depth), lambda s: (0, s, 0)), flat],
        out_shape=[
            jax.ShapeDtypeStruct((2, hidden, depth), BF),
            jax.ShapeDtypeStruct((hidden // cols, 1, cols), F32),
        ],
        compiler_params=pltpu.CompilerParams(vmem_limit_bytes=56 * MIB),
        cost_estimate=pl.CostEstimate(
            flops=(8 * groups - 4) * rows * depth * hidden, bytes_accessed=20 * rows * depth, transcendentals=0
        ),
        name="feed_grad",
    )(up, down, bias.reshape(-1, 1, cols), act, gp, *n2s, *gbs)


def shift(x, axis, count, step):
    return lax.ppermute(x, axis, [((i + step) % count, i) for i in range(count)])


def bit_of(axis, bit):
    return (lax.axis_index(axis) >> bit) & 1


def flip(x, axis, bit):
    return lax.ppermute(x, axis, [(i, i ^ (1 << bit)) for i in range(lax.axis_size(axis))])


def halve(x, bit):
    b, half = bit_of("dp", bit), x.shape[0] // 2
    xs = x.reshape((2, half) + x.shape[1:])
    send = lax.dynamic_index_in_dim(xs, 1 - b, 0, False)
    keep = lax.dynamic_index_in_dim(xs, b, 0, False)
    return (keep.astype(F32) + flip(send, "dp", bit).astype(F32)).astype(BF)


def double(x, bit):
    b, other = bit_of("dp", bit), flip(x, "dp", bit)
    return jnp.where(b == 0, jnp.concatenate([x, other]), jnp.concatenate([other, x]))


def rows_sum(x):
    bits = (lax.axis_size("dp") - 1).bit_length()
    x = halve(x, 0)
    half = x.shape[0] // 2
    parts = [x[:half], x[half:]]
    outer = tuple(range(1, bits))
    orders = [outer, outer[1:] + outer[:1]]
    for i in range(len(outer)):
        parts = [halve(p, o[i]) for p, o in zip(parts, orders)]
    for i in reversed(range(len(outer))):
        parts = [double(p, o[i]) for p, o in zip(parts, orders)]
    return double(jnp.concatenate(parts), 0)


def small_sum(x):
    for axis in ("tensor", "dp"):
        for bit in range((lax.axis_size(axis) - 1).bit_length()):
            x = x + flip(x, axis, bit)
    return x


def shards(
    tokens,
    lengths,
    cotangent,
    w_query,
    w_key,
    w_value,
    w_out,
    up_weight,
    bias_up,
    down_weight,
    bias_down,
    norm_gains,
    norm_shifts,
):
    rows, _, depth = tokens.shape
    groups, replicas = lax.axis_size("tensor"), lax.axis_size("dp")
    me, replica = lax.axis_index("tensor"), lax.axis_index("dp")
    slots = rows * groups
    width = w_query.shape[1]
    hidden = up_weight.shape[1]
    x = tokens.reshape(rows, depth).astype(F32)
    positions = me * rows + jnp.arange(rows)
    valid = (positions < lengths[0]).astype(F32)[:, None]

    def others(v):
        return [shift(v, "tensor", groups, r) for r in range(1, groups)]

    def in_order(own, rest):
        if groups == 2:
            a, b = jnp.concatenate([own, rest[0]]), jnp.concatenate([rest[0], own])
            return jnp.where(me == 0, a, b)
        stacked = jnp.stack([own] + rest)
        return jnp.roll(stacked, me, axis=0).reshape((-1,) + own.shape[1:])

    def shared_sum(part):
        total = part(0)
        for r in range(1, groups):
            total = total + shift(part(r).astype(BF), "tensor", groups, groups - r).astype(F32)
        return total

    def rows_of(v, r):
        return lax.dynamic_slice_in_dim(v, (me + r) % groups * rows, rows, 0)

    up_piece = lax.dynamic_slice_in_dim(up_weight, replica * (depth // replicas), depth // replicas, 0)
    down_piece = lax.dynamic_slice_in_dim(
        down_weight, replica * (hidden // replicas), hidden // replicas, 0
    )
    up_pieces, down_pieces, bias_rest = others(up_piece), others(down_piece), others(bias_up)
    gather = lambda v: lax.all_gather(v, "dp", axis=0, tiled=True)

    hat0, scale0 = norm_parts(x)
    normed_one = (hat0 * norm_gains[0] + norm_shifts[0]).astype(BF)
    normed_one_all = in_order(normed_one, others(normed_one))
    freqs = 10000.0 ** (-jnp.arange(HD // 2).astype(F32) * 2.0 / HD)
    angles = jnp.arange(slots).astype(F32)[:, None] * freqs[None, :]
    cosine, sine = jnp.cos(angles), jnp.sin(angles)
    cosine = jnp.concatenate([cosine] * 4, axis=1)
    sine = jnp.concatenate([-sine, sine] * 2, axis=1)
    normed_one_all, up_pieces, down_pieces, bias_rest = lax.optimization_barrier(
        (normed_one_all, up_pieces, down_pieces, bias_rest)
    )
    joint = project(normed_one_all, w_query, w_key, w_value, cosine, sine)
    mixed, lse = attend(lengths, joint, width)
    attn_sum = shared_sum(lambda r: dotg(rows_of(mixed, r), w_out))
    up_rest, down_rest = [gather(p) for p in up_pieces], [gather(p) for p in down_pieces]
    attn_sum, up_rest, down_rest = lax.optimization_barrier((attn_sum, up_rest, down_rest))
    ups, downs = [up_weight] + up_rest, [down_weight] + down_rest
    biases = jnp.concatenate([bias_up] + bias_rest).astype(F32)

    info = jnp.stack([lengths[0], me * rows]).astype(jnp.int32)
    cot = cotangent.reshape(rows, depth)
    hat1, _ = norm_parts(attn_sum)
    resid = x + hat1 * norm_gains[1] + norm_shifts[1]
    hat2, _ = norm_parts(resid)
    normed_two = (hat2 * norm_gains[2] + norm_shifts[2]).astype(BF)
    normed_two_rest = others(normed_two)
    pre, act, layer_out, g_branch, sums3 = feed(
        info, normed_two, biases, ups, downs, resid, cot, bias_down.reshape(1, depth), norm_gains, norm_shifts
    )
    g_branch_rest = others(g_branch)
    g_branch, normed_two_rest = lax.optimization_barrier((g_branch, normed_two_rest))
    g_pre, g_resid, g_attn, sums21 = feed_back(
        info, g_branch, pre, ups, downs, resid, attn_sum, cot, norm_gains
    )
    g_attn_rest = others(g_attn)
    grad_feed, bias_up_sum = feed_grad(
        up_weight, down_weight, biases[:hidden], act, g_pre,
        [normed_two] + normed_two_rest, [g_branch] + g_branch_rest,
    )
    grad_feed = grad_feed.reshape(2 * hidden, depth)
    g_attn_rest, grad_feed = lax.optimization_barrier((g_attn_rest, grad_feed))
    grad_feed = lax.psum_scatter(grad_feed, "dp", scatter_dimension=0, tiled=True)
    g_attn_all = in_order(g_attn, g_attn_rest)

    g_mixed = dotg(g_attn_all, w_out, NT).astype(BF)
    grad_out = dotg(mixed, g_attn_all, TN)
    g_query, g_key, g_value = attend_back(
        lengths, joint, mixed, g_mixed, lse, cosine, sine, width
    )
    grads = [dotg(normed_one_all, g, TN).astype(BF) for g in (g_query, g_key, g_value)]
    packed = jnp.concatenate(grads + [grad_out.astype(BF).reshape(depth, width)])
    packed, grad_feed = lax.optimization_barrier((packed, grad_feed))
    grad_feed = lax.all_gather(grad_feed, "dp", axis=0, tiled=True)
    grad_up = jnp.transpose(grad_feed[:hidden]).astype(F32)
    grad_down = grad_feed[hidden:].astype(F32)
    packed = rows_sum(packed)
    grad_query, grad_key, grad_value = (packed[i * depth : (i + 1) * depth].astype(F32) for i in range(3))
    grad_out = packed[3 * depth :].reshape(width, depth).astype(F32)

    def share(r):
        return (
            dotg(rows_of(g_query, r), w_query, NT)
            + dotg(rows_of(g_key, r), w_key, NT)
            + dotg(rows_of(g_value, r), w_value, NT)
        )

    g_normed_one = shared_sum(share)
    back0 = norm_back(g_normed_one, hat0, scale0, norm_gains[0])
    gain0, shift0 = jnp.sum(g_normed_one * hat0, axis=0), jnp.sum(g_normed_one, axis=0)
    grad_tokens = (g_resid + back0).astype(BF)

    placed = lax.dynamic_update_slice(
        jnp.zeros((groups * hidden,), F32), bias_up_sum.reshape(-1), (me * hidden,)
    ).reshape(-1, depth)
    sums = small_sum(jnp.concatenate([sums3[:3], sums21[:4], jnp.stack([gain0, shift0]), placed]))
    grad_gains = jnp.stack([sums[7], sums[5], sums[3], sums[0]])
    grad_shifts = jnp.stack([sums[8], sums[6], sums[4], sums[1]])
    grad_bias_up = lax.dynamic_slice_in_dim(sums[9:].reshape(-1), me * hidden, hidden, 0)
    whole = (rows, 1, depth)
    return (
        layer_out.reshape(whole),
        grad_tokens.reshape(whole),
        grad_query,
        grad_key,
        grad_value,
        grad_out,
        grad_up,
        grad_bias_up,
        grad_down,
        sums[2],
        grad_gains,
        grad_shifts,
    )


def solution(mesh):
    wide, tall = P(None, "tensor"), P("tensor", None)
    acts = P("tensor", "dp", None)
    return jax.shard_map(
        shards,
        mesh=mesh,
        in_specs=(acts, P("dp"), acts, wide, wide, wide, tall, wide, P("tensor"), tall, P(), P(), P()),
        out_specs=(acts, acts, wide, wide, wide, tall, wide, P("tensor"), tall, P(), P(), P()),
        check_vma=False,
    )
```

```python
import functools
import jax
import jax.numpy as jnp
from jax import lax
from jax.experimental import pallas as pl
from jax.experimental.pallas import tpu as pltpu
from jax.sharding import PartitionSpec as P

HD = 64
EPSILON = 1e-05
BF = jnp.bfloat16
F32 = jnp.float32
NT = (((1,), (1,)), ((), ()))
NN = (((1,), (0,)), ((), ()))
TN = (((0,), (0,)), ((), ()))
MIB = 1 << 20


def dotg(a, b, dims=NN):
    return lax.dot_general(a, b, dims, preferred_element_type=F32)


def rotate(x, cos, sin):
    first = lax.broadcasted_iota(jnp.int32, (x.shape[0], 128), 1) % HD < HD // 2
    parts = []
    for a in range(0, x.shape[1], 128):
        v = x[:, a : a + 128]
        swapped = jnp.where(first, pltpu.roll(v, 96, 1), pltpu.roll(v, 32, 1))
        parts.append(v * cos + swapped * sin)
    return jnp.concatenate(parts, axis=1) if len(parts) > 1 else parts[0]


def qkv_kernel(x_ref, wq_ref, wk_ref, wv_ref, cos_ref, sin_ref, o_ref):
    width = wq_ref.shape[1]
    x, cos, sin = x_ref[...], cos_ref[...], sin_ref[...]
    o_ref[:, :width] = rotate(dotg(x, wq_ref[...]), cos, sin).astype(BF)
    o_ref[:, width : 2 * width] = rotate(dotg(x, wk_ref[...]), cos, sin).astype(BF)
    o_ref[:, 2 * width :] = dotg(x, wv_ref[...]).astype(BF)


def project(where, x, w_query, w_key, w_value, cos, sin, joint=None, blk=256):
    rows, depth = x.shape
    width, slots = w_query.shape[1], cos.shape[0]
    blk = min(blk, rows)
    count = rows // blk
    weight = pl.BlockSpec((depth, width), lambda i, at: (0, 0))
    angle = pl.BlockSpec((blk, 128), lambda i, at: (at[0] * count + i, 0))
    kernel = lambda at, *refs: qkv_kernel(*refs[:6], refs[-1])
    held = [] if joint is None else [joint]
    return pl.pallas_call(
        kernel,
        grid_spec=pltpu.PrefetchScalarGridSpec(
            num_scalar_prefetch=1,
            grid=(count,),
            in_specs=[pl.BlockSpec((blk, depth), lambda i, at: (i, 0)), weight, weight, weight, angle, angle]
            + [pl.BlockSpec(memory_space=pl.ANY)] * len(held),
            out_specs=pl.BlockSpec((blk, 3 * width), lambda i, at: (at[0] * count + i, 0)),
        ),
        out_shape=jax.ShapeDtypeStruct((slots, 3 * width), BF),
        input_output_aliases={7: 0} if held else {},
        compiler_params=pltpu.CompilerParams(vmem_limit_bytes=40 * MIB),
        cost_estimate=pl.CostEstimate(flops=rows * depth, bytes_accessed=rows * depth, transcendentals=0),
        name="project",
    )(where, x, w_query, w_key, w_value, cos, sin, *held)


def attend_kernel(at_ref, len_ref, q_ref, k_ref, v_ref, w_ref, *refs, blk):
    o_ref, lse_ref, share_ref, vt, acc_ref = refs[-5:]
    pair = pl.program_id(0)
    i = at_ref[0]
    length = len_ref[0]
    vt[...] = jnp.transpose(v_ref[...])
    lane = lax.broadcasted_iota(jnp.int32, (blk, 128), 1)
    q = q_ref[...] * jnp.asarray(0.125, BF)
    zero = jnp.zeros_like(q)
    qs = (jnp.where(lane < HD, q, zero), jnp.where(lane < HD, zero, q))

    def step(j, carry, diag):
        start = pl.multiple_of(j * blk, blk)
        kb = k_ref[pl.ds(start, blk), :]
        out = []
        for h in range(2):
            m, l, acc = carry[h]
            s = dotg(kb, qs[h], NT)
            if diag:
                key = lax.broadcasted_iota(jnp.int32, (blk, blk), 0)
                qry = lax.broadcasted_iota(jnp.int32, (blk, blk), 1)
                s = jnp.where((key <= qry) & (key + start < length), s, -1e30)
            mn = jnp.maximum(m, jnp.max(s, axis=0, keepdims=True))
            p = jnp.exp(s - mn)
            al = jnp.exp(m - mn)
            l = l * al + jnp.sum(p, axis=0, keepdims=True)
            vb = vt[HD * h : HD * h + HD, pl.ds(start, blk)]
            acc = acc * al + dotg(vb, p.astype(BF))
            out.append((mn, l, acc))
        return tuple(out)

    init = tuple(
        (jnp.full((1, blk), -1e30, F32), jnp.zeros((1, blk), F32), jnp.zeros((HD, blk), F32))
        for _ in range(2)
    )
    c = lax.fori_loop(0, i, lambda j, c: step(j, c, False), init)
    c = step(i, c, True)
    ot = jnp.concatenate([c[h][2] / c[h][1] for h in range(2)], axis=0)
    low = jnp.transpose(ot).astype(BF)
    o_ref[...] = low
    lse_ref[0] = jnp.concatenate([c[h][0] + jnp.log(c[h][1]) for h in range(2)], axis=0)
    part = dotg(low, w_ref[...])

    @pl.when(pair == 0)
    def _():
        acc_ref[...] = part

    @pl.when(pair > 0)
    def _():
        acc_ref[...] += part

    @pl.when(pair == pl.num_programs(0) - 1)
    def _():
        share_ref[...] = acc_ref[...].astype(share_ref.dtype)


def attend(at, length, joint, w_out, held, kind, blk):
    rows, width, depth = joint.shape[0], w_out.shape[0], w_out.shape[1]
    pairs = width // 128
    return pl.pallas_call(
        functools.partial(attend_kernel, blk=blk),
        grid_spec=pltpu.PrefetchScalarGridSpec(
            num_scalar_prefetch=2,
            grid=(pairs,),
            in_specs=[
                pl.BlockSpec((blk, 128), lambda p, at, *_: (at[0], p)),
                pl.BlockSpec((rows, 128), lambda p, *_: (0, pairs + p)),
                pl.BlockSpec((rows, 128), lambda p, *_: (0, 2 * pairs + p)),
                pl.BlockSpec((128, depth), lambda p, *_: (p, 0)),
            ]
            + [pl.BlockSpec(memory_space=pl.ANY)] * len(held),
            out_specs=[
                pl.BlockSpec((blk, 128), lambda p, at, *_: (at[0], p)),
                pl.BlockSpec((1, 2, blk), lambda p, at, *_: (p, 0, at[0])),
                pl.BlockSpec((blk, depth), lambda p, *_: (0, 0)),
            ],
            scratch_shapes=[pltpu.VMEM((128, rows), BF), pltpu.VMEM((blk, depth), F32)],
        ),
        out_shape=[
            jax.ShapeDtypeStruct((rows, width), BF),
            jax.ShapeDtypeStruct((pairs, 2, rows), F32),
            jax.ShapeDtypeStruct((blk, depth), kind),
        ],
        input_output_aliases={6: 0, 7: 1} if held else {},
        compiler_params=pltpu.CompilerParams(vmem_limit_bytes=40 * MIB),
        cost_estimate=pl.CostEstimate(flops=rows * width, bytes_accessed=rows * width, transcendentals=0),
        name="attend",
    )(at, length, joint, joint, joint, w_out, *held)


def attend_back_kernel(
    len_ref, q_ref, k_ref, v_ref, o_ref, do_ref, lse_ref, cos_ref, sin_ref,
    dq_ref, dk_ref, dv_ref, kt, dlt, dqt, *, blk, blocks,
):
    j = pl.program_id(1)
    length = len_ref[0]

    @pl.when(j == 0)
    def _():
        kt[...] = jnp.transpose(k_ref[...])
        dqt[...] = jnp.zeros_like(dqt)

        def body(i, _):
            at = pl.ds(pl.multiple_of(i * blk, blk), blk)
            both = jnp.transpose(do_ref[at, :].astype(F32) * o_ref[at, :].astype(F32))
            for h in range(2):
                dlt[h : h + 1, at] = jnp.sum(both[HD * h : HD * h + HD], axis=0, keepdims=True)
            return 0

        lax.fori_loop(0, blocks, body, 0)

    js = pl.multiple_of(j * blk, blk)
    lane = lax.broadcasted_iota(jnp.int32, (blk, 128), 1)
    kb = k_ref[pl.ds(js, blk), :] * jnp.asarray(0.125, BF)
    vb = v_ref[pl.ds(js, blk), :]
    zero = jnp.zeros_like(kb)
    ks = (jnp.where(lane < HD, kb, zero), jnp.where(lane < HD, zero, kb))
    vs = (jnp.where(lane < HD, vb, zero), jnp.where(lane < HD, zero, vb))

    def step(i, carry, diag):
        at = pl.ds(pl.multiple_of(i * blk, blk), blk)
        qb, dob = q_ref[at, :], do_ref[at, :]
        out = []
        for h in range(2):
            dk, dv = carry[h]
            s = dotg(ks[h], qb, NT)
            if diag:
                key = lax.broadcasted_iota(jnp.int32, (blk, blk), 0)
                qry = lax.broadcasted_iota(jnp.int32, (blk, blk), 1)
                s = jnp.where((key <= qry) & (key + js < length), s, -1e30)
            p = jnp.exp(s - lse_ref[0, h : h + 1, at])
            dp = dotg(vs[h], dob, NT)
            ds = (p * (dp - dlt[h : h + 1, at])).astype(BF)
            dv = dv + dotg(p.astype(BF), dob)
            dk = dk + dotg(ds, qb)
            dqt[HD * h : HD * h + HD, at] += dotg(kt[HD * h : HD * h + HD, pl.ds(js, blk)], ds)
            out.append((dk, dv))
        return tuple(out)

    z = jnp.zeros((blk, 128), F32)
    c = step(j, ((z, z), (z, z)), True)
    c = lax.fori_loop(j + 1, blocks, lambda i, c: step(i, c, False), c)
    grad = jnp.where(lane < HD, c[0][0], c[1][0]) * 0.125
    dk_ref[...] = rotate(grad, cos_ref[pl.ds(js, blk), :], -sin_ref[pl.ds(js, blk), :]).astype(BF)
    dv_ref[...] = jnp.where(lane < HD, c[0][1], c[1][1]).astype(BF)

    @pl.when(j == blocks - 1)
    def _():
        def body(i, _):
            at = pl.ds(pl.multiple_of(i * blk, blk), blk)
            grad = jnp.transpose(dqt[:, at]) * 0.125
            dq_ref[at, :] = rotate(grad, cos_ref[at, :], -sin_ref[at, :]).astype(BF)
            return 0

        lax.fori_loop(0, blocks, body, 0)


def attend_back(length, joint, mixed, dmixed, lse, cos, sin, width, blk=512):
    rows = joint.shape[0]
    pairs, blocks = width // 128, rows // blk
    full = lambda off: pl.BlockSpec((rows, 128), lambda p, j, *_: (0, off * pairs + p))
    angle = pl.BlockSpec((rows, 128), lambda p, j, *_: (0, 0))
    block = pl.BlockSpec((blk, 128), lambda p, j, *_: (j, p))
    return pl.pallas_call(
        functools.partial(attend_back_kernel, blk=blk, blocks=blocks),
        grid_spec=pltpu.PrefetchScalarGridSpec(
            num_scalar_prefetch=1,
            grid=(pairs, blocks),
            in_specs=[full(0), full(1), full(2), full(0), full(0)]
            + [pl.BlockSpec((1, 2, rows), lambda p, j, *_: (p, 0, 0)), angle, angle],
            out_specs=[full(0), block, block],
            scratch_shapes=[
                pltpu.VMEM((128, rows), BF),
                pltpu.VMEM((2, rows), F32),
                pltpu.VMEM((128, rows), F32),
            ],
        ),
        out_shape=[jax.ShapeDtypeStruct((rows, width), BF)] * 3,
        compiler_params=pltpu.CompilerParams(vmem_limit_bytes=48 * MIB),
        cost_estimate=pl.CostEstimate(
            flops=rows * width, bytes_accessed=rows * width, transcendentals=0
        ),
        name="attend_back",
    )(length, joint, joint, joint, mixed, dmixed, lse, cos, sin)


def gelu_parts(v):
    c = 0.7978845608028654
    return c, jnp.tanh(c * (v + 0.044715 * v * v * v))


def gelu(v):
    return 0.5 * v * (1.0 + gelu_parts(v)[1])


def gelu_both(v):
    c, t = gelu_parts(v)
    half = 0.5 * (1.0 + t)
    return v * half, half + 0.5 * v * (1.0 - t * t) * c * (1.0 + 3 * 0.044715 * v * v)


def norm_parts(values):
    average = jnp.mean(values, axis=-1, keepdims=True)
    centred = values - average
    scale = lax.rsqrt(jnp.mean(centred * centred, axis=-1, keepdims=True) + EPSILON)
    return centred * scale, scale


def norm_back(grad, hat, scale, gain):
    g = grad * gain
    return scale * (
        g - jnp.mean(g, axis=-1, keepdims=True) - hat * jnp.mean(g * hat, axis=-1, keepdims=True)
    )


def column_sum(v):
    return jnp.sum(v, axis=0, keepdims=True)


def valid_rows(info_ref, start, count):
    at = info_ref[1] + start + lax.broadcasted_iota(jnp.int32, (count, 1), 0)
    return (at < info_ref[0]).astype(F32)


def loop_rows(rows, blk, body):
    def step(i, _):
        body(pl.multiple_of(i * blk, blk))
        return 0

    lax.fori_loop(0, rows // blk, step, 0)


def feed_kernel(info_ref, *refs, groups, chunks, sub):
    x_ref, bias_ref, resid_ref, cot_ref, bd_ref, gain_ref, shift_ref = refs[:7]
    ups, downs = refs[7 : 7 + groups], refs[7 + groups : 7 + 2 * groups]
    pre_ref, act_ref, out_ref, gb_ref, sums_ref, acc = refs[7 + 2 * groups :]
    step = pl.program_id(0)
    rows = x_ref.shape[0]

    @pl.when(step == 0)
    def _():
        acc[...] = jnp.zeros_like(acc) + bd_ref[...].astype(F32)

    for g in range(groups):

        @pl.when(step // chunks == g)
        def _():
            for r in range(0, rows, sub):
                pre = dotg(x_ref[r : r + sub], ups[g][...]) + bias_ref[0]
                pre_ref[r : r + sub] = pre
                act = gelu(pre).astype(BF)
                if g == 0:
                    act_ref[r : r + sub] = act
                acc[r : r + sub] += dotg(act, downs[g][...])

    @pl.when(step == groups * chunks - 1)
    def _():
        sums_ref[...] = jnp.zeros_like(sums_ref)
        gain, shift = gain_ref[3:4], shift_ref[3:4]

        def body(r):
            at = pl.ds(r, 64)
            valid = valid_rows(info_ref, r, 64)
            hat, scale = norm_parts(acc[at])
            out_ref[at] = (valid * (resid_ref[at] + hat * gain + shift)).astype(BF)
            g_out = valid * cot_ref[at].astype(F32)
            low = norm_back(g_out, hat, scale, gain).astype(BF)
            gb_ref[at] = low
            sums_ref[0:1] += column_sum(g_out * hat)
            sums_ref[1:2] += column_sum(g_out)
            sums_ref[2:3] += column_sum(low.astype(F32))

        loop_rows(rows, 64, body)


def feed(info, x, biases, ups, downs, resid, cot, bias_down, gains, shifts, cols=512):
    rows, depth = x.shape
    groups, hidden = len(ups), ups[0].shape[1]
    chunks = hidden // cols
    once = lambda shape: pl.BlockSpec(shape, lambda s, *_: (0, 0), pipeline_mode=pl.Buffered(1))
    own = lambda g: (lambda s, *_: (0, jnp.clip(s - g * chunks, 0, chunks - 1)))
    own_t = lambda g: (lambda s, *_: (jnp.clip(s - g * chunks, 0, chunks - 1), 0))
    return pl.pallas_call(
        functools.partial(feed_kernel, groups=groups, chunks=chunks, sub=min(512, rows)),
        grid_spec=pltpu.PrefetchScalarGridSpec(
            num_scalar_prefetch=1,
            grid=(groups * chunks,),
            in_specs=[
                once((rows, depth)),
                pl.BlockSpec((1, 1, cols), lambda s, *_: (s, 0, 0)),
                once((rows, depth)),
                once((rows, depth)),
                once((1, depth)),
                once(gains.shape),
                once(gains.shape),
            ]
            + [pl.BlockSpec((depth, cols), own(g)) for g in range(groups)]
            + [pl.BlockSpec((cols, depth), own_t(g)) for g in range(groups)],
            out_specs=[
                pl.BlockSpec((rows, cols), lambda s, *_: (0, s)),
                pl.BlockSpec((rows, cols), own(0)),
                once((rows, depth)),
                once((rows, depth)),
                once((8, depth)),
            ],
            scratch_shapes=[pltpu.VMEM((rows, depth), F32)],
        ),
        out_shape=[
            jax.ShapeDtypeStruct((rows, groups * hidden), F32),
            jax.ShapeDtypeStruct((rows, hidden), BF),
            jax.ShapeDtypeStruct((rows, depth), BF),
            jax.ShapeDtypeStruct((rows, depth), BF),
            jax.ShapeDtypeStruct((8, depth), F32),
        ],
        compiler_params=pltpu.CompilerParams(vmem_limit_bytes=56 * MIB),
        cost_estimate=pl.CostEstimate(
            flops=rows * depth, bytes_accessed=rows * depth, transcendentals=0
        ),
        name="feed",
    )(info, x, biases.reshape(-1, 1, cols), resid, cot, bias_down, gains, shifts, *ups, *downs)


def feed_back_kernel(info_ref, *refs, groups, chunks, sub):
    gb_ref, pre_ref, resid_ref, attn_ref, cot_ref, gain_ref = refs[:6]
    ups, downs = refs[6 : 6 + groups], refs[6 + groups : 6 + 2 * groups]
    gp_ref, gr_ref, ga_ref, sums_ref, acc = refs[6 + 2 * groups :]
    step = pl.program_id(0)
    rows = gb_ref.shape[0]

    @pl.when(step == 0)
    def _():
        acc[...] = jnp.zeros_like(acc)

    for g in range(groups):

        @pl.when(step // chunks == g)
        def _():
            for r in range(0, rows, sub):
                grad = dotg(gb_ref[r : r + sub], downs[g][...], NT)
                low = (grad * gelu_both(pre_ref[r : r + sub])[1]).astype(BF)
                if g == 0:
                    gp_ref[r : r + sub] = low
                acc[r : r + sub] += dotg(low, ups[g][...], NT)

    @pl.when(step == groups * chunks - 1)
    def _():
        sums_ref[...] = jnp.zeros_like(sums_ref)

        def body(r):
            at = pl.ds(r, 64)
            g_out = valid_rows(info_ref, r, 64) * cot_ref[at].astype(F32)
            hat, scale = norm_parts(resid_ref[at])
            g_two = acc[at]
            g_resid = g_out + norm_back(g_two, hat, scale, gain_ref[2:3])
            gr_ref[at] = g_resid
            sums_ref[0:1] += column_sum(g_two * hat)
            sums_ref[1:2] += column_sum(g_two)
            hat, scale = norm_parts(attn_ref[at])
            ga_ref[at] = norm_back(g_resid, hat, scale, gain_ref[1:2]).astype(BF)
            sums_ref[2:3] += column_sum(g_resid * hat)
            sums_ref[3:4] += column_sum(g_resid)

        loop_rows(rows, 64, body)


def feed_back(info, gb, pre, ups, downs, resid, attn_sum, cot, gains, cols=512):
    rows, depth = gb.shape
    groups, hidden = len(ups), ups[0].shape[1]
    chunks = hidden // cols
    once = lambda shape: pl.BlockSpec(shape, lambda s, *_: (0, 0), pipeline_mode=pl.Buffered(1))
    own = lambda g: (lambda s, *_: (0, jnp.clip(s - g * chunks, 0, chunks - 1)))
    own_t = lambda g: (lambda s, *_: (jnp.clip(s - g * chunks, 0, chunks - 1), 0))
    return pl.pallas_call(
        functools.partial(feed_back_kernel, groups=groups, chunks=chunks, sub=min(512, rows)),
        grid_spec=pltpu.PrefetchScalarGridSpec(
            num_scalar_prefetch=1,
            grid=(groups * chunks,),
            in_specs=[
                once((rows, depth)),
                pl.BlockSpec((rows, cols), lambda s, *_: (0, s)),
                once((rows, depth)),
                once((rows, depth)),
                once((rows, depth)),
                once(gains.shape),
            ]
            + [pl.BlockSpec((depth, cols), own(g)) for g in range(groups)]
            + [pl.BlockSpec((cols, depth), own_t(g)) for g in range(groups)],
            out_specs=[
                pl.BlockSpec((rows, cols), own(0)),
                once((rows, depth)),
                once((rows, depth)),
                once((8, depth)),
            ],
            scratch_shapes=[pltpu.VMEM((rows, depth), F32)],
        ),
        out_shape=[
            jax.ShapeDtypeStruct((rows, hidden), BF),
            jax.ShapeDtypeStruct((rows, depth), F32),
            jax.ShapeDtypeStruct((rows, depth), BF),
            jax.ShapeDtypeStruct((8, depth), F32),
        ],
        compiler_params=pltpu.CompilerParams(vmem_limit_bytes=56 * MIB),
        cost_estimate=pl.CostEstimate(
            flops=rows * depth, bytes_accessed=rows * depth, transcendentals=0
        ),
        name="feed_back",
    )(info, gb, pre, resid, attn_sum, cot, gains, *ups, *downs)


def feed_grad_kernel(*refs, groups):
    up_ref, down_ref, bias_ref, act_ref, gp_ref = refs[:5]
    n2s, gbs = refs[5 : 5 + groups], refs[5 + groups : 5 + 2 * groups]
    grad_ref, sum_ref = refs[5 + 2 * groups :]
    act, gp = act_ref[...], gp_ref[...]
    dup = dotg(gp, n2s[0][...], TN)
    ddown = dotg(act, gbs[0][...], TN)
    sums = column_sum(gp.astype(F32))
    for g in range(1, groups):
        pre = dotg(n2s[g][...], up_ref[...]) + bias_ref[0]
        act, slope = gelu_both(pre)
        act = act.astype(BF)
        gp = (dotg(gbs[g][...], down_ref[...], NT) * slope).astype(BF)
        dup += dotg(gp, n2s[g][...], TN)
        ddown += dotg(act, gbs[g][...], TN)
        sums += column_sum(gp.astype(F32))
    grad_ref[0] = dup.astype(BF)
    grad_ref[1] = ddown.astype(BF)
    sum_ref[0] = sums


def feed_grad(up, down, bias, act, gp, n2s, gbs, cols=256):
    rows, depth = n2s[0].shape
    groups, hidden = len(n2s), up.shape[1]
    once = lambda shape: pl.BlockSpec(shape, lambda s: (0, 0), pipeline_mode=pl.Buffered(1))
    wide = lambda count: pl.BlockSpec((count, cols), lambda s: (0, s))
    tall = pl.BlockSpec((cols, depth), lambda s: (s, 0))
    flat = pl.BlockSpec((1, 1, cols), lambda s: (s, 0, 0))
    return pl.pallas_call(
        functools.partial(feed_grad_kernel, groups=groups),
        grid=(hidden // cols,),
        in_specs=[wide(depth), tall, flat, wide(rows), wide(rows)] + [once((rows, depth))] * (2 * groups),
        out_specs=[pl.BlockSpec((2, cols, depth), lambda s: (0, s, 0)), flat],
        out_shape=[
            jax.ShapeDtypeStruct((2, hidden, depth), BF),
            jax.ShapeDtypeStruct((hidden // cols, 1, cols), F32),
        ],
        compiler_params=pltpu.CompilerParams(vmem_limit_bytes=56 * MIB),
        cost_estimate=pl.CostEstimate(
            flops=(8 * groups - 4) * rows * depth * hidden, bytes_accessed=20 * rows * depth, transcendentals=0
        ),
        name="feed_grad",
    )(up, down, bias.reshape(-1, 1, cols), act, gp, *n2s, *gbs)


def norm_kernel(x_ref, gain_ref, shift_ref, o_ref):
    hat, _ = norm_parts(x_ref[...].astype(F32))
    o_ref[...] = (hat * gain_ref[0:1] + shift_ref[0:1]).astype(BF)


def first_norm(x, gains, shifts, blk=128):
    rows, depth = x.shape
    whole = pl.BlockSpec(gains.shape, lambda i: (0, 0))
    block = pl.BlockSpec((blk, depth), lambda i: (i, 0))
    return pl.pallas_call(
        norm_kernel,
        grid=(rows // blk,),
        in_specs=[block, whole, whole],
        out_specs=block,
        out_shape=jax.ShapeDtypeStruct((rows, depth), BF),
        name="first_norm",
    )(x, gains, shifts)


def join_kernel(x_ref, gain_ref, shift_ref, *refs, blocks, each):
    attn_ref, resid_ref, low_ref = refs[-3:]
    step = pl.program_id(0)
    for b in range(blocks):

        @pl.when(step // each == b)
        def _():
            own, *rest = refs[b :: blocks][: (len(refs) - 3) // blocks]
            total = own[...]
            for r in rest:
                total = total + r[...].astype(F32)
            attn_ref[...] = total
            hat, _ = norm_parts(total)
            resid = x_ref[...].astype(F32) + hat * gain_ref[1:2] + shift_ref[1:2]
            resid_ref[...] = resid
            hat, _ = norm_parts(resid)
            low_ref[...] = (hat * gain_ref[2:3] + shift_ref[2:3]).astype(BF)


def join(x, gains, shifts, shares, blk=128):
    rows, depth = x.shape
    blocks = len(shares[0])
    each = rows // blocks // blk
    whole = pl.BlockSpec(gains.shape, lambda i: (0, 0))
    block = pl.BlockSpec((blk, depth), lambda i: (i, 0))
    part = lambda b: pl.BlockSpec((blk, depth), lambda i: (jnp.clip(i - b * each, 0, each - 1), 0))
    return pl.pallas_call(
        functools.partial(join_kernel, blocks=blocks, each=each),
        grid=(rows // blk,),
        in_specs=[block, whole, whole] + [part(b) for _ in shares for b in range(blocks)],
        out_specs=[block, block, block],
        out_shape=[
            jax.ShapeDtypeStruct((rows, depth), F32),
            jax.ShapeDtypeStruct((rows, depth), F32),
            jax.ShapeDtypeStruct((rows, depth), BF),
        ],
        name="join",
    )(x, gains, shifts, *[v for share in shares for v in share])


def qkv_grad_kernel(me_ref, gq_ref, gk_ref, gv_ref, *refs, groups):
    n1s, o_ref = refs[:groups], refs[groups]
    rows = n1s[0].shape[0]
    for i, g_ref in enumerate((gq_ref, gk_ref, gv_ref)):

        @pl.when(pl.program_id(0) == i)
        def _():
            total = None
            for r in range(groups):
                start = pl.multiple_of(lax.rem(me_ref[0] + r, groups) * rows, rows)
                part = dotg(n1s[r][...], g_ref[pl.ds(start, rows), :], TN)
                total = part if total is None else total + part
            o_ref[...] = total.astype(BF)


def qkv_grad(me, g_query, g_key, g_value, n1s):
    rows, depth = n1s[0].shape
    slots, width = g_query.shape
    once = lambda shape: pl.BlockSpec(shape, lambda i, *_: (0, 0), pipeline_mode=pl.Buffered(1))
    return pl.pallas_call(
        functools.partial(qkv_grad_kernel, groups=len(n1s)),
        grid_spec=pltpu.PrefetchScalarGridSpec(
            num_scalar_prefetch=1,
            grid=(3,),
            in_specs=[once((slots, width))] * 3 + [once((rows, depth))] * len(n1s),
            out_specs=pl.BlockSpec((depth, width), lambda i, *_: (i, 0)),
        ),
        out_shape=jax.ShapeDtypeStruct((3 * depth, width), BF),
        compiler_params=pltpu.CompilerParams(vmem_limit_bytes=40 * MIB),
        name="qkv_grad",
    )(me, g_query, g_key, g_value, *n1s)


def share_kernel(at_ref, gq_ref, gk_ref, gv_ref, wq_ref, wk_ref, wv_ref, o_ref):
    total = dotg(gq_ref[...], wq_ref[...], NT)
    total += dotg(gk_ref[...], wk_ref[...], NT)
    total += dotg(gv_ref[...], wv_ref[...], NT)
    o_ref[...] = total.astype(o_ref.dtype)


def share_of(at, grads, weights, rows, kind, blk=256):
    (slots, width), depth = grads[0].shape, weights[0].shape[0]
    blk = min(blk, rows)
    count = rows // blk
    return pl.pallas_call(
        share_kernel,
        grid_spec=pltpu.PrefetchScalarGridSpec(
            num_scalar_prefetch=1,
            grid=(count,),
            in_specs=[pl.BlockSpec((blk, width), lambda i, at: (at[0] * count + i, 0))] * 3
            + [pl.BlockSpec((depth, width), lambda i, at: (0, 0))] * 3,
            out_specs=pl.BlockSpec((blk, depth), lambda i, at: (i, 0)),
        ),
        out_shape=jax.ShapeDtypeStruct((rows, depth), kind),
        compiler_params=pltpu.CompilerParams(vmem_limit_bytes=40 * MIB),
        name="share_of",
    )(at, *grads, *weights)


def last_kernel(x_ref, gr_ref, gain_ref, *refs):
    shares, (o_ref, sums_ref) = refs[:-2], refs[-2:]
    total = shares[0][...]
    for r in shares[1:]:
        total = total + r[...].astype(F32)
    hat, scale = norm_parts(x_ref[...].astype(F32))
    o_ref[...] = (gr_ref[...] + norm_back(total, hat, scale, gain_ref[0:1])).astype(BF)

    @pl.when(pl.program_id(0) == 0)
    def _():
        sums_ref[...] = jnp.zeros_like(sums_ref)

    sums_ref[0:1] += column_sum(total * hat)
    sums_ref[1:2] += column_sum(total)


def last_norm(x, g_resid, gains, shares, blk=128):
    rows, depth = x.shape
    block = pl.BlockSpec((blk, depth), lambda i: (i, 0))
    return pl.pallas_call(
        last_kernel,
        grid=(rows // blk,),
        in_specs=[block, block, pl.BlockSpec(gains.shape, lambda i: (0, 0))] + [block] * len(shares),
        out_specs=[block, pl.BlockSpec((8, depth), lambda i: (0, 0))],
        out_shape=[jax.ShapeDtypeStruct((rows, depth), BF), jax.ShapeDtypeStruct((8, depth), F32)],
        name="last_norm",
    )(x, g_resid, gains, *shares)


def widen_kernel(up_ref, down_ref, dup_ref, ddown_ref):
    dup_ref[...] = jnp.transpose(up_ref[...]).astype(F32)
    ddown_ref[...] = down_ref[...].astype(F32)


def widen(grads, blk=256):
    hidden, depth = grads.shape[0] // 2, grads.shape[1]
    blk = min(blk, hidden)
    count = hidden // blk
    return pl.pallas_call(
        widen_kernel,
        grid=(count,),
        in_specs=[
            pl.BlockSpec((blk, depth), lambda i: (i, 0)),
            pl.BlockSpec((blk, depth), lambda i: (count + i, 0)),
        ],
        out_specs=[
            pl.BlockSpec((depth, blk), lambda i: (0, i)),
            pl.BlockSpec((blk, depth), lambda i: (i, 0)),
        ],
        out_shape=[
            jax.ShapeDtypeStruct((depth, hidden), F32),
            jax.ShapeDtypeStruct((hidden, depth), F32),
        ],
        name="widen",
    )(grads, grads)


def shift(x, axis, count, step):
    return lax.ppermute(x, axis, [((i + step) % count, i) for i in range(count)])


def bit_of(axis, bit):
    return (lax.axis_index(axis) >> bit) & 1


def flip(x, axis, bit):
    return lax.ppermute(x, axis, [(i, i ^ (1 << bit)) for i in range(lax.axis_size(axis))])


def halve(x, bit):
    b, half = bit_of("dp", bit), x.shape[0] // 2
    xs = x.reshape((2, half) + x.shape[1:])
    send = lax.dynamic_index_in_dim(xs, 1 - b, 0, False)
    keep = lax.dynamic_index_in_dim(xs, b, 0, False)
    return (keep.astype(F32) + flip(send, "dp", bit).astype(F32)).astype(BF)


def double(x, bit):
    b, other = bit_of("dp", bit), flip(x, "dp", bit)
    return jnp.where(b == 0, jnp.concatenate([x, other]), jnp.concatenate([other, x]))


def rows_sum(x):
    bits = (lax.axis_size("dp") - 1).bit_length()
    x = halve(x, 0)
    half = x.shape[0] // 2
    parts = [x[:half], x[half:]]
    outer = tuple(range(1, bits))
    orders = [outer, outer[1:] + outer[:1]]
    for i in range(len(outer)):
        parts = [halve(p, o[i]) for p, o in zip(parts, orders)]
    for i in reversed(range(len(outer))):
        parts = [double(p, o[i]) for p, o in zip(parts, orders)]
    return double(jnp.concatenate(parts), 0)


def small_sum(x):
    for axis in ("tensor", "dp"):
        for bit in range((lax.axis_size(axis) - 1).bit_length()):
            x = x + flip(x, axis, bit)
    return x


def shards(
    tokens,
    lengths,
    cotangent,
    w_query,
    w_key,
    w_value,
    w_out,
    up_weight,
    bias_up,
    down_weight,
    bias_down,
    norm_gains,
    norm_shifts,
):
    rows, _, depth = tokens.shape
    groups, replicas = lax.axis_size("tensor"), lax.axis_size("dp")
    me, replica = lax.axis_index("tensor"), lax.axis_index("dp")
    slots = rows * groups
    width = w_query.shape[1]
    hidden = up_weight.shape[1]
    x = tokens.reshape(rows, depth)
    here = me.reshape(1).astype(jnp.int32)
    place = lambda r: (here + r) % groups

    def others(v):
        return [shift(v, "tensor", groups, r) for r in range(1, groups)]

    def in_order(own, rest):
        if groups == 2:
            a, b = jnp.concatenate([own, rest[0]]), jnp.concatenate([rest[0], own])
            return jnp.where(me == 0, a, b)
        stacked = jnp.stack([own] + rest)
        return jnp.roll(stacked, me, axis=0).reshape((-1,) + own.shape[1:])

    def to_owner(v, r):
        return shift(v, "tensor", groups, groups - r)

    up_piece = lax.dynamic_slice_in_dim(up_weight, replica * (depth // replicas), depth // replicas, 0)
    down_piece = lax.dynamic_slice_in_dim(
        down_weight, replica * (hidden // replicas), hidden // replicas, 0
    )
    up_pieces, down_pieces, bias_rest = others(up_piece), others(down_piece), others(bias_up)
    gather = lambda v: lax.all_gather(v, "dp", axis=0, tiled=True)

    freqs = 10000.0 ** (-jnp.arange(HD // 2).astype(F32) * 2.0 / HD)
    angles = jnp.arange(slots).astype(F32)[:, None] * freqs[None, :]
    cosine, sine = jnp.cos(angles), jnp.sin(angles)
    cosine = jnp.concatenate([cosine] * 4, axis=1)
    sine = jnp.concatenate([-sine, sine] * 2, axis=1)
    normed_one = first_norm(x, norm_gains, norm_shifts)
    normed_one_rest = others(normed_one)
    weights = (w_query, w_key, w_value)
    joint = project(here, normed_one, *weights, cosine, sine)
    joint, normed_one_rest, up_pieces, down_pieces, bias_rest = lax.optimization_barrier(
        (joint, normed_one_rest, up_pieces, down_pieces, bias_rest)
    )
    for r, n in enumerate(normed_one_rest):
        joint = project(place(r + 1), n, *weights, cosine, sine, joint)
    blk = min(512, rows)
    each = rows // blk
    held, shares, arrived = (), [], []
    for r in list(range(1, groups)) + [0]:
        for b in range(each):
            if r == 0 and b == each - 1 and b > 0:
                joint, arrived[0] = lax.optimization_barrier((joint, arrived[0]))
            *held, share = attend(
                place(r) * each + b, lengths, joint, w_out, held, BF if r else F32, blk
            )
            if r:
                arrived.append(to_owner(share, r))
            else:
                shares.append(share)
    mixed, lse = held
    shares = [shares] + [arrived[i * each : (i + 1) * each] for i in range(groups - 1)]
    up_rest, down_rest = [gather(p) for p in up_pieces], [gather(p) for p in down_pieces]
    shares, up_rest, down_rest = lax.optimization_barrier((shares, up_rest, down_rest))
    ups, downs = [up_weight] + up_rest, [down_weight] + down_rest
    biases = jnp.concatenate([bias_up] + bias_rest).astype(F32)

    info = jnp.stack([lengths[0], me * rows]).astype(jnp.int32)
    cot = cotangent.reshape(rows, depth)
    attn_sum, resid, normed_two = join(x, norm_gains, norm_shifts, shares)
    normed_two_rest = others(normed_two)
    pre, act, layer_out, g_branch, sums3 = feed(
        info, normed_two, biases, ups, downs, resid, cot, bias_down.reshape(1, depth), norm_gains, norm_shifts
    )
    g_branch_rest = others(g_branch)
    g_branch, normed_two_rest = lax.optimization_barrier((g_branch, normed_two_rest))
    g_pre, g_resid, g_attn, sums21 = feed_back(
        info, g_branch, pre, ups, downs, resid, attn_sum, cot, norm_gains
    )
    g_attn_rest = others(g_attn)
    grad_feed, bias_up_sum = feed_grad(
        up_weight, down_weight, biases[:hidden], act, g_pre,
        [normed_two] + normed_two_rest, [g_branch] + g_branch_rest,
    )
    grad_feed = grad_feed.reshape(2 * hidden, depth)
    g_attn_rest, grad_feed = lax.optimization_barrier((g_attn_rest, grad_feed))
    grad_feed = lax.psum_scatter(grad_feed, "dp", scatter_dimension=0, tiled=True)
    g_attn_all = in_order(g_attn, g_attn_rest)

    g_mixed = dotg(g_attn_all, w_out, NT).astype(BF)
    grad_out = dotg(mixed, g_attn_all, TN)
    g_query, g_key, g_value = attend_back(
        lengths, joint, mixed, g_mixed, lse, cosine, sine, width
    )
    grads = (g_query, g_key, g_value)
    others_share = [share_of(place(r), grads, weights, rows, BF) for r in range(1, groups)]
    others_share, grads = lax.optimization_barrier((others_share, grads))
    others_share = [to_owner(v, r + 1) for r, v in enumerate(others_share)]
    packed = qkv_grad(here, *grads, [normed_one] + normed_one_rest)
    packed = jnp.concatenate([packed, grad_out.astype(BF).reshape(depth, width)])
    packed, grad_feed = lax.optimization_barrier((packed, grad_feed))
    grad_feed = lax.all_gather(grad_feed, "dp", axis=0, tiled=True)
    grad_up, grad_down = widen(grad_feed)
    packed = rows_sum(packed)
    grad_query, grad_key, grad_value = (packed[i * depth : (i + 1) * depth].astype(F32) for i in range(3))
    grad_out = packed[3 * depth :].reshape(width, depth).astype(F32)
    own_share = share_of(here, grads, weights, rows, F32)
    grad_tokens, sums0 = last_norm(x, g_resid, norm_gains, [own_share] + others_share)

    placed = lax.dynamic_update_slice(
        jnp.zeros((groups * hidden,), F32), bias_up_sum.reshape(-1), (me * hidden,)
    ).reshape(-1, depth)
    sums = small_sum(jnp.concatenate([sums3[:3], sums21[:4], sums0[:2], placed]))
    grad_gains = jnp.stack([sums[7], sums[5], sums[3], sums[0]])
    grad_shifts = jnp.stack([sums[8], sums[6], sums[4], sums[1]])
    grad_bias_up = lax.dynamic_slice_in_dim(sums[9:].reshape(-1), me * hidden, hidden, 0)
    whole = (rows, 1, depth)
    return (
        layer_out.reshape(whole),
        grad_tokens.reshape(whole),
        grad_query,
        grad_key,
        grad_value,
        grad_out,
        grad_up,
        grad_bias_up,
        grad_down,
        sums[2],
        grad_gains,
        grad_shifts,
    )


def solution(mesh):
    wide, tall = P(None, "tensor"), P("tensor", None)
    acts = P("tensor", "dp", None)
    return jax.shard_map(
        shards,
        mesh=mesh,
        in_specs=(acts, P("dp"), acts, wide, wide, wide, tall, wide, P("tensor"), tall, P(), P(), P()),
        out_specs=(acts, acts, wide, wide, wide, tall, wide, P("tensor"), tall, P(), P(), P()),
        check_vma=False,
    )
```

```python
import functools
import jax
import jax.numpy as jnp
from jax import lax
from jax.experimental import pallas as pl
from jax.experimental.pallas import tpu as pltpu
from jax.sharding import PartitionSpec as P

HD = 64
EPSILON = 1e-05
BF = jnp.bfloat16
F32 = jnp.float32
NT = (((1,), (1,)), ((), ()))
NN = (((1,), (0,)), ((), ()))
TN = (((0,), (0,)), ((), ()))
MIB = 1 << 20


def dotg(a, b, dims=NN):
    return lax.dot_general(a, b, dims, preferred_element_type=F32)


def rotate(x, cos, sin):
    first = lax.broadcasted_iota(jnp.int32, (x.shape[0], 128), 1) % HD < HD // 2
    parts = []
    for a in range(0, x.shape[1], 128):
        v = x[:, a : a + 128]
        swapped = jnp.where(first, pltpu.roll(v, 96, 1), pltpu.roll(v, 32, 1))
        parts.append(v * cos + swapped * sin)
    return jnp.concatenate(parts, axis=1) if len(parts) > 1 else parts[0]


def qkv_kernel(x_ref, wq_ref, wk_ref, wv_ref, cos_ref, sin_ref, o_ref):
    width = wq_ref.shape[1]
    x, cos, sin = x_ref[...], cos_ref[...], sin_ref[...]
    o_ref[:, :width] = rotate(dotg(x, wq_ref[...]), cos, sin).astype(BF)
    o_ref[:, width : 2 * width] = rotate(dotg(x, wk_ref[...]), cos, sin).astype(BF)
    o_ref[:, 2 * width :] = dotg(x, wv_ref[...]).astype(BF)


def project(where, x, w_query, w_key, w_value, cos, sin, joint=None, blk=256):
    rows, depth = x.shape
    width, slots = w_query.shape[1], cos.shape[0]
    blk = min(blk, rows)
    count = rows // blk
    weight = pl.BlockSpec((depth, width), lambda i, at: (0, 0))
    angle = pl.BlockSpec((blk, 128), lambda i, at: (at[0] * count + i, 0))
    kernel = lambda at, *refs: qkv_kernel(*refs[:6], refs[-1])
    held = [] if joint is None else [joint]
    return pl.pallas_call(
        kernel,
        grid_spec=pltpu.PrefetchScalarGridSpec(
            num_scalar_prefetch=1,
            grid=(count,),
            in_specs=[pl.BlockSpec((blk, depth), lambda i, at: (i, 0)), weight, weight, weight, angle, angle]
            + [pl.BlockSpec(memory_space=pl.ANY)] * len(held),
            out_specs=pl.BlockSpec((blk, 3 * width), lambda i, at: (at[0] * count + i, 0)),
        ),
        out_shape=jax.ShapeDtypeStruct((slots, 3 * width), BF),
        input_output_aliases={7: 0} if held else {},
        compiler_params=pltpu.CompilerParams(vmem_limit_bytes=60 * MIB),
        cost_estimate=pl.CostEstimate(flops=rows * depth, bytes_accessed=rows * depth, transcendentals=0),
        name="project",
    )(where, x, w_query, w_key, w_value, cos, sin, *held)


def attend_kernel(at_ref, len_ref, q_ref, k_ref, v_ref, w_ref, *refs, blk):
    o_ref, lse_ref, share_ref, vt, acc_ref = refs[-5:]
    pair = pl.program_id(0)
    i = at_ref[0]
    length = len_ref[0]
    def turn(j, _):
        part = pl.ds(pl.multiple_of(j * blk, blk), blk)
        vt[:, part] = jnp.transpose(v_ref[part, :])
        return 0

    lax.fori_loop(0, i + 1, turn, 0)
    lane = lax.broadcasted_iota(jnp.int32, (blk, 128), 1)
    q = q_ref[...] * jnp.asarray(0.125, BF)
    zero = jnp.zeros_like(q)
    qs = (jnp.where(lane < HD, q, zero), jnp.where(lane < HD, zero, q))

    def step(j, carry, diag):
        start = pl.multiple_of(j * blk, blk)
        kb = k_ref[pl.ds(start, blk), :]
        out = []
        for h in range(2):
            m, l, acc = carry[h]
            s = dotg(kb, qs[h], NT)
            if diag:
                key = lax.broadcasted_iota(jnp.int32, (blk, blk), 0)
                qry = lax.broadcasted_iota(jnp.int32, (blk, blk), 1)
                s = jnp.where((key <= qry) & (key + start < length), s, -1e30)
            mn = jnp.maximum(m, jnp.max(s, axis=0, keepdims=True))
            p = jnp.exp(s - mn)
            al = jnp.exp(m - mn)
            l = l * al + jnp.sum(p, axis=0, keepdims=True)
            vb = vt[HD * h : HD * h + HD, pl.ds(start, blk)]
            acc = acc * al + dotg(vb, p.astype(BF))
            out.append((mn, l, acc))
        return tuple(out)

    init = tuple(
        (jnp.full((1, blk), -1e30, F32), jnp.zeros((1, blk), F32), jnp.zeros((HD, blk), F32))
        for _ in range(2)
    )
    c = lax.fori_loop(0, i, lambda j, c: step(j, c, False), init)
    c = step(i, c, True)
    ot = jnp.concatenate([c[h][2] / c[h][1] for h in range(2)], axis=0)
    low = jnp.transpose(ot).astype(BF)
    o_ref[...] = low
    lse_ref[0] = jnp.concatenate([c[h][0] + jnp.log(c[h][1]) for h in range(2)], axis=0)
    part = dotg(low, w_ref[...])

    @pl.when(pair == 0)
    def _():
        acc_ref[...] = part

    @pl.when(pair > 0)
    def _():
        acc_ref[...] += part

    @pl.when(pair == pl.num_programs(0) - 1)
    def _():
        share_ref[...] = acc_ref[...].astype(share_ref.dtype)


def attend(at, length, joint, w_out, held, kind, blk):
    rows, width, depth = joint.shape[0], w_out.shape[0], w_out.shape[1]
    pairs = width // 128
    return pl.pallas_call(
        functools.partial(attend_kernel, blk=blk),
        grid_spec=pltpu.PrefetchScalarGridSpec(
            num_scalar_prefetch=2,
            grid=(pairs,),
            in_specs=[
                pl.BlockSpec((blk, 128), lambda p, at, *_: (at[0], p)),
                pl.BlockSpec((rows, 128), lambda p, *_: (0, pairs + p)),
                pl.BlockSpec((rows, 128), lambda p, *_: (0, 2 * pairs + p)),
                pl.BlockSpec((128, depth), lambda p, *_: (p, 0)),
            ]
            + [pl.BlockSpec(memory_space=pl.ANY)] * len(held),
            out_specs=[
                pl.BlockSpec((blk, 128), lambda p, at, *_: (at[0], p)),
                pl.BlockSpec((1, 2, blk), lambda p, at, *_: (p, 0, at[0])),
                pl.BlockSpec((blk, depth), lambda p, *_: (0, 0)),
            ],
            scratch_shapes=[pltpu.VMEM((128, rows), BF), pltpu.VMEM((blk, depth), F32)],
        ),
        out_shape=[
            jax.ShapeDtypeStruct((rows, width), BF),
            jax.ShapeDtypeStruct((pairs, 2, rows), F32),
            jax.ShapeDtypeStruct((blk, depth), kind),
        ],
        input_output_aliases={6: 0, 7: 1} if held else {},
        compiler_params=pltpu.CompilerParams(vmem_limit_bytes=60 * MIB),
        cost_estimate=pl.CostEstimate(flops=rows * width, bytes_accessed=rows * width, transcendentals=0),
        name="attend",
    )(at, length, joint, joint, joint, w_out, *held)


def attend_back_kernel(
    len_ref, q_ref, k_ref, v_ref, o_ref, do_ref, lse_ref, cos_ref, sin_ref,
    dq_ref, dk_ref, dv_ref, kt, dlt, dqt, *, blk, blocks,
):
    j = pl.program_id(1)
    length = len_ref[0]

    @pl.when(j == 0)
    def _():
        kt[...] = jnp.transpose(k_ref[...])
        dqt[...] = jnp.zeros_like(dqt)

        def body(i, _):
            at = pl.ds(pl.multiple_of(i * blk, blk), blk)
            both = jnp.transpose(do_ref[at, :].astype(F32) * o_ref[at, :].astype(F32))
            for h in range(2):
                dlt[h : h + 1, at] = jnp.sum(both[HD * h : HD * h + HD], axis=0, keepdims=True)
            return 0

        lax.fori_loop(0, blocks, body, 0)

    js = pl.multiple_of(j * blk, blk)
    lane = lax.broadcasted_iota(jnp.int32, (blk, 128), 1)
    kb = k_ref[pl.ds(js, blk), :] * jnp.asarray(0.125, BF)
    vb = v_ref[pl.ds(js, blk), :]
    zero = jnp.zeros_like(kb)
    ks = (jnp.where(lane < HD, kb, zero), jnp.where(lane < HD, zero, kb))
    vs = (jnp.where(lane < HD, vb, zero), jnp.where(lane < HD, zero, vb))

    def step(i, carry, diag):
        at = pl.ds(pl.multiple_of(i * blk, blk), blk)
        qb, dob = q_ref[at, :], do_ref[at, :]
        out = []
        for h in range(2):
            dk, dv = carry[h]
            s = dotg(ks[h], qb, NT)
            if diag:
                key = lax.broadcasted_iota(jnp.int32, (blk, blk), 0)
                qry = lax.broadcasted_iota(jnp.int32, (blk, blk), 1)
                s = jnp.where((key <= qry) & (key + js < length), s, -1e30)
            p = jnp.exp(s - lse_ref[0, h : h + 1, at])
            dp = dotg(vs[h], dob, NT)
            ds = (p * (dp - dlt[h : h + 1, at])).astype(BF)
            dv = dv + dotg(p.astype(BF), dob)
            dk = dk + dotg(ds, qb)
            dqt[HD * h : HD * h + HD, at] += dotg(kt[HD * h : HD * h + HD, pl.ds(js, blk)], ds)
            out.append((dk, dv))
        return tuple(out)

    z = jnp.zeros((blk, 128), F32)
    c = step(j, ((z, z), (z, z)), True)
    c = lax.fori_loop(j + 1, blocks, lambda i, c: step(i, c, False), c)
    grad = jnp.where(lane < HD, c[0][0], c[1][0]) * 0.125
    dk_ref[...] = rotate(grad, cos_ref[pl.ds(js, blk), :], -sin_ref[pl.ds(js, blk), :]).astype(BF)
    dv_ref[...] = jnp.where(lane < HD, c[0][1], c[1][1]).astype(BF)

    @pl.when(j == blocks - 1)
    def _():
        def body(i, _):
            at = pl.ds(pl.multiple_of(i * blk, blk), blk)
            grad = jnp.transpose(dqt[:, at]) * 0.125
            dq_ref[at, :] = rotate(grad, cos_ref[at, :], -sin_ref[at, :]).astype(BF)
            return 0

        lax.fori_loop(0, blocks, body, 0)


def attend_back(length, joint, mixed, dmixed, lse, cos, sin, width, blk=512):
    rows = joint.shape[0]
    pairs, blocks = width // 128, rows // blk
    full = lambda off: pl.BlockSpec((rows, 128), lambda p, j, *_: (0, off * pairs + p))
    angle = pl.BlockSpec((rows, 128), lambda p, j, *_: (0, 0))
    block = pl.BlockSpec((blk, 128), lambda p, j, *_: (j, p))
    return pl.pallas_call(
        functools.partial(attend_back_kernel, blk=blk, blocks=blocks),
        grid_spec=pltpu.PrefetchScalarGridSpec(
            num_scalar_prefetch=1,
            grid=(pairs, blocks),
            in_specs=[full(0), full(1), full(2), full(0), full(0)]
            + [pl.BlockSpec((1, 2, rows), lambda p, j, *_: (p, 0, 0)), angle, angle],
            out_specs=[full(0), block, block],
            scratch_shapes=[
                pltpu.VMEM((128, rows), BF),
                pltpu.VMEM((2, rows), F32),
                pltpu.VMEM((128, rows), F32),
            ],
        ),
        out_shape=[jax.ShapeDtypeStruct((rows, width), BF)] * 3,
        compiler_params=pltpu.CompilerParams(vmem_limit_bytes=60 * MIB),
        cost_estimate=pl.CostEstimate(
            flops=rows * width, bytes_accessed=rows * width, transcendentals=0
        ),
        name="attend_back",
    )(length, joint, joint, joint, mixed, dmixed, lse, cos, sin)


def gelu_parts(v):
    c = 0.7978845608028654
    return c, jnp.tanh(c * (v + 0.044715 * v * v * v))


def gelu(v):
    return 0.5 * v * (1.0 + gelu_parts(v)[1])


def gelu_both(v):
    c, t = gelu_parts(v)
    half = 0.5 * (1.0 + t)
    return v * half, half + 0.5 * v * (1.0 - t * t) * c * (1.0 + 3 * 0.044715 * v * v)


def norm_parts(values):
    average = jnp.mean(values, axis=-1, keepdims=True)
    centred = values - average
    scale = lax.rsqrt(jnp.mean(centred * centred, axis=-1, keepdims=True) + EPSILON)
    return centred * scale, scale


def norm_back(grad, hat, scale, gain):
    g = grad * gain
    return scale * (
        g - jnp.mean(g, axis=-1, keepdims=True) - hat * jnp.mean(g * hat, axis=-1, keepdims=True)
    )


def column_sum(v):
    return jnp.sum(v, axis=0, keepdims=True)


def valid_rows(info_ref, start, count):
    at = info_ref[1] + start + lax.broadcasted_iota(jnp.int32, (count, 1), 0)
    return (at < info_ref[0]).astype(F32)


def loop_rows(rows, blk, body):
    def step(i, _):
        body(pl.multiple_of(i * blk, blk))
        return 0

    lax.fori_loop(0, rows // blk, step, 0)


def feed_kernel(info_ref, *refs, groups, chunks, sub):
    x_ref, bias_ref, resid_ref, cot_ref, bd_ref, gain_ref, shift_ref = refs[:7]
    ups, downs = refs[7 : 7 + groups], refs[7 + groups : 7 + 2 * groups]
    pre_ref, act_ref, out_ref, gb_ref, sums_ref, acc = refs[7 + 2 * groups :]
    step = pl.program_id(0)
    rows = x_ref.shape[0]

    @pl.when(step == 0)
    def _():
        acc[...] = jnp.zeros_like(acc) + bd_ref[...].astype(F32)

    for g in range(groups):

        @pl.when(step // chunks == g)
        def _():
            for r in range(0, rows, sub):
                pre = dotg(x_ref[r : r + sub], ups[g][...]) + bias_ref[0]
                pre_ref[r : r + sub] = pre
                act = gelu(pre).astype(BF)
                if g == 0:
                    act_ref[r : r + sub] = act
                acc[r : r + sub] += dotg(act, downs[g][...])

    @pl.when(step == groups * chunks - 1)
    def _():
        sums_ref[...] = jnp.zeros_like(sums_ref)
        gain, shift = gain_ref[3:4], shift_ref[3:4]

        def body(r):
            at = pl.ds(r, 64)
            valid = valid_rows(info_ref, r, 64)
            hat, scale = norm_parts(acc[at])
            out_ref[at] = (valid * (resid_ref[at] + hat * gain + shift)).astype(BF)
            g_out = valid * cot_ref[at].astype(F32)
            low = norm_back(g_out, hat, scale, gain).astype(BF)
            gb_ref[at] = low
            sums_ref[0:1] += column_sum(g_out * hat)
            sums_ref[1:2] += column_sum(g_out)
            sums_ref[2:3] += column_sum(low.astype(F32))

        loop_rows(rows, 64, body)


def feed(info, x, biases, ups, downs, resid, cot, bias_down, gains, shifts, cols=512):
    rows, depth = x.shape
    groups, hidden = len(ups), ups[0].shape[1]
    chunks = hidden // cols
    once = lambda shape: pl.BlockSpec(shape, lambda s, *_: (0, 0), pipeline_mode=pl.Buffered(1))
    own = lambda g: (lambda s, *_: (0, jnp.clip(s - g * chunks, 0, chunks - 1)))
    own_t = lambda g: (lambda s, *_: (jnp.clip(s - g * chunks, 0, chunks - 1), 0))
    return pl.pallas_call(
        functools.partial(feed_kernel, groups=groups, chunks=chunks, sub=min(512, rows)),
        grid_spec=pltpu.PrefetchScalarGridSpec(
            num_scalar_prefetch=1,
            grid=(groups * chunks,),
            in_specs=[
                once((rows, depth)),
                pl.BlockSpec((1, 1, cols), lambda s, *_: (s, 0, 0)),
                once((rows, depth)),
                once((rows, depth)),
                once((1, depth)),
                once(gains.shape),
                once(gains.shape),
            ]
            + [pl.BlockSpec((depth, cols), own(g)) for g in range(groups)]
            + [pl.BlockSpec((cols, depth), own_t(g)) for g in range(groups)],
            out_specs=[
                pl.BlockSpec((rows, cols), lambda s, *_: (0, s)),
                pl.BlockSpec((rows, cols), own(0)),
                once((rows, depth)),
                once((rows, depth)),
                once((8, depth)),
            ],
            scratch_shapes=[pltpu.VMEM((rows, depth), F32)],
        ),
        out_shape=[
            jax.ShapeDtypeStruct((rows, groups * hidden), F32),
            jax.ShapeDtypeStruct((rows, hidden), BF),
            jax.ShapeDtypeStruct((rows, depth), BF),
            jax.ShapeDtypeStruct((rows, depth), BF),
            jax.ShapeDtypeStruct((8, depth), F32),
        ],
        compiler_params=pltpu.CompilerParams(vmem_limit_bytes=60 * MIB),
        cost_estimate=pl.CostEstimate(
            flops=rows * depth, bytes_accessed=rows * depth, transcendentals=0
        ),
        name="feed",
    )(info, x, biases.reshape(-1, 1, cols), resid, cot, bias_down, gains, shifts, *ups, *downs)


def feed_back_kernel(info_ref, *refs, groups, chunks, sub):
    gb_ref, pre_ref, resid_ref, attn_ref, cot_ref, gain_ref = refs[:6]
    ups, downs = refs[6 : 6 + groups], refs[6 + groups : 6 + 2 * groups]
    gp_ref, gr_ref, ga_ref, sums_ref, acc = refs[6 + 2 * groups :]
    step = pl.program_id(0)
    rows = gb_ref.shape[0]

    @pl.when(step == 0)
    def _():
        acc[...] = jnp.zeros_like(acc)

    for g in range(groups):

        @pl.when(step // chunks == g)
        def _():
            for r in range(0, rows, sub):
                grad = dotg(gb_ref[r : r + sub], downs[g][...], NT)
                low = (grad * gelu_both(pre_ref[r : r + sub])[1]).astype(BF)
                if g == 0:
                    gp_ref[r : r + sub] = low
                acc[r : r + sub] += dotg(low, ups[g][...], NT)

    @pl.when(step == groups * chunks - 1)
    def _():
        sums_ref[...] = jnp.zeros_like(sums_ref)

        def body(r):
            at = pl.ds(r, 64)
            g_out = valid_rows(info_ref, r, 64) * cot_ref[at].astype(F32)
            hat, scale = norm_parts(resid_ref[at])
            g_two = acc[at]
            g_resid = g_out + norm_back(g_two, hat, scale, gain_ref[2:3])
            gr_ref[at] = g_resid
            sums_ref[0:1] += column_sum(g_two * hat)
            sums_ref[1:2] += column_sum(g_two)
            hat, scale = norm_parts(attn_ref[at])
            ga_ref[at] = norm_back(g_resid, hat, scale, gain_ref[1:2]).astype(BF)
            sums_ref[2:3] += column_sum(g_resid * hat)
            sums_ref[3:4] += column_sum(g_resid)

        loop_rows(rows, 64, body)


def feed_back(info, gb, pre, ups, downs, resid, attn_sum, cot, gains, cols=512):
    rows, depth = gb.shape
    groups, hidden = len(ups), ups[0].shape[1]
    chunks = hidden // cols
    once = lambda shape: pl.BlockSpec(shape, lambda s, *_: (0, 0), pipeline_mode=pl.Buffered(1))
    own = lambda g: (lambda s, *_: (0, jnp.clip(s - g * chunks, 0, chunks - 1)))
    own_t = lambda g: (lambda s, *_: (jnp.clip(s - g * chunks, 0, chunks - 1), 0))
    return pl.pallas_call(
        functools.partial(feed_back_kernel, groups=groups, chunks=chunks, sub=min(512, rows)),
        grid_spec=pltpu.PrefetchScalarGridSpec(
            num_scalar_prefetch=1,
            grid=(groups * chunks,),
            in_specs=[
                once((rows, depth)),
                pl.BlockSpec((rows, cols), lambda s, *_: (0, s)),
                once((rows, depth)),
                once((rows, depth)),
                once((rows, depth)),
                once(gains.shape),
            ]
            + [pl.BlockSpec((depth, cols), own(g)) for g in range(groups)]
            + [pl.BlockSpec((cols, depth), own_t(g)) for g in range(groups)],
            out_specs=[
                pl.BlockSpec((rows, cols), own(0)),
                once((rows, depth)),
                once((rows, depth)),
                once((8, depth)),
            ],
            scratch_shapes=[pltpu.VMEM((rows, depth), F32)],
        ),
        out_shape=[
            jax.ShapeDtypeStruct((rows, hidden), BF),
            jax.ShapeDtypeStruct((rows, depth), F32),
            jax.ShapeDtypeStruct((rows, depth), BF),
            jax.ShapeDtypeStruct((8, depth), F32),
        ],
        compiler_params=pltpu.CompilerParams(vmem_limit_bytes=60 * MIB),
        cost_estimate=pl.CostEstimate(
            flops=rows * depth, bytes_accessed=rows * depth, transcendentals=0
        ),
        name="feed_back",
    )(info, gb, pre, resid, attn_sum, cot, gains, *ups, *downs)


def feed_grad_kernel(*refs, groups):
    up_ref, down_ref, bias_ref, act_ref, gp_ref = refs[:5]
    n2s, gbs = refs[5 : 5 + groups], refs[5 + groups : 5 + 2 * groups]
    grad_ref, sum_ref = refs[5 + 2 * groups :]
    act, gp = act_ref[...], gp_ref[...]
    dup = dotg(gp, n2s[0][...], TN)
    ddown = dotg(act, gbs[0][...], TN)
    sums = column_sum(gp.astype(F32))
    for g in range(1, groups):
        pre = dotg(n2s[g][...], up_ref[...]) + bias_ref[0]
        act, slope = gelu_both(pre)
        act = act.astype(BF)
        gp = (dotg(gbs[g][...], down_ref[...], NT) * slope).astype(BF)
        dup += dotg(gp, n2s[g][...], TN)
        ddown += dotg(act, gbs[g][...], TN)
        sums += column_sum(gp.astype(F32))
    grad_ref[0] = dup.astype(BF)
    grad_ref[1] = ddown.astype(BF)
    sum_ref[0] = sums


def feed_grad(up, down, bias, act, gp, n2s, gbs, cols=256):
    rows, depth = n2s[0].shape
    groups, hidden = len(n2s), up.shape[1]
    once = lambda shape: pl.BlockSpec(shape, lambda s: (0, 0), pipeline_mode=pl.Buffered(1))
    wide = lambda count: pl.BlockSpec((count, cols), lambda s: (0, s))
    tall = pl.BlockSpec((cols, depth), lambda s: (s, 0))
    flat = pl.BlockSpec((1, 1, cols), lambda s: (s, 0, 0))
    return pl.pallas_call(
        functools.partial(feed_grad_kernel, groups=groups),
        grid=(hidden // cols,),
        in_specs=[wide(depth), tall, flat, wide(rows), wide(rows)] + [once((rows, depth))] * (2 * groups),
        out_specs=[pl.BlockSpec((2, cols, depth), lambda s: (0, s, 0)), flat],
        out_shape=[
            jax.ShapeDtypeStruct((2, hidden, depth), BF),
            jax.ShapeDtypeStruct((hidden // cols, 1, cols), F32),
        ],
        compiler_params=pltpu.CompilerParams(vmem_limit_bytes=60 * MIB),
        cost_estimate=pl.CostEstimate(
            flops=(8 * groups - 4) * rows * depth * hidden, bytes_accessed=20 * rows * depth, transcendentals=0
        ),
        name="feed_grad",
    )(up, down, bias.reshape(-1, 1, cols), act, gp, *n2s, *gbs)


def norm_kernel(x_ref, gain_ref, shift_ref, o_ref):
    hat, _ = norm_parts(x_ref[...].astype(F32))
    o_ref[...] = (hat * gain_ref[0:1] + shift_ref[0:1]).astype(BF)


def first_norm(x, gains, shifts, blk=128):
    rows, depth = x.shape
    whole = pl.BlockSpec(gains.shape, lambda i: (0, 0))
    block = pl.BlockSpec((blk, depth), lambda i: (i, 0))
    return pl.pallas_call(
        norm_kernel,
        grid=(rows // blk,),
        in_specs=[block, whole, whole],
        out_specs=block,
        out_shape=jax.ShapeDtypeStruct((rows, depth), BF),
        compiler_params=pltpu.CompilerParams(vmem_limit_bytes=60 * MIB),
        name="first_norm",
    )(x, gains, shifts)


def join_kernel(pick_ref, x_ref, gain_ref, shift_ref, *refs, blocks, each):
    parts, (attn_ref, resid_ref, low_ref) = refs[:-3], refs[-3:]
    block = pl.program_id(0) // each
    total = None
    for g in range(len(parts) // blocks):
        wanted = pick_ref[g * blocks + block]
        part = parts[g * blocks][...]
        for b in range(1, blocks):
            part = jnp.where(wanted == b, parts[g * blocks + b][...], part)
        total = part if total is None else total + part.astype(F32)
    attn_ref[...] = total
    hat, _ = norm_parts(total)
    resid = x_ref[...].astype(F32) + hat * gain_ref[1:2] + shift_ref[1:2]
    resid_ref[...] = resid
    hat, _ = norm_parts(resid)
    low_ref[...] = (hat * gain_ref[2:3] + shift_ref[2:3]).astype(BF)


def join(x, gains, shifts, shares, picks, blk=256):
    rows, depth = x.shape
    blocks = len(shares[0])
    blk = min(blk, rows // blocks)
    each = rows // blocks // blk
    whole = pl.BlockSpec(gains.shape, lambda i, *_: (0, 0))
    block = pl.BlockSpec((blk, depth), lambda i, *_: (i, 0))
    part = pl.BlockSpec((blk, depth), lambda i, *_: (lax.rem(i, each), 0))
    return pl.pallas_call(
        functools.partial(join_kernel, blocks=blocks, each=each),
        grid_spec=pltpu.PrefetchScalarGridSpec(
            num_scalar_prefetch=1,
            grid=(rows // blk,),
            in_specs=[block, whole, whole] + [part] * (len(shares) * blocks),
            out_specs=[block, block, block],
        ),
        out_shape=[
            jax.ShapeDtypeStruct((rows, depth), F32),
            jax.ShapeDtypeStruct((rows, depth), F32),
            jax.ShapeDtypeStruct((rows, depth), BF),
        ],
        compiler_params=pltpu.CompilerParams(vmem_limit_bytes=60 * MIB),
        name="join",
    )(picks, x, gains, shifts, *[v for share in shares for v in share])


def attention_grad_kernel(me_ref, gq_ref, gk_ref, gv_ref, mixed_ref, *refs, groups):
    n1s, gas, o_ref = refs[:groups], refs[groups : 2 * groups], refs[2 * groups]
    rows = n1s[0].shape[0]
    for i, g_ref in enumerate((gq_ref, gk_ref, gv_ref, mixed_ref)):

        @pl.when(pl.program_id(0) == i)
        def _():
            total = None
            for r in range(groups):
                start = pl.multiple_of(lax.rem(me_ref[0] + r, groups) * rows, rows)
                left = n1s[r] if i < 3 else gas[r]
                part = dotg(left[...], g_ref[pl.ds(start, rows), :], TN)
                total = part if total is None else total + part
            o_ref[...] = total.astype(BF)


def attention_grad(me, g_query, g_key, g_value, mixed, n1s, gas):
    rows, depth = n1s[0].shape
    slots, width = g_query.shape
    once = lambda shape: pl.BlockSpec(shape, lambda i, *_: (0, 0), pipeline_mode=pl.Buffered(1))
    return pl.pallas_call(
        functools.partial(attention_grad_kernel, groups=len(n1s)),
        grid_spec=pltpu.PrefetchScalarGridSpec(
            num_scalar_prefetch=1,
            grid=(4,),
            in_specs=[once((slots, width))] * 4 + [once((rows, depth))] * (2 * len(n1s)),
            out_specs=pl.BlockSpec((depth, width), lambda i, *_: (i, 0)),
        ),
        out_shape=jax.ShapeDtypeStruct((4 * depth, width), BF),
        compiler_params=pltpu.CompilerParams(vmem_limit_bytes=60 * MIB),
        name="attention_grad",
    )(me, g_query, g_key, g_value, mixed, *n1s, *gas)


def share_kernel(at_ref, gq_ref, gk_ref, gv_ref, wq_ref, wk_ref, wv_ref, o_ref):
    total = dotg(gq_ref[...], wq_ref[...], NT)
    total += dotg(gk_ref[...], wk_ref[...], NT)
    total += dotg(gv_ref[...], wv_ref[...], NT)
    o_ref[...] = total.astype(o_ref.dtype)


def share_of(at, grads, weights, rows, kind, blk=256):
    (slots, width), depth = grads[0].shape, weights[0].shape[0]
    blk = min(blk, rows)
    count = rows // blk
    return pl.pallas_call(
        share_kernel,
        grid_spec=pltpu.PrefetchScalarGridSpec(
            num_scalar_prefetch=1,
            grid=(count,),
            in_specs=[pl.BlockSpec((blk, width), lambda i, at: (at[0] * count + i, 0))] * 3
            + [pl.BlockSpec((depth, width), lambda i, at: (0, 0))] * 3,
            out_specs=pl.BlockSpec((blk, depth), lambda i, at: (i, 0)),
        ),
        out_shape=jax.ShapeDtypeStruct((rows, depth), kind),
        compiler_params=pltpu.CompilerParams(vmem_limit_bytes=60 * MIB),
        name="share_of",
    )(at, *grads, *weights)


def last_kernel(x_ref, gr_ref, gain_ref, *refs):
    shares, (o_ref, sums_ref) = refs[:-2], refs[-2:]
    total = shares[0][...]
    for r in shares[1:]:
        total = total + r[...].astype(F32)
    hat, scale = norm_parts(x_ref[...].astype(F32))
    o_ref[...] = (gr_ref[...] + norm_back(total, hat, scale, gain_ref[0:1])).astype(BF)

    @pl.when(pl.program_id(0) == 0)
    def _():
        sums_ref[...] = jnp.zeros_like(sums_ref)

    sums_ref[0:1] += column_sum(total * hat)
    sums_ref[1:2] += column_sum(total)


def last_norm(x, g_resid, gains, shares, blk=128):
    rows, depth = x.shape
    block = pl.BlockSpec((blk, depth), lambda i: (i, 0))
    return pl.pallas_call(
        last_kernel,
        grid=(rows // blk,),
        in_specs=[block, block, pl.BlockSpec(gains.shape, lambda i: (0, 0))] + [block] * len(shares),
        out_specs=[block, pl.BlockSpec((8, depth), lambda i: (0, 0))],
        out_shape=[jax.ShapeDtypeStruct((rows, depth), BF), jax.ShapeDtypeStruct((8, depth), F32)],
        compiler_params=pltpu.CompilerParams(vmem_limit_bytes=60 * MIB),
        name="last_norm",
    )(x, g_resid, gains, *shares)


def widen_kernel(up_ref, down_ref, dup_ref, ddown_ref):
    dup_ref[...] = jnp.transpose(up_ref[...]).astype(F32)
    ddown_ref[...] = down_ref[...].astype(F32)


def widen(grads, blk=256):
    hidden, depth = grads.shape[0] // 2, grads.shape[1]
    blk = min(blk, hidden)
    count = hidden // blk
    return pl.pallas_call(
        widen_kernel,
        grid=(count,),
        in_specs=[
            pl.BlockSpec((blk, depth), lambda i: (i, 0)),
            pl.BlockSpec((blk, depth), lambda i: (count + i, 0)),
        ],
        out_specs=[
            pl.BlockSpec((depth, blk), lambda i: (0, i)),
            pl.BlockSpec((blk, depth), lambda i: (i, 0)),
        ],
        out_shape=[
            jax.ShapeDtypeStruct((depth, hidden), F32),
            jax.ShapeDtypeStruct((hidden, depth), F32),
        ],
        compiler_params=pltpu.CompilerParams(vmem_limit_bytes=60 * MIB),
        name="widen",
    )(grads, grads)

MESH = pl.DeviceIdType.MESH


def exchange(src, dst, sems, slot, bit):
    peer = lax.axis_index("dp") ^ (1 << bit)
    return pltpu.make_async_remote_copy(
        src_ref=src,
        dst_ref=dst,
        send_sem=sems[0].at[slot],
        recv_sem=sems[1].at[slot],
        device_id={"dp": peer},
        device_id_type=MESH,
    )


def greet(axes_bits):
    barrier = pltpu.get_barrier_semaphore()
    for axis, bit in axes_bits:
        peer = lax.axis_index(axis) ^ (1 << bit)
        pl.semaphore_signal(barrier, inc=1, device_id={axis: peer}, device_id_type=MESH)
    pl.semaphore_wait(barrier, len(axes_bits))


def total_kernel(g_ref, shard_ref, sum_ref, all_ref, core_buf, buf, acc, send, recv, local, *, bits):
    sems = (send, recv)
    me = lax.axis_index("dp")
    bit = lambda b: lax.rem(lax.div(me, 1 << b), 2)
    core = bit(0)
    outer = list(range(1, bits))
    orders = [outer, outer, outer, outer[1:] + outer[:1]]
    half = g_ref.shape[0] // 2
    base = pl.multiple_of(core * half, half)
    part = half // 4
    piece = shard_ref.shape[0] // 4
    slots = iter(range(send.shape[0]))
    place = tuple(bit(b) for b in reversed(range(bits)))

    def copy(src, dst, b):
        c = exchange(src, dst, sems, next(slots), b)
        c.start()
        return c

    forwards = []

    def gather(chunk):
        order = orders[chunk][::-1]
        rows = pl.ds(chunk * piece, piece)

        def region(done, other=None):
            index = [
                slice(None) if b in done else (1 - bit(b) if b == other else bit(b))
                for b in reversed(range(bits))
            ]
            return all_ref.at[tuple(index) + (rows,)]

        own = region([])
        forwards.append(copy(own, own, 0))
        for k, b in enumerate(order):
            mine = region(order[:k])
            c = copy(mine, mine, b)
            yield
            c.wait()
            got = region(order[:k], b)
            forwards.append(copy(got, got, 0))

    def reduce(chunk):
        order = orders[chunk]
        start, size = chunk * part, part
        first = chunk * (part - part // (1 << (bits - 1)))
        for b in order:
            size //= 2
            away = pl.multiple_of(start + (1 - bit(b)) * size, size)
            landing = buf.at[pl.ds(first, size)]
            c = copy(acc.at[pl.ds(away, size)], landing, b)
            start = start + bit(b) * size
            yield
            c.wait()
            step = min(size, 64)

            def body(i, _, start=start, first=first, step=step):
                at = pl.ds(pl.multiple_of(start + i * step, step), step)
                got = buf[pl.ds(pl.multiple_of(first + i * step, step), step)].astype(F32)
                acc[at] = (acc[at].astype(F32) + got).astype(BF)
                return 0

            lax.fori_loop(0, size // step, body, 0)
            first += size
        start = base + start
        sum_ref[pl.ds(pl.multiple_of(start, size), size)] = acc[
            pl.ds(pl.multiple_of(start - base, size), size)
        ]
        for b in reversed(order):
            mine = sum_ref.at[pl.ds(pl.multiple_of(start, size), size)]
            c = copy(mine, mine, b)
            yield
            c.wait()
            start = start - bit(b) * size
            size *= 2
        mine = sum_ref.at[pl.ds(pl.multiple_of(start, size), size)]
        forwards.append(copy(mine, mine, 0))

    greet([("dp", b) for b in range(bits)])
    own = pltpu.make_async_copy(shard_ref, all_ref.at[place], local)
    own.start()
    away = pl.multiple_of((1 - core) * half, half)
    cores = [
        copy(g_ref.at[pl.ds(away + c * part, part)], core_buf.at[pl.ds(c * part, part)], 0)
        for c in range(4)
    ]
    own.wait()

    def joined(chunk):
        cores[chunk].wait()

        def body(i, _):
            at = pl.ds(pl.multiple_of(chunk * part + i * 64, 64), 64)
            own = g_ref[pl.ds(pl.multiple_of(base + chunk * part + i * 64, 64), 64)].astype(F32)
            acc[at] = (own + core_buf[at].astype(F32)).astype(BF)
            return 0

        lax.fori_loop(0, part // 64, body, 0)
        yield from reduce(chunk)

    active = [f(c) for c in range(4) for f in (gather, joined)]
    while active:
        still = []
        for chain in active:
            try:
                next(chain)
                still.append(chain)
            except StopIteration:
                pass
        active = still
    for c in forwards:
        c.wait()


def total(g, shard, bits):
    rows, width = g.shape
    half = rows // 2
    landing = half - half // (1 << (bits - 1))
    count = 8 * bits + 8 * (bits - 1) + 16
    vmem = pl.BlockSpec(memory_space=pltpu.VMEM)
    anyspace = pl.BlockSpec(memory_space=pl.ANY)
    summed, every = pl.pallas_call(
        functools.partial(total_kernel, bits=bits),
        in_specs=[vmem, anyspace],
        out_specs=[vmem, anyspace],
        out_shape=[
            jax.ShapeDtypeStruct((rows, width), BF),
            jax.ShapeDtypeStruct((2,) * bits + shard.shape, BF),
        ],
        scratch_shapes=[
            pltpu.VMEM((half, width), BF),
            pltpu.VMEM((landing, width), BF),
            pltpu.VMEM((half, width), BF),
            pltpu.SemaphoreType.DMA((count,)),
            pltpu.SemaphoreType.DMA((count,)),
            pltpu.SemaphoreType.DMA,
        ],
        compiler_params=pltpu.CompilerParams(
            collective_id=1, has_side_effects=True, vmem_limit_bytes=32 * MIB
        ),
        cost_estimate=pl.CostEstimate(
            flops=100 * rows * width * width, bytes_accessed=rows * width, transcendentals=0
        ),
        name="total",
    )(g, shard)
    return summed, every.reshape((-1,) + shard.shape[1:])


def vector_kernel(x_ref, o_ref, bufs, send, recv, *, steps):
    greet(steps)
    o_ref[...] = x_ref[...]
    for k, (axis, bit) in enumerate(steps):
        copy = pltpu.make_async_remote_copy(
            src_ref=o_ref,
            dst_ref=bufs.at[k],
            send_sem=send.at[k],
            recv_sem=recv.at[k],
            device_id={axis: lax.axis_index(axis) ^ (1 << bit)},
            device_id_type=MESH,
        )
        copy.start()
        copy.wait()
        o_ref[...] += bufs[k]


def vector_sum(x, steps):
    vmem = pl.BlockSpec(memory_space=pltpu.VMEM)
    return pl.pallas_call(
        functools.partial(vector_kernel, steps=steps),
        in_specs=[vmem],
        out_specs=vmem,
        out_shape=jax.ShapeDtypeStruct(x.shape, F32),
        scratch_shapes=[
            pltpu.VMEM((len(steps),) + x.shape, F32),
            pltpu.SemaphoreType.DMA((len(steps),)),
            pltpu.SemaphoreType.DMA((len(steps),)),
        ],
        compiler_params=pltpu.CompilerParams(collective_id=2, has_side_effects=True),
        name="vector_sum",
    )(x)


def mixed_back_kernel(at_ref, x_ref, w_ref, *refs):
    refs[-1][...] = dotg(x_ref[...], w_ref[...], NT).astype(BF)


def mixed_back(where, x, w_out, slots, held, blk=256):
    rows, depth = x.shape
    width = w_out.shape[0]
    blk = min(blk, rows)
    count = rows // blk
    return pl.pallas_call(
        mixed_back_kernel,
        grid_spec=pltpu.PrefetchScalarGridSpec(
            num_scalar_prefetch=1,
            grid=(count,),
            in_specs=[
                pl.BlockSpec((blk, depth), lambda i, at: (i, 0)),
                pl.BlockSpec((width, depth), lambda i, at: (0, 0)),
            ]
            + [pl.BlockSpec(memory_space=pl.ANY)] * len(held),
            out_specs=pl.BlockSpec((blk, width), lambda i, at: (at[0] * count + i, 0)),
        ),
        out_shape=jax.ShapeDtypeStruct((slots, width), BF),
        input_output_aliases={3: 0} if held else {},
        compiler_params=pltpu.CompilerParams(vmem_limit_bytes=60 * MIB),
        cost_estimate=pl.CostEstimate(flops=rows * depth, bytes_accessed=rows * depth, transcendentals=0),
        name="mixed_back",
    )(where, x, w_out, *held)


def shift(x, axis, count, step):
    return lax.ppermute(x, axis, [((i + step) % count, i) for i in range(count)])


def shards(
    tokens,
    lengths,
    cotangent,
    w_query,
    w_key,
    w_value,
    w_out,
    up_weight,
    bias_up,
    down_weight,
    bias_down,
    norm_gains,
    norm_shifts,
):
    rows, _, depth = tokens.shape
    groups, replicas = lax.axis_size("tensor"), lax.axis_size("dp")
    me, replica = lax.axis_index("tensor"), lax.axis_index("dp")
    slots = rows * groups
    width = w_query.shape[1]
    hidden = up_weight.shape[1]
    x = tokens.reshape(rows, depth)
    here = me.reshape(1).astype(jnp.int32)
    place = lambda r: (here + r) % groups

    def others(v):
        return [shift(v, "tensor", groups, r) for r in range(1, groups)]

    def to_owner(v, r):
        return shift(v, "tensor", groups, groups - r)

    up_piece = lax.dynamic_slice_in_dim(up_weight, replica * (depth // replicas), depth // replicas, 0)
    down_piece = lax.dynamic_slice_in_dim(
        down_weight, replica * (hidden // replicas), hidden // replicas, 0
    )
    up_pieces, down_pieces, bias_rest = others(up_piece), others(down_piece), others(bias_up)
    gather = lambda v: lax.all_gather(v, "dp", axis=0, tiled=True)

    freqs = 10000.0 ** (-jnp.arange(HD // 2).astype(F32) * 2.0 / HD)
    angles = jnp.arange(slots).astype(F32)[:, None] * freqs[None, :]
    cosine, sine = jnp.cos(angles), jnp.sin(angles)
    cosine = jnp.concatenate([cosine] * 4, axis=1)
    sine = jnp.concatenate([-sine, sine] * 2, axis=1)
    normed_one = first_norm(x, norm_gains, norm_shifts)
    normed_one_rest = others(normed_one)
    weights = (w_query, w_key, w_value)
    joint = project(here, normed_one, *weights, cosine, sine)
    joint, normed_one_rest, up_pieces, down_pieces, bias_rest = lax.optimization_barrier(
        (joint, normed_one_rest, up_pieces, down_pieces, bias_rest)
    )
    for r, n in enumerate(normed_one_rest):
        joint = project(place(r + 1), n, *weights, cosine, sine, joint)
    blk = min(512, rows)
    each = rows // blk
    odd = lambda r: lax.rem(place(r), 2)
    ranks = lambda r, k: jnp.where(odd(r) == 1, each - 1 - k, k)
    held, shares, arrived = (), [], [[] for _ in range(1, groups)]
    for k in range(each):
        for r in range(1, groups):
            *held, share = attend(place(r) * each + ranks(0, k), lengths, joint, w_out, held, BF, blk)
            arrived[r - 1].append(to_owner(share, r))
        if k == each - 1 and k > 0:
            joint, arrived = lax.optimization_barrier((joint, [v[:k] for v in arrived])), arrived
            joint, early = joint
            arrived = [list(e) + v[k:] for e, v in zip(early, arrived)]
        *held, share = attend(here * each + ranks(0, k), lengths, joint, w_out, held, F32, blk)
        shares.append(share)
    mixed, lse = held
    shares = [shares] + arrived
    picks = jnp.concatenate([ranks(groups - r, k) for r in range(groups) for k in range(each)])
    up_rest, down_rest = [gather(p) for p in up_pieces], [gather(p) for p in down_pieces]
    shares, up_rest, down_rest = lax.optimization_barrier((shares, up_rest, down_rest))
    ups, downs = [up_weight] + up_rest, [down_weight] + down_rest
    biases = jnp.concatenate([bias_up] + bias_rest).astype(F32)

    info = jnp.stack([lengths[0], me * rows]).astype(jnp.int32)
    cot = cotangent.reshape(rows, depth)
    attn_sum, resid, normed_two = join(x, norm_gains, norm_shifts, shares, picks)
    normed_two_rest = others(normed_two)
    pre, act, layer_out, g_branch, sums3 = feed(
        info, normed_two, biases, ups, downs, resid, cot, bias_down.reshape(1, depth), norm_gains, norm_shifts
    )
    g_branch_rest = others(g_branch)
    g_branch, normed_two_rest = lax.optimization_barrier((g_branch, normed_two_rest))
    g_pre, g_resid, g_attn, sums21 = feed_back(
        info, g_branch, pre, ups, downs, resid, attn_sum, cot, norm_gains
    )
    g_attn_rest = others(g_attn)
    grad_feed, bias_up_sum = feed_grad(
        up_weight, down_weight, biases[:hidden], act, g_pre,
        [normed_two] + normed_two_rest, [g_branch] + g_branch_rest,
    )
    grad_feed = grad_feed.reshape(2 * hidden, depth)
    g_mixed = mixed_back(here, g_attn, w_out, slots, [])
    g_attn_rest, grad_feed, g_mixed = lax.optimization_barrier((g_attn_rest, grad_feed, g_mixed))
    grad_feed = lax.psum_scatter(grad_feed, "dp", scatter_dimension=0, tiled=True)
    for r, g in enumerate(g_attn_rest):
        g_mixed = mixed_back(place(r + 1), g, w_out, slots, [g_mixed])

    grads = attend_back(lengths, joint, mixed, g_mixed, lse, cosine, sine, width)
    other_shares = [share_of(place(r), grads, weights, rows, BF) for r in range(1, groups)]
    other_shares, grads = lax.optimization_barrier((other_shares, grads))
    other_shares = [to_owner(v, r + 1) for r, v in enumerate(other_shares)]
    packed = attention_grad(
        here, *grads, mixed, [normed_one] + normed_one_rest, [g_attn] + g_attn_rest
    )
    bits = (replicas - 1).bit_length()
    packed, grad_feed = total(packed, grad_feed, bits)
    own_share = share_of(here, grads, weights, rows, F32)
    packed, own_share, other_shares = lax.optimization_barrier((packed, own_share, other_shares))
    grad_tokens, sums0 = last_norm(x, g_resid, norm_gains, [own_share] + other_shares)
    grad_up, grad_down = widen(grad_feed)
    grad_query, grad_key, grad_value = (packed[i * depth : (i + 1) * depth].astype(F32) for i in range(3))
    grad_out = jnp.transpose(packed[3 * depth :]).astype(F32)

    placed = lax.dynamic_update_slice(
        jnp.zeros((groups * hidden,), F32), bias_up_sum.reshape(-1), (me * hidden,)
    ).reshape(-1, depth)
    steps = [("tensor", b) for b in range((groups - 1).bit_length())] + [("dp", b) for b in range(bits)]
    vectors = jnp.concatenate([sums3[:3], sums21[:4], sums0[:2], placed])
    sums = vector_sum(jnp.pad(vectors, ((0, -len(vectors) % 8), (0, 0))), steps)
    grad_gains = jnp.stack([sums[7], sums[5], sums[3], sums[0]])
    grad_shifts = jnp.stack([sums[8], sums[6], sums[4], sums[1]])
    grad_bias_up = lax.dynamic_slice_in_dim(sums[9 : 9 + groups * hidden // depth].reshape(-1), me * hidden, hidden, 0)
    whole = (rows, 1, depth)
    return (
        layer_out.reshape(whole),
        grad_tokens.reshape(whole),
        grad_query,
        grad_key,
        grad_value,
        grad_out,
        grad_up,
        grad_bias_up,
        grad_down,
        sums[2],
        grad_gains,
        grad_shifts,
    )


def solution(mesh):
    wide, tall = P(None, "tensor"), P("tensor", None)
    acts = P("tensor", "dp", None)
    return jax.shard_map(
        shards,
        mesh=mesh,
        in_specs=(acts, P("dp"), acts, wide, wide, wide, tall, wide, P("tensor"), tall, P(), P(), P()),
        out_specs=(acts, acts, wide, wide, wide, tall, wide, P("tensor"), tall, P(), P(), P()),
        check_vma=False,
    )
```

```python
import functools
import jax
import jax.numpy as jnp
from jax import lax
from jax.experimental import pallas as pl
from jax.experimental.pallas import tpu as pltpu
from jax.sharding import PartitionSpec as P

HD = 64
EPSILON = 1e-05
BF = jnp.bfloat16
F32 = jnp.float32
NT = (((1,), (1,)), ((), ()))
NN = (((1,), (0,)), ((), ()))
TN = (((0,), (0,)), ((), ()))
MIB = 1 << 20


def dotg(a, b, dims=NN):
    return lax.dot_general(a, b, dims, preferred_element_type=F32)


def rotate(x, cos, sin):
    first = lax.broadcasted_iota(jnp.int32, (x.shape[0], 128), 1) % HD < HD // 2
    parts = []
    for a in range(0, x.shape[1], 128):
        v = x[:, a : a + 128]
        swapped = jnp.where(first, pltpu.roll(v, 96, 1), pltpu.roll(v, 32, 1))
        parts.append(v * cos + swapped * sin)
    return jnp.concatenate(parts, axis=1) if len(parts) > 1 else parts[0]


def qkv_kernel(x_ref, wq_ref, wk_ref, wv_ref, cos_ref, sin_ref, o_ref):
    width = wq_ref.shape[1]
    x, cos, sin = x_ref[...], cos_ref[...], sin_ref[...]
    o_ref[:, :width] = rotate(dotg(x, wq_ref[...]), cos, sin).astype(BF)
    o_ref[:, width : 2 * width] = rotate(dotg(x, wk_ref[...]), cos, sin).astype(BF)
    o_ref[:, 2 * width :] = dotg(x, wv_ref[...]).astype(BF)


def project(where, x, w_query, w_key, w_value, cos, sin, joint=None, blk=256):
    rows, depth = x.shape
    width, slots = w_query.shape[1], cos.shape[0]
    blk = min(blk, rows)
    count = rows // blk
    weight = pl.BlockSpec((depth, width), lambda i, at: (0, 0))
    angle = pl.BlockSpec((blk, 128), lambda i, at: (at[0] * count + i, 0))
    kernel = lambda at, *refs: qkv_kernel(*refs[:6], refs[-1])
    held = [] if joint is None else [joint]
    return pl.pallas_call(
        kernel,
        grid_spec=pltpu.PrefetchScalarGridSpec(
            num_scalar_prefetch=1,
            grid=(count,),
            in_specs=[pl.BlockSpec((blk, depth), lambda i, at: (i, 0)), weight, weight, weight, angle, angle]
            + [pl.BlockSpec(memory_space=pl.ANY)] * len(held),
            out_specs=pl.BlockSpec((blk, 3 * width), lambda i, at: (at[0] * count + i, 0)),
        ),
        out_shape=jax.ShapeDtypeStruct((slots, 3 * width), BF),
        input_output_aliases={7: 0} if held else {},
        compiler_params=pltpu.CompilerParams(vmem_limit_bytes=60 * MIB),
        cost_estimate=pl.CostEstimate(flops=rows * depth, bytes_accessed=rows * depth, transcendentals=0),
        name="project",
    )(where, x, w_query, w_key, w_value, cos, sin, *held)


def attend_kernel(at_ref, len_ref, q_ref, k_ref, v_ref, w_ref, *refs, blk):
    o_ref, lse_ref, share_ref, vt, low_ref = refs[-5:]
    pair = pl.program_id(0)
    i = at_ref[0]
    length = len_ref[0]
    def turn(j, _):
        part = pl.ds(pl.multiple_of(j * blk, blk), blk)
        vt[:, part] = jnp.transpose(v_ref[part, :])
        return 0

    lax.fori_loop(0, i + 1, turn, 0)
    lane = lax.broadcasted_iota(jnp.int32, (blk, 128), 1)
    q = q_ref[...] * jnp.asarray(0.125, BF)
    zero = jnp.zeros_like(q)
    qs = (jnp.where(lane < HD, q, zero), jnp.where(lane < HD, zero, q))

    def step(j, carry, diag):
        start = pl.multiple_of(j * blk, blk)
        kb = k_ref[pl.ds(start, blk), :]
        out = []
        for h in range(2):
            m, l, acc = carry[h]
            s = dotg(kb, qs[h], NT)
            if diag:
                key = lax.broadcasted_iota(jnp.int32, (blk, blk), 0)
                qry = lax.broadcasted_iota(jnp.int32, (blk, blk), 1)
                s = jnp.where((key <= qry) & (key + start < length), s, -1e30)
            mn = jnp.maximum(m, jnp.max(s, axis=0, keepdims=True))
            p = jnp.exp(s - mn)
            al = jnp.exp(m - mn)
            l = l * al + jnp.sum(p, axis=0, keepdims=True)
            vb = vt[HD * h : HD * h + HD, pl.ds(start, blk)]
            acc = acc * al + dotg(vb, p.astype(BF))
            out.append((mn, l, acc))
        return tuple(out)

    init = tuple(
        (jnp.full((1, blk), -1e30, F32), jnp.zeros((1, blk), F32), jnp.zeros((HD, blk), F32))
        for _ in range(2)
    )
    c = lax.fori_loop(0, i, lambda j, c: step(j, c, False), init)
    c = step(i, c, True)
    ot = jnp.concatenate([c[h][2] / c[h][1] for h in range(2)], axis=0)
    low = jnp.transpose(ot).astype(BF)
    o_ref[...] = low
    lse_ref[0] = jnp.concatenate([c[h][0] + jnp.log(c[h][1]) for h in range(2)], axis=0)
    low_ref[pair] = low

    @pl.when(pair == pl.num_programs(0) - 1)
    def _():
        pairs = low_ref.shape[0]
        low = jnp.concatenate([low_ref[p] for p in range(pairs)], axis=1)
        share_ref[...] = dotg(low, w_ref[...]).astype(share_ref.dtype)


def attend(at, length, joint, w_out, held, kind, blk):
    rows, width, depth = joint.shape[0], w_out.shape[0], w_out.shape[1]
    pairs = width // 128
    return pl.pallas_call(
        functools.partial(attend_kernel, blk=blk),
        grid_spec=pltpu.PrefetchScalarGridSpec(
            num_scalar_prefetch=2,
            grid=(pairs,),
            in_specs=[
                pl.BlockSpec((blk, 128), lambda p, at, *_: (at[0], p)),
                pl.BlockSpec((rows, 128), lambda p, *_: (0, pairs + p)),
                pl.BlockSpec((rows, 128), lambda p, *_: (0, 2 * pairs + p)),
                pl.BlockSpec((width, depth), lambda p, *_: (0, 0), pipeline_mode=pl.Buffered(1)),
            ]
            + [pl.BlockSpec(memory_space=pl.ANY)] * len(held),
            out_specs=[
                pl.BlockSpec((blk, 128), lambda p, at, *_: (at[0], p)),
                pl.BlockSpec((1, 2, blk), lambda p, at, *_: (p, 0, at[0])),
                pl.BlockSpec((blk, depth), lambda p, *_: (0, 0)),
            ],
            scratch_shapes=[pltpu.VMEM((128, rows), BF), pltpu.VMEM((pairs, blk, 128), BF)],
        ),
        out_shape=[
            jax.ShapeDtypeStruct((rows, width), BF),
            jax.ShapeDtypeStruct((pairs, 2, rows), F32),
            jax.ShapeDtypeStruct((blk, depth), kind),
        ],
        input_output_aliases={6: 0, 7: 1} if held else {},
        compiler_params=pltpu.CompilerParams(vmem_limit_bytes=60 * MIB),
        cost_estimate=pl.CostEstimate(flops=rows * width, bytes_accessed=rows * width, transcendentals=0),
        name="attend",
    )(at, length, joint, joint, joint, w_out, *held)


def attend_back_kernel(
    len_ref, q_ref, k_ref, v_ref, o_ref, do_ref, lse_ref, cos_ref, sin_ref,
    dq_ref, dk_ref, dv_ref, kt, dlt, dqt, *, blk, blocks,
):
    j = pl.program_id(1)
    length = len_ref[0]

    @pl.when(j == 0)
    def _():
        kt[...] = jnp.transpose(k_ref[...])
        dqt[...] = jnp.zeros_like(dqt)

        def body(i, _):
            at = pl.ds(pl.multiple_of(i * blk, blk), blk)
            both = jnp.transpose(do_ref[at, :].astype(F32) * o_ref[at, :].astype(F32))
            for h in range(2):
                dlt[h : h + 1, at] = jnp.sum(both[HD * h : HD * h + HD], axis=0, keepdims=True)
            return 0

        lax.fori_loop(0, blocks, body, 0)

    js = pl.multiple_of(j * blk, blk)
    lane = lax.broadcasted_iota(jnp.int32, (blk, 128), 1)
    kb = k_ref[pl.ds(js, blk), :] * jnp.asarray(0.125, BF)
    vb = v_ref[pl.ds(js, blk), :]
    zero = jnp.zeros_like(kb)
    ks = (jnp.where(lane < HD, kb, zero), jnp.where(lane < HD, zero, kb))
    vs = (jnp.where(lane < HD, vb, zero), jnp.where(lane < HD, zero, vb))

    def step(i, carry, diag):
        at = pl.ds(pl.multiple_of(i * blk, blk), blk)
        qb, dob = q_ref[at, :], do_ref[at, :]
        out = []
        for h in range(2):
            dk, dv = carry[h]
            s = dotg(ks[h], qb, NT)
            if diag:
                key = lax.broadcasted_iota(jnp.int32, (blk, blk), 0)
                qry = lax.broadcasted_iota(jnp.int32, (blk, blk), 1)
                s = jnp.where((key <= qry) & (key + js < length), s, -1e30)
            p = jnp.exp(s - lse_ref[0, h : h + 1, at])
            dp = dotg(vs[h], dob, NT)
            ds = (p * (dp - dlt[h : h + 1, at])).astype(BF)
            dv = dv + dotg(p.astype(BF), dob)
            dk = dk + dotg(ds, qb)
            dqt[HD * h : HD * h + HD, at] += dotg(kt[HD * h : HD * h + HD, pl.ds(js, blk)], ds)
            out.append((dk, dv))
        return tuple(out)

    z = jnp.zeros((blk, 128), F32)
    c = step(j, ((z, z), (z, z)), True)
    c = lax.fori_loop(j + 1, blocks, lambda i, c: step(i, c, False), c)
    grad = jnp.where(lane < HD, c[0][0], c[1][0]) * 0.125
    dk_ref[...] = rotate(grad, cos_ref[pl.ds(js, blk), :], -sin_ref[pl.ds(js, blk), :]).astype(BF)
    dv_ref[...] = jnp.where(lane < HD, c[0][1], c[1][1]).astype(BF)

    @pl.when(j == blocks - 1)
    def _():
        def body(i, _):
            at = pl.ds(pl.multiple_of(i * blk, blk), blk)
            grad = jnp.transpose(dqt[:, at]) * 0.125
            dq_ref[at, :] = rotate(grad, cos_ref[at, :], -sin_ref[at, :]).astype(BF)
            return 0

        lax.fori_loop(0, blocks, body, 0)


def attend_back(length, joint, mixed, dmixed, lse, cos, sin, width, blk=512):
    rows = joint.shape[0]
    pairs, blocks = width // 128, rows // blk
    full = lambda off: pl.BlockSpec((rows, 128), lambda p, j, *_: (0, off * pairs + p))
    angle = pl.BlockSpec((rows, 128), lambda p, j, *_: (0, 0))
    block = pl.BlockSpec((blk, 128), lambda p, j, *_: (j, p))
    return pl.pallas_call(
        functools.partial(attend_back_kernel, blk=blk, blocks=blocks),
        grid_spec=pltpu.PrefetchScalarGridSpec(
            num_scalar_prefetch=1,
            grid=(pairs, blocks),
            in_specs=[full(0), full(1), full(2), full(0), full(0)]
            + [pl.BlockSpec((1, 2, rows), lambda p, j, *_: (p, 0, 0)), angle, angle],
            out_specs=[full(0), block, block],
            scratch_shapes=[
                pltpu.VMEM((128, rows), BF),
                pltpu.VMEM((2, rows), F32),
                pltpu.VMEM((128, rows), F32),
            ],
        ),
        out_shape=[jax.ShapeDtypeStruct((rows, width), BF)] * 3,
        compiler_params=pltpu.CompilerParams(vmem_limit_bytes=60 * MIB),
        cost_estimate=pl.CostEstimate(
            flops=rows * width, bytes_accessed=rows * width, transcendentals=0
        ),
        name="attend_back",
    )(length, joint, joint, joint, mixed, dmixed, lse, cos, sin)


def gelu_parts(v):
    c = 0.7978845608028654
    return c, jnp.tanh(c * (v + 0.044715 * v * v * v))


def gelu(v):
    return 0.5 * v * (1.0 + gelu_parts(v)[1])


def gelu_both(v):
    c, t = gelu_parts(v)
    half = 0.5 * (1.0 + t)
    return v * half, half + 0.5 * v * (1.0 - t * t) * c * (1.0 + 3 * 0.044715 * v * v)


def norm_parts(values):
    average = jnp.mean(values, axis=-1, keepdims=True)
    centred = values - average
    scale = lax.rsqrt(jnp.mean(centred * centred, axis=-1, keepdims=True) + EPSILON)
    return centred * scale, scale


def norm_back(grad, hat, scale, gain):
    g = grad * gain
    return scale * (
        g - jnp.mean(g, axis=-1, keepdims=True) - hat * jnp.mean(g * hat, axis=-1, keepdims=True)
    )


def column_sum(v):
    return jnp.sum(v, axis=0, keepdims=True)


def valid_rows(info_ref, start, count):
    at = info_ref[1] + start + lax.broadcasted_iota(jnp.int32, (count, 1), 0)
    return (at < info_ref[0]).astype(F32)


def loop_rows(rows, blk, body):
    def step(i, _):
        body(pl.multiple_of(i * blk, blk))
        return 0

    lax.fori_loop(0, rows // blk, step, 0)


def feed_kernel(info_ref, *refs, groups, chunks, sub):
    x_ref, bias_ref, resid_ref, cot_ref, bd_ref, gain_ref, shift_ref = refs[:7]
    ups, downs = refs[7 : 7 + groups], refs[7 + groups : 7 + 2 * groups]
    pre_ref, act_ref, out_ref, gb_ref, sums_ref, acc = refs[7 + 2 * groups :]
    step = pl.program_id(0)
    rows = x_ref.shape[0]

    @pl.when(step == 0)
    def _():
        acc[...] = jnp.zeros_like(acc) + bd_ref[...].astype(F32)

    for g in range(groups):

        @pl.when(step // chunks == g)
        def _():
            for r in range(0, rows, sub):
                pre = dotg(x_ref[r : r + sub], ups[g][...]) + bias_ref[0]
                pre_ref[r : r + sub] = pre
                act = gelu(pre).astype(BF)
                if g == 0:
                    act_ref[r : r + sub] = act
                acc[r : r + sub] += dotg(act, downs[g][...])

    @pl.when(step == groups * chunks - 1)
    def _():
        sums_ref[...] = jnp.zeros_like(sums_ref)
        gain, shift = gain_ref[3:4], shift_ref[3:4]

        def body(r):
            at = pl.ds(r, 64)
            valid = valid_rows(info_ref, r, 64)
            hat, scale = norm_parts(acc[at])
            out_ref[at] = (valid * (resid_ref[at] + hat * gain + shift)).astype(BF)
            g_out = valid * cot_ref[at].astype(F32)
            low = norm_back(g_out, hat, scale, gain).astype(BF)
            gb_ref[at] = low
            sums_ref[0:1] += column_sum(g_out * hat)
            sums_ref[1:2] += column_sum(g_out)
            sums_ref[2:3] += column_sum(low.astype(F32))

        loop_rows(rows, 64, body)


def feed(info, x, biases, ups, downs, resid, cot, bias_down, gains, shifts, cols=512):
    rows, depth = x.shape
    groups, hidden = len(ups), ups[0].shape[1]
    chunks = hidden // cols
    once = lambda shape: pl.BlockSpec(shape, lambda s, *_: (0, 0), pipeline_mode=pl.Buffered(1))
    own = lambda g: (lambda s, *_: (0, jnp.clip(s - g * chunks, 0, chunks - 1)))
    own_t = lambda g: (lambda s, *_: (jnp.clip(s - g * chunks, 0, chunks - 1), 0))
    return pl.pallas_call(
        functools.partial(feed_kernel, groups=groups, chunks=chunks, sub=min(512, rows)),
        grid_spec=pltpu.PrefetchScalarGridSpec(
            num_scalar_prefetch=1,
            grid=(groups * chunks,),
            in_specs=[
                once((rows, depth)),
                pl.BlockSpec((1, 1, cols), lambda s, *_: (s, 0, 0)),
                once((rows, depth)),
                once((rows, depth)),
                once((1, depth)),
                once(gains.shape),
                once(gains.shape),
            ]
            + [pl.BlockSpec((depth, cols), own(g)) for g in range(groups)]
            + [pl.BlockSpec((cols, depth), own_t(g)) for g in range(groups)],
            out_specs=[
                pl.BlockSpec((rows, cols), lambda s, *_: (0, s)),
                pl.BlockSpec((rows, cols), own(0)),
                once((rows, depth)),
                once((rows, depth)),
                once((8, depth)),
            ],
            scratch_shapes=[pltpu.VMEM((rows, depth), F32)],
        ),
        out_shape=[
            jax.ShapeDtypeStruct((rows, groups * hidden), F32),
            jax.ShapeDtypeStruct((rows, hidden), BF),
            jax.ShapeDtypeStruct((rows, depth), BF),
            jax.ShapeDtypeStruct((rows, depth), BF),
            jax.ShapeDtypeStruct((8, depth), F32),
        ],
        compiler_params=pltpu.CompilerParams(vmem_limit_bytes=60 * MIB),
        cost_estimate=pl.CostEstimate(
            flops=rows * depth, bytes_accessed=rows * depth, transcendentals=0
        ),
        name="feed",
    )(info, x, biases.reshape(-1, 1, cols), resid, cot, bias_down, gains, shifts, *ups, *downs)


def feed_back_kernel(info_ref, *refs, groups, chunks, sub):
    gb_ref, pre_ref, resid_ref, attn_ref, cot_ref, gain_ref = refs[:6]
    ups, downs = refs[6 : 6 + groups], refs[6 + groups : 6 + 2 * groups]
    gp_ref, gr_ref, ga_ref, sums_ref, acc = refs[6 + 2 * groups :]
    step = pl.program_id(0)
    rows = gb_ref.shape[0]

    @pl.when(step == 0)
    def _():
        acc[...] = jnp.zeros_like(acc)

    for g in range(groups):

        @pl.when(step // chunks == g)
        def _():
            for r in range(0, rows, sub):
                grad = dotg(gb_ref[r : r + sub], downs[g][...], NT)
                low = (grad * gelu_both(pre_ref[r : r + sub])[1]).astype(BF)
                if g == 0:
                    gp_ref[r : r + sub] = low
                acc[r : r + sub] += dotg(low, ups[g][...], NT)

    @pl.when(step == groups * chunks - 1)
    def _():
        sums_ref[...] = jnp.zeros_like(sums_ref)

        def body(r):
            at = pl.ds(r, 64)
            g_out = valid_rows(info_ref, r, 64) * cot_ref[at].astype(F32)
            hat, scale = norm_parts(resid_ref[at])
            g_two = acc[at]
            g_resid = g_out + norm_back(g_two, hat, scale, gain_ref[2:3])
            gr_ref[at] = g_resid
            sums_ref[0:1] += column_sum(g_two * hat)
            sums_ref[1:2] += column_sum(g_two)
            hat, scale = norm_parts(attn_ref[at])
            ga_ref[at] = norm_back(g_resid, hat, scale, gain_ref[1:2]).astype(BF)
            sums_ref[2:3] += column_sum(g_resid * hat)
            sums_ref[3:4] += column_sum(g_resid)

        loop_rows(rows, 64, body)


def feed_back(info, gb, pre, ups, downs, resid, attn_sum, cot, gains, cols=512):
    rows, depth = gb.shape
    groups, hidden = len(ups), ups[0].shape[1]
    chunks = hidden // cols
    once = lambda shape: pl.BlockSpec(shape, lambda s, *_: (0, 0), pipeline_mode=pl.Buffered(1))
    own = lambda g: (lambda s, *_: (0, jnp.clip(s - g * chunks, 0, chunks - 1)))
    own_t = lambda g: (lambda s, *_: (jnp.clip(s - g * chunks, 0, chunks - 1), 0))
    return pl.pallas_call(
        functools.partial(feed_back_kernel, groups=groups, chunks=chunks, sub=min(512, rows)),
        grid_spec=pltpu.PrefetchScalarGridSpec(
            num_scalar_prefetch=1,
            grid=(groups * chunks,),
            in_specs=[
                once((rows, depth)),
                pl.BlockSpec((rows, cols), lambda s, *_: (0, s)),
                once((rows, depth)),
                once((rows, depth)),
                once((rows, depth)),
                once(gains.shape),
            ]
            + [pl.BlockSpec((depth, cols), own(g)) for g in range(groups)]
            + [pl.BlockSpec((cols, depth), own_t(g)) for g in range(groups)],
            out_specs=[
                pl.BlockSpec((rows, cols), own(0)),
                once((rows, depth)),
                once((rows, depth)),
                once((8, depth)),
            ],
            scratch_shapes=[pltpu.VMEM((rows, depth), F32)],
        ),
        out_shape=[
            jax.ShapeDtypeStruct((rows, hidden), BF),
            jax.ShapeDtypeStruct((rows, depth), F32),
            jax.ShapeDtypeStruct((rows, depth), BF),
            jax.ShapeDtypeStruct((8, depth), F32),
        ],
        compiler_params=pltpu.CompilerParams(vmem_limit_bytes=60 * MIB),
        cost_estimate=pl.CostEstimate(
            flops=rows * depth, bytes_accessed=rows * depth, transcendentals=0
        ),
        name="feed_back",
    )(info, gb, pre, resid, attn_sum, cot, gains, *ups, *downs)


def feed_grad_kernel(*refs, groups):
    up_ref, down_ref, bias_ref, act_ref, gp_ref = refs[:5]
    n2s, gbs = refs[5 : 5 + groups], refs[5 + groups : 5 + 2 * groups]
    grad_ref, sum_ref = refs[5 + 2 * groups :]
    act, gp = act_ref[...], gp_ref[...]
    dup = dotg(gp, n2s[0][...], TN)
    ddown = dotg(act, gbs[0][...], TN)
    sums = column_sum(gp.astype(F32))
    for g in range(1, groups):
        pre = dotg(n2s[g][...], up_ref[...]) + bias_ref[0]
        act, slope = gelu_both(pre)
        act = act.astype(BF)
        gp = (dotg(gbs[g][...], down_ref[...], NT) * slope).astype(BF)
        dup += dotg(gp, n2s[g][...], TN)
        ddown += dotg(act, gbs[g][...], TN)
        sums += column_sum(gp.astype(F32))
    grad_ref[0] = dup.astype(BF)
    grad_ref[1] = ddown.astype(BF)
    sum_ref[0] = sums


def feed_grad(up, down, bias, act, gp, n2s, gbs, cols=256):
    rows, depth = n2s[0].shape
    groups, hidden = len(n2s), up.shape[1]
    once = lambda shape: pl.BlockSpec(shape, lambda s: (0, 0), pipeline_mode=pl.Buffered(1))
    wide = lambda count: pl.BlockSpec((count, cols), lambda s: (0, s))
    tall = pl.BlockSpec((cols, depth), lambda s: (s, 0))
    flat = pl.BlockSpec((1, 1, cols), lambda s: (s, 0, 0))
    return pl.pallas_call(
        functools.partial(feed_grad_kernel, groups=groups),
        grid=(hidden // cols,),
        in_specs=[wide(depth), tall, flat, wide(rows), wide(rows)] + [once((rows, depth))] * (2 * groups),
        out_specs=[pl.BlockSpec((2, cols, depth), lambda s: (0, s, 0)), flat],
        out_shape=[
            jax.ShapeDtypeStruct((2, hidden, depth), BF),
            jax.ShapeDtypeStruct((hidden // cols, 1, cols), F32),
        ],
        compiler_params=pltpu.CompilerParams(vmem_limit_bytes=60 * MIB),
        cost_estimate=pl.CostEstimate(
            flops=(8 * groups - 4) * rows * depth * hidden, bytes_accessed=20 * rows * depth, transcendentals=0
        ),
        name="feed_grad",
    )(up, down, bias.reshape(-1, 1, cols), act, gp, *n2s, *gbs)


def norm_kernel(x_ref, gain_ref, shift_ref, o_ref):
    hat, _ = norm_parts(x_ref[...].astype(F32))
    o_ref[...] = (hat * gain_ref[0:1] + shift_ref[0:1]).astype(BF)


def first_norm(x, gains, shifts, blk=128):
    rows, depth = x.shape
    whole = pl.BlockSpec(gains.shape, lambda i: (0, 0))
    block = pl.BlockSpec((blk, depth), lambda i: (i, 0))
    return pl.pallas_call(
        norm_kernel,
        grid=(rows // blk,),
        in_specs=[block, whole, whole],
        out_specs=block,
        out_shape=jax.ShapeDtypeStruct((rows, depth), BF),
        compiler_params=pltpu.CompilerParams(vmem_limit_bytes=60 * MIB),
        name="first_norm",
    )(x, gains, shifts)


def join_kernel(pick_ref, x_ref, gain_ref, shift_ref, *refs, blocks, each):
    parts, (attn_ref, resid_ref, low_ref) = refs[:-3], refs[-3:]
    block = pl.program_id(0) // each
    total = None
    for g in range(len(parts) // blocks):
        wanted = pick_ref[g * blocks + block]
        part = parts[g * blocks][...]
        for b in range(1, blocks):
            part = jnp.where(wanted == b, parts[g * blocks + b][...], part)
        total = part if total is None else total + part.astype(F32)
    attn_ref[...] = total
    hat, _ = norm_parts(total)
    resid = x_ref[...].astype(F32) + hat * gain_ref[1:2] + shift_ref[1:2]
    resid_ref[...] = resid
    hat, _ = norm_parts(resid)
    low_ref[...] = (hat * gain_ref[2:3] + shift_ref[2:3]).astype(BF)


def join(x, gains, shifts, shares, picks, blk=256):
    rows, depth = x.shape
    blocks = len(shares[0])
    blk = min(blk, rows // blocks)
    each = rows // blocks // blk
    whole = pl.BlockSpec(gains.shape, lambda i, *_: (0, 0))
    block = pl.BlockSpec((blk, depth), lambda i, *_: (i, 0))
    part = pl.BlockSpec((blk, depth), lambda i, *_: (lax.rem(i, each), 0))
    return pl.pallas_call(
        functools.partial(join_kernel, blocks=blocks, each=each),
        grid_spec=pltpu.PrefetchScalarGridSpec(
            num_scalar_prefetch=1,
            grid=(rows // blk,),
            in_specs=[block, whole, whole] + [part] * (len(shares) * blocks),
            out_specs=[block, block, block],
        ),
        out_shape=[
            jax.ShapeDtypeStruct((rows, depth), F32),
            jax.ShapeDtypeStruct((rows, depth), F32),
            jax.ShapeDtypeStruct((rows, depth), BF),
        ],
        compiler_params=pltpu.CompilerParams(vmem_limit_bytes=60 * MIB),
        name="join",
    )(picks, x, gains, shifts, *[v for share in shares for v in share])


def widen_kernel(up_ref, down_ref, dup_ref, ddown_ref):
    dup_ref[...] = jnp.transpose(up_ref[...]).astype(F32)
    ddown_ref[...] = down_ref[...].astype(F32)


def widen(grads, blk=256):
    hidden, depth = grads.shape[0] // 2, grads.shape[1]
    blk = min(blk, hidden)
    count = hidden // blk
    return pl.pallas_call(
        widen_kernel,
        grid=(count,),
        in_specs=[
            pl.BlockSpec((blk, depth), lambda i: (i, 0)),
            pl.BlockSpec((blk, depth), lambda i: (count + i, 0)),
        ],
        out_specs=[
            pl.BlockSpec((depth, blk), lambda i: (0, i)),
            pl.BlockSpec((blk, depth), lambda i: (i, 0)),
        ],
        out_shape=[
            jax.ShapeDtypeStruct((depth, hidden), F32),
            jax.ShapeDtypeStruct((hidden, depth), F32),
        ],
        compiler_params=pltpu.CompilerParams(vmem_limit_bytes=60 * MIB),
        name="widen",
    )(grads, grads)

MESH = pl.DeviceIdType.MESH


def exchange(src, dst, sems, slot, bit):
    peer = lax.axis_index("dp") ^ (1 << bit)
    return pltpu.make_async_remote_copy(
        src_ref=src,
        dst_ref=dst,
        send_sem=sems[0].at[slot],
        recv_sem=sems[1].at[slot],
        device_id={"dp": peer},
        device_id_type=MESH,
    )


def tail_kernel(
    gq_ref, gk_ref, gv_ref, mixed_ref, wq_ref, wk_ref, wv_ref, shard_ref, x_ref, gr_ref, gain_ref, vec_ref, *refs,
    bits, groups, steps,
):
    lefts, refs = refs[: 2 * groups], refs[2 * groups :]
    sum_ref, all_ref, out_ref, total_ref = refs[:4]
    right, left, weight, x, g_resid, packed, acc, core_buf, buf, sent, came, own_share, vec_buf = refs[4:17]
    send, recv, vec_send, vec_recv, x_send, x_recv, local = refs[17:]
    sems = (send, recv)
    place, me = lax.axis_index("tensor"), lax.axis_index("dp")
    bit = lambda b: lax.rem(lax.div(me, 1 << b), 2)
    core = bit(0)
    outer = list(range(1, bits))
    orders = [outer, outer, outer, outer[1:] + outer[:1]]
    rows, depth = x.shape
    width = weight.shape[2]
    half = 2 * depth
    base = pl.multiple_of(core * half, half)
    part = half // 4
    piece = shard_ref.shape[0] // 4
    slots, fetched = iter(range(send.shape[0])), iter(range(local.shape[0]))

    def fetch(src, dst):
        c = pltpu.make_async_copy(src, dst, local.at[next(fetched)])
        c.start()
        return c

    def wait_all(copies):
        for c in copies:
            c.wait()

    mine = tuple(bit(b) for b in reversed(range(bits)))
    first = [fetch(shard_ref, all_ref.at[mine])]
    second = [fetch(r, right.at[i]) for i, r in enumerate((gq_ref, gk_ref, gv_ref))]
    second += [fetch(r, weight.at[i]) for i, r in enumerate((wq_ref, wk_ref, wv_ref))]
    third = [fetch(r, left.at[i]) for i, r in enumerate(lefts)] + [fetch(mixed_ref, right.at[3])]
    fourth = [fetch(x_ref, x), fetch(gr_ref, g_resid)]

    barrier = pltpu.get_barrier_semaphore()
    for b in range(bits):
        pl.semaphore_signal(barrier, inc=1, device_id={"dp": me ^ (1 << b)}, device_id_type=MESH)
    for r in range(1, groups):
        peer = lax.rem(place + r, groups)
        pl.semaphore_signal(barrier, inc=1, device_id={"tensor": peer}, device_id_type=MESH)
    pl.semaphore_wait(barrier, bits + groups - 1)

    def copy(src, dst, b):
        c = exchange(src, dst, sems, next(slots), b)
        c.start()
        return c

    forwards = []

    def gather(chunk):
        order = orders[chunk][::-1]
        at = pl.ds(chunk * piece, piece)

        def region(done, other=None):
            index = [
                slice(None) if b in done else (1 - bit(b) if b == other else bit(b))
                for b in reversed(range(bits))
            ]
            return all_ref.at[tuple(index) + (at,)]

        own = region([])
        forwards.append(copy(own, own, 0))
        for k, b in enumerate(order):
            have = region(order[:k])
            c = copy(have, have, b)
            yield
            c.wait()
            got = region(order[:k], b)
            forwards.append(copy(got, got, 0))

    cores = {}

    def reduce(chunk):
        cores[chunk].wait()

        def join(i, _):
            at = pl.ds(pl.multiple_of(chunk * part + i * 64, 64), 64)
            own = packed[pl.ds(pl.multiple_of(base + chunk * part + i * 64, 64), 64)].astype(F32)
            acc[at] = (own + core_buf[at].astype(F32)).astype(BF)
            return 0

        lax.fori_loop(0, part // 64, join, 0)
        order = orders[chunk]
        start, size = chunk * part, part
        landing = chunk * (part - part // (1 << (bits - 1)))
        for b in order:
            size //= 2
            away = pl.multiple_of(start + (1 - bit(b)) * size, size)
            c = copy(acc.at[pl.ds(away, size)], buf.at[pl.ds(landing, size)], b)
            start = start + bit(b) * size
            yield
            c.wait()
            step = min(size, 64)

            def body(i, _, start=start, landing=landing, step=step):
                at = pl.ds(pl.multiple_of(start + i * step, step), step)
                got = buf[pl.ds(pl.multiple_of(landing + i * step, step), step)].astype(F32)
                acc[at] = (acc[at].astype(F32) + got).astype(BF)
                return 0

            lax.fori_loop(0, size // step, body, 0)
            landing += size
        start = base + start
        sum_ref[pl.ds(pl.multiple_of(start, size), size)] = acc[pl.ds(pl.multiple_of(start - base, size), size)]
        for b in reversed(order):
            have = sum_ref.at[pl.ds(pl.multiple_of(start, size), size)]
            c = copy(have, have, b)
            yield
            c.wait()
            start = start - bit(b) * size
            size *= 2
        have = sum_ref.at[pl.ds(pl.multiple_of(start, size), size)]
        forwards.append(copy(have, have, 0))

    def share(r, store):
        at = lax.rem(place + r, groups) * rows
        blk = min(256, rows)

        def body(i, _):
            g = pl.ds(pl.multiple_of(at + i * blk, blk), blk)
            value = dotg(right[0, g, :], weight[0], NT)
            value += dotg(right[1, g, :], weight[1], NT)
            value += dotg(right[2, g, :], weight[2], NT)
            store(pl.ds(pl.multiple_of(i * blk, blk), blk), value)
            return 0

        lax.fori_loop(0, rows // blk, body, 0)

    shares = []

    def share_away(r):
        def store(at, value):
            sent[r - 1, at, :] = value.astype(BF)

        share(r, store)
        c = pltpu.make_async_remote_copy(
            src_ref=sent.at[r - 1],
            dst_ref=came.at[r - 1],
            send_sem=x_send.at[r - 1],
            recv_sem=x_recv.at[r - 1],
            device_id={"tensor": lax.rem(place + r, groups)},
            device_id_type=MESH,
        )
        c.start()
        shares.append(c)

    def store_own(at, value):
        own_share[at, :] = value

    def weight_grad(k):
        number = lax.rem(2 * (1 - core) + k, 4)
        kind = lax.div(number, 3) * groups
        cols = min(256, depth)

        def body(i, _):
            lanes = pl.ds(pl.multiple_of(i * cols, cols), cols)
            value = None
            for r in range(groups):
                at = pl.ds(pl.multiple_of(lax.rem(place + r, groups) * rows, rows), rows)
                term = dotg(left[kind + r, :, lanes], right[number, at, :], TN)
                value = term if value is None else value + term
            packed[pl.ds(pl.multiple_of(number * depth + i * cols, cols), cols), :] = value.astype(BF)
            return 0

        lax.fori_loop(0, depth // cols, body, 0)
        if k < 2:
            away = pl.multiple_of((1 - core) * half, half)
            for c in (2 * k, 2 * k + 1):
                cores[c] = copy(
                    packed.at[pl.ds(away + c * part, part)], core_buf.at[pl.ds(c * part, part)], 0
                )

    def last_norm():
        wait_all(fourth)
        wait_all(shares)
        total_ref[...] = vec_ref[...]

        def body(i, _):
            at = pl.ds(pl.multiple_of(i * 64, 64), 64)
            value = own_share[at, :]
            for r in range(groups - 1):
                value += came[r, at, :].astype(F32)
            hat, scale = norm_parts(x[at, :].astype(F32))
            out_ref[at, :] = (g_resid[at, :] + norm_back(value, hat, scale, gain_ref[0:1])).astype(BF)
            total_ref[0:1] += column_sum(value * hat)
            total_ref[1:2] += column_sum(value)
            return 0

        lax.fori_loop(0, rows // 64, body, 0)

    def vectors():
        for k, (axis, b) in enumerate(steps):
            c = pltpu.make_async_remote_copy(
                src_ref=total_ref,
                dst_ref=vec_buf.at[k],
                send_sem=vec_send.at[k],
                recv_sem=vec_recv.at[k],
                device_id={axis: lax.axis_index(axis) ^ (1 << b)},
                device_id_type=MESH,
            )
            c.start()
            yield
            c.wait()
            total_ref[...] += vec_buf[k]

    def turn(chains):
        still = []
        for chain in chains:
            try:
                next(chain)
                still.append(chain)
            except StopIteration:
                pass
        return still

    wait_all(first)
    gathers = turn([gather(c) for c in range(4)])
    wait_all(second)
    for r in range(1, groups):
        share_away(r)
    wait_all(third)
    weight_grad(0)
    weight_grad(1)
    gathers = turn(gathers)
    weight_grad(2)
    weight_grad(3)
    reduces = turn([reduce(c) for c in range(4)])
    gathers = turn(gathers)
    share(0, store_own)
    reduces = turn(reduces)
    reduces = turn(reduces)
    gathers = turn(gathers)
    last_norm()
    chain = turn([vectors()])
    while reduces or gathers or chain:
        reduces, gathers, chain = turn(reduces), turn(gathers), turn(chain)
    wait_all(forwards)


def tail(grads, mixed, weights, shard, x, g_resid, gains, vectors, n1s, gas, bits, steps):
    (slots, width), (rows, depth), groups = mixed.shape, x.shape, len(n1s)
    half = 2 * depth
    landing = half - half // (1 << (bits - 1))
    count = 8 * bits + 8 * (bits - 1) + 16
    vmem = pl.BlockSpec(memory_space=pltpu.VMEM)
    anyspace = pl.BlockSpec(memory_space=pl.ANY)
    dma = pltpu.SemaphoreType.DMA
    peers = max(groups - 1, 1)
    summed, every, g_tokens, sums = pl.pallas_call(
        functools.partial(tail_kernel, bits=bits, groups=groups, steps=steps),
        in_specs=[anyspace] * 10 + [vmem] * 2 + [anyspace] * (2 * groups),
        out_specs=[vmem, anyspace, vmem, vmem],
        out_shape=[
            jax.ShapeDtypeStruct((4 * depth, width), BF),
            jax.ShapeDtypeStruct((2,) * bits + shard.shape, BF),
            jax.ShapeDtypeStruct((rows, depth), BF),
            jax.ShapeDtypeStruct(vectors.shape, F32),
        ],
        scratch_shapes=[
            pltpu.VMEM((4, slots, width), BF),
            pltpu.VMEM((2 * groups, rows, depth), BF),
            pltpu.VMEM((3, depth, width), BF),
            pltpu.VMEM((rows, depth), BF),
            pltpu.VMEM((rows, depth), F32),
            pltpu.VMEM((4 * depth, width), BF),
            pltpu.VMEM((half, width), BF),
            pltpu.VMEM((half, width), BF),
            pltpu.VMEM((landing, width), BF),
            pltpu.VMEM((peers, rows, depth), BF),
            pltpu.VMEM((peers, rows, depth), BF),
            pltpu.VMEM((rows, depth), F32),
            pltpu.VMEM((len(steps),) + vectors.shape, F32),
            dma((count,)),
            dma((count,)),
            dma((len(steps),)),
            dma((len(steps),)),
            dma((peers,)),
            dma((peers,)),
            dma((10 + 2 * groups,)),
        ],
        compiler_params=pltpu.CompilerParams(
            collective_id=1, has_side_effects=True, vmem_limit_bytes=60 * MIB
        ),
        name="tail",
    )(*grads, mixed, *weights, shard, x, g_resid, gains, vectors, *n1s, *gas)
    return summed, every.reshape((-1, depth)), g_tokens, sums


def mixed_back_kernel(at_ref, x_ref, w_ref, *refs):
    refs[-1][...] = dotg(x_ref[...], w_ref[...], NT).astype(BF)


def mixed_back(where, x, w_out, slots, held, blk=256):
    rows, depth = x.shape
    width = w_out.shape[0]
    blk = min(blk, rows)
    count = rows // blk
    return pl.pallas_call(
        mixed_back_kernel,
        grid_spec=pltpu.PrefetchScalarGridSpec(
            num_scalar_prefetch=1,
            grid=(count,),
            in_specs=[
                pl.BlockSpec((blk, depth), lambda i, at: (i, 0)),
                pl.BlockSpec((width, depth), lambda i, at: (0, 0)),
            ]
            + [pl.BlockSpec(memory_space=pl.ANY)] * len(held),
            out_specs=pl.BlockSpec((blk, width), lambda i, at: (at[0] * count + i, 0)),
        ),
        out_shape=jax.ShapeDtypeStruct((slots, width), BF),
        input_output_aliases={3: 0} if held else {},
        compiler_params=pltpu.CompilerParams(vmem_limit_bytes=60 * MIB),
        cost_estimate=pl.CostEstimate(flops=rows * depth, bytes_accessed=rows * depth, transcendentals=0),
        name="mixed_back",
    )(where, x, w_out, *held)


def shift(x, axis, count, step):
    return lax.ppermute(x, axis, [((i + step) % count, i) for i in range(count)])


def shards(
    tokens,
    lengths,
    cotangent,
    w_query,
    w_key,
    w_value,
    w_out,
    up_weight,
    bias_up,
    down_weight,
    bias_down,
    norm_gains,
    norm_shifts,
):
    rows, _, depth = tokens.shape
    groups, replicas = lax.axis_size("tensor"), lax.axis_size("dp")
    me, replica = lax.axis_index("tensor"), lax.axis_index("dp")
    slots = rows * groups
    width = w_query.shape[1]
    hidden = up_weight.shape[1]
    x = tokens.reshape(rows, depth)
    here = me.reshape(1).astype(jnp.int32)
    place = lambda r: (here + r) % groups

    def others(v):
        return [shift(v, "tensor", groups, r) for r in range(1, groups)]

    def to_owner(v, r):
        return shift(v, "tensor", groups, groups - r)

    up_piece = lax.dynamic_slice_in_dim(up_weight, replica * (depth // replicas), depth // replicas, 0)
    down_piece = lax.dynamic_slice_in_dim(
        down_weight, replica * (hidden // replicas), hidden // replicas, 0
    )
    up_pieces, down_pieces, bias_rest = others(up_piece), others(down_piece), others(bias_up)
    gather = lambda v: lax.all_gather(v, "dp", axis=0, tiled=True)

    freqs = 10000.0 ** (-jnp.arange(HD // 2).astype(F32) * 2.0 / HD)
    angles = jnp.arange(slots).astype(F32)[:, None] * freqs[None, :]
    cosine, sine = jnp.cos(angles), jnp.sin(angles)
    cosine = jnp.concatenate([cosine] * 4, axis=1)
    sine = jnp.concatenate([-sine, sine] * 2, axis=1)
    normed_one = first_norm(x, norm_gains, norm_shifts)
    normed_one_rest = others(normed_one)
    weights = (w_query, w_key, w_value)
    own, up_pieces, down_pieces = lax.optimization_barrier((normed_one, up_pieces, down_pieces))
    joint = project(here, own, *weights, cosine, sine)
    joint, normed_one_rest, bias_rest = lax.optimization_barrier((joint, normed_one_rest, bias_rest))
    for r, n in enumerate(normed_one_rest):
        joint = project(place(r + 1), n, *weights, cosine, sine, joint)
    blk = min(512, rows)
    each = rows // blk
    odd = lambda r: lax.rem(place(r), 2)
    ranks = lambda r, k: jnp.where(odd(r) == 1, each - 1 - k, k)
    held, shares, arrived = (), [], [[] for _ in range(1, groups)]
    for k in range(each):
        for r in range(1, groups):
            *held, share = attend(place(r) * each + ranks(0, k), lengths, joint, w_out, held, BF, blk)
            arrived[r - 1].append(to_owner(share, r))
        if k == each - 1 and k > 0:
            joint, arrived = lax.optimization_barrier((joint, [v[:k] for v in arrived])), arrived
            joint, early = joint
            arrived = [list(e) + v[k:] for e, v in zip(early, arrived)]
        *held, share = attend(here * each + ranks(0, k), lengths, joint, w_out, held, F32, blk)
        shares.append(share)
    mixed, lse = held
    shares = [shares] + arrived
    picks = jnp.concatenate([ranks(groups - r, k) for r in range(groups) for k in range(each)])
    up_rest, down_rest = [gather(p) for p in up_pieces], [gather(p) for p in down_pieces]
    shares, up_rest, down_rest = lax.optimization_barrier((shares, up_rest, down_rest))
    ups, downs = [up_weight] + up_rest, [down_weight] + down_rest
    biases = jnp.concatenate([bias_up] + bias_rest).astype(F32)

    info = jnp.stack([lengths[0], me * rows]).astype(jnp.int32)
    cot = cotangent.reshape(rows, depth)
    attn_sum, resid, normed_two = join(x, norm_gains, norm_shifts, shares, picks)
    normed_two_rest = others(normed_two)
    pre, act, layer_out, g_branch, sums3 = feed(
        info, normed_two, biases, ups, downs, resid, cot, bias_down.reshape(1, depth), norm_gains, norm_shifts
    )
    g_branch_rest = others(g_branch)
    g_branch, normed_two_rest = lax.optimization_barrier((g_branch, normed_two_rest))
    g_pre, g_resid, g_attn, sums21 = feed_back(
        info, g_branch, pre, ups, downs, resid, attn_sum, cot, norm_gains
    )
    g_attn_rest = others(g_attn)
    grad_feed, bias_up_sum = feed_grad(
        up_weight, down_weight, biases[:hidden], act, g_pre,
        [normed_two] + normed_two_rest, [g_branch] + g_branch_rest,
    )
    grad_feed = grad_feed.reshape(2 * hidden, depth)
    g_mixed = mixed_back(here, g_attn, w_out, slots, [])
    g_attn_rest, grad_feed, g_mixed = lax.optimization_barrier((g_attn_rest, grad_feed, g_mixed))
    grad_feed = lax.psum_scatter(grad_feed, "dp", scatter_dimension=0, tiled=True)
    for r, g in enumerate(g_attn_rest):
        g_mixed = mixed_back(place(r + 1), g, w_out, slots, [g_mixed])

    grads = attend_back(lengths, joint, mixed, g_mixed, lse, cosine, sine, width)
    placed = lax.dynamic_update_slice(
        jnp.zeros((groups * hidden,), F32), bias_up_sum.reshape(-1), (me * hidden,)
    ).reshape(-1, depth)
    bits = (replicas - 1).bit_length()
    steps = [("tensor", b) for b in range((groups - 1).bit_length())] + [("dp", b) for b in range(bits)]
    vectors = jnp.concatenate([jnp.zeros((2, depth), F32), sums3[:3], sums21[:4], placed])
    vectors = jnp.pad(vectors, ((0, -len(vectors) % 8), (0, 0)))
    packed, grad_feed, grad_tokens, sums = tail(
        grads, mixed, weights, grad_feed, x, g_resid, norm_gains, vectors,
        [normed_one] + normed_one_rest, [g_attn] + g_attn_rest, bits, steps,
    )
    grad_up, grad_down = widen(grad_feed)
    grad_query, grad_key, grad_value = (packed[i * depth : (i + 1) * depth].astype(F32) for i in range(3))
    grad_out = jnp.transpose(packed[3 * depth :]).astype(F32)
    grad_gains = jnp.stack([sums[0], sums[7], sums[5], sums[2]])
    grad_shifts = jnp.stack([sums[1], sums[8], sums[6], sums[3]])
    grad_bias_up = lax.dynamic_slice_in_dim(sums[9 : 9 + groups * hidden // depth].reshape(-1), me * hidden, hidden, 0)
    whole = (rows, 1, depth)
    return (
        layer_out.reshape(whole),
        grad_tokens.reshape(whole),
        grad_query,
        grad_key,
        grad_value,
        grad_out,
        grad_up,
        grad_bias_up,
        grad_down,
        sums[4],
        grad_gains,
        grad_shifts,
    )


def solution(mesh):
    wide, tall = P(None, "tensor"), P("tensor", None)
    acts = P("tensor", "dp", None)
    return jax.shard_map(
        shards,
        mesh=mesh,
        in_specs=(acts, P("dp"), acts, wide, wide, wide, tall, wide, P("tensor"), tall, P(), P(), P()),
        out_specs=(acts, acts, wide, wide, wide, tall, wide, P("tensor"), tall, P(), P(), P()),
        check_vma=False,
    )
```

```python
import functools
import jax
import jax.numpy as jnp
from jax import lax
from jax.experimental import pallas as pl
from jax.experimental.pallas import tpu as pltpu
from jax.sharding import PartitionSpec as P

HD = 64
EPSILON = 1e-05
BF = jnp.bfloat16
F32 = jnp.float32
NT = (((1,), (1,)), ((), ()))
NN = (((1,), (0,)), ((), ()))
TN = (((0,), (0,)), ((), ()))
MIB = 1 << 20


def dotg(a, b, dims=NN):
    return lax.dot_general(a, b, dims, preferred_element_type=F32)


def rotate(x, cos, sin):
    first = lax.broadcasted_iota(jnp.int32, (x.shape[0], 128), 1) % HD < HD // 2
    parts = []
    for a in range(0, x.shape[1], 128):
        v = x[:, a : a + 128]
        swapped = jnp.where(first, pltpu.roll(v, 96, 1), pltpu.roll(v, 32, 1))
        parts.append(v * cos + swapped * sin)
    return jnp.concatenate(parts, axis=1) if len(parts) > 1 else parts[0]


def qkv_kernel(x_ref, wq_ref, wk_ref, wv_ref, cos_ref, sin_ref, o_ref):
    width = wq_ref.shape[1]
    x, cos, sin = x_ref[...], cos_ref[...], sin_ref[...]
    o_ref[:, :width] = rotate(dotg(x, wq_ref[...]), cos, sin).astype(BF)
    o_ref[:, width : 2 * width] = rotate(dotg(x, wk_ref[...]), cos, sin).astype(BF)
    o_ref[:, 2 * width :] = dotg(x, wv_ref[...]).astype(BF)


def project(where, x, w_query, w_key, w_value, cos, sin, joint=None, blk=256):
    rows, depth = x.shape
    width, slots = w_query.shape[1], cos.shape[0]
    blk = min(blk, rows)
    count = rows // blk
    weight = pl.BlockSpec((depth, width), lambda i, at: (0, 0))
    angle = pl.BlockSpec((blk, 128), lambda i, at: (at[0] * count + i, 0))
    kernel = lambda at, *refs: qkv_kernel(*refs[:6], refs[-1])
    held = [] if joint is None else [joint]
    return pl.pallas_call(
        kernel,
        grid_spec=pltpu.PrefetchScalarGridSpec(
            num_scalar_prefetch=1,
            grid=(count,),
            in_specs=[pl.BlockSpec((blk, depth), lambda i, at: (i, 0)), weight, weight, weight, angle, angle]
            + [pl.BlockSpec(memory_space=pl.ANY)] * len(held),
            out_specs=pl.BlockSpec((blk, 3 * width), lambda i, at: (at[0] * count + i, 0)),
        ),
        out_shape=jax.ShapeDtypeStruct((slots, 3 * width), BF),
        input_output_aliases={7: 0} if held else {},
        compiler_params=pltpu.CompilerParams(vmem_limit_bytes=60 * MIB),
        cost_estimate=pl.CostEstimate(flops=rows * depth, bytes_accessed=rows * depth, transcendentals=0),
        name="project",
    )(where, x, w_query, w_key, w_value, cos, sin, *held)


def attend_kernel(at_ref, len_ref, q_ref, k_ref, v_ref, w_ref, *refs, blk):
    o_ref, lse_ref, share_ref, vt, low_ref = refs[-5:]
    pair = pl.program_id(0)
    i = at_ref[0]
    length = len_ref[0]
    def turn(j, _):
        part = pl.ds(pl.multiple_of(j * blk, blk), blk)
        vt[:, part] = jnp.transpose(v_ref[part, :])
        return 0

    lax.fori_loop(0, i + 1, turn, 0)
    lane = lax.broadcasted_iota(jnp.int32, (blk, 128), 1)
    q = q_ref[...] * jnp.asarray(0.125, BF)
    zero = jnp.zeros_like(q)
    qs = (jnp.where(lane < HD, q, zero), jnp.where(lane < HD, zero, q))

    def step(j, carry, diag):
        start = pl.multiple_of(j * blk, blk)
        kb = k_ref[pl.ds(start, blk), :]
        out = []
        for h in range(2):
            m, l, acc = carry[h]
            s = dotg(kb, qs[h], NT)
            if diag:
                key = lax.broadcasted_iota(jnp.int32, (blk, blk), 0)
                qry = lax.broadcasted_iota(jnp.int32, (blk, blk), 1)
                s = jnp.where((key <= qry) & (key + start < length), s, -1e30)
            mn = jnp.maximum(m, jnp.max(s, axis=0, keepdims=True))
            p = jnp.exp(s - mn)
            al = jnp.exp(m - mn)
            l = l * al + jnp.sum(p, axis=0, keepdims=True)
            vb = vt[HD * h : HD * h + HD, pl.ds(start, blk)]
            acc = acc * al + dotg(vb, p.astype(BF))
            out.append((mn, l, acc))
        return tuple(out)

    init = tuple(
        (jnp.full((1, blk), -1e30, F32), jnp.zeros((1, blk), F32), jnp.zeros((HD, blk), F32))
        for _ in range(2)
    )
    c = lax.fori_loop(0, i, lambda j, c: step(j, c, False), init)
    c = step(i, c, True)
    ot = jnp.concatenate([c[h][2] / c[h][1] for h in range(2)], axis=0)
    low = jnp.transpose(ot).astype(BF)
    o_ref[...] = low
    lse_ref[0] = jnp.concatenate([c[h][0] + jnp.log(c[h][1]) for h in range(2)], axis=0)
    low_ref[pair] = low

    @pl.when(pair == pl.num_programs(0) - 1)
    def _():
        pairs = low_ref.shape[0]
        low = jnp.concatenate([low_ref[p] for p in range(pairs)], axis=1)
        share_ref[...] = dotg(low, w_ref[...]).astype(share_ref.dtype)


def attend(at, length, joint, w_out, held, kind, blk):
    rows, width, depth = joint.shape[0], w_out.shape[0], w_out.shape[1]
    pairs = width // 128
    return pl.pallas_call(
        functools.partial(attend_kernel, blk=blk),
        grid_spec=pltpu.PrefetchScalarGridSpec(
            num_scalar_prefetch=2,
            grid=(pairs,),
            in_specs=[
                pl.BlockSpec((blk, 128), lambda p, at, *_: (at[0], p)),
                pl.BlockSpec((rows, 128), lambda p, *_: (0, pairs + p)),
                pl.BlockSpec((rows, 128), lambda p, *_: (0, 2 * pairs + p)),
                pl.BlockSpec((width, depth), lambda p, *_: (0, 0), pipeline_mode=pl.Buffered(1)),
            ]
            + [pl.BlockSpec(memory_space=pl.ANY)] * len(held),
            out_specs=[
                pl.BlockSpec((blk, 128), lambda p, at, *_: (at[0], p)),
                pl.BlockSpec((1, 2, blk), lambda p, at, *_: (p, 0, at[0])),
                pl.BlockSpec((blk, depth), lambda p, *_: (0, 0)),
            ],
            scratch_shapes=[pltpu.VMEM((128, rows), BF), pltpu.VMEM((pairs, blk, 128), BF)],
        ),
        out_shape=[
            jax.ShapeDtypeStruct((rows, width), BF),
            jax.ShapeDtypeStruct((pairs, 2, rows), F32),
            jax.ShapeDtypeStruct((blk, depth), kind),
        ],
        input_output_aliases={6: 0, 7: 1} if held else {},
        compiler_params=pltpu.CompilerParams(vmem_limit_bytes=60 * MIB),
        cost_estimate=pl.CostEstimate(flops=rows * width, bytes_accessed=rows * width, transcendentals=0),
        name="attend",
    )(at, length, joint, joint, joint, w_out, *held)


def attend_back_kernel(
    len_ref, q_ref, k_ref, v_ref, o_ref, do_ref, lse_ref, cos_ref, sin_ref,
    dq_ref, dk_ref, dv_ref, kt, dlt, dqt, *, blk, blocks,
):
    j = pl.program_id(1)
    length = len_ref[0]

    @pl.when(j == 0)
    def _():
        kt[...] = jnp.transpose(k_ref[...])
        dqt[...] = jnp.zeros_like(dqt)

        def body(i, _):
            at = pl.ds(pl.multiple_of(i * blk, blk), blk)
            both = jnp.transpose(do_ref[at, :].astype(F32) * o_ref[at, :].astype(F32))
            for h in range(2):
                dlt[h : h + 1, at] = jnp.sum(both[HD * h : HD * h + HD], axis=0, keepdims=True)
            return 0

        lax.fori_loop(0, blocks, body, 0)

    js = pl.multiple_of(j * blk, blk)
    lane = lax.broadcasted_iota(jnp.int32, (blk, 128), 1)
    kb = k_ref[pl.ds(js, blk), :] * jnp.asarray(0.125, BF)
    vb = v_ref[pl.ds(js, blk), :]
    zero = jnp.zeros_like(kb)
    ks = (jnp.where(lane < HD, kb, zero), jnp.where(lane < HD, zero, kb))
    vs = (jnp.where(lane < HD, vb, zero), jnp.where(lane < HD, zero, vb))

    def step(i, carry, diag):
        at = pl.ds(pl.multiple_of(i * blk, blk), blk)
        qb, dob = q_ref[at, :], do_ref[at, :]
        out = []
        for h in range(2):
            dk, dv = carry[h]
            s = dotg(ks[h], qb, NT)
            if diag:
                key = lax.broadcasted_iota(jnp.int32, (blk, blk), 0)
                qry = lax.broadcasted_iota(jnp.int32, (blk, blk), 1)
                s = jnp.where((key <= qry) & (key + js < length), s, -1e30)
            p = jnp.exp(s - lse_ref[0, h : h + 1, at])
            dp = dotg(vs[h], dob, NT)
            ds = (p * (dp - dlt[h : h + 1, at])).astype(BF)
            dv = dv + dotg(p.astype(BF), dob)
            dk = dk + dotg(ds, qb)
            dqt[HD * h : HD * h + HD, at] += dotg(kt[HD * h : HD * h + HD, pl.ds(js, blk)], ds)
            out.append((dk, dv))
        return tuple(out)

    z = jnp.zeros((blk, 128), F32)
    c = step(j, ((z, z), (z, z)), True)
    c = lax.fori_loop(j + 1, blocks, lambda i, c: step(i, c, False), c)
    grad = jnp.where(lane < HD, c[0][0], c[1][0]) * 0.125
    dk_ref[...] = rotate(grad, cos_ref[pl.ds(js, blk), :], -sin_ref[pl.ds(js, blk), :]).astype(BF)
    dv_ref[...] = jnp.where(lane < HD, c[0][1], c[1][1]).astype(BF)

    @pl.when(j == blocks - 1)
    def _():
        def body(i, _):
            at = pl.ds(pl.multiple_of(i * blk, blk), blk)
            grad = jnp.transpose(dqt[:, at]) * 0.125
            dq_ref[at, :] = rotate(grad, cos_ref[at, :], -sin_ref[at, :]).astype(BF)
            return 0

        lax.fori_loop(0, blocks, body, 0)


def attend_back(length, joint, mixed, dmixed, lse, cos, sin, width, blk=512):
    rows = joint.shape[0]
    pairs, blocks = width // 128, rows // blk
    full = lambda off: pl.BlockSpec((rows, 128), lambda p, j, *_: (0, off * pairs + p))
    angle = pl.BlockSpec((rows, 128), lambda p, j, *_: (0, 0))
    block = pl.BlockSpec((blk, 128), lambda p, j, *_: (j, p))
    return pl.pallas_call(
        functools.partial(attend_back_kernel, blk=blk, blocks=blocks),
        grid_spec=pltpu.PrefetchScalarGridSpec(
            num_scalar_prefetch=1,
            grid=(pairs, blocks),
            in_specs=[full(0), full(1), full(2), full(0), full(0)]
            + [pl.BlockSpec((1, 2, rows), lambda p, j, *_: (p, 0, 0)), angle, angle],
            out_specs=[full(0), block, block],
            scratch_shapes=[
                pltpu.VMEM((128, rows), BF),
                pltpu.VMEM((2, rows), F32),
                pltpu.VMEM((128, rows), F32),
            ],
        ),
        out_shape=[jax.ShapeDtypeStruct((rows, width), BF)] * 3,
        compiler_params=pltpu.CompilerParams(vmem_limit_bytes=60 * MIB),
        cost_estimate=pl.CostEstimate(
            flops=rows * width, bytes_accessed=rows * width, transcendentals=0
        ),
        name="attend_back",
    )(length, joint, joint, joint, mixed, dmixed, lse, cos, sin)


def gelu_parts(v):
    c = 0.7978845608028654
    return c, jnp.tanh(c * (v + 0.044715 * v * v * v))


def gelu(v):
    return 0.5 * v * (1.0 + gelu_parts(v)[1])


def gelu_both(v):
    c, t = gelu_parts(v)
    half = 0.5 * (1.0 + t)
    return v * half, half + 0.5 * v * (1.0 - t * t) * c * (1.0 + 3 * 0.044715 * v * v)


def norm_parts(values):
    average = jnp.mean(values, axis=-1, keepdims=True)
    centred = values - average
    scale = lax.rsqrt(jnp.mean(centred * centred, axis=-1, keepdims=True) + EPSILON)
    return centred * scale, scale


def norm_back(grad, hat, scale, gain):
    g = grad * gain
    return scale * (
        g - jnp.mean(g, axis=-1, keepdims=True) - hat * jnp.mean(g * hat, axis=-1, keepdims=True)
    )


def column_sum(v):
    return jnp.sum(v, axis=0, keepdims=True)


def valid_rows(info_ref, start, count):
    at = info_ref[1] + start + lax.broadcasted_iota(jnp.int32, (count, 1), 0)
    return (at < info_ref[0]).astype(F32)


def loop_rows(rows, blk, body):
    def step(i, _):
        body(pl.multiple_of(i * blk, blk))
        return 0

    lax.fori_loop(0, rows // blk, step, 0)


def feed_kernel(info_ref, *refs, groups, chunks, sub):
    x_ref, bias_ref, resid_ref, cot_ref, bd_ref, gain_ref, shift_ref = refs[:7]
    ups, downs = refs[7 : 7 + groups], refs[7 + groups : 7 + 2 * groups]
    pre_ref, act_ref, out_ref, gb_ref, sums_ref, acc = refs[7 + 2 * groups :]
    step = pl.program_id(0)
    rows = x_ref.shape[0]

    @pl.when(step == 0)
    def _():
        acc[...] = jnp.zeros_like(acc) + bd_ref[...].astype(F32)

    for g in range(groups):

        @pl.when(step // chunks == g)
        def _():
            for r in range(0, rows, sub):
                pre = dotg(x_ref[r : r + sub], ups[g][...]) + bias_ref[0]
                pre_ref[r : r + sub] = pre
                act = gelu(pre).astype(BF)
                if g == 0:
                    act_ref[r : r + sub] = act
                acc[r : r + sub] += dotg(act, downs[g][...])

    @pl.when(step == groups * chunks - 1)
    def _():
        sums_ref[...] = jnp.zeros_like(sums_ref)
        gain, shift = gain_ref[3:4], shift_ref[3:4]

        def body(r):
            at = pl.ds(r, 64)
            valid = valid_rows(info_ref, r, 64)
            hat, scale = norm_parts(acc[at])
            out_ref[at] = (valid * (resid_ref[at] + hat * gain + shift)).astype(BF)
            g_out = valid * cot_ref[at].astype(F32)
            low = norm_back(g_out, hat, scale, gain).astype(BF)
            gb_ref[at] = low
            sums_ref[0:1] += column_sum(g_out * hat)
            sums_ref[1:2] += column_sum(g_out)
            sums_ref[2:3] += column_sum(low.astype(F32))

        loop_rows(rows, 64, body)


def feed(info, x, biases, ups, downs, resid, cot, bias_down, gains, shifts, cols=512):
    rows, depth = x.shape
    groups, hidden = len(ups), ups[0].shape[1]
    chunks = hidden // cols
    once = lambda shape: pl.BlockSpec(shape, lambda s, *_: (0, 0), pipeline_mode=pl.Buffered(1))
    own = lambda g: (lambda s, *_: (0, jnp.clip(s - g * chunks, 0, chunks - 1)))
    own_t = lambda g: (lambda s, *_: (jnp.clip(s - g * chunks, 0, chunks - 1), 0))
    return pl.pallas_call(
        functools.partial(feed_kernel, groups=groups, chunks=chunks, sub=min(512, rows)),
        grid_spec=pltpu.PrefetchScalarGridSpec(
            num_scalar_prefetch=1,
            grid=(groups * chunks,),
            in_specs=[
                once((rows, depth)),
                pl.BlockSpec((1, 1, cols), lambda s, *_: (s, 0, 0)),
                once((rows, depth)),
                once((rows, depth)),
                once((1, depth)),
                once(gains.shape),
                once(gains.shape),
            ]
            + [pl.BlockSpec((depth, cols), own(g)) for g in range(groups)]
            + [pl.BlockSpec((cols, depth), own_t(g)) for g in range(groups)],
            out_specs=[
                pl.BlockSpec((rows, cols), lambda s, *_: (0, s)),
                pl.BlockSpec((rows, cols), own(0)),
                once((rows, depth)),
                once((rows, depth)),
                once((8, depth)),
            ],
            scratch_shapes=[pltpu.VMEM((rows, depth), F32)],
        ),
        out_shape=[
            jax.ShapeDtypeStruct((rows, groups * hidden), F32),
            jax.ShapeDtypeStruct((rows, hidden), BF),
            jax.ShapeDtypeStruct((rows, depth), BF),
            jax.ShapeDtypeStruct((rows, depth), BF),
            jax.ShapeDtypeStruct((8, depth), F32),
        ],
        compiler_params=pltpu.CompilerParams(vmem_limit_bytes=60 * MIB),
        cost_estimate=pl.CostEstimate(
            flops=rows * depth, bytes_accessed=rows * depth, transcendentals=0
        ),
        name="feed",
    )(info, x, biases.reshape(-1, 1, cols), resid, cot, bias_down, gains, shifts, *ups, *downs)


def feed_back_kernel(info_ref, *refs, groups, chunks, sub):
    gb_ref, pre_ref, resid_ref, attn_ref, cot_ref, gain_ref = refs[:6]
    ups, downs = refs[6 : 6 + groups], refs[6 + groups : 6 + 2 * groups]
    gp_ref, gr_ref, ga_ref, sums_ref, acc = refs[6 + 2 * groups :]
    step = pl.program_id(0)
    rows = gb_ref.shape[0]

    @pl.when(step == 0)
    def _():
        acc[...] = jnp.zeros_like(acc)

    for g in range(groups):

        @pl.when(step // chunks == g)
        def _():
            for r in range(0, rows, sub):
                grad = dotg(gb_ref[r : r + sub], downs[g][...], NT)
                low = (grad * gelu_both(pre_ref[r : r + sub])[1]).astype(BF)
                if g == 0:
                    gp_ref[r : r + sub] = low
                acc[r : r + sub] += dotg(low, ups[g][...], NT)

    @pl.when(step == groups * chunks - 1)
    def _():
        sums_ref[...] = jnp.zeros_like(sums_ref)

        def body(r):
            at = pl.ds(r, 64)
            g_out = valid_rows(info_ref, r, 64) * cot_ref[at].astype(F32)
            hat, scale = norm_parts(resid_ref[at])
            g_two = acc[at]
            g_resid = g_out + norm_back(g_two, hat, scale, gain_ref[2:3])
            gr_ref[at] = g_resid
            sums_ref[0:1] += column_sum(g_two * hat)
            sums_ref[1:2] += column_sum(g_two)
            hat, scale = norm_parts(attn_ref[at])
            ga_ref[at] = norm_back(g_resid, hat, scale, gain_ref[1:2]).astype(BF)
            sums_ref[2:3] += column_sum(g_resid * hat)
            sums_ref[3:4] += column_sum(g_resid)

        loop_rows(rows, 64, body)


def feed_back(info, gb, pre, ups, downs, resid, attn_sum, cot, gains, cols=512):
    rows, depth = gb.shape
    groups, hidden = len(ups), ups[0].shape[1]
    chunks = hidden // cols
    once = lambda shape: pl.BlockSpec(shape, lambda s, *_: (0, 0), pipeline_mode=pl.Buffered(1))
    own = lambda g: (lambda s, *_: (0, jnp.clip(s - g * chunks, 0, chunks - 1)))
    own_t = lambda g: (lambda s, *_: (jnp.clip(s - g * chunks, 0, chunks - 1), 0))
    return pl.pallas_call(
        functools.partial(feed_back_kernel, groups=groups, chunks=chunks, sub=min(512, rows)),
        grid_spec=pltpu.PrefetchScalarGridSpec(
            num_scalar_prefetch=1,
            grid=(groups * chunks,),
            in_specs=[
                once((rows, depth)),
                pl.BlockSpec((rows, cols), lambda s, *_: (0, s)),
                once((rows, depth)),
                once((rows, depth)),
                once((rows, depth)),
                once(gains.shape),
            ]
            + [pl.BlockSpec((depth, cols), own(g)) for g in range(groups)]
            + [pl.BlockSpec((cols, depth), own_t(g)) for g in range(groups)],
            out_specs=[
                pl.BlockSpec((rows, cols), own(0)),
                once((rows, depth)),
                once((rows, depth)),
                once((8, depth)),
            ],
            scratch_shapes=[pltpu.VMEM((rows, depth), F32)],
        ),
        out_shape=[
            jax.ShapeDtypeStruct((rows, hidden), BF),
            jax.ShapeDtypeStruct((rows, depth), F32),
            jax.ShapeDtypeStruct((rows, depth), BF),
            jax.ShapeDtypeStruct((8, depth), F32),
        ],
        compiler_params=pltpu.CompilerParams(vmem_limit_bytes=60 * MIB),
        cost_estimate=pl.CostEstimate(
            flops=rows * depth, bytes_accessed=rows * depth, transcendentals=0
        ),
        name="feed_back",
    )(info, gb, pre, resid, attn_sum, cot, gains, *ups, *downs)


def feed_grad_kernel(*refs, groups):
    up_ref, down_ref, bias_ref, act_ref, gp_ref = refs[:5]
    n2s, gbs = refs[5 : 5 + groups], refs[5 + groups : 5 + 2 * groups]
    grad_ref, sum_ref = refs[5 + 2 * groups :]
    act, gp = act_ref[...], gp_ref[...]
    dup = dotg(gp, n2s[0][...], TN)
    ddown = dotg(act, gbs[0][...], TN)
    sums = column_sum(gp.astype(F32))
    for g in range(1, groups):
        pre = dotg(n2s[g][...], up_ref[...]) + bias_ref[0]
        act, slope = gelu_both(pre)
        act = act.astype(BF)
        gp = (dotg(gbs[g][...], down_ref[...], NT) * slope).astype(BF)
        dup += dotg(gp, n2s[g][...], TN)
        ddown += dotg(act, gbs[g][...], TN)
        sums += column_sum(gp.astype(F32))
    grad_ref[0] = dup.astype(BF)
    grad_ref[1] = ddown.astype(BF)
    sum_ref[0] = sums


def feed_grad(up, down, bias, act, gp, n2s, gbs, cols=256):
    rows, depth = n2s[0].shape
    groups, hidden = len(n2s), up.shape[1]
    once = lambda shape: pl.BlockSpec(shape, lambda s: (0, 0), pipeline_mode=pl.Buffered(1))
    wide = lambda count: pl.BlockSpec((count, cols), lambda s: (0, s))
    tall = pl.BlockSpec((cols, depth), lambda s: (s, 0))
    flat = pl.BlockSpec((1, 1, cols), lambda s: (s, 0, 0))
    return pl.pallas_call(
        functools.partial(feed_grad_kernel, groups=groups),
        grid=(hidden // cols,),
        in_specs=[wide(depth), tall, flat, wide(rows), wide(rows)] + [once((rows, depth))] * (2 * groups),
        out_specs=[pl.BlockSpec((2, cols, depth), lambda s: (0, s, 0)), flat],
        out_shape=[
            jax.ShapeDtypeStruct((2, hidden, depth), BF),
            jax.ShapeDtypeStruct((hidden // cols, 1, cols), F32),
        ],
        compiler_params=pltpu.CompilerParams(vmem_limit_bytes=60 * MIB),
        cost_estimate=pl.CostEstimate(
            flops=(8 * groups - 4) * rows * depth * hidden, bytes_accessed=20 * rows * depth, transcendentals=0
        ),
        name="feed_grad",
    )(up, down, bias.reshape(-1, 1, cols), act, gp, *n2s, *gbs)


def norm_kernel(x_ref, gain_ref, shift_ref, o_ref):
    hat, _ = norm_parts(x_ref[...].astype(F32))
    o_ref[...] = (hat * gain_ref[0:1] + shift_ref[0:1]).astype(BF)


def first_norm(x, gains, shifts, blk=512):
    rows, depth = x.shape
    blk = min(blk, rows)
    whole = pl.BlockSpec(gains.shape, lambda i: (0, 0))
    block = pl.BlockSpec((blk, depth), lambda i: (i, 0))
    return pl.pallas_call(
        norm_kernel,
        grid=(rows // blk,),
        in_specs=[block, whole, whole],
        out_specs=block,
        out_shape=jax.ShapeDtypeStruct((rows, depth), BF),
        compiler_params=pltpu.CompilerParams(vmem_limit_bytes=60 * MIB),
        name="first_norm",
    )(x, gains, shifts)


def join_kernel(pick_ref, x_ref, gain_ref, shift_ref, *refs, blocks, each):
    parts, (attn_ref, resid_ref, low_ref) = refs[:-3], refs[-3:]
    block = pl.program_id(0) // each
    total = None
    for g in range(len(parts) // blocks):
        wanted = pick_ref[g * blocks + block]
        part = parts[g * blocks][...]
        for b in range(1, blocks):
            part = jnp.where(wanted == b, parts[g * blocks + b][...], part)
        total = part if total is None else total + part.astype(F32)
    attn_ref[...] = total
    hat, _ = norm_parts(total)
    resid = x_ref[...].astype(F32) + hat * gain_ref[1:2] + shift_ref[1:2]
    resid_ref[...] = resid
    hat, _ = norm_parts(resid)
    low_ref[...] = (hat * gain_ref[2:3] + shift_ref[2:3]).astype(BF)


def join(x, gains, shifts, shares, picks, blk=256):
    rows, depth = x.shape
    blocks = len(shares[0])
    blk = min(blk, rows // blocks)
    each = rows // blocks // blk
    whole = pl.BlockSpec(gains.shape, lambda i, *_: (0, 0))
    block = pl.BlockSpec((blk, depth), lambda i, *_: (i, 0))
    part = pl.BlockSpec((blk, depth), lambda i, *_: (lax.rem(i, each), 0))
    return pl.pallas_call(
        functools.partial(join_kernel, blocks=blocks, each=each),
        grid_spec=pltpu.PrefetchScalarGridSpec(
            num_scalar_prefetch=1,
            grid=(rows // blk,),
            in_specs=[block, whole, whole] + [part] * (len(shares) * blocks),
            out_specs=[block, block, block],
        ),
        out_shape=[
            jax.ShapeDtypeStruct((rows, depth), F32),
            jax.ShapeDtypeStruct((rows, depth), F32),
            jax.ShapeDtypeStruct((rows, depth), BF),
        ],
        compiler_params=pltpu.CompilerParams(vmem_limit_bytes=60 * MIB),
        name="join",
    )(picks, x, gains, shifts, *[v for share in shares for v in share])


def widen_kernel(up_ref, down_ref, dup_ref, ddown_ref):
    dup_ref[...] = jnp.transpose(up_ref[...]).astype(F32)
    ddown_ref[...] = down_ref[...].astype(F32)


def widen(grads, blk=256):
    hidden, depth = grads.shape[0] // 2, grads.shape[1]
    blk = min(blk, hidden)
    count = hidden // blk
    return pl.pallas_call(
        widen_kernel,
        grid=(count,),
        in_specs=[
            pl.BlockSpec((blk, depth), lambda i: (i, 0)),
            pl.BlockSpec((blk, depth), lambda i: (count + i, 0)),
        ],
        out_specs=[
            pl.BlockSpec((depth, blk), lambda i: (0, i)),
            pl.BlockSpec((blk, depth), lambda i: (i, 0)),
        ],
        out_shape=[
            jax.ShapeDtypeStruct((depth, hidden), F32),
            jax.ShapeDtypeStruct((hidden, depth), F32),
        ],
        compiler_params=pltpu.CompilerParams(vmem_limit_bytes=60 * MIB),
        name="widen",
    )(grads, grads)

MESH = pl.DeviceIdType.MESH


def exchange(src, dst, sems, slot, bit):
    peer = lax.axis_index("dp") ^ (1 << bit)
    return pltpu.make_async_remote_copy(
        src_ref=src,
        dst_ref=dst,
        send_sem=sems[0].at[slot],
        recv_sem=sems[1].at[slot],
        device_id={"dp": peer},
        device_id_type=MESH,
    )


def tail_kernel(
    gq_ref, gk_ref, gv_ref, mixed_ref, wq_ref, wk_ref, wv_ref, x_ref, gr_ref, gain_ref, vec_ref, *refs,
    bits, groups, steps,
):
    lefts, refs = refs[: 2 * groups], refs[2 * groups :]
    sum_ref, out_ref, total_ref = refs[:3]
    right, left, weight, x, g_resid, packed, acc, core_buf, buf, sent, came, own_share, vec_buf = refs[3:16]
    send, recv, vec_send, vec_recv, x_send, x_recv, local = refs[16:]
    sems = (send, recv)
    place, me = lax.axis_index("tensor"), lax.axis_index("dp")
    bit = lambda b: lax.rem(lax.div(me, 1 << b), 2)
    core = bit(0)
    outer = list(range(1, bits))
    orders = [outer, outer, outer, outer[1:] + outer[:1]]
    rows, depth = x.shape
    width = weight.shape[2]
    half = 2 * depth
    base = pl.multiple_of(core * half, half)
    part = half // 4
    slots, fetched = iter(range(send.shape[0])), iter(range(local.shape[0]))

    def fetch(src, dst):
        c = pltpu.make_async_copy(src, dst, local.at[next(fetched)])
        c.start()
        return c

    def wait_all(copies):
        for c in copies:
            c.wait()

    second = [fetch(r, right.at[i]) for i, r in enumerate((gq_ref, gk_ref, gv_ref))]
    second += [fetch(r, weight.at[i]) for i, r in enumerate((wq_ref, wk_ref, wv_ref))]
    third = [fetch(r, left.at[i]) for i, r in enumerate(lefts)] + [fetch(mixed_ref, right.at[3])]
    fourth = [fetch(x_ref, x), fetch(gr_ref, g_resid)]

    barrier = pltpu.get_barrier_semaphore()
    for b in range(bits):
        pl.semaphore_signal(barrier, inc=1, device_id={"dp": me ^ (1 << b)}, device_id_type=MESH)
    for r in range(1, groups):
        peer = lax.rem(place + r, groups)
        pl.semaphore_signal(barrier, inc=1, device_id={"tensor": peer}, device_id_type=MESH)
    pl.semaphore_wait(barrier, bits + groups - 1)

    def copy(src, dst, b):
        c = exchange(src, dst, sems, next(slots), b)
        c.start()
        return c

    forwards = []
    cores = {}

    def reduce(chunk):
        cores[chunk].wait()

        def join(i, _):
            at = pl.ds(pl.multiple_of(chunk * part + i * 64, 64), 64)
            own = packed[pl.ds(pl.multiple_of(base + chunk * part + i * 64, 64), 64)].astype(F32)
            acc[at] = (own + core_buf[at].astype(F32)).astype(BF)
            return 0

        lax.fori_loop(0, part // 64, join, 0)
        order = orders[chunk]
        start, size = chunk * part, part
        landing = chunk * (part - part // (1 << (bits - 1)))
        for b in order:
            size //= 2
            away = pl.multiple_of(start + (1 - bit(b)) * size, size)
            c = copy(acc.at[pl.ds(away, size)], buf.at[pl.ds(landing, size)], b)
            start = start + bit(b) * size
            yield
            c.wait()
            step = min(size, 64)

            def body(i, _, start=start, landing=landing, step=step):
                at = pl.ds(pl.multiple_of(start + i * step, step), step)
                got = buf[pl.ds(pl.multiple_of(landing + i * step, step), step)].astype(F32)
                acc[at] = (acc[at].astype(F32) + got).astype(BF)
                return 0

            lax.fori_loop(0, size // step, body, 0)
            landing += size
        start = base + start
        sum_ref[pl.ds(pl.multiple_of(start, size), size)] = acc[pl.ds(pl.multiple_of(start - base, size), size)]
        for b in reversed(order):
            have = sum_ref.at[pl.ds(pl.multiple_of(start, size), size)]
            c = copy(have, have, b)
            yield
            c.wait()
            start = start - bit(b) * size
            size *= 2
        have = sum_ref.at[pl.ds(pl.multiple_of(start, size), size)]
        forwards.append(copy(have, have, 0))

    def share(r, store):
        at = lax.rem(place + r, groups) * rows
        blk = min(256, rows)

        def body(i, _):
            g = pl.ds(pl.multiple_of(at + i * blk, blk), blk)
            value = dotg(right[0, g, :], weight[0], NT)
            value += dotg(right[1, g, :], weight[1], NT)
            value += dotg(right[2, g, :], weight[2], NT)
            store(pl.ds(pl.multiple_of(i * blk, blk), blk), value)
            return 0

        lax.fori_loop(0, rows // blk, body, 0)

    shares = []

    def share_away(r):
        def store(at, value):
            sent[r - 1, at, :] = value.astype(BF)

        share(r, store)
        c = pltpu.make_async_remote_copy(
            src_ref=sent.at[r - 1],
            dst_ref=came.at[r - 1],
            send_sem=x_send.at[r - 1],
            recv_sem=x_recv.at[r - 1],
            device_id={"tensor": lax.rem(place + r, groups)},
            device_id_type=MESH,
        )
        c.start()
        shares.append(c)

    def store_own(at, value):
        own_share[at, :] = value

    def weight_grad(k):
        number = lax.rem(2 * (1 - core) + k, 4)
        kind = lax.div(number, 3) * groups
        cols = min(256, depth)

        def body(i, _):
            lanes = pl.ds(pl.multiple_of(i * cols, cols), cols)
            value = None
            for r in range(groups):
                at = pl.ds(pl.multiple_of(lax.rem(place + r, groups) * rows, rows), rows)
                term = dotg(left[kind + r, :, lanes], right[number, at, :], TN)
                value = term if value is None else value + term
            packed[pl.ds(pl.multiple_of(number * depth + i * cols, cols), cols), :] = value.astype(BF)
            return 0

        lax.fori_loop(0, depth // cols, body, 0)
        if k < 2:
            away = pl.multiple_of((1 - core) * half, half)
            for c in (2 * k, 2 * k + 1):
                cores[c] = copy(
                    packed.at[pl.ds(away + c * part, part)], core_buf.at[pl.ds(c * part, part)], 0
                )

    def last_norm():
        wait_all(fourth)
        wait_all(shares)
        total_ref[...] = vec_ref[...]

        def body(i, _):
            at = pl.ds(pl.multiple_of(i * 64, 64), 64)
            value = own_share[at, :]
            for r in range(groups - 1):
                value += came[r, at, :].astype(F32)
            hat, scale = norm_parts(x[at, :].astype(F32))
            out_ref[at, :] = (g_resid[at, :] + norm_back(value, hat, scale, gain_ref[0:1])).astype(BF)
            total_ref[0:1] += column_sum(value * hat)
            total_ref[1:2] += column_sum(value)
            return 0

        lax.fori_loop(0, rows // 64, body, 0)

    def vectors():
        for k, (axis, b) in enumerate(steps):
            c = pltpu.make_async_remote_copy(
                src_ref=total_ref,
                dst_ref=vec_buf.at[k],
                send_sem=vec_send.at[k],
                recv_sem=vec_recv.at[k],
                device_id={axis: lax.axis_index(axis) ^ (1 << b)},
                device_id_type=MESH,
            )
            c.start()
            yield
            c.wait()
            total_ref[...] += vec_buf[k]

    def turn(chains):
        still = []
        for chain in chains:
            try:
                next(chain)
                still.append(chain)
            except StopIteration:
                pass
        return still

    wait_all(second)
    for r in range(1, groups):
        share_away(r)
    wait_all(third)
    weight_grad(0)
    weight_grad(1)
    weight_grad(2)
    weight_grad(3)
    reduces = turn([reduce(c) for c in range(4)])
    share(0, store_own)
    reduces = turn(reduces)
    reduces = turn(reduces)
    last_norm()
    chain = turn([vectors()])
    while reduces or chain:
        reduces, chain = turn(reduces), turn(chain)
    wait_all(forwards)


def tail(grads, mixed, weights, x, g_resid, gains, vectors, n1s, gas, bits, steps):
    (slots, width), (rows, depth), groups = mixed.shape, x.shape, len(n1s)
    half = 2 * depth
    landing = half - half // (1 << (bits - 1))
    count = 8 * (bits - 1) + 16
    vmem = pl.BlockSpec(memory_space=pltpu.VMEM)
    anyspace = pl.BlockSpec(memory_space=pl.ANY)
    dma = pltpu.SemaphoreType.DMA
    peers = max(groups - 1, 1)
    return pl.pallas_call(
        functools.partial(tail_kernel, bits=bits, groups=groups, steps=steps),
        in_specs=[anyspace] * 9 + [vmem] * 2 + [anyspace] * (2 * groups),
        out_specs=[vmem, vmem, vmem],
        out_shape=[
            jax.ShapeDtypeStruct((4 * depth, width), BF),
            jax.ShapeDtypeStruct((rows, depth), BF),
            jax.ShapeDtypeStruct(vectors.shape, F32),
        ],
        scratch_shapes=[
            pltpu.VMEM((4, slots, width), BF),
            pltpu.VMEM((2 * groups, rows, depth), BF),
            pltpu.VMEM((3, depth, width), BF),
            pltpu.VMEM((rows, depth), BF),
            pltpu.VMEM((rows, depth), F32),
            pltpu.VMEM((4 * depth, width), BF),
            pltpu.VMEM((half, width), BF),
            pltpu.VMEM((half, width), BF),
            pltpu.VMEM((landing, width), BF),
            pltpu.VMEM((peers, rows, depth), BF),
            pltpu.VMEM((peers, rows, depth), BF),
            pltpu.VMEM((rows, depth), F32),
            pltpu.VMEM((len(steps),) + vectors.shape, F32),
            dma((count,)),
            dma((count,)),
            dma((len(steps),)),
            dma((len(steps),)),
            dma((peers,)),
            dma((peers,)),
            dma((9 + 2 * groups,)),
        ],
        compiler_params=pltpu.CompilerParams(
            collective_id=1, has_side_effects=True, vmem_limit_bytes=60 * MIB
        ),
        cost_estimate=pl.CostEstimate(flops=rows * width, bytes_accessed=rows * width, transcendentals=0),
        name="tail",
    )(*grads, mixed, *weights, x, g_resid, gains, vectors, *n1s, *gas)


def mixed_back_kernel(at_ref, x_ref, w_ref, *refs):
    refs[-1][...] = dotg(x_ref[...], w_ref[...], NT).astype(BF)


def mixed_back(where, x, w_out, slots, held, blk=256):
    rows, depth = x.shape
    width = w_out.shape[0]
    blk = min(blk, rows)
    count = rows // blk
    return pl.pallas_call(
        mixed_back_kernel,
        grid_spec=pltpu.PrefetchScalarGridSpec(
            num_scalar_prefetch=1,
            grid=(count,),
            in_specs=[
                pl.BlockSpec((blk, depth), lambda i, at: (i, 0)),
                pl.BlockSpec((width, depth), lambda i, at: (0, 0)),
            ]
            + [pl.BlockSpec(memory_space=pl.ANY)] * len(held),
            out_specs=pl.BlockSpec((blk, width), lambda i, at: (at[0] * count + i, 0)),
        ),
        out_shape=jax.ShapeDtypeStruct((slots, width), BF),
        input_output_aliases={3: 0} if held else {},
        compiler_params=pltpu.CompilerParams(vmem_limit_bytes=60 * MIB),
        cost_estimate=pl.CostEstimate(flops=rows * depth, bytes_accessed=rows * depth, transcendentals=0),
        name="mixed_back",
    )(where, x, w_out, *held)


def shift(x, axis, count, step):
    return lax.ppermute(x, axis, [((i + step) % count, i) for i in range(count)])


def shards(
    tokens,
    lengths,
    cotangent,
    w_query,
    w_key,
    w_value,
    w_out,
    up_weight,
    bias_up,
    down_weight,
    bias_down,
    norm_gains,
    norm_shifts,
):
    rows, _, depth = tokens.shape
    groups, replicas = lax.axis_size("tensor"), lax.axis_size("dp")
    me, replica = lax.axis_index("tensor"), lax.axis_index("dp")
    slots = rows * groups
    width = w_query.shape[1]
    hidden = up_weight.shape[1]
    x = tokens.reshape(rows, depth)
    here = me.reshape(1).astype(jnp.int32)
    place = lambda r: (here + r) % groups

    def others(v):
        return [shift(v, "tensor", groups, r) for r in range(1, groups)]

    def to_owner(v, r):
        return shift(v, "tensor", groups, groups - r)

    up_piece = lax.dynamic_slice_in_dim(up_weight, replica * (depth // replicas), depth // replicas, 0)
    down_piece = lax.dynamic_slice_in_dim(
        down_weight, replica * (hidden // replicas), hidden // replicas, 0
    )
    up_pieces, down_pieces, bias_rest = others(up_piece), others(down_piece), others(bias_up)
    gather = lambda v: lax.all_gather(v, "dp", axis=0, tiled=True)

    freqs = 10000.0 ** (-jnp.arange(HD // 2).astype(F32) * 2.0 / HD)
    angles = jnp.arange(slots).astype(F32)[:, None] * freqs[None, :]
    cosine, sine = jnp.cos(angles), jnp.sin(angles)
    cosine = jnp.concatenate([cosine] * 4, axis=1)
    sine = jnp.concatenate([-sine, sine] * 2, axis=1)
    normed_one = first_norm(x, norm_gains, norm_shifts)
    normed_one_rest = others(normed_one)
    weights = (w_query, w_key, w_value)
    own, up_pieces, down_pieces = lax.optimization_barrier((normed_one, up_pieces, down_pieces))
    joint = project(here, own, *weights, cosine, sine)
    joint, normed_one_rest, bias_rest = lax.optimization_barrier((joint, normed_one_rest, bias_rest))
    for r, n in enumerate(normed_one_rest):
        joint = project(place(r + 1), n, *weights, cosine, sine, joint)
    blk = min(512, rows)
    each = rows // blk
    odd = lambda r: lax.rem(place(r), 2)
    ranks = lambda r, k: jnp.where(odd(r) == 1, each - 1 - k, k)
    held, shares, arrived = (), [], [[] for _ in range(1, groups)]
    for k in range(each):
        for r in range(1, groups):
            *held, share = attend(place(r) * each + ranks(0, k), lengths, joint, w_out, held, BF, blk)
            arrived[r - 1].append(to_owner(share, r))
        if k == each - 1 and k > 0:
            joint, arrived = lax.optimization_barrier((joint, [v[:k] for v in arrived])), arrived
            joint, early = joint
            arrived = [list(e) + v[k:] for e, v in zip(early, arrived)]
        *held, share = attend(here * each + ranks(0, k), lengths, joint, w_out, held, F32, blk)
        shares.append(share)
    mixed, lse = held
    shares = [shares] + arrived
    picks = jnp.concatenate([ranks(groups - r, k) for r in range(groups) for k in range(each)])
    up_rest, down_rest = [gather(p) for p in up_pieces], [gather(p) for p in down_pieces]
    shares, up_rest, down_rest = lax.optimization_barrier((shares, up_rest, down_rest))
    ups, downs = [up_weight] + up_rest, [down_weight] + down_rest
    biases = jnp.concatenate([bias_up] + bias_rest).astype(F32)

    info = jnp.stack([lengths[0], me * rows]).astype(jnp.int32)
    cot = cotangent.reshape(rows, depth)
    attn_sum, resid, normed_two = join(x, norm_gains, norm_shifts, shares, picks)
    normed_two_rest = others(normed_two)
    pre, act, layer_out, g_branch, sums3 = feed(
        info, normed_two, biases, ups, downs, resid, cot, bias_down.reshape(1, depth), norm_gains, norm_shifts
    )
    g_branch_rest = others(g_branch)
    g_pre, g_resid, g_attn, sums21 = feed_back(
        info, g_branch, pre, ups, downs, resid, attn_sum, cot, norm_gains
    )
    g_attn_rest = others(g_attn)
    g_pre, normed_two_rest = lax.optimization_barrier((g_pre, normed_two_rest))
    grad_feed, bias_up_sum = feed_grad(
        up_weight, down_weight, biases[:hidden], act, g_pre,
        [normed_two] + normed_two_rest, [g_branch] + g_branch_rest,
    )
    grad_feed = grad_feed.reshape(2 * hidden, depth)
    g_attn, g_attn_rest, grad_feed = lax.optimization_barrier((g_attn, g_attn_rest, grad_feed))
    grad_feed = lax.psum(grad_feed, "dp")
    g_mixed = mixed_back(here, g_attn, w_out, slots, [])
    for r, g in enumerate(g_attn_rest):
        g_mixed = mixed_back(place(r + 1), g, w_out, slots, [g_mixed])

    grads = attend_back(lengths, joint, mixed, g_mixed, lse, cosine, sine, width)
    placed = lax.dynamic_update_slice(
        jnp.zeros((groups * hidden,), F32), bias_up_sum.reshape(-1), (me * hidden,)
    ).reshape(-1, depth)
    bits = (replicas - 1).bit_length()
    steps = [("tensor", b) for b in range((groups - 1).bit_length())] + [("dp", b) for b in range(bits)]
    vectors = jnp.concatenate([jnp.zeros((2, depth), F32), sums3[:3], sums21[:4], placed])
    vectors = jnp.pad(vectors, ((0, -len(vectors) % 8), (0, 0)))
    packed, grad_tokens, sums = tail(
        grads, mixed, weights, x, g_resid, norm_gains, vectors,
        [normed_one] + normed_one_rest, [g_attn] + g_attn_rest, bits, steps,
    )
    grad_up, grad_down = widen(grad_feed)
    grad_query, grad_key, grad_value = (packed[i * depth : (i + 1) * depth].astype(F32) for i in range(3))
    grad_out = jnp.transpose(packed[3 * depth :]).astype(F32)
    grad_gains = jnp.stack([sums[0], sums[7], sums[5], sums[2]])
    grad_shifts = jnp.stack([sums[1], sums[8], sums[6], sums[3]])
    grad_bias_up = lax.dynamic_slice_in_dim(sums[9 : 9 + groups * hidden // depth].reshape(-1), me * hidden, hidden, 0)
    whole = (rows, 1, depth)
    return (
        layer_out.reshape(whole),
        grad_tokens.reshape(whole),
        grad_query,
        grad_key,
        grad_value,
        grad_out,
        grad_up,
        grad_bias_up,
        grad_down,
        sums[4],
        grad_gains,
        grad_shifts,
    )


def solution(mesh):
    wide, tall = P(None, "tensor"), P("tensor", None)
    acts = P("tensor", "dp", None)
    return jax.shard_map(
        shards,
        mesh=mesh,
        in_specs=(acts, P("dp"), acts, wide, wide, wide, tall, wide, P("tensor"), tall, P(), P(), P()),
        out_specs=(acts, acts, wide, wide, wide, tall, wide, P("tensor"), tall, P(), P(), P()),
        check_vma=False,
    )
```

```python
import functools
import jax
import jax.numpy as jnp
from jax import lax
from jax.experimental import pallas as pl
from jax.experimental.pallas import tpu as pltpu
from jax.sharding import PartitionSpec as P

HD = 64
EPSILON = 1e-05
BF = jnp.bfloat16
F32 = jnp.float32
NT = (((1,), (1,)), ((), ()))
NN = (((1,), (0,)), ((), ()))
TN = (((0,), (0,)), ((), ()))
MIB = 1 << 20


def dotg(a, b, dims=NN):
    return lax.dot_general(a, b, dims, preferred_element_type=F32)


def rotate(x, cos, sin):
    first = lax.broadcasted_iota(jnp.int32, (x.shape[0], 128), 1) % HD < HD // 2
    parts = []
    for a in range(0, x.shape[1], 128):
        v = x[:, a : a + 128]
        swapped = jnp.where(first, pltpu.roll(v, 96, 1), pltpu.roll(v, 32, 1))
        parts.append(v * cos + swapped * sin)
    return jnp.concatenate(parts, axis=1) if len(parts) > 1 else parts[0]


def qkv_kernel(x_ref, wq_ref, wk_ref, wv_ref, cos_ref, sin_ref, o_ref):
    width = wq_ref.shape[1]
    x, cos, sin = x_ref[...], cos_ref[...], sin_ref[...]
    o_ref[:, :width] = rotate(dotg(x, wq_ref[...]), cos, sin).astype(BF)
    o_ref[:, width : 2 * width] = rotate(dotg(x, wk_ref[...]), cos, sin).astype(BF)
    o_ref[:, 2 * width :] = dotg(x, wv_ref[...]).astype(BF)


def project(where, x, w_query, w_key, w_value, cos, sin, joint=None, blk=256):
    rows, depth = x.shape
    width, slots = w_query.shape[1], cos.shape[0]
    blk = min(blk, rows)
    count = rows // blk
    weight = pl.BlockSpec((depth, width), lambda i, at: (0, 0))
    angle = pl.BlockSpec((blk, 128), lambda i, at: (at[0] * count + i, 0))
    kernel = lambda at, *refs: qkv_kernel(*refs[:6], refs[-1])
    held = [] if joint is None else [joint]
    return pl.pallas_call(
        kernel,
        grid_spec=pltpu.PrefetchScalarGridSpec(
            num_scalar_prefetch=1,
            grid=(count,),
            in_specs=[pl.BlockSpec((blk, depth), lambda i, at: (i, 0)), weight, weight, weight, angle, angle]
            + [pl.BlockSpec(memory_space=pl.ANY)] * len(held),
            out_specs=pl.BlockSpec((blk, 3 * width), lambda i, at: (at[0] * count + i, 0)),
        ),
        out_shape=jax.ShapeDtypeStruct((slots, 3 * width), BF),
        input_output_aliases={7: 0} if held else {},
        compiler_params=pltpu.CompilerParams(vmem_limit_bytes=60 * MIB),
        cost_estimate=pl.CostEstimate(flops=rows * depth, bytes_accessed=rows * depth, transcendentals=0),
        name="project",
    )(where, x, w_query, w_key, w_value, cos, sin, *held)


def attend_kernel(at_ref, len_ref, q_ref, k_ref, v_ref, w_ref, *refs, blk):
    o_ref, lse_ref, share_ref, vt, low_ref = refs[-5:]
    pair = pl.program_id(0)
    i = at_ref[0]
    length = len_ref[0]
    def turn(j, _):
        part = pl.ds(pl.multiple_of(j * blk, blk), blk)
        vt[:, part] = jnp.transpose(v_ref[part, :])
        return 0

    lax.fori_loop(0, i + 1, turn, 0)
    lane = lax.broadcasted_iota(jnp.int32, (blk, 128), 1)
    q = q_ref[...] * jnp.asarray(0.125, BF)
    zero = jnp.zeros_like(q)
    qs = (jnp.where(lane < HD, q, zero), jnp.where(lane < HD, zero, q))

    def step(j, carry, diag):
        start = pl.multiple_of(j * blk, blk)
        kb = k_ref[pl.ds(start, blk), :]
        out = []
        for h in range(2):
            m, l, acc = carry[h]
            s = dotg(kb, qs[h], NT)
            if diag:
                key = lax.broadcasted_iota(jnp.int32, (blk, blk), 0)
                qry = lax.broadcasted_iota(jnp.int32, (blk, blk), 1)
                s = jnp.where((key <= qry) & (key + start < length), s, -1e30)
            mn = jnp.maximum(m, jnp.max(s, axis=0, keepdims=True))
            p = jnp.exp(s - mn)
            al = jnp.exp(m - mn)
            l = l * al + jnp.sum(p, axis=0, keepdims=True)
            vb = vt[HD * h : HD * h + HD, pl.ds(start, blk)]
            acc = acc * al + dotg(vb, p.astype(BF))
            out.append((mn, l, acc))
        return tuple(out)

    init = tuple(
        (jnp.full((1, blk), -1e30, F32), jnp.zeros((1, blk), F32), jnp.zeros((HD, blk), F32))
        for _ in range(2)
    )
    c = lax.fori_loop(0, i, lambda j, c: step(j, c, False), init)
    c = step(i, c, True)
    ot = jnp.concatenate([c[h][2] / c[h][1] for h in range(2)], axis=0)
    low = jnp.transpose(ot).astype(BF)
    o_ref[...] = low
    lse_ref[0] = jnp.concatenate([c[h][0] + jnp.log(c[h][1]) for h in range(2)], axis=0)
    low_ref[pair] = low

    @pl.when(pair == pl.num_programs(0) - 1)
    def _():
        pairs = low_ref.shape[0]
        low = jnp.concatenate([low_ref[p] for p in range(pairs)], axis=1)
        share_ref[...] = dotg(low, w_ref[...]).astype(share_ref.dtype)


def attend(at, length, joint, w_out, held, kind, blk):
    rows, width, depth = joint.shape[0], w_out.shape[0], w_out.shape[1]
    pairs = width // 128
    return pl.pallas_call(
        functools.partial(attend_kernel, blk=blk),
        grid_spec=pltpu.PrefetchScalarGridSpec(
            num_scalar_prefetch=2,
            grid=(pairs,),
            in_specs=[
                pl.BlockSpec((blk, 128), lambda p, at, *_: (at[0], p)),
                pl.BlockSpec((rows, 128), lambda p, *_: (0, pairs + p)),
                pl.BlockSpec((rows, 128), lambda p, *_: (0, 2 * pairs + p)),
                pl.BlockSpec((width, depth), lambda p, *_: (0, 0), pipeline_mode=pl.Buffered(1)),
            ]
            + [pl.BlockSpec(memory_space=pl.ANY)] * len(held),
            out_specs=[
                pl.BlockSpec((blk, 128), lambda p, at, *_: (at[0], p)),
                pl.BlockSpec((1, 2, blk), lambda p, at, *_: (p, 0, at[0])),
                pl.BlockSpec((blk, depth), lambda p, *_: (0, 0)),
            ],
            scratch_shapes=[pltpu.VMEM((128, rows), BF), pltpu.VMEM((pairs, blk, 128), BF)],
        ),
        out_shape=[
            jax.ShapeDtypeStruct((rows, width), BF),
            jax.ShapeDtypeStruct((pairs, 2, rows), F32),
            jax.ShapeDtypeStruct((blk, depth), kind),
        ],
        input_output_aliases={6: 0, 7: 1} if held else {},
        compiler_params=pltpu.CompilerParams(vmem_limit_bytes=60 * MIB),
        cost_estimate=pl.CostEstimate(flops=rows * width, bytes_accessed=rows * width, transcendentals=0),
        name="attend",
    )(at, length, joint, joint, joint, w_out, *held)


def attend_back_kernel(
    len_ref, q_ref, k_ref, v_ref, o_ref, do_ref, lse_ref, cos_ref, sin_ref,
    dq_ref, dk_ref, dv_ref, kt, dlt, dqt, *, blk, blocks,
):
    j = pl.program_id(1)
    length = len_ref[0]

    @pl.when(j == 0)
    def _():
        kt[...] = jnp.transpose(k_ref[...])
        dqt[...] = jnp.zeros_like(dqt)

        def body(i, _):
            at = pl.ds(pl.multiple_of(i * blk, blk), blk)
            both = jnp.transpose(do_ref[at, :].astype(F32) * o_ref[at, :].astype(F32))
            for h in range(2):
                dlt[h : h + 1, at] = jnp.sum(both[HD * h : HD * h + HD], axis=0, keepdims=True)
            return 0

        lax.fori_loop(0, blocks, body, 0)

    js = pl.multiple_of(j * blk, blk)
    lane = lax.broadcasted_iota(jnp.int32, (blk, 128), 1)
    kb = k_ref[pl.ds(js, blk), :] * jnp.asarray(0.125, BF)
    vb = v_ref[pl.ds(js, blk), :]
    zero = jnp.zeros_like(kb)
    ks = (jnp.where(lane < HD, kb, zero), jnp.where(lane < HD, zero, kb))
    vs = (jnp.where(lane < HD, vb, zero), jnp.where(lane < HD, zero, vb))

    def step(i, carry, diag):
        at = pl.ds(pl.multiple_of(i * blk, blk), blk)
        qb, dob = q_ref[at, :], do_ref[at, :]
        out = []
        for h in range(2):
            dk, dv = carry[h]
            s = dotg(ks[h], qb, NT)
            if diag:
                key = lax.broadcasted_iota(jnp.int32, (blk, blk), 0)
                qry = lax.broadcasted_iota(jnp.int32, (blk, blk), 1)
                s = jnp.where((key <= qry) & (key + js < length), s, -1e30)
            p = jnp.exp(s - lse_ref[0, h : h + 1, at])
            dp = dotg(vs[h], dob, NT)
            ds = (p * (dp - dlt[h : h + 1, at])).astype(BF)
            dv = dv + dotg(p.astype(BF), dob)
            dk = dk + dotg(ds, qb)
            dqt[HD * h : HD * h + HD, at] += dotg(kt[HD * h : HD * h + HD, pl.ds(js, blk)], ds)
            out.append((dk, dv))
        return tuple(out)

    z = jnp.zeros((blk, 128), F32)
    c = step(j, ((z, z), (z, z)), True)
    c = lax.fori_loop(j + 1, blocks, lambda i, c: step(i, c, False), c)
    grad = jnp.where(lane < HD, c[0][0], c[1][0]) * 0.125
    dk_ref[...] = rotate(grad, cos_ref[pl.ds(js, blk), :], -sin_ref[pl.ds(js, blk), :]).astype(BF)
    dv_ref[...] = jnp.where(lane < HD, c[0][1], c[1][1]).astype(BF)

    @pl.when(j == blocks - 1)
    def _():
        def body(i, _):
            at = pl.ds(pl.multiple_of(i * blk, blk), blk)
            grad = jnp.transpose(dqt[:, at]) * 0.125
            dq_ref[at, :] = rotate(grad, cos_ref[at, :], -sin_ref[at, :]).astype(BF)
            return 0

        lax.fori_loop(0, blocks, body, 0)


def attend_back(length, joint, mixed, dmixed, lse, cos, sin, width, blk=512):
    rows = joint.shape[0]
    pairs, blocks = width // 128, rows // blk
    full = lambda off: pl.BlockSpec((rows, 128), lambda p, j, *_: (0, off * pairs + p))
    angle = pl.BlockSpec((rows, 128), lambda p, j, *_: (0, 0))
    block = pl.BlockSpec((blk, 128), lambda p, j, *_: (j, p))
    return pl.pallas_call(
        functools.partial(attend_back_kernel, blk=blk, blocks=blocks),
        grid_spec=pltpu.PrefetchScalarGridSpec(
            num_scalar_prefetch=1,
            grid=(pairs, blocks),
            in_specs=[full(0), full(1), full(2), full(0), full(0)]
            + [pl.BlockSpec((1, 2, rows), lambda p, j, *_: (p, 0, 0)), angle, angle],
            out_specs=[full(0), block, block],
            scratch_shapes=[
                pltpu.VMEM((128, rows), BF),
                pltpu.VMEM((2, rows), F32),
                pltpu.VMEM((128, rows), F32),
            ],
        ),
        out_shape=[jax.ShapeDtypeStruct((rows, width), BF)] * 3,
        compiler_params=pltpu.CompilerParams(vmem_limit_bytes=60 * MIB),
        cost_estimate=pl.CostEstimate(
            flops=rows * width, bytes_accessed=rows * width, transcendentals=0
        ),
        name="attend_back",
    )(length, joint, joint, joint, mixed, dmixed, lse, cos, sin)


def gelu_parts(v):
    c = 0.7978845608028654
    return c, jnp.tanh(c * (v + 0.044715 * v * v * v))


def gelu_both(v):
    c, t = gelu_parts(v)
    half = 0.5 * (1.0 + t)
    return v * half, half + 0.5 * v * (1.0 - t * t) * c * (1.0 + 3 * 0.044715 * v * v)


def norm_parts(values):
    average = jnp.mean(values, axis=-1, keepdims=True)
    centred = values - average
    scale = lax.rsqrt(jnp.mean(centred * centred, axis=-1, keepdims=True) + EPSILON)
    return centred * scale, scale


def norm_back(grad, hat, scale, gain):
    g = grad * gain
    return scale * (
        g - jnp.mean(g, axis=-1, keepdims=True) - hat * jnp.mean(g * hat, axis=-1, keepdims=True)
    )


def column_sum(v):
    return jnp.sum(v, axis=0, keepdims=True)


def valid_rows(info_ref, start, count):
    at = info_ref[1] + start + lax.broadcasted_iota(jnp.int32, (count, 1), 0)
    return (at < info_ref[0]).astype(F32)


def loop_rows(rows, blk, body):
    def step(i, _):
        body(pl.multiple_of(i * blk, blk))
        return 0

    lax.fori_loop(0, rows // blk, step, 0)


def feed_kernel(info_ref, *refs, groups, chunks, sub):
    x_ref, bias_ref, resid_hbm, cot_hbm, bd_ref, gain_ref, shift_ref = refs[:7]
    ups, downs = refs[7 : 7 + groups], refs[7 + groups : 7 + 2 * groups]
    slope_ref, act_ref, out_ref, gb_ref, sums_ref, acc, resid_ref, cot_ref, sems = refs[7 + 2 * groups :]
    step = pl.program_id(0)
    rows = x_ref.shape[0]
    late = [
        pltpu.make_async_copy(resid_hbm, resid_ref, sems.at[0]),
        pltpu.make_async_copy(cot_hbm, cot_ref, sems.at[1]),
    ]

    @pl.when(step == 0)
    def _():
        for c in late:
            c.start()
        acc[...] = jnp.zeros_like(acc) + bd_ref[...].astype(F32)

    for g in range(groups):

        @pl.when(step // chunks == g)
        def _():
            for r in range(0, rows, sub):
                act, slope = gelu_both(dotg(x_ref[r : r + sub], ups[g][...]) + bias_ref[0])
                slope_ref[r : r + sub] = slope.astype(BF)
                act = act.astype(BF)
                if g == 0:
                    act_ref[r : r + sub] = act
                acc[r : r + sub] += dotg(act, downs[g][...])

    @pl.when(step == groups * chunks - 1)
    def _():
        for c in late:
            c.wait()
        sums_ref[...] = jnp.zeros_like(sums_ref)
        gain, shift = gain_ref[3:4], shift_ref[3:4]
        blk = min(256, rows)

        def body(r):
            at = pl.ds(r, blk)
            valid = valid_rows(info_ref, r, blk)
            hat, scale = norm_parts(acc[at])
            out_ref[at] = (valid * (resid_ref[at] + hat * gain + shift)).astype(BF)
            g_out = valid * cot_ref[at].astype(F32)
            low = norm_back(g_out, hat, scale, gain).astype(BF)
            gb_ref[at] = low
            sums_ref[0:1] += column_sum(g_out * hat)
            sums_ref[1:2] += column_sum(g_out)
            sums_ref[2:3] += column_sum(low.astype(F32))

        loop_rows(rows, blk, body)


def feed(info, x, biases, ups, downs, resid, cot, bias_down, gains, shifts, cols=512):
    rows, depth = x.shape
    groups, hidden = len(ups), ups[0].shape[1]
    chunks = hidden // cols
    once = lambda shape: pl.BlockSpec(shape, lambda s, *_: (0, 0), pipeline_mode=pl.Buffered(1))
    anyspace = pl.BlockSpec(memory_space=pl.ANY)
    own = lambda g: (lambda s, *_: (0, jnp.clip(s - g * chunks, 0, chunks - 1)))
    own_t = lambda g: (lambda s, *_: (jnp.clip(s - g * chunks, 0, chunks - 1), 0))
    return pl.pallas_call(
        functools.partial(feed_kernel, groups=groups, chunks=chunks, sub=min(512, rows)),
        grid_spec=pltpu.PrefetchScalarGridSpec(
            num_scalar_prefetch=1,
            grid=(groups * chunks,),
            in_specs=[
                once((rows, depth)),
                pl.BlockSpec((1, 1, cols), lambda s, *_: (s, 0, 0)),
                anyspace,
                anyspace,
                once((1, depth)),
                once(gains.shape),
                once(gains.shape),
            ]
            + [pl.BlockSpec((depth, cols), own(g)) for g in range(groups)]
            + [pl.BlockSpec((cols, depth), own_t(g)) for g in range(groups)],
            out_specs=[
                pl.BlockSpec((rows, cols), lambda s, *_: (0, s)),
                pl.BlockSpec((rows, cols), own(0)),
                once((rows, depth)),
                once((rows, depth)),
                once((8, depth)),
            ],
            scratch_shapes=[
                pltpu.VMEM((rows, depth), F32),
                pltpu.VMEM((rows, depth), F32),
                pltpu.VMEM((rows, depth), BF),
                pltpu.SemaphoreType.DMA((2,)),
            ],
        ),
        out_shape=[
            jax.ShapeDtypeStruct((rows, groups * hidden), BF),
            jax.ShapeDtypeStruct((rows, hidden), BF),
            jax.ShapeDtypeStruct((rows, depth), BF),
            jax.ShapeDtypeStruct((rows, depth), BF),
            jax.ShapeDtypeStruct((8, depth), F32),
        ],
        compiler_params=pltpu.CompilerParams(vmem_limit_bytes=60 * MIB),
        cost_estimate=pl.CostEstimate(flops=rows * depth, bytes_accessed=rows * depth, transcendentals=0),
        name="feed",
    )(info, x, biases.reshape(-1, 1, cols), resid, cot, bias_down, gains, shifts, *ups, *downs)


def feed_back_kernel(info_ref, *refs, groups, chunks, sub):
    gb_ref, slope_ref, resid_hbm, attn_hbm, cot_hbm, gain_ref = refs[:6]
    ups, downs = refs[6 : 6 + groups], refs[6 + groups : 6 + 2 * groups]
    gp_ref, gr_ref, ga_ref, sums_ref, acc, resid_ref, attn_ref, cot_ref, sems = refs[6 + 2 * groups :]
    step = pl.program_id(0)
    rows = gb_ref.shape[0]
    late = [
        pltpu.make_async_copy(src, dst, sems.at[i])
        for i, (src, dst) in enumerate(((resid_hbm, resid_ref), (attn_hbm, attn_ref), (cot_hbm, cot_ref)))
    ]

    @pl.when(step == 0)
    def _():
        for c in late:
            c.start()
        acc[...] = jnp.zeros_like(acc)

    for g in range(groups):

        @pl.when(step // chunks == g)
        def _():
            for r in range(0, rows, sub):
                grad = dotg(gb_ref[r : r + sub], downs[g][...], NT)
                low = (grad * slope_ref[r : r + sub].astype(F32)).astype(BF)
                if g == 0:
                    gp_ref[r : r + sub] = low
                acc[r : r + sub] += dotg(low, ups[g][...], NT)

    @pl.when(step == groups * chunks - 1)
    def _():
        for c in late:
            c.wait()
        sums_ref[...] = jnp.zeros_like(sums_ref)
        blk = min(256, rows)

        def body(r):
            at = pl.ds(r, blk)
            g_out = valid_rows(info_ref, r, blk) * cot_ref[at].astype(F32)
            hat, scale = norm_parts(resid_ref[at])
            g_two = acc[at]
            g_resid = g_out + norm_back(g_two, hat, scale, gain_ref[2:3])
            gr_ref[at] = g_resid
            sums_ref[0:1] += column_sum(g_two * hat)
            sums_ref[1:2] += column_sum(g_two)
            hat, scale = norm_parts(attn_ref[at])
            ga_ref[at] = norm_back(g_resid, hat, scale, gain_ref[1:2]).astype(BF)
            sums_ref[2:3] += column_sum(g_resid * hat)
            sums_ref[3:4] += column_sum(g_resid)

        loop_rows(rows, blk, body)


def feed_back(info, gb, slope, ups, downs, resid, attn_sum, cot, gains, cols=512):
    rows, depth = gb.shape
    groups, hidden = len(ups), ups[0].shape[1]
    chunks = hidden // cols
    once = lambda shape: pl.BlockSpec(shape, lambda s, *_: (0, 0), pipeline_mode=pl.Buffered(1))
    anyspace = pl.BlockSpec(memory_space=pl.ANY)
    own = lambda g: (lambda s, *_: (0, jnp.clip(s - g * chunks, 0, chunks - 1)))
    own_t = lambda g: (lambda s, *_: (jnp.clip(s - g * chunks, 0, chunks - 1), 0))
    return pl.pallas_call(
        functools.partial(feed_back_kernel, groups=groups, chunks=chunks, sub=min(512, rows)),
        grid_spec=pltpu.PrefetchScalarGridSpec(
            num_scalar_prefetch=1,
            grid=(groups * chunks,),
            in_specs=[
                once((rows, depth)),
                pl.BlockSpec((rows, cols), lambda s, *_: (0, s)),
                anyspace,
                anyspace,
                anyspace,
                once(gains.shape),
            ]
            + [pl.BlockSpec((depth, cols), own(g)) for g in range(groups)]
            + [pl.BlockSpec((cols, depth), own_t(g)) for g in range(groups)],
            out_specs=[
                pl.BlockSpec((rows, cols), own(0)),
                once((rows, depth)),
                once((rows, depth)),
                once((8, depth)),
            ],
            scratch_shapes=[
                pltpu.VMEM((rows, depth), F32),
                pltpu.VMEM((rows, depth), F32),
                pltpu.VMEM((rows, depth), F32),
                pltpu.VMEM((rows, depth), BF),
                pltpu.SemaphoreType.DMA((3,)),
            ],
        ),
        out_shape=[
            jax.ShapeDtypeStruct((rows, hidden), BF),
            jax.ShapeDtypeStruct((rows, depth), F32),
            jax.ShapeDtypeStruct((rows, depth), BF),
            jax.ShapeDtypeStruct((8, depth), F32),
        ],
        compiler_params=pltpu.CompilerParams(vmem_limit_bytes=60 * MIB),
        cost_estimate=pl.CostEstimate(flops=rows * depth, bytes_accessed=rows * depth, transcendentals=0),
        name="feed_back",
    )(info, gb, slope, resid, attn_sum, cot, gains, *ups, *downs)


def feed_grad_kernel(*refs, groups):
    up_ref, down_ref, bias_ref, act_ref, gp_ref = refs[:5]
    n2s, gbs = refs[5 : 5 + groups], refs[5 + groups : 5 + 2 * groups]
    grad_ref, sum_ref = refs[5 + 2 * groups :]
    act, gp = act_ref[...], gp_ref[...]
    dup = dotg(gp, n2s[0][...], TN)
    ddown = dotg(act, gbs[0][...], TN)
    sums = column_sum(gp.astype(F32))
    for g in range(1, groups):
        pre = dotg(n2s[g][...], up_ref[...]) + bias_ref[0]
        act, slope = gelu_both(pre)
        act = act.astype(BF)
        gp = (dotg(gbs[g][...], down_ref[...], NT) * slope).astype(BF)
        dup += dotg(gp, n2s[g][...], TN)
        ddown += dotg(act, gbs[g][...], TN)
        sums += column_sum(gp.astype(F32))
    grad_ref[0] = dup.astype(BF)
    grad_ref[1] = ddown.astype(BF)
    sum_ref[0] = sums


def feed_grad(up, down, bias, act, gp, n2s, gbs, cols=512):
    rows, depth = n2s[0].shape
    groups, hidden = len(n2s), up.shape[1]
    once = lambda shape: pl.BlockSpec(shape, lambda s: (0, 0), pipeline_mode=pl.Buffered(1))
    wide = lambda count: pl.BlockSpec((count, cols), lambda s: (0, s))
    tall = pl.BlockSpec((cols, depth), lambda s: (s, 0))
    flat = pl.BlockSpec((1, 1, cols), lambda s: (s, 0, 0))
    return pl.pallas_call(
        functools.partial(feed_grad_kernel, groups=groups),
        grid=(hidden // cols,),
        in_specs=[wide(depth), tall, flat, wide(rows), wide(rows)] + [once((rows, depth))] * (2 * groups),
        out_specs=[pl.BlockSpec((2, cols, depth), lambda s: (0, s, 0)), flat],
        out_shape=[
            jax.ShapeDtypeStruct((2, hidden, depth), BF),
            jax.ShapeDtypeStruct((hidden // cols, 1, cols), F32),
        ],
        compiler_params=pltpu.CompilerParams(vmem_limit_bytes=60 * MIB),
        cost_estimate=pl.CostEstimate(
            flops=(8 * groups - 4) * rows * depth * hidden, bytes_accessed=20 * rows * depth, transcendentals=0
        ),
        name="feed_grad",
    )(up, down, bias.reshape(-1, 1, cols), act, gp, *n2s, *gbs)


def norm_kernel(x_ref, gain_ref, shift_ref, o_ref):
    hat, _ = norm_parts(x_ref[...].astype(F32))
    o_ref[...] = (hat * gain_ref[0:1] + shift_ref[0:1]).astype(BF)


def first_norm(x, gains, shifts, blk=512):
    rows, depth = x.shape
    blk = min(blk, rows)
    whole = pl.BlockSpec(gains.shape, lambda i: (0, 0))
    block = pl.BlockSpec((blk, depth), lambda i: (i, 0))
    return pl.pallas_call(
        norm_kernel,
        grid=(rows // blk,),
        in_specs=[block, whole, whole],
        out_specs=block,
        out_shape=jax.ShapeDtypeStruct((rows, depth), BF),
        compiler_params=pltpu.CompilerParams(vmem_limit_bytes=60 * MIB),
        name="first_norm",
    )(x, gains, shifts)


def join_kernel(pick_ref, x_ref, gain_ref, shift_ref, *refs, blocks, each):
    parts, (attn_ref, resid_ref, low_ref) = refs[:-3], refs[-3:]
    block = pl.program_id(0) // each
    total = None
    for g in range(len(parts) // blocks):
        wanted = pick_ref[g * blocks + block]
        part = parts[g * blocks][...]
        for b in range(1, blocks):
            part = jnp.where(wanted == b, parts[g * blocks + b][...], part)
        total = part if total is None else total + part.astype(F32)
    attn_ref[...] = total
    hat, _ = norm_parts(total)
    resid = x_ref[...].astype(F32) + hat * gain_ref[1:2] + shift_ref[1:2]
    resid_ref[...] = resid
    hat, _ = norm_parts(resid)
    low_ref[...] = (hat * gain_ref[2:3] + shift_ref[2:3]).astype(BF)


def join(x, gains, shifts, shares, picks, blk=256):
    rows, depth = x.shape
    blocks = len(shares[0])
    blk = min(blk, rows // blocks)
    each = rows // blocks // blk
    whole = pl.BlockSpec(gains.shape, lambda i, *_: (0, 0))
    block = pl.BlockSpec((blk, depth), lambda i, *_: (i, 0))
    part = pl.BlockSpec((blk, depth), lambda i, *_: (lax.rem(i, each), 0))
    return pl.pallas_call(
        functools.partial(join_kernel, blocks=blocks, each=each),
        grid_spec=pltpu.PrefetchScalarGridSpec(
            num_scalar_prefetch=1,
            grid=(rows // blk,),
            in_specs=[block, whole, whole] + [part] * (len(shares) * blocks),
            out_specs=[block, block, block],
        ),
        out_shape=[
            jax.ShapeDtypeStruct((rows, depth), F32),
            jax.ShapeDtypeStruct((rows, depth), F32),
            jax.ShapeDtypeStruct((rows, depth), BF),
        ],
        compiler_params=pltpu.CompilerParams(vmem_limit_bytes=60 * MIB),
        name="join",
    )(picks, x, gains, shifts, *[v for share in shares for v in share])


def widen_kernel(up_ref, down_ref, dup_ref, ddown_ref):
    dup_ref[...] = jnp.transpose(up_ref[...]).astype(F32)
    ddown_ref[...] = down_ref[...].astype(F32)


def widen(grads, blk=256):
    hidden, depth = grads.shape[0] // 2, grads.shape[1]
    blk = min(blk, hidden)
    count = hidden // blk
    return pl.pallas_call(
        widen_kernel,
        grid=(count,),
        in_specs=[
            pl.BlockSpec((blk, depth), lambda i: (i, 0)),
            pl.BlockSpec((blk, depth), lambda i: (count + i, 0)),
        ],
        out_specs=[
            pl.BlockSpec((depth, blk), lambda i: (0, i)),
            pl.BlockSpec((blk, depth), lambda i: (i, 0)),
        ],
        out_shape=[
            jax.ShapeDtypeStruct((depth, hidden), F32),
            jax.ShapeDtypeStruct((hidden, depth), F32),
        ],
        compiler_params=pltpu.CompilerParams(vmem_limit_bytes=60 * MIB),
        name="widen",
    )(grads, grads)

MESH = pl.DeviceIdType.MESH


def exchange(src, dst, sems, slot, bit):
    peer = lax.axis_index("dp") ^ (1 << bit)
    return pltpu.make_async_remote_copy(
        src_ref=src,
        dst_ref=dst,
        send_sem=sems[0].at[slot],
        recv_sem=sems[1].at[slot],
        device_id={"dp": peer},
        device_id_type=MESH,
    )


def tail_kernel(
    gq_ref, gk_ref, gv_ref, mixed_ref, wq_ref, wk_ref, wv_ref, x_ref, gr_ref, gain_ref, vec_ref, *refs,
    bits, groups, steps,
):
    lefts, refs = refs[: 2 * groups], refs[2 * groups :]
    sum_ref, out_ref, total_ref = refs[:3]
    right, left, weight, x, g_resid, packed, acc, core_buf, buf, sent, came, own_share, vec_buf = refs[3:16]
    send, recv, vec_send, vec_recv, x_send, x_recv, local = refs[16:]
    sems = (send, recv)
    place, me = lax.axis_index("tensor"), lax.axis_index("dp")
    bit = lambda b: lax.rem(lax.div(me, 1 << b), 2)
    core = bit(0)
    order = list(range(1, bits))
    rows, depth = x.shape
    width = weight.shape[2]
    half = 2 * depth
    base = pl.multiple_of(core * half, half)
    part = min(512, depth)
    chunks = half // part
    slots, fetched = iter(range(send.shape[0])), iter(range(local.shape[0]))

    def fetch(src, dst):
        c = pltpu.make_async_copy(src, dst, local.at[next(fetched)])
        c.start()
        return c

    def wait_all(copies):
        for c in copies:
            c.wait()

    second = [fetch(r, right.at[i]) for i, r in enumerate((gq_ref, gk_ref, gv_ref))]
    second += [fetch(r, weight.at[i]) for i, r in enumerate((wq_ref, wk_ref, wv_ref))]
    third = [fetch(r, left.at[i]) for i, r in enumerate(lefts)] + [fetch(mixed_ref, right.at[3])]
    fourth = [fetch(x_ref, x), fetch(gr_ref, g_resid)]

    greeted = [{"dp": me ^ (1 << b)} for b in range(bits)]
    greeted += [{"tensor": lax.rem(place + r, groups)} for r in range(1, groups)]
    known = {frozenset([("dp", b)]) for b in range(bits)} | {
        frozenset([("tensor", b)]) for b in range((groups - 1).bit_length())
    }
    for bits_of in steps:
        for mask in range(1, 1 << len(bits_of)):
            chosen = [bits_of[i] for i in range(len(bits_of)) if mask >> i & 1]
            if frozenset(chosen) not in known and any(axis == "dp" for axis, _ in chosen):
                known.add(frozenset(chosen))
                peer = {}
                for axis, b in chosen:
                    peer[axis] = peer.get(axis, lax.axis_index(axis)) ^ (1 << b)
                greeted.append(peer)
    barrier = pltpu.get_barrier_semaphore()
    for peer in greeted:
        pl.semaphore_signal(barrier, inc=1, device_id=peer, device_id_type=MESH)
    pl.semaphore_wait(barrier, len(greeted))

    def copy(src, dst, b):
        c = exchange(src, dst, sems, next(slots), b)
        c.start()
        return c

    forwards = []
    cores = {}

    def reduce(chunk):
        cores[chunk].wait()

        def join(i, _):
            at = pl.ds(pl.multiple_of(chunk * part + i * 64, 64), 64)
            own = packed[pl.ds(pl.multiple_of(base + chunk * part + i * 64, 64), 64)].astype(F32)
            acc[at] = (own + core_buf[at].astype(F32)).astype(BF)
            return 0

        lax.fori_loop(0, part // 64, join, 0)
        start, size = chunk * part, part
        landing = chunk * (part - part // (1 << (bits - 1)))
        for b in order:
            size //= 2
            away = pl.multiple_of(start + (1 - bit(b)) * size, size)
            c = copy(acc.at[pl.ds(away, size)], buf.at[pl.ds(landing, size)], b)
            start = start + bit(b) * size
            yield
            c.wait()
            step = min(size, 64)

            def body(i, _, start=start, landing=landing, step=step):
                at = pl.ds(pl.multiple_of(start + i * step, step), step)
                got = buf[pl.ds(pl.multiple_of(landing + i * step, step), step)].astype(F32)
                acc[at] = (acc[at].astype(F32) + got).astype(BF)
                return 0

            lax.fori_loop(0, size // step, body, 0)
            landing += size
        start = base + start
        sum_ref[pl.ds(pl.multiple_of(start, size), size)] = acc[pl.ds(pl.multiple_of(start - base, size), size)]
        for b in reversed(order):
            have = sum_ref.at[pl.ds(pl.multiple_of(start, size), size)]
            c = copy(have, have, b)
            yield
            c.wait()
            start = start - bit(b) * size
            size *= 2
        have = sum_ref.at[pl.ds(pl.multiple_of(start, size), size)]
        forwards.append(copy(have, have, 0))

    def share(r, store):
        at = lax.rem(place + r, groups) * rows
        blk = min(256, rows)

        def body(i, _):
            g = pl.ds(pl.multiple_of(at + i * blk, blk), blk)
            value = dotg(right[0, g, :], weight[0], NT)
            value += dotg(right[1, g, :], weight[1], NT)
            value += dotg(right[2, g, :], weight[2], NT)
            store(pl.ds(pl.multiple_of(i * blk, blk), blk), value)
            return 0

        lax.fori_loop(0, rows // blk, body, 0)

    shares = []

    def share_away(r):
        def store(at, value):
            sent[r - 1, at, :] = value.astype(BF)

        share(r, store)
        c = pltpu.make_async_remote_copy(
            src_ref=sent.at[r - 1],
            dst_ref=came.at[r - 1],
            send_sem=x_send.at[r - 1],
            recv_sem=x_recv.at[r - 1],
            device_id={"tensor": lax.rem(place + r, groups)},
            device_id_type=MESH,
        )
        c.start()
        shares.append(c)

    def store_own(at, value):
        own_share[at, :] = value

    def weight_grad(side, some):
        cols = min(256, part)
        each = part // cols

        def body(i, _):
            first = pl.multiple_of(lax.rem(core + side, 2) * half + i * cols, cols)
            number = lax.div(first, depth)
            kind = lax.div(number, 3) * groups
            lanes = pl.ds(pl.multiple_of(lax.rem(first, depth), cols), cols)
            value = None
            for r in range(groups):
                at = pl.ds(pl.multiple_of(lax.rem(place + r, groups) * rows, rows), rows)
                term = dotg(left[kind + r, :, lanes], right[number, at, :], TN)
                value = term if value is None else value + term
            packed[pl.ds(first, cols), :] = value.astype(BF)
            return 0

        lax.fori_loop(some[0] * each, (some[-1] + 1) * each, body, 0)
        if side:
            for c in some:
                at = pl.ds(pl.multiple_of((1 - core) * half + c * part, part), part)
                cores[c] = copy(packed.at[at], core_buf.at[pl.ds(c * part, part)], 0)

    def last_norm():
        blk = min(64, rows)

        def body(i, _):
            at = pl.ds(pl.multiple_of(i * blk, blk), blk)
            value = own_share[at, :]
            for r in range(groups - 1):
                value += came[r, at, :].astype(F32)
            hat, scale = norm_parts(x[at, :].astype(F32))
            out_ref[at, :] = (g_resid[at, :] + norm_back(value, hat, scale, gain_ref[0:1])).astype(BF)
            total_ref[0:1] += column_sum(value * hat)
            total_ref[1:2] += column_sum(value)
            return 0

        lax.fori_loop(0, rows // blk, body, 0)

    def vectors():
        slot = 0
        for bits_of in steps:
            sends = []
            for mask in range(1, 1 << len(bits_of)):
                peer = {}
                for i, (axis, b) in enumerate(bits_of):
                    if mask >> i & 1:
                        peer[axis] = peer.get(axis, lax.axis_index(axis)) ^ (1 << b)
                sends.append(
                    pltpu.make_async_remote_copy(
                        src_ref=total_ref,
                        dst_ref=vec_buf.at[slot],
                        send_sem=vec_send.at[slot],
                        recv_sem=vec_recv.at[slot],
                        device_id=peer,
                        device_id_type=MESH,
                    )
                )
                sends[-1].start()
                slot += 1
            yield
            wait_all(sends)
            total = total_ref[...]
            for i in range(len(sends)):
                total += vec_buf[slot - len(sends) + i]
            total_ref[...] = total

    def turn(chains):
        still = []
        for chain in chains:
            try:
                next(chain)
                still.append(chain)
            except StopIteration:
                pass
        return still

    wait_all(second)
    for r in range(1, groups):
        share_away(r)
    wait_all(third)
    all_chunks = list(range(chunks))
    for some in (all_chunks[: chunks // 2], all_chunks[chunks // 2 :]):
        weight_grad(1, some)
    reduces = []
    for chunk in all_chunks:
        weight_grad(0, [chunk])
        reduces = turn(reduces + [reduce(chunk)])
    share(0, store_own)
    reduces = turn(reduces)
    wait_all(fourth)
    wait_all(shares)
    total_ref[...] = vec_ref[...]
    last_norm()
    chain = turn([vectors()])
    while reduces or chain:
        reduces, chain = turn(reduces), turn(chain)
    wait_all(forwards)


def tail(grads, mixed, weights, x, g_resid, gains, vectors, n1s, gas, bits, steps):
    (slots, width), (rows, depth), groups = mixed.shape, x.shape, len(n1s)
    half = 2 * depth
    landing = half - half // (1 << (bits - 1))
    count = half // min(512, depth) * (2 * bits + 1)
    vecs = sum((1 << len(b)) - 1 for b in steps)
    vmem = pl.BlockSpec(memory_space=pltpu.VMEM)
    anyspace = pl.BlockSpec(memory_space=pl.ANY)
    dma = pltpu.SemaphoreType.DMA
    peers = max(groups - 1, 1)
    return pl.pallas_call(
        functools.partial(tail_kernel, bits=bits, groups=groups, steps=steps),
        in_specs=[anyspace] * 9 + [vmem] * 2 + [anyspace] * (2 * groups),
        out_specs=[vmem, vmem, vmem],
        out_shape=[
            jax.ShapeDtypeStruct((4 * depth, width), BF),
            jax.ShapeDtypeStruct((rows, depth), BF),
            jax.ShapeDtypeStruct(vectors.shape, F32),
        ],
        scratch_shapes=[
            pltpu.VMEM((4, slots, width), BF),
            pltpu.VMEM((2 * groups, rows, depth), BF),
            pltpu.VMEM((3, depth, width), BF),
            pltpu.VMEM((rows, depth), BF),
            pltpu.VMEM((rows, depth), F32),
            pltpu.VMEM((4 * depth, width), BF),
            pltpu.VMEM((half, width), BF),
            pltpu.VMEM((half, width), BF),
            pltpu.VMEM((landing, width), BF),
            pltpu.VMEM((peers, rows, depth), BF),
            pltpu.VMEM((peers, rows, depth), BF),
            pltpu.VMEM((rows, depth), F32),
            pltpu.VMEM((vecs,) + vectors.shape, F32),
            dma((count,)),
            dma((count,)),
            dma((vecs,)),
            dma((vecs,)),
            dma((peers,)),
            dma((peers,)),
            dma((9 + 2 * groups,)),
        ],
        compiler_params=pltpu.CompilerParams(
            collective_id=1, has_side_effects=True, vmem_limit_bytes=60 * MIB
        ),
        cost_estimate=pl.CostEstimate(flops=rows * width, bytes_accessed=rows * width, transcendentals=0),
        name="tail",
    )(*grads, mixed, *weights, x, g_resid, gains, vectors, *n1s, *gas)


def mixed_back_kernel(at_ref, x_ref, w_ref, *refs):
    refs[-1][...] = dotg(x_ref[...], w_ref[...], NT).astype(BF)


def mixed_back(where, x, w_out, slots, held, blk=256):
    rows, depth = x.shape
    width = w_out.shape[0]
    blk = min(blk, rows)
    count = rows // blk
    return pl.pallas_call(
        mixed_back_kernel,
        grid_spec=pltpu.PrefetchScalarGridSpec(
            num_scalar_prefetch=1,
            grid=(count,),
            in_specs=[
                pl.BlockSpec((blk, depth), lambda i, at: (i, 0)),
                pl.BlockSpec((width, depth), lambda i, at: (0, 0)),
            ]
            + [pl.BlockSpec(memory_space=pl.ANY)] * len(held),
            out_specs=pl.BlockSpec((blk, width), lambda i, at: (at[0] * count + i, 0)),
        ),
        out_shape=jax.ShapeDtypeStruct((slots, width), BF),
        input_output_aliases={3: 0} if held else {},
        compiler_params=pltpu.CompilerParams(vmem_limit_bytes=60 * MIB),
        cost_estimate=pl.CostEstimate(flops=rows * depth, bytes_accessed=rows * depth, transcendentals=0),
        name="mixed_back",
    )(where, x, w_out, *held)


def shift(x, axis, count, step):
    return lax.ppermute(x, axis, [((i + step) % count, i) for i in range(count)])


def shards(
    tokens,
    lengths,
    cotangent,
    w_query,
    w_key,
    w_value,
    w_out,
    up_weight,
    bias_up,
    down_weight,
    bias_down,
    norm_gains,
    norm_shifts,
):
    rows, _, depth = tokens.shape
    groups, replicas = lax.axis_size("tensor"), lax.axis_size("dp")
    me, replica = lax.axis_index("tensor"), lax.axis_index("dp")
    slots = rows * groups
    width = w_query.shape[1]
    hidden = up_weight.shape[1]
    x = tokens.reshape(rows, depth)
    here = me.reshape(1).astype(jnp.int32)
    place = lambda r: (here + r) % groups

    def others(v):
        return [shift(v, "tensor", groups, r) for r in range(1, groups)]

    def to_owner(v, r):
        return shift(v, "tensor", groups, groups - r)

    up_piece = lax.dynamic_slice_in_dim(up_weight, replica * (depth // replicas), depth // replicas, 0)
    down_piece = lax.dynamic_slice_in_dim(
        down_weight, replica * (hidden // replicas), hidden // replicas, 0
    )
    up_pieces, down_pieces, bias_rest = others(up_piece), others(down_piece), others(bias_up)
    gather = lambda v: lax.all_gather(v, "dp", axis=0, tiled=True)

    freqs = 10000.0 ** (-jnp.arange(HD // 2).astype(F32) * 2.0 / HD)
    angles = jnp.arange(slots).astype(F32)[:, None] * freqs[None, :]
    cosine, sine = jnp.cos(angles), jnp.sin(angles)
    cosine = jnp.concatenate([cosine] * 4, axis=1)
    sine = jnp.concatenate([-sine, sine] * 2, axis=1)
    normed_one = first_norm(x, norm_gains, norm_shifts)
    normed_one_rest = others(normed_one)
    weights = (w_query, w_key, w_value)
    own, up_pieces = lax.optimization_barrier((normed_one, up_pieces))
    joint = project(here, own, *weights, cosine, sine)
    joint, normed_one_rest, down_pieces, bias_rest = lax.optimization_barrier(
        (joint, normed_one_rest, down_pieces, bias_rest)
    )
    for r, n in enumerate(normed_one_rest):
        joint = project(place(r + 1), n, *weights, cosine, sine, joint)
    blk = min(512, rows)
    each = rows // blk
    odd = lambda r: lax.rem(place(r), 2)
    ranks = lambda r, k: jnp.where(odd(r) == 1, each - 1 - k, k)
    held, shares, arrived = (), [], [[] for _ in range(1, groups)]
    for k in range(each):
        for r in range(1, groups):
            *held, share = attend(place(r) * each + ranks(0, k), lengths, joint, w_out, held, BF, blk)
            arrived[r - 1].append(to_owner(share, r))
        if k == each - 1 and k > 0:
            joint, arrived = lax.optimization_barrier((joint, [v[:k] for v in arrived])), arrived
            joint, early = joint
            arrived = [list(e) + v[k:] for e, v in zip(early, arrived)]
        *held, share = attend(here * each + ranks(0, k), lengths, joint, w_out, held, F32, blk)
        shares.append(share)
    mixed, lse = held
    shares = [shares] + arrived
    picks = jnp.concatenate([ranks(groups - r, k) for r in range(groups) for k in range(each)])
    up_rest, down_rest = [gather(p) for p in up_pieces], [gather(p) for p in down_pieces]
    shares, up_rest, down_rest = lax.optimization_barrier((shares, up_rest, down_rest))
    ups, downs = [up_weight] + up_rest, [down_weight] + down_rest
    biases = jnp.concatenate([bias_up] + bias_rest).astype(F32)

    info = jnp.stack([lengths[0], me * rows]).astype(jnp.int32)
    cot = cotangent.reshape(rows, depth)
    attn_sum, resid, normed_two = join(x, norm_gains, norm_shifts, shares, picks)
    normed_two_rest = others(normed_two)
    slope, act, layer_out, g_branch, sums3 = feed(
        info, normed_two, biases, ups, downs, resid, cot, bias_down.reshape(1, depth), norm_gains, norm_shifts
    )
    g_branch_rest = others(g_branch)
    g_pre, g_resid, g_attn, sums21 = feed_back(
        info, g_branch, slope, ups, downs, resid, attn_sum, cot, norm_gains
    )
    g_attn_rest = others(g_attn)
    g_pre, normed_two_rest = lax.optimization_barrier((g_pre, normed_two_rest))
    grad_feed, bias_up_sum = feed_grad(
        up_weight, down_weight, biases[:hidden], act, g_pre,
        [normed_two] + normed_two_rest, [g_branch] + g_branch_rest,
    )
    grad_feed = grad_feed.reshape(2 * hidden, depth)
    g_attn, g_attn_rest, grad_feed = lax.optimization_barrier((g_attn, g_attn_rest, grad_feed))
    grad_feed = lax.psum(grad_feed, "dp")
    g_mixed = mixed_back(here, g_attn, w_out, slots, [])
    for r, g in enumerate(g_attn_rest):
        g_mixed = mixed_back(place(r + 1), g, w_out, slots, [g_mixed])

    grads = attend_back(lengths, joint, mixed, g_mixed, lse, cosine, sine, width)
    placed = lax.dynamic_update_slice(
        jnp.zeros((groups * hidden,), F32), bias_up_sum.reshape(-1), (me * hidden,)
    ).reshape(-1, depth)
    bits = (replicas - 1).bit_length()
    steps = [("tensor", b) for b in range((groups - 1).bit_length())] + [("dp", b) for b in range(bits)]
    steps = [tuple(steps[i : i + 2]) for i in range(0, len(steps), 2)]
    vectors = jnp.concatenate([jnp.zeros((2, depth), F32), sums3[:3], sums21[:4], placed])
    vectors = jnp.pad(vectors, ((0, -len(vectors) % 8), (0, 0)))
    packed, grad_tokens, sums = tail(
        grads, mixed, weights, x, g_resid, norm_gains, vectors,
        [normed_one] + normed_one_rest, [g_attn] + g_attn_rest, bits, steps,
    )
    grad_up, grad_down = widen(grad_feed)
    grad_query, grad_key, grad_value = (packed[i * depth : (i + 1) * depth].astype(F32) for i in range(3))
    grad_out = jnp.transpose(packed[3 * depth :]).astype(F32)
    grad_gains = jnp.stack([sums[0], sums[7], sums[5], sums[2]])
    grad_shifts = jnp.stack([sums[1], sums[8], sums[6], sums[3]])
    grad_bias_up = lax.dynamic_slice_in_dim(sums[9 : 9 + groups * hidden // depth].reshape(-1), me * hidden, hidden, 0)
    whole = (rows, 1, depth)
    return (
        layer_out.reshape(whole),
        grad_tokens.reshape(whole),
        grad_query,
        grad_key,
        grad_value,
        grad_out,
        grad_up,
        grad_bias_up,
        grad_down,
        sums[4],
        grad_gains,
        grad_shifts,
    )


def solution(mesh):
    wide, tall = P(None, "tensor"), P("tensor", None)
    acts = P("tensor", "dp", None)
    return jax.shard_map(
        shards,
        mesh=mesh,
        in_specs=(acts, P("dp"), acts, wide, wide, wide, tall, wide, P("tensor"), tall, P(), P(), P()),
        out_specs=(acts, acts, wide, wide, wide, tall, wide, P("tensor"), tall, P(), P(), P()),
        check_vma=False,
    )
```

```python
import functools
import jax
import jax.numpy as jnp
from jax import lax
from jax.experimental import pallas as pl
from jax.experimental.pallas import tpu as pltpu
from jax.sharding import PartitionSpec as P

HD = 64
EPSILON = 1e-05
BF = jnp.bfloat16
F32 = jnp.float32
NT = (((1,), (1,)), ((), ()))
NN = (((1,), (0,)), ((), ()))
TN = (((0,), (0,)), ((), ()))
MIB = 1 << 20


def dotg(a, b, dims=NN):
    return lax.dot_general(a, b, dims, preferred_element_type=F32)


def rotate(x, cos, sin):
    first = lax.broadcasted_iota(jnp.int32, (x.shape[0], 128), 1) % HD < HD // 2
    parts = []
    for a in range(0, x.shape[1], 128):
        v = x[:, a : a + 128]
        swapped = jnp.where(first, pltpu.roll(v, 96, 1), pltpu.roll(v, 32, 1))
        parts.append(v * cos + swapped * sin)
    return jnp.concatenate(parts, axis=1) if len(parts) > 1 else parts[0]


def qkv_kernel(x_ref, wq_ref, wk_ref, wv_ref, cos_ref, sin_ref, o_ref):
    width = wq_ref.shape[1]
    x, cos, sin = x_ref[...], cos_ref[...], sin_ref[...]
    o_ref[:, :width] = rotate(dotg(x, wq_ref[...]), cos, sin).astype(BF)
    o_ref[:, width : 2 * width] = rotate(dotg(x, wk_ref[...]), cos, sin).astype(BF)
    o_ref[:, 2 * width :] = dotg(x, wv_ref[...]).astype(BF)


def project(where, x, w_query, w_key, w_value, cos, sin, joint=None, blk=256):
    rows, depth = x.shape
    width, slots = w_query.shape[1], cos.shape[0]
    blk = min(blk, rows)
    count = rows // blk
    weight = pl.BlockSpec((depth, width), lambda i, at: (0, 0))
    angle = pl.BlockSpec((blk, 128), lambda i, at: (at[0] * count + i, 0))
    kernel = lambda at, *refs: qkv_kernel(*refs[:6], refs[-1])
    held = [] if joint is None else [joint]
    return pl.pallas_call(
        kernel,
        grid_spec=pltpu.PrefetchScalarGridSpec(
            num_scalar_prefetch=1,
            grid=(count,),
            in_specs=[pl.BlockSpec((blk, depth), lambda i, at: (i, 0)), weight, weight, weight, angle, angle]
            + [pl.BlockSpec(memory_space=pl.ANY)] * len(held),
            out_specs=pl.BlockSpec((blk, 3 * width), lambda i, at: (at[0] * count + i, 0)),
        ),
        out_shape=jax.ShapeDtypeStruct((slots, 3 * width), BF),
        input_output_aliases={7: 0} if held else {},
        compiler_params=pltpu.CompilerParams(vmem_limit_bytes=60 * MIB),
        cost_estimate=pl.CostEstimate(flops=rows * depth, bytes_accessed=rows * depth, transcendentals=0),
        name="project",
    )(where, x, w_query, w_key, w_value, cos, sin, *held)


def attend_kernel(at_ref, len_ref, q_ref, k_ref, v_ref, w_ref, *refs, blk):
    o_ref, lse_ref, share_ref, vt, low_ref = refs[-5:]
    pair = pl.program_id(0)
    i = at_ref[0]
    length = len_ref[0]
    def turn(j, _):
        part = pl.ds(pl.multiple_of(j * blk, blk), blk)
        vt[:, part] = jnp.transpose(v_ref[part, :])
        return 0

    lax.fori_loop(0, i + 1, turn, 0)
    lane = lax.broadcasted_iota(jnp.int32, (blk, 128), 1)
    q = q_ref[...] * jnp.asarray(0.125, BF)
    zero = jnp.zeros_like(q)
    qs = (jnp.where(lane < HD, q, zero), jnp.where(lane < HD, zero, q))

    def step(j, carry, diag):
        start = pl.multiple_of(j * blk, blk)
        kb = k_ref[pl.ds(start, blk), :]
        out = []
        for h in range(2):
            m, l, acc = carry[h]
            s = dotg(kb, qs[h], NT)
            if diag:
                key = lax.broadcasted_iota(jnp.int32, (blk, blk), 0)
                qry = lax.broadcasted_iota(jnp.int32, (blk, blk), 1)
                s = jnp.where((key <= qry) & (key + start < length), s, -1e30)
            mn = jnp.maximum(m, jnp.max(s, axis=0, keepdims=True))
            p = jnp.exp(s - mn)
            al = jnp.exp(m - mn)
            l = l * al + jnp.sum(p, axis=0, keepdims=True)
            vb = vt[HD * h : HD * h + HD, pl.ds(start, blk)]
            acc = acc * al + dotg(vb, p.astype(BF))
            out.append((mn, l, acc))
        return tuple(out)

    init = tuple(
        (jnp.full((1, blk), -1e30, F32), jnp.zeros((1, blk), F32), jnp.zeros((HD, blk), F32))
        for _ in range(2)
    )
    c = lax.fori_loop(0, i, lambda j, c: step(j, c, False), init)
    c = step(i, c, True)
    ot = jnp.concatenate([c[h][2] / c[h][1] for h in range(2)], axis=0)
    low = jnp.transpose(ot).astype(BF)
    o_ref[...] = low
    lse_ref[0] = jnp.concatenate([c[h][0] + jnp.log(c[h][1]) for h in range(2)], axis=0)
    low_ref[pair] = low

    @pl.when(pair == pl.num_programs(0) - 1)
    def _():
        pairs = low_ref.shape[0]
        low = jnp.concatenate([low_ref[p] for p in range(pairs)], axis=1)
        share_ref[...] = dotg(low, w_ref[...]).astype(share_ref.dtype)


def attend(at, length, joint, w_out, held, kind, blk):
    rows, width, depth = joint.shape[0], w_out.shape[0], w_out.shape[1]
    pairs = width // 128
    return pl.pallas_call(
        functools.partial(attend_kernel, blk=blk),
        grid_spec=pltpu.PrefetchScalarGridSpec(
            num_scalar_prefetch=2,
            grid=(pairs,),
            in_specs=[
                pl.BlockSpec((blk, 128), lambda p, at, *_: (at[0], p)),
                pl.BlockSpec((rows, 128), lambda p, *_: (0, pairs + p)),
                pl.BlockSpec((rows, 128), lambda p, *_: (0, 2 * pairs + p)),
                pl.BlockSpec((width, depth), lambda p, *_: (0, 0), pipeline_mode=pl.Buffered(1)),
            ]
            + [pl.BlockSpec(memory_space=pl.ANY)] * len(held),
            out_specs=[
                pl.BlockSpec((blk, 128), lambda p, at, *_: (at[0], p)),
                pl.BlockSpec((1, 2, blk), lambda p, at, *_: (p, 0, at[0])),
                pl.BlockSpec((blk, depth), lambda p, *_: (0, 0)),
            ],
            scratch_shapes=[pltpu.VMEM((128, rows), BF), pltpu.VMEM((pairs, blk, 128), BF)],
        ),
        out_shape=[
            jax.ShapeDtypeStruct((rows, width), BF),
            jax.ShapeDtypeStruct((pairs, 2, rows), F32),
            jax.ShapeDtypeStruct((blk, depth), kind),
        ],
        input_output_aliases={6: 0, 7: 1} if held else {},
        compiler_params=pltpu.CompilerParams(vmem_limit_bytes=60 * MIB),
        cost_estimate=pl.CostEstimate(flops=rows * width, bytes_accessed=rows * width, transcendentals=0),
        name="attend",
    )(at, length, joint, joint, joint, w_out, *held)


def attend_back_kernel(
    len_ref, q_ref, k_ref, v_ref, o_ref, do_ref, lse_ref, cos_ref, sin_ref,
    dq_ref, dk_ref, dv_ref, kt, dlt, dqt, *, blk, blocks,
):
    j = pl.program_id(1)
    length = len_ref[0]

    @pl.when(j == 0)
    def _():
        kt[...] = jnp.transpose(k_ref[...])
        dqt[...] = jnp.zeros_like(dqt)

        def body(i, _):
            at = pl.ds(pl.multiple_of(i * blk, blk), blk)
            both = jnp.transpose(do_ref[at, :].astype(F32) * o_ref[at, :].astype(F32))
            for h in range(2):
                dlt[h : h + 1, at] = jnp.sum(both[HD * h : HD * h + HD], axis=0, keepdims=True)
            return 0

        lax.fori_loop(0, blocks, body, 0)

    js = pl.multiple_of(j * blk, blk)
    lane = lax.broadcasted_iota(jnp.int32, (blk, 128), 1)
    kb = k_ref[pl.ds(js, blk), :] * jnp.asarray(0.125, BF)
    vb = v_ref[pl.ds(js, blk), :]
    zero = jnp.zeros_like(kb)
    ks = (jnp.where(lane < HD, kb, zero), jnp.where(lane < HD, zero, kb))
    vs = (jnp.where(lane < HD, vb, zero), jnp.where(lane < HD, zero, vb))

    def step(i, carry, diag):
        at = pl.ds(pl.multiple_of(i * blk, blk), blk)
        qb, dob = q_ref[at, :], do_ref[at, :]
        out = []
        for h in range(2):
            dk, dv = carry[h]
            s = dotg(ks[h], qb, NT)
            if diag:
                key = lax.broadcasted_iota(jnp.int32, (blk, blk), 0)
                qry = lax.broadcasted_iota(jnp.int32, (blk, blk), 1)
                s = jnp.where((key <= qry) & (key + js < length), s, -1e30)
            p = jnp.exp(s - lse_ref[0, h : h + 1, at])
            dp = dotg(vs[h], dob, NT)
            ds = (p * (dp - dlt[h : h + 1, at])).astype(BF)
            dv = dv + dotg(p.astype(BF), dob)
            dk = dk + dotg(ds, qb)
            dqt[HD * h : HD * h + HD, at] += dotg(kt[HD * h : HD * h + HD, pl.ds(js, blk)], ds)
            out.append((dk, dv))
        return tuple(out)

    z = jnp.zeros((blk, 128), F32)
    c = step(j, ((z, z), (z, z)), True)
    c = lax.fori_loop(j + 1, blocks, lambda i, c: step(i, c, False), c)
    grad = jnp.where(lane < HD, c[0][0], c[1][0]) * 0.125
    dk_ref[...] = rotate(grad, cos_ref[pl.ds(js, blk), :], -sin_ref[pl.ds(js, blk), :]).astype(BF)
    dv_ref[...] = jnp.where(lane < HD, c[0][1], c[1][1]).astype(BF)

    @pl.when(j == blocks - 1)
    def _():
        def body(i, _):
            at = pl.ds(pl.multiple_of(i * blk, blk), blk)
            grad = jnp.transpose(dqt[:, at]) * 0.125
            dq_ref[at, :] = rotate(grad, cos_ref[at, :], -sin_ref[at, :]).astype(BF)
            return 0

        lax.fori_loop(0, blocks, body, 0)


def attend_back(length, joint, mixed, dmixed, lse, cos, sin, width, blk=512):
    rows = joint.shape[0]
    pairs, blocks = width // 128, rows // blk
    full = lambda off: pl.BlockSpec((rows, 128), lambda p, j, *_: (0, off * pairs + p))
    angle = pl.BlockSpec((rows, 128), lambda p, j, *_: (0, 0))
    block = pl.BlockSpec((blk, 128), lambda p, j, *_: (j, p))
    return pl.pallas_call(
        functools.partial(attend_back_kernel, blk=blk, blocks=blocks),
        grid_spec=pltpu.PrefetchScalarGridSpec(
            num_scalar_prefetch=1,
            grid=(pairs, blocks),
            in_specs=[full(0), full(1), full(2), full(0), full(0)]
            + [pl.BlockSpec((1, 2, rows), lambda p, j, *_: (p, 0, 0)), angle, angle],
            out_specs=[full(0), block, block],
            scratch_shapes=[
                pltpu.VMEM((128, rows), BF),
                pltpu.VMEM((2, rows), F32),
                pltpu.VMEM((128, rows), F32),
            ],
        ),
        out_shape=[jax.ShapeDtypeStruct((rows, width), BF)] * 3,
        compiler_params=pltpu.CompilerParams(vmem_limit_bytes=60 * MIB),
        cost_estimate=pl.CostEstimate(
            flops=rows * width, bytes_accessed=rows * width, transcendentals=0
        ),
        name="attend_back",
    )(length, joint, joint, joint, mixed, dmixed, lse, cos, sin)


def gelu_parts(v):
    c = 0.7978845608028654
    return c, jnp.tanh(c * (v + 0.044715 * v * v * v))


def gelu_both(v):
    c, t = gelu_parts(v)
    half = 0.5 * (1.0 + t)
    return v * half, half + 0.5 * v * (1.0 - t * t) * c * (1.0 + 3 * 0.044715 * v * v)


def norm_parts(values):
    average = jnp.mean(values, axis=-1, keepdims=True)
    centred = values - average
    scale = lax.rsqrt(jnp.mean(centred * centred, axis=-1, keepdims=True) + EPSILON)
    return centred * scale, scale


def norm_back(grad, hat, scale, gain):
    g = grad * gain
    return scale * (
        g - jnp.mean(g, axis=-1, keepdims=True) - hat * jnp.mean(g * hat, axis=-1, keepdims=True)
    )


def column_sum(v):
    return jnp.sum(v, axis=0, keepdims=True)


def valid_rows(info_ref, start, count):
    at = info_ref[1] + start + lax.broadcasted_iota(jnp.int32, (count, 1), 0)
    return (at < info_ref[0]).astype(F32)


def loop_rows(rows, blk, body):
    def step(i, _):
        body(pl.multiple_of(i * blk, blk))
        return 0

    lax.fori_loop(0, rows // blk, step, 0)


def feed_kernel(info_ref, *refs, groups, chunks, sub):
    x_ref, bias_ref, resid_hbm, cot_hbm, bd_ref, gain_ref, shift_ref = refs[:7]
    ups, downs = refs[7 : 7 + groups], refs[7 + groups : 7 + 2 * groups]
    slope_ref, act_ref, out_ref, gb_ref, sums_ref, acc, resid_ref, cot_ref, sems = refs[7 + 2 * groups :]
    step = pl.program_id(0)
    rows = x_ref.shape[0]
    late = [
        pltpu.make_async_copy(resid_hbm, resid_ref, sems.at[0]),
        pltpu.make_async_copy(cot_hbm, cot_ref, sems.at[1]),
    ]

    @pl.when(step == 0)
    def _():
        for c in late:
            c.start()
        acc[...] = jnp.zeros_like(acc) + bd_ref[...].astype(F32)

    for g in range(groups):

        @pl.when(step // chunks == g)
        def _():
            for r in range(0, rows, sub):
                act, slope = gelu_both(dotg(x_ref[r : r + sub], ups[g][...]) + bias_ref[0])
                slope_ref[r : r + sub] = slope.astype(BF)
                act = act.astype(BF)
                if g == 0:
                    act_ref[r : r + sub] = act
                acc[r : r + sub] += dotg(act, downs[g][...])

    @pl.when(step == groups * chunks - 1)
    def _():
        for c in late:
            c.wait()
        sums_ref[...] = jnp.zeros_like(sums_ref)
        gain, shift = gain_ref[3:4], shift_ref[3:4]
        blk = min(256, rows)

        def body(r):
            at = pl.ds(r, blk)
            valid = valid_rows(info_ref, r, blk)
            hat, scale = norm_parts(acc[at])
            out_ref[at] = (valid * (resid_ref[at] + hat * gain + shift)).astype(BF)
            g_out = valid * cot_ref[at].astype(F32)
            low = norm_back(g_out, hat, scale, gain).astype(BF)
            gb_ref[at] = low
            sums_ref[0:1] += column_sum(g_out * hat)
            sums_ref[1:2] += column_sum(g_out)
            sums_ref[2:3] += column_sum(low.astype(F32))

        loop_rows(rows, blk, body)


def feed(info, x, biases, ups, downs, resid, cot, bias_down, gains, shifts, cols=512):
    rows, depth = x.shape
    groups, hidden = len(ups), ups[0].shape[1]
    chunks = hidden // cols
    once = lambda shape: pl.BlockSpec(shape, lambda s, *_: (0, 0), pipeline_mode=pl.Buffered(1))
    anyspace = pl.BlockSpec(memory_space=pl.ANY)
    own = lambda g: (lambda s, *_: (0, jnp.clip(s - g * chunks, 0, chunks - 1)))
    own_t = lambda g: (lambda s, *_: (jnp.clip(s - g * chunks, 0, chunks - 1), 0))
    return pl.pallas_call(
        functools.partial(feed_kernel, groups=groups, chunks=chunks, sub=min(512, rows)),
        grid_spec=pltpu.PrefetchScalarGridSpec(
            num_scalar_prefetch=1,
            grid=(groups * chunks,),
            in_specs=[
                once((rows, depth)),
                pl.BlockSpec((1, 1, cols), lambda s, *_: (s, 0, 0)),
                anyspace,
                anyspace,
                once((1, depth)),
                once(gains.shape),
                once(gains.shape),
            ]
            + [pl.BlockSpec((depth, cols), own(g)) for g in range(groups)]
            + [pl.BlockSpec((cols, depth), own_t(g)) for g in range(groups)],
            out_specs=[
                pl.BlockSpec((rows, cols), lambda s, *_: (0, s)),
                pl.BlockSpec((rows, cols), own(0)),
                once((rows, depth)),
                once((rows, depth)),
                once((8, depth)),
            ],
            scratch_shapes=[
                pltpu.VMEM((rows, depth), F32),
                pltpu.VMEM((rows, depth), F32),
                pltpu.VMEM((rows, depth), BF),
                pltpu.SemaphoreType.DMA((2,)),
            ],
        ),
        out_shape=[
            jax.ShapeDtypeStruct((rows, groups * hidden), BF),
            jax.ShapeDtypeStruct((rows, hidden), BF),
            jax.ShapeDtypeStruct((rows, depth), BF),
            jax.ShapeDtypeStruct((rows, depth), BF),
            jax.ShapeDtypeStruct((8, depth), F32),
        ],
        compiler_params=pltpu.CompilerParams(vmem_limit_bytes=60 * MIB),
        cost_estimate=pl.CostEstimate(flops=rows * depth, bytes_accessed=rows * depth, transcendentals=0),
        name="feed",
    )(info, x, biases.reshape(-1, 1, cols), resid, cot, bias_down, gains, shifts, *ups, *downs)


def feed_back_kernel(info_ref, *refs, groups, chunks, sub):
    gb_ref, slope_ref, resid_hbm, attn_hbm, cot_hbm, gain_ref = refs[:6]
    ups, downs = refs[6 : 6 + groups], refs[6 + groups : 6 + 2 * groups]
    gp_ref, gr_ref, ga_ref, sums_ref, acc, resid_ref, attn_ref, cot_ref, sems = refs[6 + 2 * groups :]
    step = pl.program_id(0)
    rows = gb_ref.shape[0]
    late = [
        pltpu.make_async_copy(src, dst, sems.at[i])
        for i, (src, dst) in enumerate(((resid_hbm, resid_ref), (attn_hbm, attn_ref), (cot_hbm, cot_ref)))
    ]

    @pl.when(step == 0)
    def _():
        for c in late:
            c.start()
        acc[...] = jnp.zeros_like(acc)

    for g in range(groups):

        @pl.when(step // chunks == g)
        def _():
            for r in range(0, rows, sub):
                grad = dotg(gb_ref[r : r + sub], downs[g][...], NT)
                low = (grad * slope_ref[r : r + sub].astype(F32)).astype(BF)
                if g == 0:
                    gp_ref[r : r + sub] = low
                acc[r : r + sub] += dotg(low, ups[g][...], NT)

    @pl.when(step == groups * chunks - 1)
    def _():
        for c in late:
            c.wait()
        sums_ref[...] = jnp.zeros_like(sums_ref)
        blk = min(256, rows)

        def body(r):
            at = pl.ds(r, blk)
            g_out = valid_rows(info_ref, r, blk) * cot_ref[at].astype(F32)
            hat, scale = norm_parts(resid_ref[at])
            g_two = acc[at]
            g_resid = g_out + norm_back(g_two, hat, scale, gain_ref[2:3])
            gr_ref[at] = g_resid
            sums_ref[0:1] += column_sum(g_two * hat)
            sums_ref[1:2] += column_sum(g_two)
            hat, scale = norm_parts(attn_ref[at])
            ga_ref[at] = norm_back(g_resid, hat, scale, gain_ref[1:2]).astype(BF)
            sums_ref[2:3] += column_sum(g_resid * hat)
            sums_ref[3:4] += column_sum(g_resid)

        loop_rows(rows, blk, body)


def feed_back(info, gb, slope, ups, downs, resid, attn_sum, cot, gains, cols=512):
    rows, depth = gb.shape
    groups, hidden = len(ups), ups[0].shape[1]
    chunks = hidden // cols
    once = lambda shape: pl.BlockSpec(shape, lambda s, *_: (0, 0), pipeline_mode=pl.Buffered(1))
    anyspace = pl.BlockSpec(memory_space=pl.ANY)
    own = lambda g: (lambda s, *_: (0, jnp.clip(s - g * chunks, 0, chunks - 1)))
    own_t = lambda g: (lambda s, *_: (jnp.clip(s - g * chunks, 0, chunks - 1), 0))
    return pl.pallas_call(
        functools.partial(feed_back_kernel, groups=groups, chunks=chunks, sub=min(512, rows)),
        grid_spec=pltpu.PrefetchScalarGridSpec(
            num_scalar_prefetch=1,
            grid=(groups * chunks,),
            in_specs=[
                once((rows, depth)),
                pl.BlockSpec((rows, cols), lambda s, *_: (0, s)),
                anyspace,
                anyspace,
                anyspace,
                once(gains.shape),
            ]
            + [pl.BlockSpec((depth, cols), own(g)) for g in range(groups)]
            + [pl.BlockSpec((cols, depth), own_t(g)) for g in range(groups)],
            out_specs=[
                pl.BlockSpec((rows, cols), own(0)),
                once((rows, depth)),
                once((rows, depth)),
                once((8, depth)),
            ],
            scratch_shapes=[
                pltpu.VMEM((rows, depth), F32),
                pltpu.VMEM((rows, depth), F32),
                pltpu.VMEM((rows, depth), F32),
                pltpu.VMEM((rows, depth), BF),
                pltpu.SemaphoreType.DMA((3,)),
            ],
        ),
        out_shape=[
            jax.ShapeDtypeStruct((rows, hidden), BF),
            jax.ShapeDtypeStruct((rows, depth), F32),
            jax.ShapeDtypeStruct((rows, depth), BF),
            jax.ShapeDtypeStruct((8, depth), F32),
        ],
        compiler_params=pltpu.CompilerParams(vmem_limit_bytes=60 * MIB),
        cost_estimate=pl.CostEstimate(flops=rows * depth, bytes_accessed=rows * depth, transcendentals=0),
        name="feed_back",
    )(info, gb, slope, resid, attn_sum, cot, gains, *ups, *downs)


def feed_grad_kernel(*refs, groups):
    up_ref, down_ref, bias_ref, act_ref, gp_ref = refs[:5]
    n2s, gbs = refs[5 : 5 + groups], refs[5 + groups : 5 + 2 * groups]
    grad_ref, sum_ref = refs[5 + 2 * groups :]
    act, gp = act_ref[...], gp_ref[...]
    dup = dotg(gp, n2s[0][...], TN)
    ddown = dotg(act, gbs[0][...], TN)
    sums = column_sum(gp.astype(F32))
    for g in range(1, groups):
        pre = dotg(n2s[g][...], up_ref[...]) + bias_ref[0]
        act, slope = gelu_both(pre)
        act = act.astype(BF)
        gp = (dotg(gbs[g][...], down_ref[...], NT) * slope).astype(BF)
        dup += dotg(gp, n2s[g][...], TN)
        ddown += dotg(act, gbs[g][...], TN)
        sums += column_sum(gp.astype(F32))
    grad_ref[0] = dup.astype(BF)
    grad_ref[1] = ddown.astype(BF)
    sum_ref[0] = sums


def feed_grad(up, down, bias, act, gp, n2s, gbs, cols=512):
    rows, depth = n2s[0].shape
    groups, hidden = len(n2s), up.shape[1]
    once = lambda shape: pl.BlockSpec(shape, lambda s: (0, 0), pipeline_mode=pl.Buffered(1))
    wide = lambda count: pl.BlockSpec((count, cols), lambda s: (0, s))
    tall = pl.BlockSpec((cols, depth), lambda s: (s, 0))
    flat = pl.BlockSpec((1, 1, cols), lambda s: (s, 0, 0))
    return pl.pallas_call(
        functools.partial(feed_grad_kernel, groups=groups),
        grid=(hidden // cols,),
        in_specs=[wide(depth), tall, flat, wide(rows), wide(rows)] + [once((rows, depth))] * (2 * groups),
        out_specs=[pl.BlockSpec((2, cols, depth), lambda s: (0, s, 0)), flat],
        out_shape=[
            jax.ShapeDtypeStruct((2, hidden, depth), BF),
            jax.ShapeDtypeStruct((hidden // cols, 1, cols), F32),
        ],
        compiler_params=pltpu.CompilerParams(vmem_limit_bytes=60 * MIB),
        cost_estimate=pl.CostEstimate(
            flops=(8 * groups - 4) * rows * depth * hidden, bytes_accessed=20 * rows * depth, transcendentals=0
        ),
        name="feed_grad",
    )(up, down, bias.reshape(-1, 1, cols), act, gp, *n2s, *gbs)


def norm_kernel(x_ref, gain_ref, shift_ref, o_ref):
    hat, _ = norm_parts(x_ref[...].astype(F32))
    o_ref[...] = (hat * gain_ref[0:1] + shift_ref[0:1]).astype(BF)


def first_norm(x, gains, shifts, blk=512):
    rows, depth = x.shape
    blk = min(blk, rows)
    whole = pl.BlockSpec(gains.shape, lambda i: (0, 0))
    block = pl.BlockSpec((blk, depth), lambda i: (i, 0))
    return pl.pallas_call(
        norm_kernel,
        grid=(rows // blk,),
        in_specs=[block, whole, whole],
        out_specs=block,
        out_shape=jax.ShapeDtypeStruct((rows, depth), BF),
        compiler_params=pltpu.CompilerParams(vmem_limit_bytes=60 * MIB),
        name="first_norm",
    )(x, gains, shifts)


def join_kernel(pick_ref, x_ref, gain_ref, shift_ref, *refs, blocks, each):
    parts, (attn_ref, resid_ref, low_ref) = refs[:-3], refs[-3:]
    block = pl.program_id(0) // each
    total = None
    for g in range(len(parts) // blocks):
        wanted = pick_ref[g * blocks + block]
        part = parts[g * blocks][...]
        for b in range(1, blocks):
            part = jnp.where(wanted == b, parts[g * blocks + b][...], part)
        total = part if total is None else total + part.astype(F32)
    attn_ref[...] = total
    hat, _ = norm_parts(total)
    resid = x_ref[...].astype(F32) + hat * gain_ref[1:2] + shift_ref[1:2]
    resid_ref[...] = resid
    hat, _ = norm_parts(resid)
    low_ref[...] = (hat * gain_ref[2:3] + shift_ref[2:3]).astype(BF)


def join(x, gains, shifts, shares, picks, blk=256):
    rows, depth = x.shape
    blocks = len(shares[0])
    blk = min(blk, rows // blocks)
    each = rows // blocks // blk
    whole = pl.BlockSpec(gains.shape, lambda i, *_: (0, 0))
    block = pl.BlockSpec((blk, depth), lambda i, *_: (i, 0))
    part = pl.BlockSpec((blk, depth), lambda i, *_: (lax.rem(i, each), 0))
    return pl.pallas_call(
        functools.partial(join_kernel, blocks=blocks, each=each),
        grid_spec=pltpu.PrefetchScalarGridSpec(
            num_scalar_prefetch=1,
            grid=(rows // blk,),
            in_specs=[block, whole, whole] + [part] * (len(shares) * blocks),
            out_specs=[block, block, block],
        ),
        out_shape=[
            jax.ShapeDtypeStruct((rows, depth), F32),
            jax.ShapeDtypeStruct((rows, depth), F32),
            jax.ShapeDtypeStruct((rows, depth), BF),
        ],
        compiler_params=pltpu.CompilerParams(vmem_limit_bytes=60 * MIB),
        name="join",
    )(picks, x, gains, shifts, *[v for share in shares for v in share])


def widen_kernel(up_ref, down_ref, dup_ref, ddown_ref):
    dup_ref[...] = jnp.transpose(up_ref[...]).astype(F32)
    ddown_ref[...] = down_ref[...].astype(F32)


def widen(grads, blk=256):
    hidden, depth = grads.shape[0] // 2, grads.shape[1]
    blk = min(blk, hidden)
    count = hidden // blk
    return pl.pallas_call(
        widen_kernel,
        grid=(count,),
        in_specs=[
            pl.BlockSpec((blk, depth), lambda i: (i, 0)),
            pl.BlockSpec((blk, depth), lambda i: (count + i, 0)),
        ],
        out_specs=[
            pl.BlockSpec((depth, blk), lambda i: (0, i)),
            pl.BlockSpec((blk, depth), lambda i: (i, 0)),
        ],
        out_shape=[
            jax.ShapeDtypeStruct((depth, hidden), F32),
            jax.ShapeDtypeStruct((hidden, depth), F32),
        ],
        compiler_params=pltpu.CompilerParams(vmem_limit_bytes=60 * MIB),
        name="widen",
    )(grads, grads)

MESH = pl.DeviceIdType.MESH


def exchange(src, dst, sems, slot, bit):
    peer = lax.axis_index("dp") ^ (1 << bit)
    return pltpu.make_async_remote_copy(
        src_ref=src,
        dst_ref=dst,
        send_sem=sems[0].at[slot],
        recv_sem=sems[1].at[slot],
        device_id={"dp": peer},
        device_id_type=MESH,
    )


def tail_kernel(
    gq_ref, gk_ref, gv_ref, mixed_ref, wq_ref, wk_ref, wv_ref, x_ref, gr_ref, gain_ref, vec_ref, *refs,
    bits, groups, steps,
):
    lefts, refs = refs[: 2 * groups], refs[2 * groups :]
    sum_ref, out_ref, total_ref = refs[:3]
    right, left, weight, x, g_resid, packed, acc, core_buf, buf, sent, came, own_share, vec_buf = refs[3:16]
    send, recv, vec_send, vec_recv, x_send, x_recv, local = refs[16:]
    sems = (send, recv)
    place, me = lax.axis_index("tensor"), lax.axis_index("dp")
    bit = lambda b: lax.rem(lax.div(me, 1 << b), 2)
    core = bit(0)
    order = list(range(1, bits))
    rows, depth = x.shape
    width = weight.shape[2]
    half = 2 * depth
    base = pl.multiple_of(core * half, half)
    part = min(512, depth)
    chunks = half // part
    slots, fetched = iter(range(send.shape[0])), iter(range(local.shape[0]))

    def fetch(src, dst):
        c = pltpu.make_async_copy(src, dst, local.at[next(fetched)])
        c.start()
        return c

    def wait_all(copies):
        for c in copies:
            c.wait()

    second = [fetch(r, right.at[i]) for i, r in enumerate((gq_ref, gk_ref, gv_ref))]
    second += [fetch(r, weight.at[i]) for i, r in enumerate((wq_ref, wk_ref, wv_ref))]
    third = [fetch(r, left.at[i]) for i, r in enumerate(lefts)] + [fetch(mixed_ref, right.at[3])]
    fourth = [fetch(x_ref, x), fetch(gr_ref, g_resid)]

    greeted = [{"dp": me ^ (1 << b)} for b in range(bits)]
    greeted += [{"tensor": lax.rem(place + r, groups)} for r in range(1, groups)]
    known = {frozenset([("dp", b)]) for b in range(bits)} | {
        frozenset([("tensor", b)]) for b in range((groups - 1).bit_length())
    }
    for bits_of in steps:
        for mask in range(1, 1 << len(bits_of)):
            chosen = [bits_of[i] for i in range(len(bits_of)) if mask >> i & 1]
            if frozenset(chosen) not in known and any(axis == "dp" for axis, _ in chosen):
                known.add(frozenset(chosen))
                peer = {}
                for axis, b in chosen:
                    peer[axis] = peer.get(axis, lax.axis_index(axis)) ^ (1 << b)
                greeted.append(peer)
    barrier = pltpu.get_barrier_semaphore()
    for peer in greeted:
        pl.semaphore_signal(barrier, inc=1, device_id=peer, device_id_type=MESH)
    pl.semaphore_wait(barrier, len(greeted))

    def copy(src, dst, b):
        c = exchange(src, dst, sems, next(slots), b)
        c.start()
        return c

    forwards = []
    cores = {}

    def reduce(chunk):
        cores[chunk].wait()

        def join(i, _):
            at = pl.ds(pl.multiple_of(chunk * part + i * 64, 64), 64)
            own = packed[pl.ds(pl.multiple_of(base + chunk * part + i * 64, 64), 64)].astype(F32)
            acc[at] = (own + core_buf[at].astype(F32)).astype(BF)
            return 0

        lax.fori_loop(0, part // 64, join, 0)
        start, size = chunk * part, part
        landing = chunk * (part - part // (1 << (bits - 1)))
        for b in order:
            size //= 2
            away = pl.multiple_of(start + (1 - bit(b)) * size, size)
            c = copy(acc.at[pl.ds(away, size)], buf.at[pl.ds(landing, size)], b)
            start = start + bit(b) * size
            yield
            c.wait()
            step = min(size, 64)

            def body(i, _, start=start, landing=landing, step=step):
                at = pl.ds(pl.multiple_of(start + i * step, step), step)
                got = buf[pl.ds(pl.multiple_of(landing + i * step, step), step)].astype(F32)
                acc[at] = (acc[at].astype(F32) + got).astype(BF)
                return 0

            lax.fori_loop(0, size // step, body, 0)
            landing += size
        start = base + start
        sum_ref[pl.ds(pl.multiple_of(start, size), size)] = acc[pl.ds(pl.multiple_of(start - base, size), size)]
        for b in reversed(order):
            have = sum_ref.at[pl.ds(pl.multiple_of(start, size), size)]
            c = copy(have, have, b)
            yield
            c.wait()
            start = start - bit(b) * size
            size *= 2
        have = sum_ref.at[pl.ds(pl.multiple_of(start, size), size)]
        forwards.append(copy(have, have, 0))

    def share(r, store):
        at = lax.rem(place + r, groups) * rows
        blk = min(256, rows)

        def body(i, _):
            g = pl.ds(pl.multiple_of(at + i * blk, blk), blk)
            value = dotg(right[0, g, :], weight[0], NT)
            value += dotg(right[1, g, :], weight[1], NT)
            value += dotg(right[2, g, :], weight[2], NT)
            store(pl.ds(pl.multiple_of(i * blk, blk), blk), value)
            return 0

        lax.fori_loop(0, rows // blk, body, 0)

    shares = []

    def share_away(r):
        def store(at, value):
            sent[r - 1, at, :] = value.astype(BF)

        share(r, store)
        c = pltpu.make_async_remote_copy(
            src_ref=sent.at[r - 1],
            dst_ref=came.at[r - 1],
            send_sem=x_send.at[r - 1],
            recv_sem=x_recv.at[r - 1],
            device_id={"tensor": lax.rem(place + r, groups)},
            device_id_type=MESH,
        )
        c.start()
        shares.append(c)

    def store_own(at, value):
        own_share[at, :] = value

    def weight_grad(side, some):
        cols = min(256, part)
        each = part // cols

        def body(i, _):
            first = pl.multiple_of(lax.rem(core + side, 2) * half + i * cols, cols)
            number = lax.div(first, depth)
            kind = lax.div(number, 3) * groups
            lanes = pl.ds(pl.multiple_of(lax.rem(first, depth), cols), cols)
            value = None
            for r in range(groups):
                at = pl.ds(pl.multiple_of(lax.rem(place + r, groups) * rows, rows), rows)
                term = dotg(left[kind + r, :, lanes], right[number, at, :], TN)
                value = term if value is None else value + term
            packed[pl.ds(first, cols), :] = value.astype(BF)
            return 0

        lax.fori_loop(some[0] * each, (some[-1] + 1) * each, body, 0)
        if side:
            for c in some:
                at = pl.ds(pl.multiple_of((1 - core) * half + c * part, part), part)
                cores[c] = copy(packed.at[at], core_buf.at[pl.ds(c * part, part)], 0)

    def last_norm():
        blk = min(64, rows)

        def body(i, _):
            at = pl.ds(pl.multiple_of(i * blk, blk), blk)
            value = own_share[at, :]
            for r in range(groups - 1):
                value += came[r, at, :].astype(F32)
            hat, scale = norm_parts(x[at, :].astype(F32))
            out_ref[at, :] = (g_resid[at, :] + norm_back(value, hat, scale, gain_ref[0:1])).astype(BF)
            total_ref[0:1] += column_sum(value * hat)
            total_ref[1:2] += column_sum(value)
            return 0

        lax.fori_loop(0, rows // blk, body, 0)

    def vectors():
        slot = 0
        for bits_of in steps:
            sends = []
            for mask in range(1, 1 << len(bits_of)):
                peer = {}
                for i, (axis, b) in enumerate(bits_of):
                    if mask >> i & 1:
                        peer[axis] = peer.get(axis, lax.axis_index(axis)) ^ (1 << b)
                sends.append(
                    pltpu.make_async_remote_copy(
                        src_ref=total_ref,
                        dst_ref=vec_buf.at[slot],
                        send_sem=vec_send.at[slot],
                        recv_sem=vec_recv.at[slot],
                        device_id=peer,
                        device_id_type=MESH,
                    )
                )
                sends[-1].start()
                slot += 1
            yield
            wait_all(sends)
            total = total_ref[...]
            for i in range(len(sends)):
                total += vec_buf[slot - len(sends) + i]
            total_ref[...] = total

    def turn(chains):
        still = []
        for chain in chains:
            try:
                next(chain)
                still.append(chain)
            except StopIteration:
                pass
        return still

    wait_all(second)
    for r in range(1, groups):
        share_away(r)
    wait_all(third)
    all_chunks = list(range(chunks))
    for some in (all_chunks[: chunks // 2], all_chunks[chunks // 2 :]):
        weight_grad(1, some)
    reduces = []
    for chunk in all_chunks:
        weight_grad(0, [chunk])
        reduces = turn(reduces + [reduce(chunk)])
    share(0, store_own)
    reduces = turn(reduces)
    wait_all(fourth)
    wait_all(shares)
    total_ref[...] = vec_ref[...]
    last_norm()
    chain = turn([vectors()])
    while reduces or chain:
        reduces, chain = turn(reduces), turn(chain)
    wait_all(forwards)


def tail(grads, mixed, weights, x, g_resid, gains, vectors, n1s, gas, bits, steps):
    (slots, width), (rows, depth), groups = mixed.shape, x.shape, len(n1s)
    half = 2 * depth
    landing = half - half // (1 << (bits - 1))
    count = half // min(512, depth) * (2 * bits + 1)
    vecs = sum((1 << len(b)) - 1 for b in steps)
    vmem = pl.BlockSpec(memory_space=pltpu.VMEM)
    anyspace = pl.BlockSpec(memory_space=pl.ANY)
    dma = pltpu.SemaphoreType.DMA
    peers = max(groups - 1, 1)
    return pl.pallas_call(
        functools.partial(tail_kernel, bits=bits, groups=groups, steps=steps),
        in_specs=[anyspace] * 9 + [vmem] * 2 + [anyspace] * (2 * groups),
        out_specs=[vmem, vmem, vmem],
        out_shape=[
            jax.ShapeDtypeStruct((4 * depth, width), BF),
            jax.ShapeDtypeStruct((rows, depth), BF),
            jax.ShapeDtypeStruct(vectors.shape, F32),
        ],
        scratch_shapes=[
            pltpu.VMEM((4, slots, width), BF),
            pltpu.VMEM((2 * groups, rows, depth), BF),
            pltpu.VMEM((3, depth, width), BF),
            pltpu.VMEM((rows, depth), BF),
            pltpu.VMEM((rows, depth), F32),
            pltpu.VMEM((4 * depth, width), BF),
            pltpu.VMEM((half, width), BF),
            pltpu.VMEM((half, width), BF),
            pltpu.VMEM((landing, width), BF),
            pltpu.VMEM((peers, rows, depth), BF),
            pltpu.VMEM((peers, rows, depth), BF),
            pltpu.VMEM((rows, depth), F32),
            pltpu.VMEM((vecs,) + vectors.shape, F32),
            dma((count,)),
            dma((count,)),
            dma((vecs,)),
            dma((vecs,)),
            dma((peers,)),
            dma((peers,)),
            dma((9 + 2 * groups,)),
        ],
        compiler_params=pltpu.CompilerParams(
            collective_id=1, has_side_effects=True, vmem_limit_bytes=60 * MIB
        ),
        cost_estimate=pl.CostEstimate(flops=rows * width, bytes_accessed=rows * width, transcendentals=0),
        name="tail",
    )(*grads, mixed, *weights, x, g_resid, gains, vectors, *n1s, *gas)


def mixed_back_kernel(at_ref, x_ref, w_ref, *refs):
    refs[-1][...] = dotg(x_ref[...], w_ref[...], NT).astype(BF)


def mixed_back(where, x, w_out, slots, held, blk=256):
    rows, depth = x.shape
    width = w_out.shape[0]
    blk = min(blk, rows)
    count = rows // blk
    return pl.pallas_call(
        mixed_back_kernel,
        grid_spec=pltpu.PrefetchScalarGridSpec(
            num_scalar_prefetch=1,
            grid=(count,),
            in_specs=[
                pl.BlockSpec((blk, depth), lambda i, at: (i, 0)),
                pl.BlockSpec((width, depth), lambda i, at: (0, 0)),
            ]
            + [pl.BlockSpec(memory_space=pl.ANY)] * len(held),
            out_specs=pl.BlockSpec((blk, width), lambda i, at: (at[0] * count + i, 0)),
        ),
        out_shape=jax.ShapeDtypeStruct((slots, width), BF),
        input_output_aliases={3: 0} if held else {},
        compiler_params=pltpu.CompilerParams(vmem_limit_bytes=60 * MIB),
        cost_estimate=pl.CostEstimate(flops=rows * depth, bytes_accessed=rows * depth, transcendentals=0),
        name="mixed_back",
    )(where, x, w_out, *held)


def shift(x, axis, count, step):
    return lax.ppermute(x, axis, [((i + step) % count, i) for i in range(count)])


def shards(
    tokens,
    lengths,
    cotangent,
    w_query,
    w_key,
    w_value,
    w_out,
    up_weight,
    bias_up,
    down_weight,
    bias_down,
    norm_gains,
    norm_shifts,
):
    rows, _, depth = tokens.shape
    groups, replicas = lax.axis_size("tensor"), lax.axis_size("dp")
    me, replica = lax.axis_index("tensor"), lax.axis_index("dp")
    slots = rows * groups
    width = w_query.shape[1]
    hidden = up_weight.shape[1]
    x = tokens.reshape(rows, depth)
    here = me.reshape(1).astype(jnp.int32)
    place = lambda r: (here + r) % groups

    def others(v):
        return [shift(v, "tensor", groups, r) for r in range(1, groups)]

    def to_owner(v, r):
        return shift(v, "tensor", groups, groups - r)

    up_piece = lax.dynamic_slice_in_dim(up_weight, replica * (depth // replicas), depth // replicas, 0)
    down_piece = lax.dynamic_slice_in_dim(
        down_weight, replica * (hidden // replicas), hidden // replicas, 0
    )
    gather = lambda v: lax.all_gather(v, "dp", axis=0, tiled=True)

    freqs = 10000.0 ** (-jnp.arange(HD // 2).astype(F32) * 2.0 / HD)
    angles = jnp.arange(slots).astype(F32)[:, None] * freqs[None, :]
    cosine, sine = jnp.cos(angles), jnp.sin(angles)
    cosine = jnp.concatenate([cosine] * 4, axis=1)
    sine = jnp.concatenate([-sine, sine] * 2, axis=1)
    x_rest = others(x)
    normed_one = first_norm(x, norm_gains, norm_shifts)
    weights = (w_query, w_key, w_value)
    up_pieces, down_pieces, bias_rest = others(up_piece), others(down_piece), others(bias_up)
    joint = project(here, normed_one, *weights, cosine, sine)
    joint, x_rest, up_pieces, down_pieces, bias_rest = lax.optimization_barrier(
        (joint, x_rest, up_pieces, down_pieces, bias_rest)
    )
    normed_one_rest = [first_norm(v, norm_gains, norm_shifts) for v in x_rest]
    for r, n in enumerate(normed_one_rest):
        joint = project(place(r + 1), n, *weights, cosine, sine, joint)
    blk = min(512, rows)
    each = rows // blk
    odd = lambda r: lax.rem(place(r), 2)
    ranks = lambda r, k: jnp.where(odd(r) == 1, each - 1 - k, k)
    held, shares, arrived = (), [], [[] for _ in range(1, groups)]
    for k in range(each):
        for r in range(1, groups):
            *held, share = attend(place(r) * each + ranks(0, k), lengths, joint, w_out, held, BF, blk)
            arrived[r - 1].append(to_owner(share, r))
        if k == each - 1 and k > 0:
            joint, arrived = lax.optimization_barrier((joint, [v[:k] for v in arrived])), arrived
            joint, early = joint
            arrived = [list(e) + v[k:] for e, v in zip(early, arrived)]
        *held, share = attend(here * each + ranks(0, k), lengths, joint, w_out, held, F32, blk)
        shares.append(share)
    mixed, lse = held
    shares = [shares] + arrived
    picks = jnp.concatenate([ranks(groups - r, k) for r in range(groups) for k in range(each)])
    up_rest, down_rest = [gather(p) for p in up_pieces], [gather(p) for p in down_pieces]
    biases = jnp.concatenate([bias_up] + bias_rest).astype(F32)

    info = jnp.stack([lengths[0], me * rows]).astype(jnp.int32)
    cot = cotangent.reshape(rows, depth)
    attn_sum, resid, normed_two = join(x, norm_gains, norm_shifts, shares, picks)
    normed_two, up_rest, down_rest = lax.optimization_barrier((normed_two, up_rest, down_rest))
    normed_two_rest = others(normed_two)
    ups, downs = [up_weight] + up_rest, [down_weight] + down_rest
    slope, act, layer_out, g_branch, sums3 = feed(
        info, normed_two, biases, ups, downs, resid, cot, bias_down.reshape(1, depth), norm_gains, norm_shifts
    )
    g_branch_rest = others(g_branch)
    g_pre, g_resid, g_attn, sums21 = feed_back(
        info, g_branch, slope, ups, downs, resid, attn_sum, cot, norm_gains
    )
    g_attn_rest = others(g_attn)
    g_pre, normed_two_rest = lax.optimization_barrier((g_pre, normed_two_rest))
    g_mixed = mixed_back(here, g_attn, w_out, slots, [])
    g_pre, g_mixed = lax.optimization_barrier((g_pre, g_mixed))
    grad_feed, bias_up_sum = feed_grad(
        up_weight, down_weight, biases[:hidden], act, g_pre,
        [normed_two] + normed_two_rest, [g_branch] + g_branch_rest,
    )
    grad_feed = grad_feed.reshape(2 * hidden, depth)
    g_mixed, g_attn_rest, grad_feed = lax.optimization_barrier((g_mixed, g_attn_rest, grad_feed))
    grad_feed = lax.psum(grad_feed, "dp")
    for r, g in enumerate(g_attn_rest):
        g_mixed = mixed_back(place(r + 1), g, w_out, slots, [g_mixed])

    grads = attend_back(lengths, joint, mixed, g_mixed, lse, cosine, sine, width)
    placed = lax.dynamic_update_slice(
        jnp.zeros((groups * hidden,), F32), bias_up_sum.reshape(-1), (me * hidden,)
    ).reshape(-1, depth)
    bits = (replicas - 1).bit_length()
    steps = [("tensor", b) for b in range((groups - 1).bit_length())] + [("dp", b) for b in range(bits)]
    steps = [tuple(steps[i : i + 2]) for i in range(0, len(steps), 2)]
    vectors = jnp.concatenate([jnp.zeros((2, depth), F32), sums3[:3], sums21[:4], placed])
    vectors = jnp.pad(vectors, ((0, -len(vectors) % 8), (0, 0)))
    packed, grad_tokens, sums = tail(
        grads, mixed, weights, x, g_resid, norm_gains, vectors,
        [normed_one] + normed_one_rest, [g_attn] + g_attn_rest, bits, steps,
    )
    grad_up, grad_down = widen(grad_feed)
    grad_query, grad_key, grad_value = (packed[i * depth : (i + 1) * depth].astype(F32) for i in range(3))
    grad_out = jnp.transpose(packed[3 * depth :]).astype(F32)
    grad_gains = jnp.stack([sums[0], sums[7], sums[5], sums[2]])
    grad_shifts = jnp.stack([sums[1], sums[8], sums[6], sums[3]])
    grad_bias_up = lax.dynamic_slice_in_dim(sums[9 : 9 + groups * hidden // depth].reshape(-1), me * hidden, hidden, 0)
    whole = (rows, 1, depth)
    return (
        layer_out.reshape(whole),
        grad_tokens.reshape(whole),
        grad_query,
        grad_key,
        grad_value,
        grad_out,
        grad_up,
        grad_bias_up,
        grad_down,
        sums[4],
        grad_gains,
        grad_shifts,
    )


def solution(mesh):
    wide, tall = P(None, "tensor"), P("tensor", None)
    acts = P("tensor", "dp", None)
    return jax.shard_map(
        shards,
        mesh=mesh,
        in_specs=(acts, P("dp"), acts, wide, wide, wide, tall, wide, P("tensor"), tall, P(), P(), P()),
        out_specs=(acts, acts, wide, wide, wide, tall, wide, P("tensor"), tall, P(), P(), P()),
        check_vma=False,
    )
```

```python
import functools
import jax
import jax.numpy as jnp
from jax import lax
from jax.experimental import pallas as pl
from jax.experimental.pallas import tpu as pltpu
from jax.sharding import PartitionSpec as P

HD = 64
EPSILON = 1e-05
BF = jnp.bfloat16
F32 = jnp.float32
NT = (((1,), (1,)), ((), ()))
NN = (((1,), (0,)), ((), ()))
TN = (((0,), (0,)), ((), ()))
MIB = 1 << 20


def dotg(a, b, dims=NN):
    return lax.dot_general(a, b, dims, preferred_element_type=F32)


def rotate(x, cos, sin):
    first = lax.broadcasted_iota(jnp.int32, (x.shape[0], 128), 1) % HD < HD // 2
    parts = []
    for a in range(0, x.shape[1], 128):
        v = x[:, a : a + 128]
        swapped = jnp.where(first, pltpu.roll(v, 96, 1), pltpu.roll(v, 32, 1))
        parts.append(v * cos + swapped * sin)
    return jnp.concatenate(parts, axis=1) if len(parts) > 1 else parts[0]


def qkv_kernel(x_ref, wq_ref, wk_ref, wv_ref, cos_ref, sin_ref, o_ref):
    width = wq_ref.shape[1]
    x, cos, sin = x_ref[...], cos_ref[...], sin_ref[...]
    o_ref[:, :width] = rotate(dotg(x, wq_ref[...]), cos, sin).astype(BF)
    o_ref[:, width : 2 * width] = rotate(dotg(x, wk_ref[...]), cos, sin).astype(BF)
    o_ref[:, 2 * width :] = dotg(x, wv_ref[...]).astype(BF)


def project(where, x, w_query, w_key, w_value, cos, sin, joint=None, blk=256):
    rows, depth = x.shape
    width, slots = w_query.shape[1], cos.shape[0]
    blk = min(blk, rows)
    count = rows // blk
    weight = pl.BlockSpec((depth, width), lambda i, at: (0, 0))
    angle = pl.BlockSpec((blk, 128), lambda i, at: (at[0] * count + i, 0))
    kernel = lambda at, *refs: qkv_kernel(*refs[:6], refs[-1])
    held = [] if joint is None else [joint]
    return pl.pallas_call(
        kernel,
        grid_spec=pltpu.PrefetchScalarGridSpec(
            num_scalar_prefetch=1,
            grid=(count,),
            in_specs=[pl.BlockSpec((blk, depth), lambda i, at: (i, 0)), weight, weight, weight, angle, angle]
            + [pl.BlockSpec(memory_space=pl.ANY)] * len(held),
            out_specs=pl.BlockSpec((blk, 3 * width), lambda i, at: (at[0] * count + i, 0)),
        ),
        out_shape=jax.ShapeDtypeStruct((slots, 3 * width), BF),
        input_output_aliases={7: 0} if held else {},
        compiler_params=pltpu.CompilerParams(vmem_limit_bytes=60 * MIB),
        cost_estimate=pl.CostEstimate(flops=rows * depth, bytes_accessed=rows * depth, transcendentals=0),
        name="project",
    )(where, x, w_query, w_key, w_value, cos, sin, *held)


def attend_kernel(at_ref, len_ref, q_ref, k_ref, v_ref, w_ref, *refs, blk):
    o_ref, lse_ref, share_ref, vt, low_ref = refs[-5:]
    pair = pl.program_id(0)
    i = at_ref[0]
    length = len_ref[0]
    def turn(j, _):
        part = pl.ds(pl.multiple_of(j * blk, blk), blk)
        vt[:, part] = jnp.transpose(v_ref[part, :])
        return 0

    lax.fori_loop(0, i + 1, turn, 0)
    lane = lax.broadcasted_iota(jnp.int32, (blk, 128), 1)
    q = q_ref[...] * jnp.asarray(0.125, BF)
    zero = jnp.zeros_like(q)
    qs = (jnp.where(lane < HD, q, zero), jnp.where(lane < HD, zero, q))

    def step(j, carry, diag):
        start = pl.multiple_of(j * blk, blk)
        kb = k_ref[pl.ds(start, blk), :]
        sub = min(256, blk)
        n = blk // sub
        if diag:
            key = lax.broadcasted_iota(jnp.int32, (sub, blk), 0)
            qry = lax.broadcasted_iota(jnp.int32, (sub, blk), 1)
        state = [carry[h] for h in range(2)]
        chains = [(h, t) for t in range(n) for h in range(2)]
        live = {}

        def first(c):
            h, t = chains[c]
            live[c] = dotg(kb[t * sub : t * sub + sub], qs[h], NT)

        def middle(c):
            h, t = chains[c]
            s = live[c]
            if diag:
                s = jnp.where((key + t * sub <= qry) & (key + t * sub + start < length), s, -1e30)
            m, l, acc = state[h]
            mn = jnp.maximum(m, jnp.max(s, axis=0, keepdims=True))
            p = jnp.exp(s - mn)
            al = jnp.exp(m - mn)
            state[h] = (mn, l * al + jnp.sum(p, axis=0, keepdims=True), acc)
            live[c] = (p.astype(BF), al)

        def last(c):
            h, t = chains[c]
            p, al = live.pop(c)
            m, l, acc = state[h]
            state[h] = (m, l, acc * al + dotg(vt[HD * h : HD * h + HD, pl.ds(start + t * sub, sub)], p))

        stages = (first, middle, last)
        for i in range(len(chains) + 4):
            for k in range(3):
                c = i - 2 * k
                if 0 <= c < len(chains):
                    stages[k](c)
        return tuple(state)

    init = tuple(
        (jnp.full((1, blk), -1e30, F32), jnp.zeros((1, blk), F32), jnp.zeros((HD, blk), F32))
        for _ in range(2)
    )
    c = lax.fori_loop(0, i, lambda j, c: step(j, c, False), init)
    c = step(i, c, True)
    ot = jnp.concatenate([c[h][2] / c[h][1] for h in range(2)], axis=0)
    low = jnp.transpose(ot).astype(BF)
    o_ref[...] = low
    lse_ref[0] = jnp.concatenate([c[h][0] + jnp.log(c[h][1]) for h in range(2)], axis=0)
    low_ref[pair] = low

    @pl.when(pair == pl.num_programs(0) - 1)
    def _():
        pairs = low_ref.shape[0]
        low = jnp.concatenate([low_ref[p] for p in range(pairs)], axis=1)
        share_ref[...] = dotg(low, w_ref[...]).astype(share_ref.dtype)


def attend(at, length, joint, w_out, held, kind, blk):
    rows, width, depth = joint.shape[0], w_out.shape[0], w_out.shape[1]
    pairs = width // 128
    return pl.pallas_call(
        functools.partial(attend_kernel, blk=blk),
        grid_spec=pltpu.PrefetchScalarGridSpec(
            num_scalar_prefetch=2,
            grid=(pairs,),
            in_specs=[
                pl.BlockSpec((blk, 128), lambda p, at, *_: (at[0], p)),
                pl.BlockSpec((rows, 128), lambda p, *_: (0, pairs + p)),
                pl.BlockSpec((rows, 128), lambda p, *_: (0, 2 * pairs + p)),
                pl.BlockSpec((width, depth), lambda p, *_: (0, 0), pipeline_mode=pl.Buffered(1)),
            ]
            + [pl.BlockSpec(memory_space=pl.ANY)] * len(held),
            out_specs=[
                pl.BlockSpec((blk, 128), lambda p, at, *_: (at[0], p)),
                pl.BlockSpec((1, 2, blk), lambda p, at, *_: (p, 0, at[0])),
                pl.BlockSpec((blk, depth), lambda p, *_: (0, 0)),
            ],
            scratch_shapes=[pltpu.VMEM((128, rows), BF), pltpu.VMEM((pairs, blk, 128), BF)],
        ),
        out_shape=[
            jax.ShapeDtypeStruct((rows, width), BF),
            jax.ShapeDtypeStruct((pairs, 2, rows), F32),
            jax.ShapeDtypeStruct((blk, depth), kind),
        ],
        input_output_aliases={6: 0, 7: 1} if held else {},
        compiler_params=pltpu.CompilerParams(vmem_limit_bytes=60 * MIB),
        cost_estimate=pl.CostEstimate(flops=rows * width, bytes_accessed=rows * width, transcendentals=0),
        name="attend",
    )(at, length, joint, joint, joint, w_out, *held)


def attend_back_kernel(
    len_ref, q_ref, k_ref, v_ref, o_ref, do_ref, lse_ref, cos_ref, sin_ref,
    dq_ref, dk_ref, dv_ref, kt, dlt, dqt, *, blk, blocks,
):
    j = pl.program_id(1)
    length = len_ref[0]

    @pl.when(j == 0)
    def _():
        kt[...] = jnp.transpose(k_ref[...])
        dqt[...] = jnp.zeros_like(dqt)

        def body(i, _):
            at = pl.ds(pl.multiple_of(i * blk, blk), blk)
            both = jnp.transpose(do_ref[at, :].astype(F32) * o_ref[at, :].astype(F32))
            for h in range(2):
                dlt[h : h + 1, at] = jnp.sum(both[HD * h : HD * h + HD], axis=0, keepdims=True)
            return 0

        lax.fori_loop(0, blocks, body, 0)

    js = pl.multiple_of(j * blk, blk)
    lane = lax.broadcasted_iota(jnp.int32, (blk, 128), 1)
    kb = k_ref[pl.ds(js, blk), :] * jnp.asarray(0.125, BF)
    vb = v_ref[pl.ds(js, blk), :]
    zero = jnp.zeros_like(kb)
    ks = (jnp.where(lane < HD, kb, zero), jnp.where(lane < HD, zero, kb))
    vs = (jnp.where(lane < HD, vb, zero), jnp.where(lane < HD, zero, vb))

    def step(i, carry, diag):
        at = pl.ds(pl.multiple_of(i * blk, blk), blk)
        qb, dob = q_ref[at, :], do_ref[at, :]
        out = []
        for h in range(2):
            dk, dv = carry[h]
            s = dotg(ks[h], qb, NT)
            if diag:
                key = lax.broadcasted_iota(jnp.int32, (blk, blk), 0)
                qry = lax.broadcasted_iota(jnp.int32, (blk, blk), 1)
                s = jnp.where((key <= qry) & (key + js < length), s, -1e30)
            p = jnp.exp(s - lse_ref[0, h : h + 1, at])
            dp = dotg(vs[h], dob, NT)
            ds = (p * (dp - dlt[h : h + 1, at])).astype(BF)
            dv = dv + dotg(p.astype(BF), dob)
            dk = dk + dotg(ds, qb)
            dqt[HD * h : HD * h + HD, at] += dotg(kt[HD * h : HD * h + HD, pl.ds(js, blk)], ds)
            out.append((dk, dv))
        return tuple(out)

    z = jnp.zeros((blk, 128), F32)
    c = step(j, ((z, z), (z, z)), True)
    c = lax.fori_loop(j + 1, blocks, lambda i, c: step(i, c, False), c)
    grad = jnp.where(lane < HD, c[0][0], c[1][0]) * 0.125
    dk_ref[...] = rotate(grad, cos_ref[pl.ds(js, blk), :], -sin_ref[pl.ds(js, blk), :]).astype(BF)
    dv_ref[...] = jnp.where(lane < HD, c[0][1], c[1][1]).astype(BF)

    @pl.when(j == blocks - 1)
    def _():
        def body(i, _):
            at = pl.ds(pl.multiple_of(i * blk, blk), blk)
            grad = jnp.transpose(dqt[:, at]) * 0.125
            dq_ref[at, :] = rotate(grad, cos_ref[at, :], -sin_ref[at, :]).astype(BF)
            return 0

        lax.fori_loop(0, blocks, body, 0)


def attend_back(length, joint, mixed, dmixed, lse, cos, sin, width, blk=512):
    rows = joint.shape[0]
    pairs, blocks = width // 128, rows // blk
    full = lambda off: pl.BlockSpec((rows, 128), lambda p, j, *_: (0, off * pairs + p))
    angle = pl.BlockSpec((rows, 128), lambda p, j, *_: (0, 0))
    block = pl.BlockSpec((blk, 128), lambda p, j, *_: (j, p))
    return pl.pallas_call(
        functools.partial(attend_back_kernel, blk=blk, blocks=blocks),
        grid_spec=pltpu.PrefetchScalarGridSpec(
            num_scalar_prefetch=1,
            grid=(pairs, blocks),
            in_specs=[full(0), full(1), full(2), full(0), full(0)]
            + [pl.BlockSpec((1, 2, rows), lambda p, j, *_: (p, 0, 0)), angle, angle],
            out_specs=[full(0), block, block],
            scratch_shapes=[
                pltpu.VMEM((128, rows), BF),
                pltpu.VMEM((2, rows), F32),
                pltpu.VMEM((128, rows), F32),
            ],
        ),
        out_shape=[jax.ShapeDtypeStruct((rows, width), BF)] * 3,
        compiler_params=pltpu.CompilerParams(vmem_limit_bytes=60 * MIB),
        cost_estimate=pl.CostEstimate(
            flops=rows * width, bytes_accessed=rows * width, transcendentals=0
        ),
        name="attend_back",
    )(length, joint, joint, joint, mixed, dmixed, lse, cos, sin)


def gelu_parts(v):
    c = 0.7978845608028654
    return c, jnp.tanh(c * (v + 0.044715 * v * v * v))


def gelu_both(v):
    c, t = gelu_parts(v)
    half = 0.5 * (1.0 + t)
    return v * half, half + 0.5 * v * (1.0 - t * t) * c * (1.0 + 3 * 0.044715 * v * v)


def norm_parts(values):
    average = jnp.mean(values, axis=-1, keepdims=True)
    centred = values - average
    scale = lax.rsqrt(jnp.mean(centred * centred, axis=-1, keepdims=True) + EPSILON)
    return centred * scale, scale


def norm_back(grad, hat, scale, gain):
    g = grad * gain
    return scale * (
        g - jnp.mean(g, axis=-1, keepdims=True) - hat * jnp.mean(g * hat, axis=-1, keepdims=True)
    )


def column_sum(v):
    return jnp.sum(v, axis=0, keepdims=True)


def valid_rows(info_ref, start, count):
    at = info_ref[1] + start + lax.broadcasted_iota(jnp.int32, (count, 1), 0)
    return (at < info_ref[0]).astype(F32)


def loop_rows(rows, blk, body):
    def step(i, _):
        body(pl.multiple_of(i * blk, blk))
        return 0

    lax.fori_loop(0, rows // blk, step, 0)


def feed_kernel(info_ref, *refs, groups, chunks, sub, own):
    x_ref, bias_ref = refs[:2]
    ups, downs, refs = refs[2 : 2 + groups], refs[2 + groups : 2 + 2 * groups], refs[2 + 2 * groups :]
    step = pl.program_id(0)
    rows = x_ref.shape[0]
    if own:
        bd_ref, slope_ref, act_ref, acc = refs
        late = []
    else:
        resid_hbm, cot_hbm, before_hbm, gain_ref, shift_ref = refs[:5]
        slope_ref, out_ref, gb_ref, sums_ref, acc, resid_ref, cot_ref, sems = refs[5:]
        late = [
            pltpu.make_async_copy(resid_hbm, resid_ref, sems.at[0]),
            pltpu.make_async_copy(cot_hbm, cot_ref, sems.at[1]),
        ]

    @pl.when(step == 0)
    def _():
        if own:
            acc[...] = jnp.zeros_like(acc) + bd_ref[...].astype(F32)
        else:
            before = pltpu.make_async_copy(before_hbm, acc, sems.at[2])
            before.start()
            before.wait()
        for c in late:
            c.start()

    for g in range(groups):

        @pl.when(step // chunks == g)
        def _():
            for r in range(0, rows, sub):
                act, slope = gelu_both(dotg(x_ref[r : r + sub], ups[g][...]) + bias_ref[0])
                slope_ref[r : r + sub] = slope.astype(BF)
                act = act.astype(BF)
                if own:
                    act_ref[r : r + sub] = act
                acc[r : r + sub] += dotg(act, downs[g][...])

    if own:
        return

    @pl.when(step == groups * chunks - 1)
    def _():
        for c in late:
            c.wait()
        sums_ref[...] = jnp.zeros_like(sums_ref)
        gain, shift = gain_ref[3:4], shift_ref[3:4]
        blk = min(256, rows)

        def body(r):
            at = pl.ds(r, blk)
            valid = valid_rows(info_ref, r, blk)
            hat, scale = norm_parts(acc[at])
            out_ref[at] = (valid * (resid_ref[at] + hat * gain + shift)).astype(BF)
            g_out = valid * cot_ref[at].astype(F32)
            low = norm_back(g_out, hat, scale, gain).astype(BF)
            gb_ref[at] = low
            sums_ref[0:1] += column_sum(g_out * hat)
            sums_ref[1:2] += column_sum(g_out)
            sums_ref[2:3] += column_sum(low.astype(F32))

        loop_rows(rows, blk, body)


def feed(info, x, biases, ups, downs, own=None, rest=None, cols=512):
    rows, depth = x.shape
    groups, hidden = len(ups), ups[0].shape[1]
    chunks = hidden // cols
    once = lambda shape: pl.BlockSpec(shape, lambda s, *_: (0, 0), pipeline_mode=pl.Buffered(1))
    anyspace = pl.BlockSpec(memory_space=pl.ANY)
    part = lambda g: (lambda s, *_: (0, jnp.clip(s - g * chunks, 0, chunks - 1)))
    part_t = lambda g: (lambda s, *_: (jnp.clip(s - g * chunks, 0, chunks - 1), 0))
    wide = pl.BlockSpec((rows, cols), lambda s, *_: (0, s))
    low = jax.ShapeDtypeStruct((rows, depth), BF)
    slope = jax.ShapeDtypeStruct((rows, groups * hidden), BF)
    if rest is None:
        more, args = [once((1, depth))], [own]
        out_specs = [wide, wide, once((rows, depth))]
        out_shape = [slope, slope, jax.ShapeDtypeStruct((rows, depth), F32)]
        scratch = []
    else:
        before, resid, cot, gains, shifts = rest
        more, args = [anyspace] * 3 + [once(gains.shape)] * 2, [resid, cot, before, gains, shifts]
        out_specs = [wide, once((rows, depth)), once((rows, depth)), once((8, depth))]
        out_shape = [slope, low, low, jax.ShapeDtypeStruct((8, depth), F32)]
        scratch = [
            pltpu.VMEM((rows, depth), F32),
            pltpu.VMEM((rows, depth), F32),
            pltpu.VMEM((rows, depth), BF),
            pltpu.SemaphoreType.DMA((3,)),
        ]
    return pl.pallas_call(
        functools.partial(feed_kernel, groups=groups, chunks=chunks, sub=min(512, rows), own=rest is None),
        grid_spec=pltpu.PrefetchScalarGridSpec(
            num_scalar_prefetch=1,
            grid=(groups * chunks,),
            in_specs=[once((rows, depth)), pl.BlockSpec((1, 1, cols), lambda s, *_: (s, 0, 0))]
            + [pl.BlockSpec((depth, cols), part(g)) for g in range(groups)]
            + [pl.BlockSpec((cols, depth), part_t(g)) for g in range(groups)]
            + more,
            out_specs=out_specs,
            scratch_shapes=scratch,
        ),
        out_shape=out_shape,
        compiler_params=pltpu.CompilerParams(vmem_limit_bytes=60 * MIB),
        cost_estimate=pl.CostEstimate(flops=rows * depth, bytes_accessed=rows * depth, transcendentals=0),
        name="feed",
    )(info, x, biases.reshape(-1, 1, cols), *ups, *downs, *args)


def feed_back_kernel(info_ref, *refs, groups, chunks, sub):
    gb_ref, own_slope, rest_slope, resid_hbm, attn_hbm, cot_hbm, gain_ref = refs[:7]
    ups, downs = refs[7 : 7 + groups], refs[7 + groups : 7 + 2 * groups]
    gp_ref, gr_ref, ga_ref, sums_ref, acc, resid_ref, attn_ref, cot_ref, sems = refs[7 + 2 * groups :]
    step = pl.program_id(0)
    rows = gb_ref.shape[0]
    late = [
        pltpu.make_async_copy(src, dst, sems.at[i])
        for i, (src, dst) in enumerate(((resid_hbm, resid_ref), (attn_hbm, attn_ref), (cot_hbm, cot_ref)))
    ]

    @pl.when(step == 0)
    def _():
        for c in late:
            c.start()
        acc[...] = jnp.zeros_like(acc)

    for g in range(groups):

        @pl.when(step // chunks == g)
        def _():
            for r in range(0, rows, sub):
                grad = dotg(gb_ref[r : r + sub], downs[g][...], NT)
                slope_ref = rest_slope if g else own_slope
                low = (grad * slope_ref[r : r + sub].astype(F32)).astype(BF)
                if g == 0:
                    gp_ref[r : r + sub] = low
                acc[r : r + sub] += dotg(low, ups[g][...], NT)

    @pl.when(step == groups * chunks - 1)
    def _():
        for c in late:
            c.wait()
        sums_ref[...] = jnp.zeros_like(sums_ref)
        blk = min(256, rows)

        def body(r):
            at = pl.ds(r, blk)
            g_out = valid_rows(info_ref, r, blk) * cot_ref[at].astype(F32)
            hat, scale = norm_parts(resid_ref[at])
            g_two = acc[at]
            g_resid = g_out + norm_back(g_two, hat, scale, gain_ref[2:3])
            gr_ref[at] = g_resid
            sums_ref[0:1] += column_sum(g_two * hat)
            sums_ref[1:2] += column_sum(g_two)
            hat, scale = norm_parts(attn_ref[at])
            ga_ref[at] = norm_back(g_resid, hat, scale, gain_ref[1:2]).astype(BF)
            sums_ref[2:3] += column_sum(g_resid * hat)
            sums_ref[3:4] += column_sum(g_resid)

        loop_rows(rows, blk, body)


def feed_back(info, gb, own_slope, rest_slope, ups, downs, resid, attn_sum, cot, gains, cols=512):
    rows, depth = gb.shape
    groups, hidden = len(ups), ups[0].shape[1]
    chunks = hidden // cols
    once = lambda shape: pl.BlockSpec(shape, lambda s, *_: (0, 0), pipeline_mode=pl.Buffered(1))
    anyspace = pl.BlockSpec(memory_space=pl.ANY)
    own = lambda g: (lambda s, *_: (0, jnp.clip(s - g * chunks, 0, chunks - 1)))
    own_t = lambda g: (lambda s, *_: (jnp.clip(s - g * chunks, 0, chunks - 1), 0))
    return pl.pallas_call(
        functools.partial(feed_back_kernel, groups=groups, chunks=chunks, sub=min(512, rows)),
        grid_spec=pltpu.PrefetchScalarGridSpec(
            num_scalar_prefetch=1,
            grid=(groups * chunks,),
            in_specs=[
                once((rows, depth)),
                pl.BlockSpec((rows, cols), own(0)),
                pl.BlockSpec((rows, cols), lambda s, *_: (0, jnp.maximum(s - chunks, 0))),
                anyspace,
                anyspace,
                anyspace,
                once(gains.shape),
            ]
            + [pl.BlockSpec((depth, cols), own(g)) for g in range(groups)]
            + [pl.BlockSpec((cols, depth), own_t(g)) for g in range(groups)],
            out_specs=[
                pl.BlockSpec((rows, cols), own(0)),
                once((rows, depth)),
                once((rows, depth)),
                once((8, depth)),
            ],
            scratch_shapes=[
                pltpu.VMEM((rows, depth), F32),
                pltpu.VMEM((rows, depth), F32),
                pltpu.VMEM((rows, depth), F32),
                pltpu.VMEM((rows, depth), BF),
                pltpu.SemaphoreType.DMA((3,)),
            ],
        ),
        out_shape=[
            jax.ShapeDtypeStruct((rows, hidden), BF),
            jax.ShapeDtypeStruct((rows, depth), F32),
            jax.ShapeDtypeStruct((rows, depth), BF),
            jax.ShapeDtypeStruct((8, depth), F32),
        ],
        compiler_params=pltpu.CompilerParams(vmem_limit_bytes=60 * MIB),
        cost_estimate=pl.CostEstimate(flops=rows * depth, bytes_accessed=rows * depth, transcendentals=0),
        name="feed_back",
    )(info, gb, own_slope, rest_slope, resid, attn_sum, cot, gains, *ups, *downs)


def feed_grad_kernel(*refs, groups):
    up_ref, down_ref, bias_ref, act_ref, gp_ref = refs[:5]
    n2s, gbs = refs[5 : 5 + groups], refs[5 + groups : 5 + 2 * groups]
    grad_ref, sum_ref = refs[5 + 2 * groups :]
    act, gp = act_ref[...], gp_ref[...]
    dup = dotg(gp, n2s[0][...], TN)
    ddown = dotg(act, gbs[0][...], TN)
    sums = column_sum(gp.astype(F32))
    for g in range(1, groups):
        pre = dotg(n2s[g][...], up_ref[...]) + bias_ref[0]
        act, slope = gelu_both(pre)
        act = act.astype(BF)
        gp = (dotg(gbs[g][...], down_ref[...], NT) * slope).astype(BF)
        dup += dotg(gp, n2s[g][...], TN)
        ddown += dotg(act, gbs[g][...], TN)
        sums += column_sum(gp.astype(F32))
    grad_ref[0] = dup.astype(BF)
    grad_ref[1] = ddown.astype(BF)
    sum_ref[0] = sums


def feed_grad(up, down, bias, act, gp, n2s, gbs, cols=512):
    rows, depth = n2s[0].shape
    groups, hidden = len(n2s), up.shape[1]
    once = lambda shape: pl.BlockSpec(shape, lambda s: (0, 0), pipeline_mode=pl.Buffered(1))
    wide = lambda count: pl.BlockSpec((count, cols), lambda s: (0, s))
    tall = pl.BlockSpec((cols, depth), lambda s: (s, 0))
    flat = pl.BlockSpec((1, 1, cols), lambda s: (s, 0, 0))
    return pl.pallas_call(
        functools.partial(feed_grad_kernel, groups=groups),
        grid=(hidden // cols,),
        in_specs=[wide(depth), tall, flat, wide(rows), wide(rows)] + [once((rows, depth))] * (2 * groups),
        out_specs=[pl.BlockSpec((2, cols, depth), lambda s: (0, s, 0)), flat],
        out_shape=[
            jax.ShapeDtypeStruct((2, hidden, depth), BF),
            jax.ShapeDtypeStruct((hidden // cols, 1, cols), F32),
        ],
        compiler_params=pltpu.CompilerParams(vmem_limit_bytes=60 * MIB),
        cost_estimate=pl.CostEstimate(
            flops=(8 * groups - 4) * rows * depth * hidden, bytes_accessed=20 * rows * depth, transcendentals=0
        ),
        name="feed_grad",
    )(up, down, bias.reshape(-1, 1, cols), act, gp, *n2s, *gbs)


def norm_kernel(x_ref, gain_ref, shift_ref, o_ref):
    hat, _ = norm_parts(x_ref[...].astype(F32))
    o_ref[...] = (hat * gain_ref[0:1] + shift_ref[0:1]).astype(BF)


def first_norm(x, gains, shifts, blk=512):
    rows, depth = x.shape
    blk = min(blk, rows)
    whole = pl.BlockSpec(gains.shape, lambda i: (0, 0))
    block = pl.BlockSpec((blk, depth), lambda i: (i, 0))
    return pl.pallas_call(
        norm_kernel,
        grid=(rows // blk,),
        in_specs=[block, whole, whole],
        out_specs=block,
        out_shape=jax.ShapeDtypeStruct((rows, depth), BF),
        compiler_params=pltpu.CompilerParams(vmem_limit_bytes=60 * MIB),
        name="first_norm",
    )(x, gains, shifts)


def join_kernel(pick_ref, x_ref, gain_ref, shift_ref, *refs, blocks, each):
    parts, (attn_ref, resid_ref, low_ref) = refs[:-3], refs[-3:]
    block = pl.program_id(0) // each
    total = None
    for g in range(len(parts) // blocks):
        wanted = pick_ref[g * blocks + block]
        part = parts[g * blocks][...]
        for b in range(1, blocks):
            part = jnp.where(wanted == b, parts[g * blocks + b][...], part)
        total = part if total is None else total + part.astype(F32)
    attn_ref[...] = total
    hat, _ = norm_parts(total)
    resid = x_ref[...].astype(F32) + hat * gain_ref[1:2] + shift_ref[1:2]
    resid_ref[...] = resid
    hat, _ = norm_parts(resid)
    low_ref[...] = (hat * gain_ref[2:3] + shift_ref[2:3]).astype(BF)


def join(x, gains, shifts, shares, picks, blk=256):
    rows, depth = x.shape
    blocks = len(shares[0])
    blk = min(blk, rows // blocks)
    each = rows // blocks // blk
    whole = pl.BlockSpec(gains.shape, lambda i, *_: (0, 0))
    block = pl.BlockSpec((blk, depth), lambda i, *_: (i, 0))
    part = pl.BlockSpec((blk, depth), lambda i, *_: (lax.rem(i, each), 0))
    return pl.pallas_call(
        functools.partial(join_kernel, blocks=blocks, each=each),
        grid_spec=pltpu.PrefetchScalarGridSpec(
            num_scalar_prefetch=1,
            grid=(rows // blk,),
            in_specs=[block, whole, whole] + [part] * (len(shares) * blocks),
            out_specs=[block, block, block],
        ),
        out_shape=[
            jax.ShapeDtypeStruct((rows, depth), F32),
            jax.ShapeDtypeStruct((rows, depth), F32),
            jax.ShapeDtypeStruct((rows, depth), BF),
        ],
        compiler_params=pltpu.CompilerParams(vmem_limit_bytes=60 * MIB),
        name="join",
    )(picks, x, gains, shifts, *[v for share in shares for v in share])


def widen_kernel(up_ref, down_ref, dup_ref, ddown_ref):
    dup_ref[...] = jnp.transpose(up_ref[...]).astype(F32)
    ddown_ref[...] = down_ref[...].astype(F32)


def widen(grads, blk=256):
    hidden, depth = grads.shape[0] // 2, grads.shape[1]
    blk = min(blk, hidden)
    count = hidden // blk
    return pl.pallas_call(
        widen_kernel,
        grid=(count,),
        in_specs=[
            pl.BlockSpec((blk, depth), lambda i: (i, 0)),
            pl.BlockSpec((blk, depth), lambda i: (count + i, 0)),
        ],
        out_specs=[
            pl.BlockSpec((depth, blk), lambda i: (0, i)),
            pl.BlockSpec((blk, depth), lambda i: (i, 0)),
        ],
        out_shape=[
            jax.ShapeDtypeStruct((depth, hidden), F32),
            jax.ShapeDtypeStruct((hidden, depth), F32),
        ],
        compiler_params=pltpu.CompilerParams(vmem_limit_bytes=60 * MIB),
        name="widen",
    )(grads, grads)

MESH = pl.DeviceIdType.MESH


def exchange(src, dst, sems, slot, bit):
    peer = lax.axis_index("dp") ^ (1 << bit)
    return pltpu.make_async_remote_copy(
        src_ref=src,
        dst_ref=dst,
        send_sem=sems[0].at[slot],
        recv_sem=sems[1].at[slot],
        device_id={"dp": peer},
        device_id_type=MESH,
    )


def tail_kernel(
    gq_ref, gk_ref, gv_ref, mixed_ref, wq_ref, wk_ref, wv_ref, x_ref, gr_ref, gain_ref, vec_ref, *refs,
    bits, groups, steps,
):
    lefts, refs = refs[: 2 * groups], refs[2 * groups :]
    sum_ref, out_ref, total_ref = refs[:3]
    right, left, weight, x, g_resid, packed, acc, core_buf, buf, sent, came, own_share, vec_buf = refs[3:16]
    send, recv, vec_send, vec_recv, x_send, x_recv, local = refs[16:]
    sems = (send, recv)
    place, me = lax.axis_index("tensor"), lax.axis_index("dp")
    bit = lambda b: lax.rem(lax.div(me, 1 << b), 2)
    core = bit(0)
    order = list(range(1, bits))
    rows, depth = x.shape
    width = weight.shape[2]
    half = 2 * depth
    base = pl.multiple_of(core * half, half)
    part = min(512, depth)
    chunks = half // part
    slots, fetched = iter(range(send.shape[0])), iter(range(local.shape[0]))

    def fetch(src, dst):
        c = pltpu.make_async_copy(src, dst, local.at[next(fetched)])
        c.start()
        return c

    def wait_all(copies):
        for c in copies:
            c.wait()

    second = [fetch(r, right.at[i]) for i, r in enumerate((gq_ref, gk_ref, gv_ref))]
    second += [fetch(r, weight.at[i]) for i, r in enumerate((wq_ref, wk_ref, wv_ref))]
    third = [fetch(r, left.at[i]) for i, r in enumerate(lefts)] + [fetch(mixed_ref, right.at[3])]
    fourth = [fetch(x_ref, x), fetch(gr_ref, g_resid)]

    greeted = [{"dp": me ^ (1 << b)} for b in range(bits)]
    greeted += [{"tensor": lax.rem(place + r, groups)} for r in range(1, groups)]
    known = {frozenset([("dp", b)]) for b in range(bits)} | {
        frozenset([("tensor", b)]) for b in range((groups - 1).bit_length())
    }
    for bits_of in steps:
        for mask in range(1, 1 << len(bits_of)):
            chosen = [bits_of[i] for i in range(len(bits_of)) if mask >> i & 1]
            if frozenset(chosen) not in known and any(axis == "dp" for axis, _ in chosen):
                known.add(frozenset(chosen))
                peer = {}
                for axis, b in chosen:
                    peer[axis] = peer.get(axis, lax.axis_index(axis)) ^ (1 << b)
                greeted.append(peer)
    barrier = pltpu.get_barrier_semaphore()
    for peer in greeted:
        pl.semaphore_signal(barrier, inc=1, device_id=peer, device_id_type=MESH)
    pl.semaphore_wait(barrier, len(greeted))

    def copy(src, dst, b):
        c = exchange(src, dst, sems, next(slots), b)
        c.start()
        return c

    forwards = []
    cores = {}

    def reduce(chunk):
        cores[chunk].wait()

        def join(i, _):
            at = pl.ds(pl.multiple_of(chunk * part + i * 64, 64), 64)
            own = packed[pl.ds(pl.multiple_of(base + chunk * part + i * 64, 64), 64)].astype(F32)
            acc[at] = (own + core_buf[at].astype(F32)).astype(BF)
            return 0

        lax.fori_loop(0, part // 64, join, 0)
        start, size = chunk * part, part
        landing = chunk * (part - part // (1 << (bits - 1)))
        for b in order:
            size //= 2
            away = pl.multiple_of(start + (1 - bit(b)) * size, size)
            c = copy(acc.at[pl.ds(away, size)], buf.at[pl.ds(landing, size)], b)
            start = start + bit(b) * size
            yield
            c.wait()
            step = min(size, 64)

            def body(i, _, start=start, landing=landing, step=step):
                at = pl.ds(pl.multiple_of(start + i * step, step), step)
                got = buf[pl.ds(pl.multiple_of(landing + i * step, step), step)].astype(F32)
                acc[at] = (acc[at].astype(F32) + got).astype(BF)
                return 0

            lax.fori_loop(0, size // step, body, 0)
            landing += size
        start = base + start
        sum_ref[pl.ds(pl.multiple_of(start, size), size)] = acc[pl.ds(pl.multiple_of(start - base, size), size)]
        for b in reversed(order):
            have = sum_ref.at[pl.ds(pl.multiple_of(start, size), size)]
            c = copy(have, have, b)
            yield
            c.wait()
            start = start - bit(b) * size
            size *= 2
        have = sum_ref.at[pl.ds(pl.multiple_of(start, size), size)]
        forwards.append(copy(have, have, 0))

    def share(r, store):
        at = lax.rem(place + r, groups) * rows
        blk = min(256, rows)

        def body(i, _):
            g = pl.ds(pl.multiple_of(at + i * blk, blk), blk)
            value = dotg(right[0, g, :], weight[0], NT)
            value += dotg(right[1, g, :], weight[1], NT)
            value += dotg(right[2, g, :], weight[2], NT)
            store(pl.ds(pl.multiple_of(i * blk, blk), blk), value)
            return 0

        lax.fori_loop(0, rows // blk, body, 0)

    shares = []

    def share_away(r):
        def store(at, value):
            sent[r - 1, at, :] = value.astype(BF)

        share(r, store)
        c = pltpu.make_async_remote_copy(
            src_ref=sent.at[r - 1],
            dst_ref=came.at[r - 1],
            send_sem=x_send.at[r - 1],
            recv_sem=x_recv.at[r - 1],
            device_id={"tensor": lax.rem(place + r, groups)},
            device_id_type=MESH,
        )
        c.start()
        shares.append(c)

    def store_own(at, value):
        own_share[at, :] = value

    def weight_grad(side, some):
        cols = min(256, part)
        each = part // cols

        def body(i, _):
            first = pl.multiple_of(lax.rem(core + side, 2) * half + i * cols, cols)
            number = lax.div(first, depth)
            kind = lax.div(number, 3) * groups
            lanes = pl.ds(pl.multiple_of(lax.rem(first, depth), cols), cols)
            value = None
            for r in range(groups):
                at = pl.ds(pl.multiple_of(lax.rem(place + r, groups) * rows, rows), rows)
                term = dotg(left[kind + r, :, lanes], right[number, at, :], TN)
                value = term if value is None else value + term
            packed[pl.ds(first, cols), :] = value.astype(BF)
            return 0

        lax.fori_loop(some[0] * each, (some[-1] + 1) * each, body, 0)
        if side:
            for c in some:
                at = pl.ds(pl.multiple_of((1 - core) * half + c * part, part), part)
                cores[c] = copy(packed.at[at], core_buf.at[pl.ds(c * part, part)], 0)

    def last_norm():
        blk = min(64, rows)

        def body(i, _):
            at = pl.ds(pl.multiple_of(i * blk, blk), blk)
            value = own_share[at, :]
            for r in range(groups - 1):
                value += came[r, at, :].astype(F32)
            hat, scale = norm_parts(x[at, :].astype(F32))
            out_ref[at, :] = (g_resid[at, :] + norm_back(value, hat, scale, gain_ref[0:1])).astype(BF)
            total_ref[0:1] += column_sum(value * hat)
            total_ref[1:2] += column_sum(value)
            return 0

        lax.fori_loop(0, rows // blk, body, 0)

    def vectors():
        slot = 0
        for bits_of in steps:
            sends = []
            for mask in range(1, 1 << len(bits_of)):
                peer = {}
                for i, (axis, b) in enumerate(bits_of):
                    if mask >> i & 1:
                        peer[axis] = peer.get(axis, lax.axis_index(axis)) ^ (1 << b)
                sends.append(
                    pltpu.make_async_remote_copy(
                        src_ref=total_ref,
                        dst_ref=vec_buf.at[slot],
                        send_sem=vec_send.at[slot],
                        recv_sem=vec_recv.at[slot],
                        device_id=peer,
                        device_id_type=MESH,
                    )
                )
                sends[-1].start()
                slot += 1
            yield
            wait_all(sends)
            total = total_ref[...]
            for i in range(len(sends)):
                total += vec_buf[slot - len(sends) + i]
            total_ref[...] = total

    def turn(chains):
        still = []
        for chain in chains:
            try:
                next(chain)
                still.append(chain)
            except StopIteration:
                pass
        return still

    wait_all(second)
    for r in range(1, groups):
        share_away(r)
    wait_all(third)
    all_chunks = list(range(chunks))
    for some in (all_chunks[: chunks // 2], all_chunks[chunks // 2 :]):
        weight_grad(1, some)
    reduces = []
    for chunk in all_chunks:
        weight_grad(0, [chunk])
        reduces = turn(reduces + [reduce(chunk)])
    share(0, store_own)
    reduces = turn(reduces)
    wait_all(fourth)
    wait_all(shares)
    total_ref[...] = vec_ref[...]
    last_norm()
    chain = turn([vectors()])
    while reduces or chain:
        reduces, chain = turn(reduces), turn(chain)
    wait_all(forwards)


def tail(grads, mixed, weights, x, g_resid, gains, vectors, n1s, gas, bits, steps):
    (slots, width), (rows, depth), groups = mixed.shape, x.shape, len(n1s)
    half = 2 * depth
    landing = half - half // (1 << (bits - 1))
    count = half // min(512, depth) * (2 * bits + 1)
    vecs = sum((1 << len(b)) - 1 for b in steps)
    vmem = pl.BlockSpec(memory_space=pltpu.VMEM)
    anyspace = pl.BlockSpec(memory_space=pl.ANY)
    dma = pltpu.SemaphoreType.DMA
    peers = max(groups - 1, 1)
    return pl.pallas_call(
        functools.partial(tail_kernel, bits=bits, groups=groups, steps=steps),
        in_specs=[anyspace] * 9 + [vmem] * 2 + [anyspace] * (2 * groups),
        out_specs=[vmem, vmem, vmem],
        out_shape=[
            jax.ShapeDtypeStruct((4 * depth, width), BF),
            jax.ShapeDtypeStruct((rows, depth), BF),
            jax.ShapeDtypeStruct(vectors.shape, F32),
        ],
        scratch_shapes=[
            pltpu.VMEM((4, slots, width), BF),
            pltpu.VMEM((2 * groups, rows, depth), BF),
            pltpu.VMEM((3, depth, width), BF),
            pltpu.VMEM((rows, depth), BF),
            pltpu.VMEM((rows, depth), F32),
            pltpu.VMEM((4 * depth, width), BF),
            pltpu.VMEM((half, width), BF),
            pltpu.VMEM((half, width), BF),
            pltpu.VMEM((landing, width), BF),
            pltpu.VMEM((peers, rows, depth), BF),
            pltpu.VMEM((peers, rows, depth), BF),
            pltpu.VMEM((rows, depth), F32),
            pltpu.VMEM((vecs,) + vectors.shape, F32),
            dma((count,)),
            dma((count,)),
            dma((vecs,)),
            dma((vecs,)),
            dma((peers,)),
            dma((peers,)),
            dma((9 + 2 * groups,)),
        ],
        compiler_params=pltpu.CompilerParams(
            collective_id=1, has_side_effects=True, vmem_limit_bytes=60 * MIB
        ),
        cost_estimate=pl.CostEstimate(flops=rows * width, bytes_accessed=rows * width, transcendentals=0),
        name="tail",
    )(*grads, mixed, *weights, x, g_resid, gains, vectors, *n1s, *gas)


def mixed_back_kernel(at_ref, x_ref, w_ref, *refs):
    refs[-1][...] = dotg(x_ref[...], w_ref[...], NT).astype(BF)


def mixed_back(where, x, w_out, slots, held, blk=256):
    rows, depth = x.shape
    width = w_out.shape[0]
    blk = min(blk, rows)
    count = rows // blk
    return pl.pallas_call(
        mixed_back_kernel,
        grid_spec=pltpu.PrefetchScalarGridSpec(
            num_scalar_prefetch=1,
            grid=(count,),
            in_specs=[
                pl.BlockSpec((blk, depth), lambda i, at: (i, 0)),
                pl.BlockSpec((width, depth), lambda i, at: (0, 0)),
            ]
            + [pl.BlockSpec(memory_space=pl.ANY)] * len(held),
            out_specs=pl.BlockSpec((blk, width), lambda i, at: (at[0] * count + i, 0)),
        ),
        out_shape=jax.ShapeDtypeStruct((slots, width), BF),
        input_output_aliases={3: 0} if held else {},
        compiler_params=pltpu.CompilerParams(vmem_limit_bytes=60 * MIB),
        cost_estimate=pl.CostEstimate(flops=rows * depth, bytes_accessed=rows * depth, transcendentals=0),
        name="mixed_back",
    )(where, x, w_out, *held)


def shift(x, axis, count, step):
    return lax.ppermute(x, axis, [((i + step) % count, i) for i in range(count)])


def shards(
    tokens,
    lengths,
    cotangent,
    w_query,
    w_key,
    w_value,
    w_out,
    up_weight,
    bias_up,
    down_weight,
    bias_down,
    norm_gains,
    norm_shifts,
):
    rows, _, depth = tokens.shape
    groups, replicas = lax.axis_size("tensor"), lax.axis_size("dp")
    me, replica = lax.axis_index("tensor"), lax.axis_index("dp")
    slots = rows * groups
    width = w_query.shape[1]
    hidden = up_weight.shape[1]
    x = tokens.reshape(rows, depth)
    here = me.reshape(1).astype(jnp.int32)
    place = lambda r: (here + r) % groups

    def others(v):
        return [shift(v, "tensor", groups, r) for r in range(1, groups)]

    def to_owner(v, r):
        return shift(v, "tensor", groups, groups - r)

    up_piece = lax.dynamic_slice_in_dim(up_weight, replica * (depth // replicas), depth // replicas, 0)
    down_piece = lax.dynamic_slice_in_dim(
        down_weight, replica * (hidden // replicas), hidden // replicas, 0
    )
    gather = lambda v: lax.all_gather(v, "dp", axis=0, tiled=True)

    freqs = 10000.0 ** (-jnp.arange(HD // 2).astype(F32) * 2.0 / HD)
    angles = jnp.arange(slots).astype(F32)[:, None] * freqs[None, :]
    cosine, sine = jnp.cos(angles), jnp.sin(angles)
    cosine = jnp.concatenate([cosine] * 4, axis=1)
    sine = jnp.concatenate([-sine, sine] * 2, axis=1)
    x_rest = others(x)
    normed_one = first_norm(x, norm_gains, norm_shifts)
    weights = (w_query, w_key, w_value)
    joint = project(here, normed_one, *weights, cosine, sine)
    joint, x_rest, up_piece, down_piece, bias = lax.optimization_barrier((joint, x_rest, up_piece, down_piece, bias_up))
    up_pieces, down_pieces, bias_rest = others(up_piece), others(down_piece), others(bias)
    normed_one_rest = [first_norm(v, norm_gains, norm_shifts) for v in x_rest]
    for r, n in enumerate(normed_one_rest):
        joint = project(place(r + 1), n, *weights, cosine, sine, joint)
    joint, up_pieces, down_pieces, bias_rest = lax.optimization_barrier((joint, up_pieces, down_pieces, bias_rest))
    blk = min(512, rows)
    each = rows // blk
    odd = lambda r: lax.rem(place(r), 2)
    ranks = lambda r, k: jnp.where(odd(r) == 1, each - 1 - k, k)
    held, shares, arrived = (), [], [[] for _ in range(1, groups)]
    for k in range(each):
        for r in range(1, groups):
            *held, share = attend(place(r) * each + ranks(0, k), lengths, joint, w_out, held, BF, blk)
            arrived[r - 1].append(to_owner(share, r))
        if k == each - 1 and k > 0:
            joint, arrived = lax.optimization_barrier((joint, [v[:k] for v in arrived])), arrived
            joint, early = joint
            arrived = [list(e) + v[k:] for e, v in zip(early, arrived)]
        *held, share = attend(here * each + ranks(0, k), lengths, joint, w_out, held, F32, blk)
        shares.append(share)
    mixed, lse = held
    shares = [shares] + arrived
    picks = jnp.concatenate([ranks(groups - r, k) for r in range(groups) for k in range(each)])
    up_rest, down_rest = [gather(p) for p in up_pieces], [gather(p) for p in down_pieces]
    biases = jnp.concatenate([bias_up] + bias_rest).astype(F32)

    info = jnp.stack([lengths[0], me * rows]).astype(jnp.int32)
    cot = cotangent.reshape(rows, depth)
    attn_sum, resid, normed_two = join(x, norm_gains, norm_shifts, shares, picks)
    normed_two_rest = others(normed_two)
    slope, act, branch = feed(
        info, normed_two, biases[:hidden], [up_weight], [down_weight], own=bias_down.reshape(1, depth)
    )
    slope_rest, layer_out, g_branch, sums3 = feed(
        info, normed_two, biases[hidden:], up_rest, down_rest, rest=(branch, resid, cot, norm_gains, norm_shifts)
    )
    ups, downs = [up_weight] + up_rest, [down_weight] + down_rest
    g_branch_rest = others(g_branch)
    g_pre, g_resid, g_attn, sums21 = feed_back(
        info, g_branch, slope, slope_rest, ups, downs, resid, attn_sum, cot, norm_gains
    )
    g_attn_rest = others(g_attn)
    g_pre, normed_two_rest = lax.optimization_barrier((g_pre, normed_two_rest))
    g_mixed = mixed_back(here, g_attn, w_out, slots, [])
    g_pre, g_mixed = lax.optimization_barrier((g_pre, g_mixed))
    grad_feed, bias_up_sum = feed_grad(
        up_weight, down_weight, biases[:hidden], act, g_pre,
        [normed_two] + normed_two_rest, [g_branch] + g_branch_rest,
    )
    grad_feed = grad_feed.reshape(2 * hidden, depth)
    g_mixed, g_attn_rest, grad_feed = lax.optimization_barrier((g_mixed, g_attn_rest, grad_feed))
    grad_feed = lax.psum(grad_feed, "dp")
    for r, g in enumerate(g_attn_rest):
        g_mixed = mixed_back(place(r + 1), g, w_out, slots, [g_mixed])

    grads = attend_back(lengths, joint, mixed, g_mixed, lse, cosine, sine, width)
    placed = lax.dynamic_update_slice(
        jnp.zeros((groups * hidden,), F32), bias_up_sum.reshape(-1), (me * hidden,)
    ).reshape(-1, depth)
    bits = (replicas - 1).bit_length()
    steps = [("tensor", b) for b in range((groups - 1).bit_length())] + [("dp", b) for b in range(bits)]
    steps = [tuple(steps[i : i + 2]) for i in range(0, len(steps), 2)]
    vectors = jnp.concatenate([jnp.zeros((2, depth), F32), sums3[:3], sums21[:4], placed])
    vectors = jnp.pad(vectors, ((0, -len(vectors) % 8), (0, 0)))
    packed, grad_tokens, sums = tail(
        grads, mixed, weights, x, g_resid, norm_gains, vectors,
        [normed_one] + normed_one_rest, [g_attn] + g_attn_rest, bits, steps,
    )
    grad_up, grad_down = widen(grad_feed)
    grad_query, grad_key, grad_value = (packed[i * depth : (i + 1) * depth].astype(F32) for i in range(3))
    grad_out = jnp.transpose(packed[3 * depth :]).astype(F32)
    grad_gains = jnp.stack([sums[0], sums[7], sums[5], sums[2]])
    grad_shifts = jnp.stack([sums[1], sums[8], sums[6], sums[3]])
    grad_bias_up = lax.dynamic_slice_in_dim(sums[9 : 9 + groups * hidden // depth].reshape(-1), me * hidden, hidden, 0)
    whole = (rows, 1, depth)
    return (
        layer_out.reshape(whole),
        grad_tokens.reshape(whole),
        grad_query,
        grad_key,
        grad_value,
        grad_out,
        grad_up,
        grad_bias_up,
        grad_down,
        sums[4],
        grad_gains,
        grad_shifts,
    )


def solution(mesh):
    wide, tall = P(None, "tensor"), P("tensor", None)
    acts = P("tensor", "dp", None)
    return jax.shard_map(
        shards,
        mesh=mesh,
        in_specs=(acts, P("dp"), acts, wide, wide, wide, tall, wide, P("tensor"), tall, P(), P(), P()),
        out_specs=(acts, acts, wide, wide, wide, tall, wide, P("tensor"), tall, P(), P(), P()),
        check_vma=False,
    )
```

```python
import functools
import jax
import jax.numpy as jnp
from jax import lax
from jax.experimental import pallas as pl
from jax.experimental.pallas import tpu as pltpu
from jax.sharding import PartitionSpec as P

HD = 64
EPSILON = 1e-05
BF = jnp.bfloat16
F32 = jnp.float32
NT = (((1,), (1,)), ((), ()))
NN = (((1,), (0,)), ((), ()))
TN = (((0,), (0,)), ((), ()))
MIB = 1 << 20


def dotg(a, b, dims=NN):
    return lax.dot_general(a, b, dims, preferred_element_type=F32)


def rotate(x, cos, sin):
    first = lax.broadcasted_iota(jnp.int32, (x.shape[0], 128), 1) % HD < HD // 2
    parts = []
    for a in range(0, x.shape[1], 128):
        v = x[:, a : a + 128]
        swapped = jnp.where(first, pltpu.roll(v, 96, 1), pltpu.roll(v, 32, 1))
        parts.append(v * cos + swapped * sin)
    return jnp.concatenate(parts, axis=1) if len(parts) > 1 else parts[0]


def qkv_kernel(x_ref, wq_ref, wk_ref, wv_ref, cos_ref, sin_ref, o_ref):
    width = wq_ref.shape[1]
    x, cos, sin = x_ref[...], cos_ref[...], sin_ref[...]
    o_ref[:, :width] = rotate(dotg(x, wq_ref[...]), cos, sin).astype(BF)
    o_ref[:, width : 2 * width] = rotate(dotg(x, wk_ref[...]), cos, sin).astype(BF)
    o_ref[:, 2 * width :] = dotg(x, wv_ref[...]).astype(BF)


def project(where, x, w_query, w_key, w_value, cos, sin, joint=None, part=0, parts=1, blk=256):
    rows, depth = x.shape
    width, slots = w_query.shape[1], cos.shape[0]
    blk = min(blk, rows // parts)
    whole = rows // blk
    count = whole // parts
    weight = pl.BlockSpec((depth, width), lambda i, at: (0, 0))
    angle = pl.BlockSpec((blk, 128), lambda i, at: (at[0] * whole + part * count + i, 0))
    kernel = lambda at, *refs: qkv_kernel(*refs[:6], refs[-1])
    held = [] if joint is None else [joint]
    return pl.pallas_call(
        kernel,
        grid_spec=pltpu.PrefetchScalarGridSpec(
            num_scalar_prefetch=1,
            grid=(count,),
            in_specs=[pl.BlockSpec((blk, depth), lambda i, at: (part * count + i, 0)), weight, weight, weight, angle, angle]
            + [pl.BlockSpec(memory_space=pl.ANY)] * len(held),
            out_specs=pl.BlockSpec((blk, 3 * width), lambda i, at: (at[0] * whole + part * count + i, 0)),
        ),
        out_shape=jax.ShapeDtypeStruct((slots, 3 * width), BF),
        input_output_aliases={7: 0} if held else {},
        compiler_params=pltpu.CompilerParams(vmem_limit_bytes=60 * MIB),
        cost_estimate=pl.CostEstimate(flops=rows * depth, bytes_accessed=rows * depth, transcendentals=0),
        name="project",
    )(where, x, w_query, w_key, w_value, cos, sin, *held)


def attend_kernel(at_ref, len_ref, q_ref, k_ref, v_ref, w_ref, *refs, blk):
    o_ref, lse_ref, share_ref, vt, low_ref = refs[-5:]
    pair = pl.program_id(0)
    i = at_ref[0]
    length = len_ref[0]
    def turn(j, _):
        part = pl.ds(pl.multiple_of(j * blk, blk), blk)
        vt[:, part] = jnp.transpose(v_ref[part, :])
        return 0

    lax.fori_loop(0, i + 1, turn, 0)
    lane = lax.broadcasted_iota(jnp.int32, (blk, 128), 1)
    q = q_ref[...] * jnp.asarray(0.125, BF)
    zero = jnp.zeros_like(q)
    qs = (jnp.where(lane < HD, q, zero), jnp.where(lane < HD, zero, q))

    def step(j, carry, diag):
        start = pl.multiple_of(j * blk, blk)
        kb = k_ref[pl.ds(start, blk), :]
        sub = min(256, blk)
        n = blk // sub
        if diag:
            key = lax.broadcasted_iota(jnp.int32, (sub, blk), 0)
            qry = lax.broadcasted_iota(jnp.int32, (sub, blk), 1)
        state = [carry[h] for h in range(2)]
        chains = [(h, t) for t in range(n) for h in range(2)]
        live = {}

        def first(c):
            h, t = chains[c]
            live[c] = dotg(kb[t * sub : t * sub + sub], qs[h], NT)

        def middle(c):
            h, t = chains[c]
            s = live[c]
            if diag:
                s = jnp.where((key + t * sub <= qry) & (key + t * sub + start < length), s, -1e30)
            m, l, acc = state[h]
            mn = jnp.maximum(m, jnp.max(s, axis=0, keepdims=True))
            p = jnp.exp(s - mn)
            al = jnp.exp(m - mn)
            state[h] = (mn, l * al + jnp.sum(p, axis=0, keepdims=True), acc)
            live[c] = (p.astype(BF), al)

        def last(c):
            h, t = chains[c]
            p, al = live.pop(c)
            m, l, acc = state[h]
            state[h] = (m, l, acc * al + dotg(vt[HD * h : HD * h + HD, pl.ds(start + t * sub, sub)], p))

        stages = (first, middle, last)
        for i in range(len(chains) + 4):
            for k in range(3):
                c = i - 2 * k
                if 0 <= c < len(chains):
                    stages[k](c)
        return tuple(state)

    init = tuple(
        (jnp.full((1, blk), -1e30, F32), jnp.zeros((1, blk), F32), jnp.zeros((HD, blk), F32))
        for _ in range(2)
    )
    c = lax.fori_loop(0, i, lambda j, c: step(j, c, False), init)
    c = step(i, c, True)
    ot = jnp.concatenate([c[h][2] / c[h][1] for h in range(2)], axis=0)
    low = jnp.transpose(ot).astype(BF)
    o_ref[...] = low
    lse_ref[0] = jnp.concatenate([c[h][0] + jnp.log(c[h][1]) for h in range(2)], axis=0)
    low_ref[pair] = low

    @pl.when(pair == pl.num_programs(0) - 1)
    def _():
        pairs = low_ref.shape[0]
        low = jnp.concatenate([low_ref[p] for p in range(pairs)], axis=1)
        share_ref[...] = dotg(low, w_ref[...]).astype(share_ref.dtype)


def attend(at, length, joint, w_out, held, kind, blk):
    rows, width, depth = joint.shape[0], w_out.shape[0], w_out.shape[1]
    pairs = width // 128
    return pl.pallas_call(
        functools.partial(attend_kernel, blk=blk),
        grid_spec=pltpu.PrefetchScalarGridSpec(
            num_scalar_prefetch=2,
            grid=(pairs,),
            in_specs=[
                pl.BlockSpec((blk, 128), lambda p, at, *_: (at[0], p)),
                pl.BlockSpec((rows, 128), lambda p, *_: (0, pairs + p)),
                pl.BlockSpec((rows, 128), lambda p, *_: (0, 2 * pairs + p)),
                pl.BlockSpec((width, depth), lambda p, *_: (0, 0), pipeline_mode=pl.Buffered(1)),
            ]
            + [pl.BlockSpec(memory_space=pl.ANY)] * len(held),
            out_specs=[
                pl.BlockSpec((blk, 128), lambda p, at, *_: (at[0], p)),
                pl.BlockSpec((1, 2, blk), lambda p, at, *_: (p, 0, at[0])),
                pl.BlockSpec((blk, depth), lambda p, *_: (0, 0)),
            ],
            scratch_shapes=[pltpu.VMEM((128, rows), BF), pltpu.VMEM((pairs, blk, 128), BF)],
        ),
        out_shape=[
            jax.ShapeDtypeStruct((rows, width), BF),
            jax.ShapeDtypeStruct((pairs, 2, rows), F32),
            jax.ShapeDtypeStruct((blk, depth), kind),
        ],
        input_output_aliases={6: 0, 7: 1} if held else {},
        compiler_params=pltpu.CompilerParams(vmem_limit_bytes=60 * MIB),
        cost_estimate=pl.CostEstimate(flops=rows * width, bytes_accessed=rows * width, transcendentals=0),
        name="attend",
    )(at, length, joint, joint, joint, w_out, *held)


def attend_back_kernel(
    len_ref, q_ref, k_ref, v_ref, o_ref, do_ref, lse_ref, cos_ref, sin_ref,
    dq_ref, dk_ref, dv_ref, kt, dlt, dqt, *, blk, blocks,
):
    length = len_ref[0]
    kt[...] = jnp.transpose(k_ref[...])
    dqt[...] = jnp.zeros_like(dqt)

    def products(i, _):
        at = pl.ds(pl.multiple_of(i * blk, blk), blk)
        both = jnp.transpose(do_ref[at, :].astype(F32) * o_ref[at, :].astype(F32))
        for h in range(2):
            dlt[h : h + 1, at] = jnp.sum(both[HD * h : HD * h + HD], axis=0, keepdims=True)
        return 0

    lax.fori_loop(0, blocks, products, 0)

    def keys(j, _):
        attend_back_keys(
            j, length, q_ref, k_ref, v_ref, do_ref, lse_ref, cos_ref, sin_ref, dk_ref, dv_ref, kt, dlt, dqt, blk, blocks
        )
        return 0

    lax.fori_loop(0, blocks, keys, 0)

    def turn(i, _):
        at = pl.ds(pl.multiple_of(i * blk, blk), blk)
        grad = jnp.transpose(dqt[:, at]) * 0.125
        dq_ref[at, :] = rotate(grad, cos_ref[at, :], -sin_ref[at, :]).astype(BF)
        return 0

    lax.fori_loop(0, blocks, turn, 0)


def attend_back_keys(
    j, length, q_ref, k_ref, v_ref, do_ref, lse_ref, cos_ref, sin_ref, dk_ref, dv_ref, kt, dlt, dqt, blk, blocks
):
    js = pl.multiple_of(j * blk, blk)
    lane = lax.broadcasted_iota(jnp.int32, (blk, 128), 1)
    kb = k_ref[pl.ds(js, blk), :] * jnp.asarray(0.125, BF)
    vb = v_ref[pl.ds(js, blk), :]
    zero = jnp.zeros_like(kb)
    ks = (jnp.where(lane < HD, kb, zero), jnp.where(lane < HD, zero, kb))
    vs = (jnp.where(lane < HD, vb, zero), jnp.where(lane < HD, zero, vb))

    def step(i, carry, diag):
        at = pl.ds(pl.multiple_of(i * blk, blk), blk)
        qb, dob = q_ref[at, :], do_ref[at, :]
        out = []
        for h in range(2):
            dk, dv = carry[h]
            s = dotg(ks[h], qb, NT)
            if diag:
                key = lax.broadcasted_iota(jnp.int32, (blk, blk), 0)
                qry = lax.broadcasted_iota(jnp.int32, (blk, blk), 1)
                s = jnp.where((key <= qry) & (key + js < length), s, -1e30)
            p = jnp.exp(s - lse_ref[0, h : h + 1, at])
            dp = dotg(vs[h], dob, NT)
            ds = (p * (dp - dlt[h : h + 1, at])).astype(BF)
            dv = dv + dotg(p.astype(BF), dob)
            dk = dk + dotg(ds, qb)
            dqt[HD * h : HD * h + HD, at] += dotg(kt[HD * h : HD * h + HD, pl.ds(js, blk)], ds)
            out.append((dk, dv))
        return tuple(out)

    z = jnp.zeros((blk, 128), F32)
    c = step(j, ((z, z), (z, z)), True)
    c = lax.fori_loop(j + 1, blocks, lambda i, c: step(i, c, False), c)
    grad = jnp.where(lane < HD, c[0][0], c[1][0]) * 0.125
    dk_ref[pl.ds(js, blk), :] = rotate(grad, cos_ref[pl.ds(js, blk), :], -sin_ref[pl.ds(js, blk), :]).astype(BF)
    dv_ref[pl.ds(js, blk), :] = jnp.where(lane < HD, c[0][1], c[1][1]).astype(BF)


def attend_back(length, joint, mixed, dmixed, lse, cos, sin, width, blk=512):
    rows = joint.shape[0]
    pairs, blocks = width // 128, rows // blk
    full = lambda off: pl.BlockSpec((rows, 128), lambda p, *_: (0, off * pairs + p))
    angle = pl.BlockSpec((rows, 128), lambda p, *_: (0, 0))
    return pl.pallas_call(
        functools.partial(attend_back_kernel, blk=blk, blocks=blocks),
        grid_spec=pltpu.PrefetchScalarGridSpec(
            num_scalar_prefetch=1,
            grid=(pairs,),
            in_specs=[full(0), full(1), full(2), full(0), full(0)]
            + [pl.BlockSpec((1, 2, rows), lambda p, *_: (p, 0, 0)), angle, angle],
            out_specs=[full(0)] * 3,
            scratch_shapes=[
                pltpu.VMEM((128, rows), BF),
                pltpu.VMEM((2, rows), F32),
                pltpu.VMEM((128, rows), F32),
            ],
        ),
        out_shape=[jax.ShapeDtypeStruct((rows, width), BF)] * 3,
        compiler_params=pltpu.CompilerParams(vmem_limit_bytes=60 * MIB),
        cost_estimate=pl.CostEstimate(
            flops=rows * width, bytes_accessed=rows * width, transcendentals=0
        ),
        name="attend_back",
    )(length, joint, joint, joint, mixed, dmixed, lse, cos, sin)


def gelu_parts(v):
    c = 0.7978845608028654
    return c, jnp.tanh(c * (v + 0.044715 * v * v * v))


def gelu_both(v):
    c, t = gelu_parts(v)
    half = 0.5 * (1.0 + t)
    return v * half, half + 0.5 * v * (1.0 - t * t) * c * (1.0 + 3 * 0.044715 * v * v)


def norm_parts(values):
    average = jnp.mean(values, axis=-1, keepdims=True)
    centred = values - average
    scale = lax.rsqrt(jnp.mean(centred * centred, axis=-1, keepdims=True) + EPSILON)
    return centred * scale, scale


def norm_back(grad, hat, scale, gain):
    g = grad * gain
    return scale * (
        g - jnp.mean(g, axis=-1, keepdims=True) - hat * jnp.mean(g * hat, axis=-1, keepdims=True)
    )


def column_sum(v):
    return jnp.sum(v, axis=0, keepdims=True)


def valid_rows(info_ref, start, count):
    at = info_ref[1] + start + lax.broadcasted_iota(jnp.int32, (count, 1), 0)
    return (at < info_ref[0]).astype(F32)


def loop_rows(rows, blk, body):
    def step(i, _):
        body(pl.multiple_of(i * blk, blk))
        return 0

    lax.fori_loop(0, rows // blk, step, 0)


def feed_kernel(info_ref, *refs, groups, chunks, sub, own):
    x_ref, bias_ref = refs[:2]
    ups, downs, refs = refs[2 : 2 + groups], refs[2 + groups : 2 + 2 * groups], refs[2 + 2 * groups :]
    step = pl.program_id(0)
    rows = x_ref.shape[0]
    if own:
        bd_ref, slope_ref, act_ref, acc = refs
        late = []
    else:
        resid_hbm, cot_hbm, before_hbm, gain_ref, shift_ref = refs[:5]
        slope_ref, out_ref, gb_ref, sums_ref, acc, resid_ref, before_ref, cot_ref, sems = refs[5:]
        late = [
            pltpu.make_async_copy(resid_hbm, resid_ref, sems.at[0]),
            pltpu.make_async_copy(cot_hbm, cot_ref, sems.at[1]),
            pltpu.make_async_copy(before_hbm, before_ref, sems.at[2]),
        ]

    @pl.when(step == 0)
    def _():
        acc[...] = jnp.zeros_like(acc) + bd_ref[...].astype(F32) if own else jnp.zeros_like(acc)
        for c in late:
            c.start()

    for g in range(groups):

        @pl.when(step // chunks == g)
        def _():
            for r in range(0, rows, sub):
                act, slope = gelu_both(dotg(x_ref[r : r + sub], ups[g][...]) + bias_ref[0])
                slope_ref[r : r + sub] = slope.astype(BF)
                act = act.astype(BF)
                if own:
                    act_ref[r : r + sub] = act
                acc[r : r + sub] += dotg(act, downs[g][...])

    if own:
        return

    @pl.when(step == groups * chunks - 1)
    def _():
        for c in late:
            c.wait()
        sums_ref[...] = jnp.zeros_like(sums_ref)
        gain, shift = gain_ref[3:4], shift_ref[3:4]
        blk = min(256, rows)

        def body(r):
            at = pl.ds(r, blk)
            valid = valid_rows(info_ref, r, blk)
            hat, scale = norm_parts(acc[at] + before_ref[at])
            out_ref[at] = (valid * (resid_ref[at] + hat * gain + shift)).astype(BF)
            g_out = valid * cot_ref[at].astype(F32)
            low = norm_back(g_out, hat, scale, gain).astype(BF)
            gb_ref[at] = low
            sums_ref[0:1] += column_sum(g_out * hat)
            sums_ref[1:2] += column_sum(g_out)
            sums_ref[2:3] += column_sum(low.astype(F32))

        loop_rows(rows, blk, body)


def feed(info, x, biases, ups, downs, own=None, rest=None, cols=512):
    rows, depth = x.shape
    groups, hidden = len(ups), ups[0].shape[1]
    chunks = hidden // cols
    once = lambda shape: pl.BlockSpec(shape, lambda s, *_: (0, 0), pipeline_mode=pl.Buffered(1))
    anyspace = pl.BlockSpec(memory_space=pl.ANY)
    part = lambda g: (lambda s, *_: (0, jnp.clip(s - g * chunks, 0, chunks - 1)))
    part_t = lambda g: (lambda s, *_: (jnp.clip(s - g * chunks, 0, chunks - 1), 0))
    wide = pl.BlockSpec((rows, cols), lambda s, *_: (0, s))
    low = jax.ShapeDtypeStruct((rows, depth), BF)
    slope = jax.ShapeDtypeStruct((rows, groups * hidden), BF)
    if rest is None:
        more, args = [once((1, depth))], [own]
        out_specs = [wide, wide, once((rows, depth))]
        out_shape = [slope, slope, jax.ShapeDtypeStruct((rows, depth), F32)]
        scratch = []
    else:
        before, resid, cot, gains, shifts = rest
        more, args = [anyspace] * 3 + [once(gains.shape)] * 2, [resid, cot, before, gains, shifts]
        out_specs = [wide, once((rows, depth)), once((rows, depth)), once((8, depth))]
        out_shape = [slope, low, low, jax.ShapeDtypeStruct((8, depth), F32)]
        scratch = [
            pltpu.VMEM((rows, depth), F32),
            pltpu.VMEM((rows, depth), F32),
            pltpu.VMEM((rows, depth), F32),
            pltpu.VMEM((rows, depth), BF),
            pltpu.SemaphoreType.DMA((3,)),
        ]
    return pl.pallas_call(
        functools.partial(feed_kernel, groups=groups, chunks=chunks, sub=min(512, rows), own=rest is None),
        grid_spec=pltpu.PrefetchScalarGridSpec(
            num_scalar_prefetch=1,
            grid=(groups * chunks,),
            in_specs=[once((rows, depth)), pl.BlockSpec((1, 1, cols), lambda s, *_: (s, 0, 0))]
            + [pl.BlockSpec((depth, cols), part(g)) for g in range(groups)]
            + [pl.BlockSpec((cols, depth), part_t(g)) for g in range(groups)]
            + more,
            out_specs=out_specs,
            scratch_shapes=scratch,
        ),
        out_shape=out_shape,
        compiler_params=pltpu.CompilerParams(vmem_limit_bytes=60 * MIB),
        cost_estimate=pl.CostEstimate(flops=rows * depth, bytes_accessed=rows * depth, transcendentals=0),
        name="feed",
    )(info, x, biases.reshape(-1, 1, cols), *ups, *downs, *args)


def feed_back_kernel(info_ref, *refs, groups, chunks, sub):
    gb_ref, own_slope, rest_slope, resid_hbm, attn_hbm, cot_hbm, gain_ref = refs[:7]
    ups, downs = refs[7 : 7 + groups], refs[7 + groups : 7 + 2 * groups]
    gp_ref, gr_ref, ga_ref, sums_ref, acc, resid_ref, attn_ref, cot_ref, sems = refs[7 + 2 * groups :]
    step = pl.program_id(0)
    rows = gb_ref.shape[0]
    late = [
        pltpu.make_async_copy(src, dst, sems.at[i])
        for i, (src, dst) in enumerate(((resid_hbm, resid_ref), (attn_hbm, attn_ref), (cot_hbm, cot_ref)))
    ]

    @pl.when(step == 0)
    def _():
        for c in late:
            c.start()
        acc[...] = jnp.zeros_like(acc)

    for g in range(groups):

        @pl.when(step // chunks == g)
        def _():
            for r in range(0, rows, sub):
                grad = dotg(gb_ref[r : r + sub], downs[g][...], NT)
                slope_ref = rest_slope if g else own_slope
                low = (grad * slope_ref[r : r + sub].astype(F32)).astype(BF)
                if g == 0:
                    gp_ref[r : r + sub] = low
                acc[r : r + sub] += dotg(low, ups[g][...], NT)

    @pl.when(step == groups * chunks - 1)
    def _():
        for c in late:
            c.wait()
        sums_ref[...] = jnp.zeros_like(sums_ref)
        blk = min(256, rows)

        def body(r):
            at = pl.ds(r, blk)
            g_out = valid_rows(info_ref, r, blk) * cot_ref[at].astype(F32)
            hat, scale = norm_parts(resid_ref[at])
            g_two = acc[at]
            g_resid = g_out + norm_back(g_two, hat, scale, gain_ref[2:3])
            gr_ref[at] = g_resid
            sums_ref[0:1] += column_sum(g_two * hat)
            sums_ref[1:2] += column_sum(g_two)
            hat, scale = norm_parts(attn_ref[at])
            ga_ref[at] = norm_back(g_resid, hat, scale, gain_ref[1:2]).astype(BF)
            sums_ref[2:3] += column_sum(g_resid * hat)
            sums_ref[3:4] += column_sum(g_resid)

        loop_rows(rows, blk, body)


def feed_back(info, gb, own_slope, rest_slope, ups, downs, resid, attn_sum, cot, gains, cols=512):
    rows, depth = gb.shape
    groups, hidden = len(ups), ups[0].shape[1]
    chunks = hidden // cols
    once = lambda shape: pl.BlockSpec(shape, lambda s, *_: (0, 0), pipeline_mode=pl.Buffered(1))
    anyspace = pl.BlockSpec(memory_space=pl.ANY)
    own = lambda g: (lambda s, *_: (0, jnp.clip(s - g * chunks, 0, chunks - 1)))
    own_t = lambda g: (lambda s, *_: (jnp.clip(s - g * chunks, 0, chunks - 1), 0))
    return pl.pallas_call(
        functools.partial(feed_back_kernel, groups=groups, chunks=chunks, sub=min(512, rows)),
        grid_spec=pltpu.PrefetchScalarGridSpec(
            num_scalar_prefetch=1,
            grid=(groups * chunks,),
            in_specs=[
                once((rows, depth)),
                pl.BlockSpec((rows, cols), own(0)),
                pl.BlockSpec((rows, cols), lambda s, *_: (0, jnp.maximum(s - chunks, 0))),
                anyspace,
                anyspace,
                anyspace,
                once(gains.shape),
            ]
            + [pl.BlockSpec((depth, cols), own(g)) for g in range(groups)]
            + [pl.BlockSpec((cols, depth), own_t(g)) for g in range(groups)],
            out_specs=[
                pl.BlockSpec((rows, cols), own(0)),
                once((rows, depth)),
                once((rows, depth)),
                once((8, depth)),
            ],
            scratch_shapes=[
                pltpu.VMEM((rows, depth), F32),
                pltpu.VMEM((rows, depth), F32),
                pltpu.VMEM((rows, depth), F32),
                pltpu.VMEM((rows, depth), BF),
                pltpu.SemaphoreType.DMA((3,)),
            ],
        ),
        out_shape=[
            jax.ShapeDtypeStruct((rows, hidden), BF),
            jax.ShapeDtypeStruct((rows, depth), F32),
            jax.ShapeDtypeStruct((rows, depth), BF),
            jax.ShapeDtypeStruct((8, depth), F32),
        ],
        compiler_params=pltpu.CompilerParams(vmem_limit_bytes=60 * MIB),
        cost_estimate=pl.CostEstimate(flops=rows * depth, bytes_accessed=rows * depth, transcendentals=0),
        name="feed_back",
    )(info, gb, own_slope, rest_slope, resid, attn_sum, cot, gains, *ups, *downs)


def feed_grad_kernel(*refs, groups):
    up_ref, down_ref, bias_ref, act_ref, gp_ref = refs[:5]
    n2s, gbs = refs[5 : 5 + groups], refs[5 + groups : 5 + 2 * groups]
    grad_ref, sum_ref = refs[5 + 2 * groups :]
    act, gp = act_ref[...], gp_ref[...]
    dup = dotg(gp, n2s[0][...], TN)
    ddown = dotg(act, gbs[0][...], TN)
    sums = column_sum(gp.astype(F32))
    for g in range(1, groups):
        pre = dotg(n2s[g][...], up_ref[...]) + bias_ref[0]
        act, slope = gelu_both(pre)
        act = act.astype(BF)
        gp = (dotg(gbs[g][...], down_ref[...], NT) * slope).astype(BF)
        dup += dotg(gp, n2s[g][...], TN)
        ddown += dotg(act, gbs[g][...], TN)
        sums += column_sum(gp.astype(F32))
    grad_ref[0] = dup.astype(BF)
    grad_ref[1] = ddown.astype(BF)
    sum_ref[0] = sums


def feed_grad(up, down, bias, act, gp, n2s, gbs, cols=512):
    rows, depth = n2s[0].shape
    groups, hidden = len(n2s), up.shape[1]
    once = lambda shape: pl.BlockSpec(shape, lambda s: (0, 0), pipeline_mode=pl.Buffered(1))
    wide = lambda count: pl.BlockSpec((count, cols), lambda s: (0, s))
    tall = pl.BlockSpec((cols, depth), lambda s: (s, 0))
    flat = pl.BlockSpec((1, 1, cols), lambda s: (s, 0, 0))
    return pl.pallas_call(
        functools.partial(feed_grad_kernel, groups=groups),
        grid=(hidden // cols,),
        in_specs=[wide(depth), tall, flat, wide(rows), wide(rows)] + [once((rows, depth))] * (2 * groups),
        out_specs=[pl.BlockSpec((2, cols, depth), lambda s: (0, s, 0)), flat],
        out_shape=[
            jax.ShapeDtypeStruct((2, hidden, depth), BF),
            jax.ShapeDtypeStruct((hidden // cols, 1, cols), F32),
        ],
        compiler_params=pltpu.CompilerParams(vmem_limit_bytes=60 * MIB),
        cost_estimate=pl.CostEstimate(
            flops=(8 * groups - 4) * rows * depth * hidden, bytes_accessed=20 * rows * depth, transcendentals=0
        ),
        name="feed_grad",
    )(up, down, bias.reshape(-1, 1, cols), act, gp, *n2s, *gbs)


def norm_kernel(at_ref, x_ref, gain_ref, shift_ref, *refs):
    hat, _ = norm_parts(x_ref[...].astype(F32))
    refs[-1][...] = (hat * gain_ref[0:1] + shift_ref[0:1]).astype(BF)


def first_norm(where, x, gains, shifts, rows, held, blk=512):
    part, depth = x.shape
    blk = min(blk, part)
    count = part // blk
    whole = pl.BlockSpec(gains.shape, lambda i, at: (0, 0))
    return pl.pallas_call(
        norm_kernel,
        grid_spec=pltpu.PrefetchScalarGridSpec(
            num_scalar_prefetch=1,
            grid=(count,),
            in_specs=[pl.BlockSpec((blk, depth), lambda i, at: (i, 0)), whole, whole]
            + [pl.BlockSpec(memory_space=pl.ANY)] * len(held),
            out_specs=pl.BlockSpec((blk, depth), lambda i, at: (at[0] * count + i, 0)),
        ),
        out_shape=jax.ShapeDtypeStruct((rows, depth), BF),
        input_output_aliases={4: 0} if held else {},
        compiler_params=pltpu.CompilerParams(vmem_limit_bytes=60 * MIB),
        name="first_norm",
    )(where, x, gains, shifts, *held)


def join_kernel(pick_ref, x_ref, gain_ref, shift_ref, *refs, blocks, each):
    parts, (attn_ref, resid_ref, low_ref) = refs[:-3], refs[-3:]
    block = pl.program_id(0) // each
    total = None
    for g in range(len(parts) // blocks):
        wanted = pick_ref[g * blocks + block]
        part = parts[g * blocks][...]
        for b in range(1, blocks):
            part = jnp.where(wanted == b, parts[g * blocks + b][...], part)
        total = part if total is None else total + part.astype(F32)
    attn_ref[...] = total
    hat, _ = norm_parts(total)
    resid = x_ref[...].astype(F32) + hat * gain_ref[1:2] + shift_ref[1:2]
    resid_ref[...] = resid
    hat, _ = norm_parts(resid)
    low_ref[...] = (hat * gain_ref[2:3] + shift_ref[2:3]).astype(BF)


def join(x, gains, shifts, shares, picks, blk=256):
    rows, depth = x.shape
    blocks = len(shares[0])
    blk = min(blk, rows // blocks)
    each = rows // blocks // blk
    whole = pl.BlockSpec(gains.shape, lambda i, *_: (0, 0))
    block = pl.BlockSpec((blk, depth), lambda i, *_: (i, 0))
    part = pl.BlockSpec((blk, depth), lambda i, *_: (lax.rem(i, each), 0))
    return pl.pallas_call(
        functools.partial(join_kernel, blocks=blocks, each=each),
        grid_spec=pltpu.PrefetchScalarGridSpec(
            num_scalar_prefetch=1,
            grid=(rows // blk,),
            in_specs=[block, whole, whole] + [part] * (len(shares) * blocks),
            out_specs=[block, block, block],
        ),
        out_shape=[
            jax.ShapeDtypeStruct((rows, depth), F32),
            jax.ShapeDtypeStruct((rows, depth), F32),
            jax.ShapeDtypeStruct((rows, depth), BF),
        ],
        compiler_params=pltpu.CompilerParams(vmem_limit_bytes=60 * MIB),
        name="join",
    )(picks, x, gains, shifts, *[v for share in shares for v in share])


def widen_kernel(up_ref, down_ref, dup_ref, ddown_ref):
    dup_ref[...] = jnp.transpose(up_ref[...]).astype(F32)
    ddown_ref[...] = down_ref[...].astype(F32)


def widen(grads, blk=256):
    hidden, depth = grads.shape[0] // 2, grads.shape[1]
    blk = min(blk, hidden)
    count = hidden // blk
    return pl.pallas_call(
        widen_kernel,
        grid=(count,),
        in_specs=[
            pl.BlockSpec((blk, depth), lambda i: (i, 0)),
            pl.BlockSpec((blk, depth), lambda i: (count + i, 0)),
        ],
        out_specs=[
            pl.BlockSpec((depth, blk), lambda i: (0, i)),
            pl.BlockSpec((blk, depth), lambda i: (i, 0)),
        ],
        out_shape=[
            jax.ShapeDtypeStruct((depth, hidden), F32),
            jax.ShapeDtypeStruct((hidden, depth), F32),
        ],
        compiler_params=pltpu.CompilerParams(vmem_limit_bytes=60 * MIB),
        name="widen",
    )(grads, grads)

MESH = pl.DeviceIdType.MESH


def exchange(src, dst, sems, slot, bit):
    peer = lax.axis_index("dp") ^ (1 << bit)
    return pltpu.make_async_remote_copy(
        src_ref=src,
        dst_ref=dst,
        send_sem=sems[0].at[slot],
        recv_sem=sems[1].at[slot],
        device_id={"dp": peer},
        device_id_type=MESH,
    )


def tail_kernel(
    gq_ref, gk_ref, gv_ref, mixed_ref, wq_ref, wk_ref, wv_ref, x_ref, gr_ref, gain_ref, vec_ref, *refs,
    bits, groups, steps,
):
    lefts, refs = refs[: 2 * groups], refs[2 * groups :]
    sum_ref, out_ref, total_ref = refs[:3]
    right, left, weight, x, g_resid, packed, acc, core_buf, buf, sent, came, own_share, vec_buf = refs[3:16]
    send, recv, vec_send, vec_recv, x_send, x_recv, local = refs[16:]
    sems = (send, recv)
    place, me = lax.axis_index("tensor"), lax.axis_index("dp")
    bit = lambda b: lax.rem(lax.div(me, 1 << b), 2)
    core = bit(0)
    order = list(range(1, bits))
    rows, depth = x.shape
    width = weight.shape[2]
    half = 2 * depth
    base = pl.multiple_of(core * half, half)
    part = min(512, depth)
    chunks = half // part
    slots, fetched = iter(range(send.shape[0])), iter(range(local.shape[0]))

    def fetch(src, dst):
        c = pltpu.make_async_copy(src, dst, local.at[next(fetched)])
        c.start()
        return c

    def wait_all(copies):
        for c in copies:
            c.wait()

    second = [fetch(r, right.at[i]) for i, r in enumerate((gq_ref, gk_ref, gv_ref))]
    second += [fetch(r, weight.at[i]) for i, r in enumerate((wq_ref, wk_ref, wv_ref))]
    third = [fetch(r, left.at[i]) for i, r in enumerate(lefts)] + [fetch(mixed_ref, right.at[3])]
    fourth = [fetch(x_ref, x), fetch(gr_ref, g_resid)]

    greeted = [{"dp": me ^ (1 << b)} for b in range(bits)]
    greeted += [{"tensor": lax.rem(place + r, groups)} for r in range(1, groups)]
    known = {frozenset([("dp", b)]) for b in range(bits)} | {
        frozenset([("tensor", b)]) for b in range((groups - 1).bit_length())
    }
    for bits_of in steps:
        for mask in range(1, 1 << len(bits_of)):
            chosen = [bits_of[i] for i in range(len(bits_of)) if mask >> i & 1]
            if frozenset(chosen) not in known and any(axis == "dp" for axis, _ in chosen):
                known.add(frozenset(chosen))
                peer = {}
                for axis, b in chosen:
                    peer[axis] = peer.get(axis, lax.axis_index(axis)) ^ (1 << b)
                greeted.append(peer)
    barrier = pltpu.get_barrier_semaphore()
    for peer in greeted:
        pl.semaphore_signal(barrier, inc=1, device_id=peer, device_id_type=MESH)
    pl.semaphore_wait(barrier, len(greeted))

    def copy(src, dst, b):
        c = exchange(src, dst, sems, next(slots), b)
        c.start()
        return c

    forwards = []
    cores = {}

    def reduce(chunk):
        cores[chunk].wait()

        def join(i, _):
            at = pl.ds(pl.multiple_of(chunk * part + i * 64, 64), 64)
            own = packed[pl.ds(pl.multiple_of(base + chunk * part + i * 64, 64), 64)].astype(F32)
            acc[at] = (own + core_buf[at].astype(F32)).astype(BF)
            return 0

        lax.fori_loop(0, part // 64, join, 0)
        start, size = chunk * part, part
        landing = chunk * (part - part // (1 << (bits - 1)))
        for b in order:
            size //= 2
            away = pl.multiple_of(start + (1 - bit(b)) * size, size)
            c = copy(acc.at[pl.ds(away, size)], buf.at[pl.ds(landing, size)], b)
            start = start + bit(b) * size
            yield
            c.wait()
            step = min(size, 64)

            def body(i, _, start=start, landing=landing, step=step):
                at = pl.ds(pl.multiple_of(start + i * step, step), step)
                got = buf[pl.ds(pl.multiple_of(landing + i * step, step), step)].astype(F32)
                acc[at] = (acc[at].astype(F32) + got).astype(BF)
                return 0

            lax.fori_loop(0, size // step, body, 0)
            landing += size
        start = base + start
        sum_ref[pl.ds(pl.multiple_of(start, size), size)] = acc[pl.ds(pl.multiple_of(start - base, size), size)]
        for b in reversed(order):
            have = sum_ref.at[pl.ds(pl.multiple_of(start, size), size)]
            c = copy(have, have, b)
            yield
            c.wait()
            start = start - bit(b) * size
            size *= 2
        have = sum_ref.at[pl.ds(pl.multiple_of(start, size), size)]
        forwards.append(copy(have, have, 0))

    def share(r, store):
        at = lax.rem(place + r, groups) * rows
        blk = min(256, rows)

        def body(i, _):
            g = pl.ds(pl.multiple_of(at + i * blk, blk), blk)
            value = dotg(right[0, g, :], weight[0], NT)
            value += dotg(right[1, g, :], weight[1], NT)
            value += dotg(right[2, g, :], weight[2], NT)
            store(pl.ds(pl.multiple_of(i * blk, blk), blk), value)
            return 0

        lax.fori_loop(0, rows // blk, body, 0)

    shares = []

    def share_away(r):
        def store(at, value):
            sent[r - 1, at, :] = value.astype(BF)

        share(r, store)
        c = pltpu.make_async_remote_copy(
            src_ref=sent.at[r - 1],
            dst_ref=came.at[r - 1],
            send_sem=x_send.at[r - 1],
            recv_sem=x_recv.at[r - 1],
            device_id={"tensor": lax.rem(place + r, groups)},
            device_id_type=MESH,
        )
        c.start()
        shares.append(c)

    def store_own(at, value):
        own_share[at, :] = value

    def weight_grad(side, some):
        cols = min(256, part)
        each = part // cols

        def body(i, _):
            first = pl.multiple_of(lax.rem(core + side, 2) * half + i * cols, cols)
            number = lax.div(first, depth)
            kind = lax.div(number, 3) * groups
            lanes = pl.ds(pl.multiple_of(lax.rem(first, depth), cols), cols)
            value = None
            for r in range(groups):
                at = pl.ds(pl.multiple_of(lax.rem(place + r, groups) * rows, rows), rows)
                term = dotg(left[kind + r, :, lanes], right[number, at, :], TN)
                value = term if value is None else value + term
            packed[pl.ds(first, cols), :] = value.astype(BF)
            return 0

        lax.fori_loop(some[0] * each, (some[-1] + 1) * each, body, 0)
        if side:
            for c in some:
                at = pl.ds(pl.multiple_of((1 - core) * half + c * part, part), part)
                cores[c] = copy(packed.at[at], core_buf.at[pl.ds(c * part, part)], 0)

    def last_norm():
        blk = min(64, rows)

        def body(i, _):
            at = pl.ds(pl.multiple_of(i * blk, blk), blk)
            value = own_share[at, :]
            for r in range(groups - 1):
                value += came[r, at, :].astype(F32)
            hat, scale = norm_parts(x[at, :].astype(F32))
            out_ref[at, :] = (g_resid[at, :] + norm_back(value, hat, scale, gain_ref[0:1])).astype(BF)
            total_ref[0:1] += column_sum(value * hat)
            total_ref[1:2] += column_sum(value)
            return 0

        lax.fori_loop(0, rows // blk, body, 0)

    def vectors():
        slot = 0
        for bits_of in steps:
            sends = []
            for mask in range(1, 1 << len(bits_of)):
                peer = {}
                for i, (axis, b) in enumerate(bits_of):
                    if mask >> i & 1:
                        peer[axis] = peer.get(axis, lax.axis_index(axis)) ^ (1 << b)
                sends.append(
                    pltpu.make_async_remote_copy(
                        src_ref=total_ref,
                        dst_ref=vec_buf.at[slot],
                        send_sem=vec_send.at[slot],
                        recv_sem=vec_recv.at[slot],
                        device_id=peer,
                        device_id_type=MESH,
                    )
                )
                sends[-1].start()
                slot += 1
            yield
            wait_all(sends)
            total = total_ref[...]
            for i in range(len(sends)):
                total += vec_buf[slot - len(sends) + i]
            total_ref[...] = total

    def turn(chains):
        still = []
        for chain in chains:
            try:
                next(chain)
                still.append(chain)
            except StopIteration:
                pass
        return still

    wait_all(second)
    for r in range(1, groups):
        share_away(r)
    wait_all(third)
    all_chunks = list(range(chunks))
    for some in (all_chunks[: chunks // 2], all_chunks[chunks // 2 :]):
        weight_grad(1, some)
    reduces = []
    for chunk in all_chunks:
        weight_grad(0, [chunk])
        reduces = turn(reduces + [reduce(chunk)])
    share(0, store_own)
    reduces = turn(reduces)
    wait_all(fourth)
    wait_all(shares)
    total_ref[...] = vec_ref[...]
    last_norm()
    chain = turn([vectors()])
    while reduces or chain:
        reduces, chain = turn(reduces), turn(chain)
    wait_all(forwards)


def tail(grads, mixed, weights, x, g_resid, gains, vectors, n1s, gas, bits, steps):
    (slots, width), (rows, depth), groups = mixed.shape, x.shape, len(n1s)
    half = 2 * depth
    landing = half - half // (1 << (bits - 1))
    count = half // min(512, depth) * (2 * bits + 1)
    vecs = sum((1 << len(b)) - 1 for b in steps)
    vmem = pl.BlockSpec(memory_space=pltpu.VMEM)
    anyspace = pl.BlockSpec(memory_space=pl.ANY)
    dma = pltpu.SemaphoreType.DMA
    peers = max(groups - 1, 1)
    return pl.pallas_call(
        functools.partial(tail_kernel, bits=bits, groups=groups, steps=steps),
        in_specs=[anyspace] * 9 + [vmem] * 2 + [anyspace] * (2 * groups),
        out_specs=[vmem, vmem, vmem],
        out_shape=[
            jax.ShapeDtypeStruct((4 * depth, width), BF),
            jax.ShapeDtypeStruct((rows, depth), BF),
            jax.ShapeDtypeStruct(vectors.shape, F32),
        ],
        scratch_shapes=[
            pltpu.VMEM((4, slots, width), BF),
            pltpu.VMEM((2 * groups, rows, depth), BF),
            pltpu.VMEM((3, depth, width), BF),
            pltpu.VMEM((rows, depth), BF),
            pltpu.VMEM((rows, depth), F32),
            pltpu.VMEM((4 * depth, width), BF),
            pltpu.VMEM((half, width), BF),
            pltpu.VMEM((half, width), BF),
            pltpu.VMEM((landing, width), BF),
            pltpu.VMEM((peers, rows, depth), BF),
            pltpu.VMEM((peers, rows, depth), BF),
            pltpu.VMEM((rows, depth), F32),
            pltpu.VMEM((vecs,) + vectors.shape, F32),
            dma((count,)),
            dma((count,)),
            dma((vecs,)),
            dma((vecs,)),
            dma((peers,)),
            dma((peers,)),
            dma((9 + 2 * groups,)),
        ],
        compiler_params=pltpu.CompilerParams(
            collective_id=1, has_side_effects=True, vmem_limit_bytes=60 * MIB
        ),
        cost_estimate=pl.CostEstimate(flops=rows * width, bytes_accessed=rows * width, transcendentals=0),
        name="tail",
    )(*grads, mixed, *weights, x, g_resid, gains, vectors, *n1s, *gas)


def mixed_back_kernel(at_ref, x_ref, w_ref, *refs):
    refs[-1][...] = dotg(x_ref[...], w_ref[...], NT).astype(BF)


def mixed_back(where, x, w_out, slots, held, blk=256):
    rows, depth = x.shape
    width = w_out.shape[0]
    blk = min(blk, rows)
    count = rows // blk
    return pl.pallas_call(
        mixed_back_kernel,
        grid_spec=pltpu.PrefetchScalarGridSpec(
            num_scalar_prefetch=1,
            grid=(count,),
            in_specs=[
                pl.BlockSpec((blk, depth), lambda i, at: (i, 0)),
                pl.BlockSpec((width, depth), lambda i, at: (0, 0)),
            ]
            + [pl.BlockSpec(memory_space=pl.ANY)] * len(held),
            out_specs=pl.BlockSpec((blk, width), lambda i, at: (at[0] * count + i, 0)),
        ),
        out_shape=jax.ShapeDtypeStruct((slots, width), BF),
        input_output_aliases={3: 0} if held else {},
        compiler_params=pltpu.CompilerParams(vmem_limit_bytes=60 * MIB),
        cost_estimate=pl.CostEstimate(flops=rows * depth, bytes_accessed=rows * depth, transcendentals=0),
        name="mixed_back",
    )(where, x, w_out, *held)


def shift(x, axis, count, step):
    return lax.ppermute(x, axis, [((i + step) % count, i) for i in range(count)])


def shards(
    tokens,
    lengths,
    cotangent,
    w_query,
    w_key,
    w_value,
    w_out,
    up_weight,
    bias_up,
    down_weight,
    bias_down,
    norm_gains,
    norm_shifts,
):
    rows, _, depth = tokens.shape
    groups, replicas = lax.axis_size("tensor"), lax.axis_size("dp")
    me, replica = lax.axis_index("tensor"), lax.axis_index("dp")
    slots = rows * groups
    width = w_query.shape[1]
    hidden = up_weight.shape[1]
    x = tokens.reshape(rows, depth)
    here = me.reshape(1).astype(jnp.int32)
    place = lambda r: (here + r) % groups

    def others(v):
        return [shift(v, "tensor", groups, r) for r in range(1, groups)]

    def to_owner(v, r):
        return shift(v, "tensor", groups, groups - r)

    up_piece = lax.dynamic_slice_in_dim(up_weight, replica * (depth // replicas), depth // replicas, 0)
    down_piece = lax.dynamic_slice_in_dim(
        down_weight, replica * (hidden // replicas), hidden // replicas, 0
    )
    gather = lambda v: lax.all_gather(v, "dp", axis=0, tiled=True)

    freqs = 10000.0 ** (-jnp.arange(HD // 2).astype(F32) * 2.0 / HD)
    angles = jnp.arange(slots).astype(F32)[:, None] * freqs[None, :]
    cosine, sine = jnp.cos(angles), jnp.sin(angles)
    cosine = jnp.concatenate([cosine] * 4, axis=1)
    sine = jnp.concatenate([-sine, sine] * 2, axis=1)
    halves = 2
    index = lambda k: jnp.full((1,), k, jnp.int32)
    x_rest = [others(v) for v in jnp.split(x, halves)]
    normed_one = first_norm(index(0), x, norm_gains, norm_shifts, rows, [])
    up_pieces = others(up_piece)
    weights = (w_query, w_key, w_value)
    joint = project(here, normed_one, *weights, cosine, sine)
    normed_one_rest = [[] for _ in range(1, groups)]
    for k in range(halves):
        pieces = (down_piece, bias_up) if k == halves - 1 else up_pieces
        joint, x_rest[k], pieces = lax.optimization_barrier((joint, x_rest[k], pieces))
        if k < halves - 1:
            up_pieces = pieces
        else:
            down_pieces, bias_rest = (others(v) for v in pieces)
        for r in range(1, groups):
            n = first_norm(index(k), x_rest[k][r - 1], norm_gains, norm_shifts, rows, normed_one_rest[r - 1])
            normed_one_rest[r - 1] = [n]
            joint = project(place(r), n, *weights, cosine, sine, joint, k, halves)
    normed_one_rest = [v[0] for v in normed_one_rest]
    blk = min(512, rows)
    each = rows // blk
    odd = lambda r: lax.rem(place(r), 2)
    ranks = lambda r, k: jnp.where(odd(r) == 1, each - 1 - k, k)
    held, shares, arrived = (), [], [[] for _ in range(1, groups)]
    for k in range(each):
        for r in range(1, groups):
            *held, share = attend(place(r) * each + ranks(0, k), lengths, joint, w_out, held, BF, blk)
            arrived[r - 1].append(to_owner(share, r))
        if k == 0:
            joint, down_pieces, bias_rest = lax.optimization_barrier((joint, down_pieces, bias_rest))
        if k == each - 1 and k > 0:
            joint, arrived = lax.optimization_barrier((joint, [v[:k] for v in arrived])), arrived
            joint, early = joint
            arrived = [list(e) + v[k:] for e, v in zip(early, arrived)]
        *held, share = attend(here * each + ranks(0, k), lengths, joint, w_out, held, F32, blk)
        shares.append(share)
    mixed, lse = held
    shares = [shares] + arrived
    picks = jnp.concatenate([ranks(groups - r, k) for r in range(groups) for k in range(each)])
    up_rest, down_rest = [gather(p) for p in up_pieces], [gather(p) for p in down_pieces]
    biases = jnp.concatenate([bias_up] + bias_rest).astype(F32)

    info = jnp.stack([lengths[0], me * rows]).astype(jnp.int32)
    cot = cotangent.reshape(rows, depth)
    attn_sum, resid, normed_two = join(x, norm_gains, norm_shifts, shares, picks)
    normed_two_rest = others(normed_two)
    slope, act, branch = feed(
        info, normed_two, biases[:hidden], [up_weight], [down_weight], own=bias_down.reshape(1, depth)
    )
    slope_rest, layer_out, g_branch, sums3 = feed(
        info, normed_two, biases[hidden:], up_rest, down_rest, rest=(branch, resid, cot, norm_gains, norm_shifts)
    )
    ups, downs = [up_weight] + up_rest, [down_weight] + down_rest
    g_branch_rest = others(g_branch)
    g_pre, g_resid, g_attn, sums21 = feed_back(
        info, g_branch, slope, slope_rest, ups, downs, resid, attn_sum, cot, norm_gains
    )
    g_attn_rest = others(g_attn)
    g_pre, normed_two_rest = lax.optimization_barrier((g_pre, normed_two_rest))
    g_mixed = mixed_back(here, g_attn, w_out, slots, [])
    g_pre, g_mixed = lax.optimization_barrier((g_pre, g_mixed))
    grad_feed, bias_up_sum = feed_grad(
        up_weight, down_weight, biases[:hidden], act, g_pre,
        [normed_two] + normed_two_rest, [g_branch] + g_branch_rest,
    )
    grad_feed = grad_feed.reshape(2 * hidden, depth)
    g_mixed, g_attn_rest, grad_feed = lax.optimization_barrier((g_mixed, g_attn_rest, grad_feed))
    grad_feed = lax.psum(grad_feed, "dp")
    for r, g in enumerate(g_attn_rest):
        g_mixed = mixed_back(place(r + 1), g, w_out, slots, [g_mixed])

    grads = attend_back(lengths, joint, mixed, g_mixed, lse, cosine, sine, width)
    placed = lax.dynamic_update_slice(
        jnp.zeros((groups * hidden,), F32), bias_up_sum.reshape(-1), (me * hidden,)
    ).reshape(-1, depth)
    bits = (replicas - 1).bit_length()
    steps = [("tensor", b) for b in range((groups - 1).bit_length())] + [("dp", b) for b in range(bits)]
    steps = [tuple(steps[i : i + 2]) for i in range(0, len(steps), 2)]
    vectors = jnp.concatenate([jnp.zeros((2, depth), F32), sums3[:3], sums21[:4], placed])
    vectors = jnp.pad(vectors, ((0, -len(vectors) % 8), (0, 0)))
    packed, grad_tokens, sums = tail(
        grads, mixed, weights, x, g_resid, norm_gains, vectors,
        [normed_one] + normed_one_rest, [g_attn] + g_attn_rest, bits, steps,
    )
    grad_up, grad_down = widen(grad_feed)
    grad_query, grad_key, grad_value = (packed[i * depth : (i + 1) * depth].astype(F32) for i in range(3))
    grad_out = jnp.transpose(packed[3 * depth :]).astype(F32)
    grad_gains = jnp.stack([sums[0], sums[7], sums[5], sums[2]])
    grad_shifts = jnp.stack([sums[1], sums[8], sums[6], sums[3]])
    grad_bias_up = lax.dynamic_slice_in_dim(sums[9 : 9 + groups * hidden // depth].reshape(-1), me * hidden, hidden, 0)
    whole = (rows, 1, depth)
    return (
        layer_out.reshape(whole),
        grad_tokens.reshape(whole),
        grad_query,
        grad_key,
        grad_value,
        grad_out,
        grad_up,
        grad_bias_up,
        grad_down,
        sums[4],
        grad_gains,
        grad_shifts,
    )


def solution(mesh):
    wide, tall = P(None, "tensor"), P("tensor", None)
    acts = P("tensor", "dp", None)
    return jax.shard_map(
        shards,
        mesh=mesh,
        in_specs=(acts, P("dp"), acts, wide, wide, wide, tall, wide, P("tensor"), tall, P(), P(), P()),
        out_specs=(acts, acts, wide, wide, wide, tall, wide, P("tensor"), tall, P(), P(), P()),
        check_vma=False,
    )
```

```python
import functools
import jax
import jax.numpy as jnp
from jax import lax
from jax.experimental import pallas as pl
from jax.experimental.pallas import tpu as pltpu
from jax.sharding import PartitionSpec as P

HD = 64
EPSILON = 1e-05
BF = jnp.bfloat16
F32 = jnp.float32
NT = (((1,), (1,)), ((), ()))
NN = (((1,), (0,)), ((), ()))
TN = (((0,), (0,)), ((), ()))
MIB = 1 << 20


def dotg(a, b, dims=NN):
    return lax.dot_general(a, b, dims, preferred_element_type=F32)


def rotate(x, cos, sin):
    first = lax.broadcasted_iota(jnp.int32, (x.shape[0], 128), 1) % HD < HD // 2
    parts = []
    for a in range(0, x.shape[1], 128):
        v = x[:, a : a + 128]
        swapped = jnp.where(first, pltpu.roll(v, 96, 1), pltpu.roll(v, 32, 1))
        parts.append(v * cos + swapped * sin)
    return jnp.concatenate(parts, axis=1) if len(parts) > 1 else parts[0]


def qkv_kernel(x_ref, wq_ref, wk_ref, wv_ref, cos_ref, sin_ref, o_ref):
    width = wq_ref.shape[1]
    x, cos, sin = x_ref[...], cos_ref[...], sin_ref[...]
    o_ref[:, :width] = rotate(dotg(x, wq_ref[...]), cos, sin).astype(BF)
    o_ref[:, width : 2 * width] = rotate(dotg(x, wk_ref[...]), cos, sin).astype(BF)
    o_ref[:, 2 * width :] = dotg(x, wv_ref[...]).astype(BF)


def project(where, x, w_query, w_key, w_value, cos, sin, joint=None, blk=256):
    rows, depth = x.shape
    width, slots = w_query.shape[1], cos.shape[0]
    blk = min(blk, rows)
    count = rows // blk
    weight = pl.BlockSpec((depth, width), lambda i, at: (0, 0))
    angle = pl.BlockSpec((blk, 128), lambda i, at: (at[0] * count + i, 0))
    kernel = lambda at, *refs: qkv_kernel(*refs[:6], refs[-1])
    held = [] if joint is None else [joint]
    return pl.pallas_call(
        kernel,
        grid_spec=pltpu.PrefetchScalarGridSpec(
            num_scalar_prefetch=1,
            grid=(count,),
            in_specs=[pl.BlockSpec((blk, depth), lambda i, at: (i, 0)), weight, weight, weight, angle, angle]
            + [pl.BlockSpec(memory_space=pl.ANY)] * len(held),
            out_specs=pl.BlockSpec((blk, 3 * width), lambda i, at: (at[0] * count + i, 0)),
        ),
        out_shape=jax.ShapeDtypeStruct((slots, 3 * width), BF),
        input_output_aliases={7: 0} if held else {},
        compiler_params=pltpu.CompilerParams(vmem_limit_bytes=60 * MIB),
        cost_estimate=pl.CostEstimate(flops=rows * depth, bytes_accessed=rows * depth, transcendentals=0),
        name="project",
    )(where, x, w_query, w_key, w_value, cos, sin, *held)


def attend_kernel(at_ref, len_ref, q_ref, k_ref, v_ref, w_ref, *refs, blk):
    o_ref, lse_ref, share_ref, vt, low_ref = refs[-5:]
    pair = pl.program_id(0)
    i = at_ref[0]
    length = len_ref[0]
    def turn(j, _):
        part = pl.ds(pl.multiple_of(j * blk, blk), blk)
        vt[:, part] = jnp.transpose(v_ref[part, :])
        return 0

    lax.fori_loop(0, i + 1, turn, 0)
    lane = lax.broadcasted_iota(jnp.int32, (blk, 128), 1)
    q = q_ref[...] * jnp.asarray(0.125, BF)
    zero = jnp.zeros_like(q)
    qs = (jnp.where(lane < HD, q, zero), jnp.where(lane < HD, zero, q))

    def step(j, carry, diag):
        start = pl.multiple_of(j * blk, blk)
        kb = k_ref[pl.ds(start, blk), :]
        sub = min(256, blk)
        n = blk // sub
        if diag:
            key = lax.broadcasted_iota(jnp.int32, (sub, blk), 0)
            qry = lax.broadcasted_iota(jnp.int32, (sub, blk), 1)
        state = [carry[h] for h in range(2)]
        chains = [(h, t) for t in range(n) for h in range(2)]
        live = {}

        def first(c):
            h, t = chains[c]
            live[c] = dotg(kb[t * sub : t * sub + sub], qs[h], NT)

        def middle(c):
            h, t = chains[c]
            s = live[c]
            if diag:
                s = jnp.where((key + t * sub <= qry) & (key + t * sub + start < length), s, -1e30)
            m, l, acc = state[h]
            mn = jnp.maximum(m, jnp.max(s, axis=0, keepdims=True))
            p = jnp.exp(s - mn)
            al = jnp.exp(m - mn)
            state[h] = (mn, l * al + jnp.sum(p, axis=0, keepdims=True), acc)
            live[c] = (p.astype(BF), al)

        def last(c):
            h, t = chains[c]
            p, al = live.pop(c)
            m, l, acc = state[h]
            state[h] = (m, l, acc * al + dotg(vt[HD * h : HD * h + HD, pl.ds(start + t * sub, sub)], p))

        stages = (first, middle, last)
        for i in range(len(chains) + 4):
            for k in range(3):
                c = i - 2 * k
                if 0 <= c < len(chains):
                    stages[k](c)
        return tuple(state)

    init = tuple(
        (jnp.full((1, blk), -1e30, F32), jnp.zeros((1, blk), F32), jnp.zeros((HD, blk), F32))
        for _ in range(2)
    )
    c = lax.fori_loop(0, i, lambda j, c: step(j, c, False), init)
    c = step(i, c, True)
    ot = jnp.concatenate([c[h][2] / c[h][1] for h in range(2)], axis=0)
    low = jnp.transpose(ot).astype(BF)
    o_ref[...] = low
    lse_ref[0] = jnp.concatenate([c[h][0] + jnp.log(c[h][1]) for h in range(2)], axis=0)
    low_ref[pair] = low

    @pl.when(pair == pl.num_programs(0) - 1)
    def _():
        pairs = low_ref.shape[0]
        low = jnp.concatenate([low_ref[p] for p in range(pairs)], axis=1)
        share_ref[...] = dotg(low, w_ref[...]).astype(share_ref.dtype)


def attend(at, length, joint, w_out, held, kind, blk):
    rows, width, depth = joint.shape[0], w_out.shape[0], w_out.shape[1]
    pairs = width // 128
    return pl.pallas_call(
        functools.partial(attend_kernel, blk=blk),
        grid_spec=pltpu.PrefetchScalarGridSpec(
            num_scalar_prefetch=2,
            grid=(pairs,),
            in_specs=[
                pl.BlockSpec((blk, 128), lambda p, at, *_: (at[0], p)),
                pl.BlockSpec((rows, 128), lambda p, *_: (0, pairs + p)),
                pl.BlockSpec((rows, 128), lambda p, *_: (0, 2 * pairs + p)),
                pl.BlockSpec((width, depth), lambda p, *_: (0, 0), pipeline_mode=pl.Buffered(1)),
            ]
            + [pl.BlockSpec(memory_space=pl.ANY)] * len(held),
            out_specs=[
                pl.BlockSpec((blk, 128), lambda p, at, *_: (at[0], p)),
                pl.BlockSpec((1, 2, blk), lambda p, at, *_: (p, 0, at[0])),
                pl.BlockSpec((blk, depth), lambda p, *_: (0, 0)),
            ],
            scratch_shapes=[pltpu.VMEM((128, rows), BF), pltpu.VMEM((pairs, blk, 128), BF)],
        ),
        out_shape=[
            jax.ShapeDtypeStruct((rows, width), BF),
            jax.ShapeDtypeStruct((pairs, 2, rows), F32),
            jax.ShapeDtypeStruct((blk, depth), kind),
        ],
        input_output_aliases={6: 0, 7: 1} if held else {},
        compiler_params=pltpu.CompilerParams(vmem_limit_bytes=60 * MIB),
        cost_estimate=pl.CostEstimate(flops=rows * width, bytes_accessed=rows * width, transcendentals=0),
        name="attend",
    )(at, length, joint, joint, joint, w_out, *held)


def attend_back_kernel(
    len_ref, q_ref, k_ref, v_ref, o_ref, do_ref, lse_ref, cos_ref, sin_ref,
    dq_ref, dk_ref, dv_ref, kt, dlt, dqt, *, blk, blocks,
):
    length = len_ref[0]
    kt[...] = jnp.transpose(k_ref[...])
    dqt[...] = jnp.zeros_like(dqt)

    def products(i, _):
        at = pl.ds(pl.multiple_of(i * blk, blk), blk)
        both = jnp.transpose(do_ref[at, :].astype(F32) * o_ref[at, :].astype(F32))
        for h in range(2):
            dlt[h : h + 1, at] = jnp.sum(both[HD * h : HD * h + HD], axis=0, keepdims=True)
        return 0

    lax.fori_loop(0, blocks, products, 0)

    def keys(j, _):
        attend_back_keys(
            j, length, q_ref, k_ref, v_ref, do_ref, lse_ref, cos_ref, sin_ref, dk_ref, dv_ref, kt, dlt, dqt, blk, blocks
        )
        return 0

    lax.fori_loop(0, blocks, keys, 0)

    def turn(i, _):
        at = pl.ds(pl.multiple_of(i * blk, blk), blk)
        grad = jnp.transpose(dqt[:, at]) * 0.125
        dq_ref[at, :] = rotate(grad, cos_ref[at, :], -sin_ref[at, :]).astype(BF)
        return 0

    lax.fori_loop(0, blocks, turn, 0)


def attend_back_keys(
    j, length, q_ref, k_ref, v_ref, do_ref, lse_ref, cos_ref, sin_ref, dk_ref, dv_ref, kt, dlt, dqt, blk, blocks
):
    js = pl.multiple_of(j * blk, blk)
    lane = lax.broadcasted_iota(jnp.int32, (blk, 128), 1)
    kb = k_ref[pl.ds(js, blk), :] * jnp.asarray(0.125, BF)
    vb = v_ref[pl.ds(js, blk), :]
    zero = jnp.zeros_like(kb)
    ks = (jnp.where(lane < HD, kb, zero), jnp.where(lane < HD, zero, kb))
    vs = (jnp.where(lane < HD, vb, zero), jnp.where(lane < HD, zero, vb))

    def step(i, carry, diag):
        at = pl.ds(pl.multiple_of(i * blk, blk), blk)
        qb, dob = q_ref[at, :], do_ref[at, :]
        out = []
        for h in range(2):
            dk, dv = carry[h]
            s = dotg(ks[h], qb, NT)
            if diag:
                key = lax.broadcasted_iota(jnp.int32, (blk, blk), 0)
                qry = lax.broadcasted_iota(jnp.int32, (blk, blk), 1)
                s = jnp.where((key <= qry) & (key + js < length), s, -1e30)
            p = jnp.exp(s - lse_ref[0, h : h + 1, at])
            dp = dotg(vs[h], dob, NT)
            ds = (p * (dp - dlt[h : h + 1, at])).astype(BF)
            dv = dv + dotg(p.astype(BF), dob)
            dk = dk + dotg(ds, qb)
            dqt[HD * h : HD * h + HD, at] += dotg(kt[HD * h : HD * h + HD, pl.ds(js, blk)], ds)
            out.append((dk, dv))
        return tuple(out)

    z = jnp.zeros((blk, 128), F32)
    c = step(j, ((z, z), (z, z)), True)
    c = lax.fori_loop(j + 1, blocks, lambda i, c: step(i, c, False), c)
    grad = jnp.where(lane < HD, c[0][0], c[1][0]) * 0.125
    dk_ref[pl.ds(js, blk), :] = rotate(grad, cos_ref[pl.ds(js, blk), :], -sin_ref[pl.ds(js, blk), :]).astype(BF)
    dv_ref[pl.ds(js, blk), :] = jnp.where(lane < HD, c[0][1], c[1][1]).astype(BF)


def attend_back(length, joint, mixed, dmixed, lse, cos, sin, width, blk=512):
    rows = joint.shape[0]
    pairs, blocks = width // 128, rows // blk
    full = lambda off: pl.BlockSpec((rows, 128), lambda p, *_: (0, off * pairs + p))
    angle = pl.BlockSpec((rows, 128), lambda p, *_: (0, 0))
    return pl.pallas_call(
        functools.partial(attend_back_kernel, blk=blk, blocks=blocks),
        grid_spec=pltpu.PrefetchScalarGridSpec(
            num_scalar_prefetch=1,
            grid=(pairs,),
            in_specs=[full(0), full(1), full(2), full(0), full(0)]
            + [pl.BlockSpec((1, 2, rows), lambda p, *_: (p, 0, 0)), angle, angle],
            out_specs=[full(0)] * 3,
            scratch_shapes=[
                pltpu.VMEM((128, rows), BF),
                pltpu.VMEM((2, rows), F32),
                pltpu.VMEM((128, rows), F32),
            ],
        ),
        out_shape=[jax.ShapeDtypeStruct((rows, width), BF)] * 3,
        compiler_params=pltpu.CompilerParams(vmem_limit_bytes=60 * MIB),
        cost_estimate=pl.CostEstimate(
            flops=rows * width, bytes_accessed=rows * width, transcendentals=0
        ),
        name="attend_back",
    )(length, joint, joint, joint, mixed, dmixed, lse, cos, sin)


def gelu_parts(v):
    c = 0.7978845608028654
    return c, jnp.tanh(c * (v + 0.044715 * v * v * v))


def gelu_both(v):
    c, t = gelu_parts(v)
    half = 0.5 * (1.0 + t)
    return v * half, half + 0.5 * v * (1.0 - t * t) * c * (1.0 + 3 * 0.044715 * v * v)


def norm_parts(values):
    average = jnp.mean(values, axis=-1, keepdims=True)
    centred = values - average
    scale = lax.rsqrt(jnp.mean(centred * centred, axis=-1, keepdims=True) + EPSILON)
    return centred * scale, scale


def norm_back(grad, hat, scale, gain):
    g = grad * gain
    return scale * (
        g - jnp.mean(g, axis=-1, keepdims=True) - hat * jnp.mean(g * hat, axis=-1, keepdims=True)
    )


def column_sum(v):
    return jnp.sum(v, axis=0, keepdims=True)


def valid_rows(info_ref, start, count):
    at = info_ref[1] + start + lax.broadcasted_iota(jnp.int32, (count, 1), 0)
    return (at < info_ref[0]).astype(F32)


def loop_rows(rows, blk, body):
    def step(i, _):
        body(pl.multiple_of(i * blk, blk))
        return 0

    lax.fori_loop(0, rows // blk, step, 0)


def feed_kernel(info_ref, *refs, groups, chunks, sub, own):
    x_ref, bias_ref = refs[:2]
    ups, downs, refs = refs[2 : 2 + groups], refs[2 + groups : 2 + 2 * groups], refs[2 + 2 * groups :]
    step = pl.program_id(0)
    rows = x_ref.shape[0]
    if own:
        bd_ref, slope_ref, act_ref, acc = refs
        late = []
    else:
        resid_hbm, cot_hbm, before_hbm, gain_ref, shift_ref = refs[:5]
        slope_ref, out_ref, gb_ref, sums_ref, acc, resid_ref, before_ref, cot_ref, sems = refs[5:]
        late = [
            pltpu.make_async_copy(resid_hbm, resid_ref, sems.at[0]),
            pltpu.make_async_copy(cot_hbm, cot_ref, sems.at[1]),
            pltpu.make_async_copy(before_hbm, before_ref, sems.at[2]),
        ]

    @pl.when(step == 0)
    def _():
        acc[...] = jnp.zeros_like(acc) + bd_ref[...].astype(F32) if own else jnp.zeros_like(acc)
        for c in late:
            c.start()

    for g in range(groups):

        @pl.when(step // chunks == g)
        def _():
            for r in range(0, rows, sub):
                act, slope = gelu_both(dotg(x_ref[r : r + sub], ups[g][...]) + bias_ref[0])
                slope_ref[r : r + sub] = slope.astype(BF)
                act = act.astype(BF)
                if own:
                    act_ref[r : r + sub] = act
                acc[r : r + sub] += dotg(act, downs[g][...])

    if own:
        return

    @pl.when(step == groups * chunks - 1)
    def _():
        for c in late:
            c.wait()
        sums_ref[...] = jnp.zeros_like(sums_ref)
        gain, shift = gain_ref[3:4], shift_ref[3:4]
        blk = min(256, rows)

        def body(r):
            at = pl.ds(r, blk)
            valid = valid_rows(info_ref, r, blk)
            hat, scale = norm_parts(acc[at] + before_ref[at])
            out_ref[at] = (valid * (resid_ref[at] + hat * gain + shift)).astype(BF)
            g_out = valid * cot_ref[at].astype(F32)
            low = norm_back(g_out, hat, scale, gain).astype(BF)
            gb_ref[at] = low
            sums_ref[0:1] += column_sum(g_out * hat)
            sums_ref[1:2] += column_sum(g_out)
            sums_ref[2:3] += column_sum(low.astype(F32))

        loop_rows(rows, blk, body)


def feed(info, x, biases, ups, downs, own=None, rest=None, cols=512):
    rows, depth = x.shape
    groups, hidden = len(ups), ups[0].shape[1]
    chunks = hidden // cols
    once = lambda shape: pl.BlockSpec(shape, lambda s, *_: (0, 0), pipeline_mode=pl.Buffered(1))
    anyspace = pl.BlockSpec(memory_space=pl.ANY)
    part = lambda g: (lambda s, *_: (0, jnp.clip(s - g * chunks, 0, chunks - 1)))
    part_t = lambda g: (lambda s, *_: (jnp.clip(s - g * chunks, 0, chunks - 1), 0))
    wide = pl.BlockSpec((rows, cols), lambda s, *_: (0, s))
    low = jax.ShapeDtypeStruct((rows, depth), BF)
    slope = jax.ShapeDtypeStruct((rows, groups * hidden), BF)
    if rest is None:
        more, args = [once((1, depth))], [own]
        out_specs = [wide, wide, once((rows, depth))]
        out_shape = [slope, slope, jax.ShapeDtypeStruct((rows, depth), F32)]
        scratch = []
    else:
        before, resid, cot, gains, shifts = rest
        more, args = [anyspace] * 3 + [once(gains.shape)] * 2, [resid, cot, before, gains, shifts]
        out_specs = [wide, once((rows, depth)), once((rows, depth)), once((8, depth))]
        out_shape = [slope, low, low, jax.ShapeDtypeStruct((8, depth), F32)]
        scratch = [
            pltpu.VMEM((rows, depth), F32),
            pltpu.VMEM((rows, depth), F32),
            pltpu.VMEM((rows, depth), F32),
            pltpu.VMEM((rows, depth), BF),
            pltpu.SemaphoreType.DMA((3,)),
        ]
    return pl.pallas_call(
        functools.partial(feed_kernel, groups=groups, chunks=chunks, sub=min(512, rows), own=rest is None),
        grid_spec=pltpu.PrefetchScalarGridSpec(
            num_scalar_prefetch=1,
            grid=(groups * chunks,),
            in_specs=[once((rows, depth)), pl.BlockSpec((1, 1, cols), lambda s, *_: (s, 0, 0))]
            + [pl.BlockSpec((depth, cols), part(g)) for g in range(groups)]
            + [pl.BlockSpec((cols, depth), part_t(g)) for g in range(groups)]
            + more,
            out_specs=out_specs,
            scratch_shapes=scratch,
        ),
        out_shape=out_shape,
        compiler_params=pltpu.CompilerParams(vmem_limit_bytes=60 * MIB),
        cost_estimate=pl.CostEstimate(flops=rows * depth, bytes_accessed=rows * depth, transcendentals=0),
        name="feed",
    )(info, x, biases.reshape(-1, 1, cols), *ups, *downs, *args)


def feed_back_kernel(info_ref, *refs, groups, chunks, sub):
    gb_ref, own_slope, rest_slope, resid_hbm, attn_hbm, cot_hbm, gain_ref = refs[:7]
    ups, downs = refs[7 : 7 + groups], refs[7 + groups : 7 + 2 * groups]
    gp_ref, gr_ref, ga_ref, sums_ref, acc, resid_ref, attn_ref, cot_ref, sems = refs[7 + 2 * groups :]
    step = pl.program_id(0)
    rows = gb_ref.shape[0]
    late = [
        pltpu.make_async_copy(src, dst, sems.at[i])
        for i, (src, dst) in enumerate(((resid_hbm, resid_ref), (attn_hbm, attn_ref), (cot_hbm, cot_ref)))
    ]

    @pl.when(step == 0)
    def _():
        for c in late:
            c.start()
        acc[...] = jnp.zeros_like(acc)

    for g in range(groups):

        @pl.when(step // chunks == g)
        def _():
            for r in range(0, rows, sub):
                grad = dotg(gb_ref[r : r + sub], downs[g][...], NT)
                slope_ref = rest_slope if g else own_slope
                low = (grad * slope_ref[r : r + sub].astype(F32)).astype(BF)
                if g == 0:
                    gp_ref[r : r + sub] = low
                acc[r : r + sub] += dotg(low, ups[g][...], NT)

    @pl.when(step == groups * chunks - 1)
    def _():
        for c in late:
            c.wait()
        sums_ref[...] = jnp.zeros_like(sums_ref)
        blk = min(256, rows)

        def body(r):
            at = pl.ds(r, blk)
            g_out = valid_rows(info_ref, r, blk) * cot_ref[at].astype(F32)
            hat, scale = norm_parts(resid_ref[at])
            g_two = acc[at]
            g_resid = g_out + norm_back(g_two, hat, scale, gain_ref[2:3])
            gr_ref[at] = g_resid
            sums_ref[0:1] += column_sum(g_two * hat)
            sums_ref[1:2] += column_sum(g_two)
            hat, scale = norm_parts(attn_ref[at])
            ga_ref[at] = norm_back(g_resid, hat, scale, gain_ref[1:2]).astype(BF)
            sums_ref[2:3] += column_sum(g_resid * hat)
            sums_ref[3:4] += column_sum(g_resid)

        loop_rows(rows, blk, body)


def feed_back(info, gb, own_slope, rest_slope, ups, downs, resid, attn_sum, cot, gains, cols=512):
    rows, depth = gb.shape
    groups, hidden = len(ups), ups[0].shape[1]
    chunks = hidden // cols
    once = lambda shape: pl.BlockSpec(shape, lambda s, *_: (0, 0), pipeline_mode=pl.Buffered(1))
    anyspace = pl.BlockSpec(memory_space=pl.ANY)
    own = lambda g: (lambda s, *_: (0, jnp.clip(s - g * chunks, 0, chunks - 1)))
    own_t = lambda g: (lambda s, *_: (jnp.clip(s - g * chunks, 0, chunks - 1), 0))
    return pl.pallas_call(
        functools.partial(feed_back_kernel, groups=groups, chunks=chunks, sub=min(512, rows)),
        grid_spec=pltpu.PrefetchScalarGridSpec(
            num_scalar_prefetch=1,
            grid=(groups * chunks,),
            in_specs=[
                once((rows, depth)),
                pl.BlockSpec((rows, cols), own(0)),
                pl.BlockSpec((rows, cols), lambda s, *_: (0, jnp.maximum(s - chunks, 0))),
                anyspace,
                anyspace,
                anyspace,
                once(gains.shape),
            ]
            + [pl.BlockSpec((depth, cols), own(g)) for g in range(groups)]
            + [pl.BlockSpec((cols, depth), own_t(g)) for g in range(groups)],
            out_specs=[
                pl.BlockSpec((rows, cols), own(0)),
                once((rows, depth)),
                once((rows, depth)),
                once((8, depth)),
            ],
            scratch_shapes=[
                pltpu.VMEM((rows, depth), F32),
                pltpu.VMEM((rows, depth), F32),
                pltpu.VMEM((rows, depth), F32),
                pltpu.VMEM((rows, depth), BF),
                pltpu.SemaphoreType.DMA((3,)),
            ],
        ),
        out_shape=[
            jax.ShapeDtypeStruct((rows, hidden), BF),
            jax.ShapeDtypeStruct((rows, depth), F32),
            jax.ShapeDtypeStruct((rows, depth), BF),
            jax.ShapeDtypeStruct((8, depth), F32),
        ],
        compiler_params=pltpu.CompilerParams(vmem_limit_bytes=60 * MIB),
        cost_estimate=pl.CostEstimate(flops=rows * depth, bytes_accessed=rows * depth, transcendentals=0),
        name="feed_back",
    )(info, gb, own_slope, rest_slope, resid, attn_sum, cot, gains, *ups, *downs)


def feed_grad_kernel(*refs, groups):
    up_ref, down_ref, bias_ref, act_ref, gp_ref = refs[:5]
    n2s, gbs = refs[5 : 5 + groups], refs[5 + groups : 5 + 2 * groups]
    grad_ref, sum_ref = refs[5 + 2 * groups :]
    act, gp = act_ref[...], gp_ref[...]
    dup = dotg(gp, n2s[0][...], TN)
    ddown = dotg(act, gbs[0][...], TN)
    sums = column_sum(gp.astype(F32))
    for g in range(1, groups):
        pre = dotg(n2s[g][...], up_ref[...]) + bias_ref[0]
        act, slope = gelu_both(pre)
        act = act.astype(BF)
        gp = (dotg(gbs[g][...], down_ref[...], NT) * slope).astype(BF)
        dup += dotg(gp, n2s[g][...], TN)
        ddown += dotg(act, gbs[g][...], TN)
        sums += column_sum(gp.astype(F32))
    grad_ref[0] = dup.astype(BF)
    grad_ref[1] = ddown.astype(BF)
    sum_ref[0] = sums


def feed_grad(up, down, bias, act, gp, n2s, gbs, cols=512):
    rows, depth = n2s[0].shape
    groups, hidden = len(n2s), up.shape[1]
    once = lambda shape: pl.BlockSpec(shape, lambda s: (0, 0), pipeline_mode=pl.Buffered(1))
    wide = lambda count: pl.BlockSpec((count, cols), lambda s: (0, s))
    tall = pl.BlockSpec((cols, depth), lambda s: (s, 0))
    flat = pl.BlockSpec((1, 1, cols), lambda s: (s, 0, 0))
    return pl.pallas_call(
        functools.partial(feed_grad_kernel, groups=groups),
        grid=(hidden // cols,),
        in_specs=[wide(depth), tall, flat, wide(rows), wide(rows)] + [once((rows, depth))] * (2 * groups),
        out_specs=[pl.BlockSpec((2, cols, depth), lambda s: (0, s, 0)), flat],
        out_shape=[
            jax.ShapeDtypeStruct((2, hidden, depth), BF),
            jax.ShapeDtypeStruct((hidden // cols, 1, cols), F32),
        ],
        compiler_params=pltpu.CompilerParams(vmem_limit_bytes=60 * MIB),
        cost_estimate=pl.CostEstimate(
            flops=(8 * groups - 4) * rows * depth * hidden, bytes_accessed=20 * rows * depth, transcendentals=0
        ),
        name="feed_grad",
    )(up, down, bias.reshape(-1, 1, cols), act, gp, *n2s, *gbs)


def norm_kernel(x_ref, gain_ref, shift_ref, o_ref):
    hat, _ = norm_parts(x_ref[...].astype(F32))
    o_ref[...] = (hat * gain_ref[0:1] + shift_ref[0:1]).astype(BF)


def first_norm(x, gains, shifts, blk=512):
    rows, depth = x.shape
    blk = min(blk, rows)
    whole = pl.BlockSpec(gains.shape, lambda i: (0, 0))
    block = pl.BlockSpec((blk, depth), lambda i: (i, 0))
    return pl.pallas_call(
        norm_kernel,
        grid=(rows // blk,),
        in_specs=[block, whole, whole],
        out_specs=block,
        out_shape=jax.ShapeDtypeStruct((rows, depth), BF),
        compiler_params=pltpu.CompilerParams(vmem_limit_bytes=60 * MIB),
        name="first_norm",
    )(x, gains, shifts)


def join_kernel(pick_ref, x_ref, gain_ref, shift_ref, *refs, blocks, each):
    parts, (attn_ref, resid_ref, low_ref) = refs[:-3], refs[-3:]
    block = pl.program_id(0) // each
    total = None
    for g in range(len(parts) // blocks):
        wanted = pick_ref[g * blocks + block]
        part = parts[g * blocks][...]
        for b in range(1, blocks):
            part = jnp.where(wanted == b, parts[g * blocks + b][...], part)
        total = part if total is None else total + part.astype(F32)
    attn_ref[...] = total
    hat, _ = norm_parts(total)
    resid = x_ref[...].astype(F32) + hat * gain_ref[1:2] + shift_ref[1:2]
    resid_ref[...] = resid
    hat, _ = norm_parts(resid)
    low_ref[...] = (hat * gain_ref[2:3] + shift_ref[2:3]).astype(BF)


def join(x, gains, shifts, shares, picks, blk=256):
    rows, depth = x.shape
    blocks = len(shares[0])
    blk = min(blk, rows // blocks)
    each = rows // blocks // blk
    whole = pl.BlockSpec(gains.shape, lambda i, *_: (0, 0))
    block = pl.BlockSpec((blk, depth), lambda i, *_: (i, 0))
    part = pl.BlockSpec((blk, depth), lambda i, *_: (lax.rem(i, each), 0))
    return pl.pallas_call(
        functools.partial(join_kernel, blocks=blocks, each=each),
        grid_spec=pltpu.PrefetchScalarGridSpec(
            num_scalar_prefetch=1,
            grid=(rows // blk,),
            in_specs=[block, whole, whole] + [part] * (len(shares) * blocks),
            out_specs=[block, block, block],
        ),
        out_shape=[
            jax.ShapeDtypeStruct((rows, depth), F32),
            jax.ShapeDtypeStruct((rows, depth), F32),
            jax.ShapeDtypeStruct((rows, depth), BF),
        ],
        compiler_params=pltpu.CompilerParams(vmem_limit_bytes=60 * MIB),
        name="join",
    )(picks, x, gains, shifts, *[v for share in shares for v in share])


def widen_kernel(up_ref, down_ref, dup_ref, ddown_ref):
    dup_ref[...] = jnp.transpose(up_ref[...]).astype(F32)
    ddown_ref[...] = down_ref[...].astype(F32)


def widen(grads, blk=256):
    hidden, depth = grads.shape[0] // 2, grads.shape[1]
    blk = min(blk, hidden)
    count = hidden // blk
    return pl.pallas_call(
        widen_kernel,
        grid=(count,),
        in_specs=[
            pl.BlockSpec((blk, depth), lambda i: (i, 0)),
            pl.BlockSpec((blk, depth), lambda i: (count + i, 0)),
        ],
        out_specs=[
            pl.BlockSpec((depth, blk), lambda i: (0, i)),
            pl.BlockSpec((blk, depth), lambda i: (i, 0)),
        ],
        out_shape=[
            jax.ShapeDtypeStruct((depth, hidden), F32),
            jax.ShapeDtypeStruct((hidden, depth), F32),
        ],
        compiler_params=pltpu.CompilerParams(vmem_limit_bytes=60 * MIB),
        name="widen",
    )(grads, grads)

MESH = pl.DeviceIdType.MESH


def exchange(src, dst, sems, slot, flipped):
    return pltpu.make_async_remote_copy(
        src_ref=src,
        dst_ref=dst,
        send_sem=sems[0].at[slot],
        recv_sem=sems[1].at[slot],
        device_id={"dp": lax.axis_index("dp") ^ flipped},
        device_id_type=MESH,
    )


def tail_kernel(
    gq_ref, gk_ref, gv_ref, mixed_ref, wq_ref, wk_ref, wv_ref, x_ref, gr_ref, gain_ref, vec_ref, *refs,
    bits, groups, steps,
):
    lefts, refs = refs[: 2 * groups], refs[2 * groups :]
    sum_ref, out_ref, total_ref = refs[:3]
    right, left, weight, x, g_resid, packed, acc, core_buf, buf, sent, came, own_share, vec_buf = refs[3:16]
    send, recv, vec_send, vec_recv, x_send, x_recv, local = refs[16:]
    sems = (send, recv)
    place, me = lax.axis_index("tensor"), lax.axis_index("dp")
    bit = lambda b: lax.rem(lax.div(me, 1 << b), 2)
    core = bit(0)
    outer = list(range(1, bits))
    order = [[b] for b in outer]
    rows, depth = x.shape
    width = weight.shape[2]
    half = 2 * depth
    base = pl.multiple_of(core * half, half)
    part = min(512, depth)
    chunks = half // part
    slots, fetched = iter(range(send.shape[0])), iter(range(local.shape[0]))

    def fetch(src, dst):
        c = pltpu.make_async_copy(src, dst, local.at[next(fetched)])
        c.start()
        return c

    def wait_all(copies):
        for c in copies:
            c.wait()

    second = [fetch(r, right.at[i]) for i, r in enumerate((gq_ref, gk_ref, gv_ref))]
    second += [fetch(r, weight.at[i]) for i, r in enumerate((wq_ref, wk_ref, wv_ref))]
    third = [fetch(r, left.at[i]) for i, r in enumerate(lefts)] + [fetch(mixed_ref, right.at[3])]
    fourth = [fetch(x_ref, x), fetch(gr_ref, g_resid)]

    flips = {1 << b for b in range(bits)}
    flips |= {sum(1 << b for b in some) for some in order}
    greeted = [{"dp": me ^ f} for f in sorted(flips)]
    greeted += [{"tensor": lax.rem(place + r, groups)} for r in range(1, groups)]
    for bits_of in steps:
        for mask in range(1, 1 << len(bits_of)):
            chosen = [bits_of[i] for i in range(len(bits_of)) if mask >> i & 1]
            flip = sum(1 << b for axis, b in chosen if axis == "dp")
            turn_by = sum(1 << b for axis, b in chosen if axis == "tensor")
            if flip and turn_by:
                greeted.append({"dp": me ^ flip, "tensor": place ^ turn_by})
            elif flip and flip not in flips:
                flips.add(flip)
                greeted.append({"dp": me ^ flip})
    barrier = pltpu.get_barrier_semaphore()
    for peer in greeted:
        pl.semaphore_signal(barrier, inc=1, device_id=peer, device_id_type=MESH)
    pl.semaphore_wait(barrier, len(greeted))

    def copy(src, dst, flipped):
        c = exchange(src, dst, sems, next(slots), flipped)
        c.start()
        return c

    def rank(some):
        return sum(bit(b) << i for i, b in enumerate(some))

    def other(mine, mask):
        for i in range(mask.bit_length()):
            if mask >> i & 1:
                mine = mine + (1 << i) * (1 - 2 * lax.rem(lax.div(mine, 1 << i), 2))
        return mine

    def peer(some, mask):
        return sum(1 << b for i, b in enumerate(some) if mask >> i & 1)

    forwards = []
    cores = {}

    def reduce(chunk):
        cores[chunk].wait()

        def join(i, _):
            at = pl.ds(pl.multiple_of(chunk * part + i * 64, 64), 64)
            own = packed[pl.ds(pl.multiple_of(base + chunk * part + i * 64, 64), 64)].astype(F32)
            acc[at] = (own + core_buf[at].astype(F32)).astype(BF)
            return 0

        lax.fori_loop(0, part // 64, join, 0)
        start, size = chunk * part, part
        landing = chunk * (part - part // (1 << (bits - 1)))
        for some in order:
            size //= 1 << len(some)
            mine = rank(some)
            copies = []
            for mask in range(1, 1 << len(some)):
                away = pl.multiple_of(start + other(mine, mask) * size, size)
                at = pl.ds(landing + (mask - 1) * size, size)
                copies.append(copy(acc.at[pl.ds(away, size)], buf.at[at], peer(some, mask)))
            start = start + mine * size
            yield
            wait_all(copies)
            step = min(size, 64)

            def body(i, _, start=start, landing=landing, step=step, size=size, count=len(copies)):
                at = pl.ds(pl.multiple_of(start + i * step, step), step)
                value = acc[at].astype(F32)
                for n in range(count):
                    value += buf[pl.ds(pl.multiple_of(landing + n * size + i * step, step), step)].astype(F32)
                acc[at] = value.astype(BF)
                return 0

            lax.fori_loop(0, size // step, body, 0)
            landing += len(copies) * size
        start = base + start
        sum_ref[pl.ds(pl.multiple_of(start, size), size)] = acc[pl.ds(pl.multiple_of(start - base, size), size)]
        for some in reversed(order):
            have = sum_ref.at[pl.ds(pl.multiple_of(start, size), size)]
            copies = [copy(have, have, peer(some, mask)) for mask in range(1, 1 << len(some))]
            yield
            wait_all(copies)
            start = start - rank(some) * size
            size *= 1 << len(some)
        have = sum_ref.at[pl.ds(pl.multiple_of(start, size), size)]
        forwards.append(copy(have, have, 1))

    quarter = rows // 4

    def share(r, piece):
        g = pl.ds(pl.multiple_of(lax.rem(place + r, groups) * rows + piece * quarter, quarter), quarter)
        value = dotg(right[0, g, :], weight[0], NT)
        value += dotg(right[1, g, :], weight[1], NT)
        value += dotg(right[2, g, :], weight[2], NT)
        return value

    shares = {}

    def share_away(r):
        def body(i, _):
            sent[r - 1, pl.ds(pl.multiple_of(i * quarter, quarter), quarter), :] = share(r, i).astype(BF)
            return 0

        for piece in range(4):
            lax.fori_loop(piece, piece + 1, body, 0)
            at, slot = pl.ds(piece * quarter, quarter), (r - 1) * 4 + piece
            c = pltpu.make_async_remote_copy(
                src_ref=sent.at[r - 1, at],
                dst_ref=came.at[r - 1, at],
                send_sem=x_send.at[slot],
                recv_sem=x_recv.at[slot],
                device_id={"tensor": lax.rem(place + r, groups)},
                device_id_type=MESH,
            )
            c.start()
            shares[r, piece] = c

    def share_own():
        def body(i, _):
            own_share[pl.ds(pl.multiple_of(i * quarter, quarter), quarter), :] = share(0, i)
            return 0

        lax.fori_loop(0, 4, body, 0)

    def weight_grad(side, some):
        cols = min(256, part)
        each = part // cols

        def body(i, _):
            first = pl.multiple_of(lax.rem(core + side, 2) * half + i * cols, cols)
            number = lax.div(first, depth)
            kind = lax.div(number, 3) * groups
            lanes = pl.ds(pl.multiple_of(lax.rem(first, depth), cols), cols)
            value = None
            for r in range(groups):
                at = pl.ds(pl.multiple_of(lax.rem(place + r, groups) * rows, rows), rows)
                term = dotg(left[kind + r, :, lanes], right[number, at, :], TN)
                value = term if value is None else value + term
            packed[pl.ds(first, cols), :] = value.astype(BF)
            return 0

        lax.fori_loop(some[0] * each, (some[-1] + 1) * each, body, 0)
        if side:
            for c in some:
                at = pl.ds(pl.multiple_of((1 - core) * half + c * part, part), part)
                cores[c] = copy(packed.at[at], core_buf.at[pl.ds(c * part, part)], 1)

    def last_norm(piece):
        wait_all([shares[r, piece] for r in range(1, groups)])
        blk = min(64, quarter)

        def body(i, _):
            at = pl.ds(pl.multiple_of(piece * quarter + i * blk, blk), blk)
            value = own_share[at, :]
            for r in range(groups - 1):
                value += came[r, at, :].astype(F32)
            hat, scale = norm_parts(x[at, :].astype(F32))
            out_ref[at, :] = (g_resid[at, :] + norm_back(value, hat, scale, gain_ref[0:1])).astype(BF)
            total_ref[0:1] += column_sum(value * hat)
            total_ref[1:2] += column_sum(value)
            return 0

        lax.fori_loop(0, quarter // blk, body, 0)

    def vectors():
        slot = 0
        for bits_of in steps:
            sends = []
            for mask in range(1, 1 << len(bits_of)):
                peer = {}
                for i, (axis, b) in enumerate(bits_of):
                    if mask >> i & 1:
                        peer[axis] = peer.get(axis, lax.axis_index(axis)) ^ (1 << b)
                sends.append(
                    pltpu.make_async_remote_copy(
                        src_ref=total_ref,
                        dst_ref=vec_buf.at[slot],
                        send_sem=vec_send.at[slot],
                        recv_sem=vec_recv.at[slot],
                        device_id=peer,
                        device_id_type=MESH,
                    )
                )
                sends[-1].start()
                slot += 1
            yield
            wait_all(sends)
            total = total_ref[...]
            for i in range(len(sends)):
                total += vec_buf[slot - len(sends) + i]
            total_ref[...] = total

    def turn(chains):
        still = []
        for chain in chains:
            try:
                next(chain)
                still.append(chain)
            except StopIteration:
                pass
        return still

    wait_all(second)
    for r in range(1, groups):
        share_away(r)
    wait_all(third)
    all_chunks = list(range(chunks))
    for some in (all_chunks[: chunks // 2], all_chunks[chunks // 2 :]):
        weight_grad(1, some)
    wait_all(fourth)
    total_ref[...] = vec_ref[...]
    reduces = []
    for i, chunk in enumerate(all_chunks):
        weight_grad(0, [chunk])
        reduces = turn(reduces + [reduce(chunk)])
    share_own()
    reduces = turn(reduces)
    last_norm(0)
    last_norm(1)
    reduces = turn(reduces)
    last_norm(2)
    reduces = turn(reduces)
    last_norm(3)
    chain = turn([vectors()])
    while reduces or chain:
        reduces, chain = turn(reduces), turn(chain)
    wait_all(forwards)


def tail(grads, mixed, weights, x, g_resid, gains, vectors, n1s, gas, bits, steps):
    (slots, width), (rows, depth), groups = mixed.shape, x.shape, len(n1s)
    half = 2 * depth
    landing = half - half // (1 << (bits - 1))
    count = half // min(512, depth) * (3 * bits + 2)
    vecs = sum((1 << len(b)) - 1 for b in steps)
    vmem = pl.BlockSpec(memory_space=pltpu.VMEM)
    anyspace = pl.BlockSpec(memory_space=pl.ANY)
    dma = pltpu.SemaphoreType.DMA
    peers = max(groups - 1, 1)
    return pl.pallas_call(
        functools.partial(tail_kernel, bits=bits, groups=groups, steps=steps),
        in_specs=[anyspace] * 9 + [vmem] * 2 + [anyspace] * (2 * groups),
        out_specs=[vmem, vmem, vmem],
        out_shape=[
            jax.ShapeDtypeStruct((4 * depth, width), BF),
            jax.ShapeDtypeStruct((rows, depth), BF),
            jax.ShapeDtypeStruct(vectors.shape, F32),
        ],
        scratch_shapes=[
            pltpu.VMEM((4, slots, width), BF),
            pltpu.VMEM((2 * groups, rows, depth), BF),
            pltpu.VMEM((3, depth, width), BF),
            pltpu.VMEM((rows, depth), BF),
            pltpu.VMEM((rows, depth), F32),
            pltpu.VMEM((4 * depth, width), BF),
            pltpu.VMEM((half, width), BF),
            pltpu.VMEM((half, width), BF),
            pltpu.VMEM((landing, width), BF),
            pltpu.VMEM((peers, rows, depth), BF),
            pltpu.VMEM((peers, rows, depth), BF),
            pltpu.VMEM((rows, depth), F32),
            pltpu.VMEM((vecs,) + vectors.shape, F32),
            dma((count,)),
            dma((count,)),
            dma((vecs,)),
            dma((vecs,)),
            dma((4 * peers,)),
            dma((4 * peers,)),
            dma((9 + 2 * groups,)),
        ],
        compiler_params=pltpu.CompilerParams(
            collective_id=1, has_side_effects=True, vmem_limit_bytes=60 * MIB
        ),
        cost_estimate=pl.CostEstimate(flops=rows * width, bytes_accessed=rows * width, transcendentals=0),
        name="tail",
    )(*grads, mixed, *weights, x, g_resid, gains, vectors, *n1s, *gas)


def mixed_back_kernel(at_ref, x_ref, w_ref, *refs):
    refs[-1][...] = dotg(x_ref[...], w_ref[...], NT).astype(BF)


def mixed_back(where, x, w_out, slots, held, blk=256):
    rows, depth = x.shape
    width = w_out.shape[0]
    blk = min(blk, rows)
    count = rows // blk
    return pl.pallas_call(
        mixed_back_kernel,
        grid_spec=pltpu.PrefetchScalarGridSpec(
            num_scalar_prefetch=1,
            grid=(count,),
            in_specs=[
                pl.BlockSpec((blk, depth), lambda i, at: (i, 0)),
                pl.BlockSpec((width, depth), lambda i, at: (0, 0)),
            ]
            + [pl.BlockSpec(memory_space=pl.ANY)] * len(held),
            out_specs=pl.BlockSpec((blk, width), lambda i, at: (at[0] * count + i, 0)),
        ),
        out_shape=jax.ShapeDtypeStruct((slots, width), BF),
        input_output_aliases={3: 0} if held else {},
        compiler_params=pltpu.CompilerParams(vmem_limit_bytes=60 * MIB),
        cost_estimate=pl.CostEstimate(flops=rows * depth, bytes_accessed=rows * depth, transcendentals=0),
        name="mixed_back",
    )(where, x, w_out, *held)


def shift(x, axis, count, step):
    return lax.ppermute(x, axis, [((i + step) % count, i) for i in range(count)])


def shards(
    tokens,
    lengths,
    cotangent,
    w_query,
    w_key,
    w_value,
    w_out,
    up_weight,
    bias_up,
    down_weight,
    bias_down,
    norm_gains,
    norm_shifts,
):
    rows, _, depth = tokens.shape
    groups, replicas = lax.axis_size("tensor"), lax.axis_size("dp")
    me, replica = lax.axis_index("tensor"), lax.axis_index("dp")
    slots = rows * groups
    width = w_query.shape[1]
    hidden = up_weight.shape[1]
    x = tokens.reshape(rows, depth)
    here = me.reshape(1).astype(jnp.int32)
    place = lambda r: (here + r) % groups

    def others(v):
        return [shift(v, "tensor", groups, r) for r in range(1, groups)]

    def to_owner(v, r):
        return shift(v, "tensor", groups, groups - r)

    up_piece = lax.dynamic_slice_in_dim(up_weight, replica * (depth // replicas), depth // replicas, 0)
    down_piece = lax.dynamic_slice_in_dim(
        down_weight, replica * (hidden // replicas), hidden // replicas, 0
    )
    gather = lambda v: lax.all_gather(v, "dp", axis=0, tiled=True)

    freqs = 10000.0 ** (-jnp.arange(HD // 2).astype(F32) * 2.0 / HD)
    angles = jnp.arange(slots).astype(F32)[:, None] * freqs[None, :]
    cosine, sine = jnp.cos(angles), jnp.sin(angles)
    cosine = jnp.concatenate([cosine] * 4, axis=1)
    sine = jnp.concatenate([-sine, sine] * 2, axis=1)
    x_rest = others(x)
    normed_one = first_norm(x, norm_gains, norm_shifts)
    weights = (w_query, w_key, w_value)
    joint = project(here, normed_one, *weights, cosine, sine)
    joint, x_rest, up_piece, down_piece, bias = lax.optimization_barrier((joint, x_rest, up_piece, down_piece, bias_up))
    up_pieces, down_pieces, bias_rest = others(up_piece), others(down_piece), others(bias)
    normed_one_rest = [first_norm(v, norm_gains, norm_shifts) for v in x_rest]
    for r, n in enumerate(normed_one_rest):
        joint = project(place(r + 1), n, *weights, cosine, sine, joint)
    joint, up_pieces, down_pieces, bias_rest = lax.optimization_barrier((joint, up_pieces, down_pieces, bias_rest))
    blk = min(512, rows)
    each = rows // blk
    odd = lambda r: lax.rem(place(r), 2)
    ranks = lambda r, k: jnp.where(odd(r) == 1, each - 1 - k, k)
    held, shares, arrived = (), [], [[] for _ in range(1, groups)]
    for k in range(each):
        for r in range(1, groups):
            *held, share = attend(place(r) * each + ranks(0, k), lengths, joint, w_out, held, BF, blk)
            arrived[r - 1].append(to_owner(share, r))
        if k == each - 1 and k > 0:
            joint, arrived = lax.optimization_barrier((joint, [v[:k] for v in arrived])), arrived
            joint, early = joint
            arrived = [list(e) + v[k:] for e, v in zip(early, arrived)]
        *held, share = attend(here * each + ranks(0, k), lengths, joint, w_out, held, F32, blk)
        shares.append(share)
    mixed, lse = held
    shares = [shares] + arrived
    picks = jnp.concatenate([ranks(groups - r, k) for r in range(groups) for k in range(each)])
    up_rest, down_rest = [gather(p) for p in up_pieces], [gather(p) for p in down_pieces]
    biases = jnp.concatenate([bias_up] + bias_rest).astype(F32)

    info = jnp.stack([lengths[0], me * rows]).astype(jnp.int32)
    cot = cotangent.reshape(rows, depth)
    attn_sum, resid, normed_two = join(x, norm_gains, norm_shifts, shares, picks)
    normed_two_rest = others(normed_two)
    slope, act, branch = feed(
        info, normed_two, biases[:hidden], [up_weight], [down_weight], own=bias_down.reshape(1, depth)
    )
    slope_rest, layer_out, g_branch, sums3 = feed(
        info, normed_two, biases[hidden:], up_rest, down_rest, rest=(branch, resid, cot, norm_gains, norm_shifts)
    )
    ups, downs = [up_weight] + up_rest, [down_weight] + down_rest
    g_branch_rest = others(g_branch)
    g_pre, g_resid, g_attn, sums21 = feed_back(
        info, g_branch, slope, slope_rest, ups, downs, resid, attn_sum, cot, norm_gains
    )
    g_attn_rest = others(g_attn)
    g_pre, normed_two_rest = lax.optimization_barrier((g_pre, normed_two_rest))
    g_mixed = mixed_back(here, g_attn, w_out, slots, [])
    g_pre, g_mixed = lax.optimization_barrier((g_pre, g_mixed))
    grad_feed, bias_up_sum = feed_grad(
        up_weight, down_weight, biases[:hidden], act, g_pre,
        [normed_two] + normed_two_rest, [g_branch] + g_branch_rest,
    )
    grad_feed = grad_feed.reshape(2 * hidden, depth)
    g_mixed, g_attn_rest, grad_feed = lax.optimization_barrier((g_mixed, g_attn_rest, grad_feed))
    grad_feed = lax.psum(grad_feed, "dp")
    for r, g in enumerate(g_attn_rest):
        g_mixed = mixed_back(place(r + 1), g, w_out, slots, [g_mixed])

    grads = attend_back(lengths, joint, mixed, g_mixed, lse, cosine, sine, width)
    placed = lax.dynamic_update_slice(
        jnp.zeros((groups * hidden,), F32), bias_up_sum.reshape(-1), (me * hidden,)
    ).reshape(-1, depth)
    bits = (replicas - 1).bit_length()
    steps = [("tensor", b) for b in range((groups - 1).bit_length())] + [("dp", b) for b in range(bits)]
    steps = [tuple(steps[i : i + 2]) for i in range(0, len(steps), 2)]
    vectors = jnp.concatenate([jnp.zeros((2, depth), F32), sums3[:3], sums21[:4], placed])
    vectors = jnp.pad(vectors, ((0, -len(vectors) % 8), (0, 0)))
    packed, grad_tokens, sums = tail(
        grads, mixed, weights, x, g_resid, norm_gains, vectors,
        [normed_one] + normed_one_rest, [g_attn] + g_attn_rest, bits, steps,
    )
    grad_up, grad_down = widen(grad_feed)
    grad_query, grad_key, grad_value = (packed[i * depth : (i + 1) * depth].astype(F32) for i in range(3))
    grad_out = jnp.transpose(packed[3 * depth :]).astype(F32)
    grad_gains = jnp.stack([sums[0], sums[7], sums[5], sums[2]])
    grad_shifts = jnp.stack([sums[1], sums[8], sums[6], sums[3]])
    grad_bias_up = lax.dynamic_slice_in_dim(sums[9 : 9 + groups * hidden // depth].reshape(-1), me * hidden, hidden, 0)
    whole = (rows, 1, depth)
    return (
        layer_out.reshape(whole),
        grad_tokens.reshape(whole),
        grad_query,
        grad_key,
        grad_value,
        grad_out,
        grad_up,
        grad_bias_up,
        grad_down,
        sums[4],
        grad_gains,
        grad_shifts,
    )


def solution(mesh):
    wide, tall = P(None, "tensor"), P("tensor", None)
    acts = P("tensor", "dp", None)
    return jax.shard_map(
        shards,
        mesh=mesh,
        in_specs=(acts, P("dp"), acts, wide, wide, wide, tall, wide, P("tensor"), tall, P(), P(), P()),
        out_specs=(acts, acts, wide, wide, wide, tall, wide, P("tensor"), tall, P(), P(), P()),
        check_vma=False,
    )
```

```python
import functools
import jax
import jax.numpy as jnp
from jax import lax
from jax.experimental import pallas as pl
from jax.experimental.pallas import tpu as pltpu
from jax.sharding import PartitionSpec as P

HD = 64
EPSILON = 1e-05
BF = jnp.bfloat16
F32 = jnp.float32
NT = (((1,), (1,)), ((), ()))
NN = (((1,), (0,)), ((), ()))
TN = (((0,), (0,)), ((), ()))
MIB = 1 << 20


def dotg(a, b, dims=NN):
    return lax.dot_general(a, b, dims, preferred_element_type=F32)


def rotate(x, cos, sin):
    first = lax.broadcasted_iota(jnp.int32, (x.shape[0], 128), 1) % HD < HD // 2
    parts = []
    for a in range(0, x.shape[1], 128):
        v = x[:, a : a + 128]
        swapped = jnp.where(first, pltpu.roll(v, 96, 1), pltpu.roll(v, 32, 1))
        parts.append(v * cos + swapped * sin)
    return jnp.concatenate(parts, axis=1) if len(parts) > 1 else parts[0]


def qkv_kernel(x_ref, wq_ref, wk_ref, wv_ref, cos_ref, sin_ref, o_ref):
    width = wq_ref.shape[1]
    x, cos, sin = x_ref[...], cos_ref[...], sin_ref[...]
    o_ref[:, :width] = rotate(dotg(x, wq_ref[...]), cos, sin).astype(BF)
    o_ref[:, width : 2 * width] = rotate(dotg(x, wk_ref[...]), cos, sin).astype(BF)
    o_ref[:, 2 * width :] = dotg(x, wv_ref[...]).astype(BF)


def project(where, x, w_query, w_key, w_value, cos, sin, joint=None, blk=256):
    rows, depth = x.shape
    width, slots = w_query.shape[1], cos.shape[0]
    blk = min(blk, rows)
    count = rows // blk
    weight = pl.BlockSpec((depth, width), lambda i, at: (0, 0))
    angle = pl.BlockSpec((blk, 128), lambda i, at: (at[0] * count + i, 0))
    kernel = lambda at, *refs: qkv_kernel(*refs[:6], refs[-1])
    held = [] if joint is None else [joint]
    return pl.pallas_call(
        kernel,
        grid_spec=pltpu.PrefetchScalarGridSpec(
            num_scalar_prefetch=1,
            grid=(count,),
            in_specs=[pl.BlockSpec((blk, depth), lambda i, at: (i, 0)), weight, weight, weight, angle, angle]
            + [pl.BlockSpec(memory_space=pl.ANY)] * len(held),
            out_specs=pl.BlockSpec((blk, 3 * width), lambda i, at: (at[0] * count + i, 0)),
        ),
        out_shape=jax.ShapeDtypeStruct((slots, 3 * width), BF),
        input_output_aliases={7: 0} if held else {},
        compiler_params=pltpu.CompilerParams(vmem_limit_bytes=60 * MIB),
        cost_estimate=pl.CostEstimate(flops=rows * depth, bytes_accessed=rows * depth, transcendentals=0),
        name="project",
    )(where, x, w_query, w_key, w_value, cos, sin, *held)


def attend_kernel(at_ref, len_ref, q_ref, k_ref, v_ref, w_ref, *refs, blk):
    o_ref, lse_ref, share_ref, vt, low_ref = refs[-5:]
    pair = pl.program_id(0)
    i = at_ref[0]
    length = len_ref[0]
    def turn(j, _):
        part = pl.ds(pl.multiple_of(j * blk, blk), blk)
        vt[:, part] = jnp.transpose(v_ref[part, :])
        return 0

    lax.fori_loop(0, i + 1, turn, 0)
    lane = lax.broadcasted_iota(jnp.int32, (blk, 128), 1)
    q = q_ref[...] * jnp.asarray(0.125, BF)
    zero = jnp.zeros_like(q)
    qs = (jnp.where(lane < HD, q, zero), jnp.where(lane < HD, zero, q))

    def step(j, carry, diag):
        start = pl.multiple_of(j * blk, blk)
        kb = k_ref[pl.ds(start, blk), :]
        sub = min(256, blk)
        n = blk // sub
        if diag:
            key = lax.broadcasted_iota(jnp.int32, (sub, blk), 0)
            qry = lax.broadcasted_iota(jnp.int32, (sub, blk), 1)
        state = [carry[h] for h in range(2)]
        chains = [(h, t) for t in range(n) for h in range(2)]
        live = {}

        def first(c):
            h, t = chains[c]
            live[c] = dotg(kb[t * sub : t * sub + sub], qs[h], NT)

        def middle(c):
            h, t = chains[c]
            s = live[c]
            if diag:
                s = jnp.where((key + t * sub <= qry) & (key + t * sub + start < length), s, -1e30)
            m, l, acc = state[h]
            mn = jnp.maximum(m, jnp.max(s, axis=0, keepdims=True))
            p = jnp.exp(s - mn)
            al = jnp.exp(m - mn)
            state[h] = (mn, l * al + jnp.sum(p, axis=0, keepdims=True), acc)
            live[c] = (p.astype(BF), al)

        def last(c):
            h, t = chains[c]
            p, al = live.pop(c)
            m, l, acc = state[h]
            state[h] = (m, l, acc * al + dotg(vt[HD * h : HD * h + HD, pl.ds(start + t * sub, sub)], p))

        stages = (first, middle, last)
        for i in range(len(chains) + 4):
            for k in range(3):
                c = i - 2 * k
                if 0 <= c < len(chains):
                    stages[k](c)
        return tuple(state)

    init = tuple(
        (jnp.full((1, blk), -1e30, F32), jnp.zeros((1, blk), F32), jnp.zeros((HD, blk), F32))
        for _ in range(2)
    )
    c = lax.fori_loop(0, i, lambda j, c: step(j, c, False), init)
    c = step(i, c, True)
    ot = jnp.concatenate([c[h][2] / c[h][1] for h in range(2)], axis=0)
    low = jnp.transpose(ot).astype(BF)
    o_ref[...] = low
    lse_ref[0] = jnp.concatenate([c[h][0] + jnp.log(c[h][1]) for h in range(2)], axis=0)
    low_ref[pair] = low

    @pl.when(pair == pl.num_programs(0) - 1)
    def _():
        pairs = low_ref.shape[0]
        low = jnp.concatenate([low_ref[p] for p in range(pairs)], axis=1)
        share_ref[...] = dotg(low, w_ref[...]).astype(share_ref.dtype)


def attend(at, length, joint, w_out, held, kind, blk):
    rows, width, depth = joint.shape[0], w_out.shape[0], w_out.shape[1]
    pairs = width // 128
    return pl.pallas_call(
        functools.partial(attend_kernel, blk=blk),
        grid_spec=pltpu.PrefetchScalarGridSpec(
            num_scalar_prefetch=2,
            grid=(pairs,),
            in_specs=[
                pl.BlockSpec((blk, 128), lambda p, at, *_: (at[0], p)),
                pl.BlockSpec((rows, 128), lambda p, *_: (0, pairs + p)),
                pl.BlockSpec((rows, 128), lambda p, *_: (0, 2 * pairs + p)),
                pl.BlockSpec((width, depth), lambda p, *_: (0, 0), pipeline_mode=pl.Buffered(1)),
            ]
            + [pl.BlockSpec(memory_space=pl.ANY)] * len(held),
            out_specs=[
                pl.BlockSpec((blk, 128), lambda p, at, *_: (at[0], p)),
                pl.BlockSpec((1, 2, blk), lambda p, at, *_: (p, 0, at[0])),
                pl.BlockSpec((blk, depth), lambda p, *_: (0, 0)),
            ],
            scratch_shapes=[pltpu.VMEM((128, rows), BF), pltpu.VMEM((pairs, blk, 128), BF)],
        ),
        out_shape=[
            jax.ShapeDtypeStruct((rows, width), BF),
            jax.ShapeDtypeStruct((pairs, 2, rows), F32),
            jax.ShapeDtypeStruct((blk, depth), kind),
        ],
        input_output_aliases={6: 0, 7: 1} if held else {},
        compiler_params=pltpu.CompilerParams(vmem_limit_bytes=60 * MIB),
        cost_estimate=pl.CostEstimate(flops=rows * width, bytes_accessed=rows * width, transcendentals=0),
        name="attend",
    )(at, length, joint, joint, joint, w_out, *held)


def attend_back_kernel(
    len_ref, q_ref, k_ref, v_ref, o_ref, do_ref, lse_ref, cos_ref, sin_ref,
    dq_ref, dk_ref, dv_ref, kt, dlt, dqt, *, blk, blocks,
):
    length = len_ref[0]
    kt[...] = jnp.transpose(k_ref[...])
    dqt[...] = jnp.zeros_like(dqt)

    def products(i, _):
        at = pl.ds(pl.multiple_of(i * blk, blk), blk)
        both = jnp.transpose(do_ref[at, :].astype(F32) * o_ref[at, :].astype(F32))
        for h in range(2):
            dlt[h : h + 1, at] = jnp.sum(both[HD * h : HD * h + HD], axis=0, keepdims=True)
        return 0

    lax.fori_loop(0, blocks, products, 0)

    def keys(j, _):
        attend_back_keys(
            j, length, q_ref, k_ref, v_ref, do_ref, lse_ref, cos_ref, sin_ref, dk_ref, dv_ref, kt, dlt, dqt, blk, blocks
        )
        return 0

    lax.fori_loop(0, blocks, keys, 0)

    def turn(i, _):
        at = pl.ds(pl.multiple_of(i * blk, blk), blk)
        grad = jnp.transpose(dqt[:, at]) * 0.125
        dq_ref[at, :] = rotate(grad, cos_ref[at, :], -sin_ref[at, :]).astype(BF)
        return 0

    lax.fori_loop(0, blocks, turn, 0)


def attend_back_keys(
    j, length, q_ref, k_ref, v_ref, do_ref, lse_ref, cos_ref, sin_ref, dk_ref, dv_ref, kt, dlt, dqt, blk, blocks
):
    js = pl.multiple_of(j * blk, blk)
    lane = lax.broadcasted_iota(jnp.int32, (blk, 128), 1)
    kb = k_ref[pl.ds(js, blk), :] * jnp.asarray(0.125, BF)
    vb = v_ref[pl.ds(js, blk), :]
    zero = jnp.zeros_like(kb)
    ks = (jnp.where(lane < HD, kb, zero), jnp.where(lane < HD, zero, kb))
    vs = (jnp.where(lane < HD, vb, zero), jnp.where(lane < HD, zero, vb))

    def step(i, carry, diag):
        at = pl.ds(pl.multiple_of(i * blk, blk), blk)
        qb, dob = q_ref[at, :], do_ref[at, :]
        out = []
        for h in range(2):
            dk, dv = carry[h]
            s = dotg(ks[h], qb, NT)
            if diag:
                key = lax.broadcasted_iota(jnp.int32, (blk, blk), 0)
                qry = lax.broadcasted_iota(jnp.int32, (blk, blk), 1)
                s = jnp.where((key <= qry) & (key + js < length), s, -1e30)
            p = jnp.exp(s - lse_ref[0, h : h + 1, at])
            dp = dotg(vs[h], dob, NT)
            ds = (p * (dp - dlt[h : h + 1, at])).astype(BF)
            dv = dv + dotg(p.astype(BF), dob)
            dk = dk + dotg(ds, qb)
            dqt[HD * h : HD * h + HD, at] += dotg(kt[HD * h : HD * h + HD, pl.ds(js, blk)], ds)
            out.append((dk, dv))
        return tuple(out)

    z = jnp.zeros((blk, 128), F32)
    c = step(j, ((z, z), (z, z)), True)
    c = lax.fori_loop(j + 1, blocks, lambda i, c: step(i, c, False), c)
    grad = jnp.where(lane < HD, c[0][0], c[1][0]) * 0.125
    dk_ref[pl.ds(js, blk), :] = rotate(grad, cos_ref[pl.ds(js, blk), :], -sin_ref[pl.ds(js, blk), :]).astype(BF)
    dv_ref[pl.ds(js, blk), :] = jnp.where(lane < HD, c[0][1], c[1][1]).astype(BF)


def attend_back(length, joint, mixed, dmixed, lse, cos, sin, width, blk=512):
    rows = joint.shape[0]
    pairs, blocks = width // 128, rows // blk
    full = lambda off: pl.BlockSpec((rows, 128), lambda p, *_: (0, off * pairs + p))
    angle = pl.BlockSpec((rows, 128), lambda p, *_: (0, 0))
    return pl.pallas_call(
        functools.partial(attend_back_kernel, blk=blk, blocks=blocks),
        grid_spec=pltpu.PrefetchScalarGridSpec(
            num_scalar_prefetch=1,
            grid=(pairs,),
            in_specs=[full(0), full(1), full(2), full(0), full(0)]
            + [pl.BlockSpec((1, 2, rows), lambda p, *_: (p, 0, 0)), angle, angle],
            out_specs=[full(0)] * 3,
            scratch_shapes=[
                pltpu.VMEM((128, rows), BF),
                pltpu.VMEM((2, rows), F32),
                pltpu.VMEM((128, rows), F32),
            ],
        ),
        out_shape=[jax.ShapeDtypeStruct((rows, width), BF)] * 3,
        compiler_params=pltpu.CompilerParams(vmem_limit_bytes=60 * MIB),
        cost_estimate=pl.CostEstimate(
            flops=rows * width, bytes_accessed=rows * width, transcendentals=0
        ),
        name="attend_back",
    )(length, joint, joint, joint, mixed, dmixed, lse, cos, sin)


def gelu_parts(v):
    c = 0.7978845608028654
    return c, jnp.tanh(c * (v + 0.044715 * v * v * v))


def gelu_both(v):
    c, t = gelu_parts(v)
    half = 0.5 * (1.0 + t)
    return v * half, half + 0.5 * v * (1.0 - t * t) * c * (1.0 + 3 * 0.044715 * v * v)


def norm_parts(values):
    average = jnp.mean(values, axis=-1, keepdims=True)
    centred = values - average
    scale = lax.rsqrt(jnp.mean(centred * centred, axis=-1, keepdims=True) + EPSILON)
    return centred * scale, scale


def norm_back(grad, hat, scale, gain):
    g = grad * gain
    return scale * (
        g - jnp.mean(g, axis=-1, keepdims=True) - hat * jnp.mean(g * hat, axis=-1, keepdims=True)
    )


def column_sum(v):
    return jnp.sum(v, axis=0, keepdims=True)


def valid_rows(info_ref, start, count):
    at = info_ref[1] + start + lax.broadcasted_iota(jnp.int32, (count, 1), 0)
    return (at < info_ref[0]).astype(F32)


def loop_rows(rows, blk, body):
    def step(i, _):
        body(pl.multiple_of(i * blk, blk))
        return 0

    lax.fori_loop(0, rows // blk, step, 0)


def feed_kernel(info_ref, *refs, groups, chunks, sub):
    x_ref, bias_ref, resid_hbm, cot_hbm, bd_ref, gain_ref, shift_ref = refs[:7]
    ups, downs = refs[7 : 7 + groups], refs[7 + groups : 7 + 2 * groups]
    slope_ref, act_ref, out_ref, gb_ref, sums_ref, acc, resid_ref, cot_ref, sems = refs[7 + 2 * groups :]
    step = pl.program_id(0)
    rows = x_ref.shape[0]
    late = [
        pltpu.make_async_copy(resid_hbm, resid_ref, sems.at[0]),
        pltpu.make_async_copy(cot_hbm, cot_ref, sems.at[1]),
    ]

    @pl.when(step == 0)
    def _():
        for c in late:
            c.start()
        acc[...] = jnp.zeros_like(acc) + bd_ref[...].astype(F32)

    for g in range(groups):

        @pl.when(step // chunks == g)
        def _():
            for r in range(0, rows, sub):
                act, slope = gelu_both(dotg(x_ref[r : r + sub], ups[g][...], NT if g else NN) + bias_ref[0])
                slope_ref[r : r + sub] = slope.astype(BF)
                act = act.astype(BF)
                if g == 0:
                    act_ref[r : r + sub] = act
                acc[r : r + sub] += dotg(act, downs[g][...])

    @pl.when(step == groups * chunks - 1)
    def _():
        for c in late:
            c.wait()
        sums_ref[...] = jnp.zeros_like(sums_ref)
        gain, shift = gain_ref[3:4], shift_ref[3:4]
        blk = min(256, rows)

        def body(r):
            at = pl.ds(r, blk)
            valid = valid_rows(info_ref, r, blk)
            hat, scale = norm_parts(acc[at])
            out_ref[at] = (valid * (resid_ref[at] + hat * gain + shift)).astype(BF)
            g_out = valid * cot_ref[at].astype(F32)
            low = norm_back(g_out, hat, scale, gain).astype(BF)
            gb_ref[at] = low
            sums_ref[0:1] += column_sum(g_out * hat)
            sums_ref[1:2] += column_sum(g_out)
            sums_ref[2:3] += column_sum(low.astype(F32))

        loop_rows(rows, blk, body)


def feed_specs(depth, cols, chunks, rest):
    own = [
        pl.BlockSpec((depth, cols), lambda s, *_: (0, jnp.minimum(s, chunks - 1))),
        pl.BlockSpec((cols, depth), lambda s, *_: (jnp.minimum(s, chunks - 1), 0)),
    ]
    part = lambda g, i: pl.BlockSpec(
        (None, cols, depth), lambda s, *_: (i, jnp.clip(s - g * chunks, 0, chunks - 1), 0)
    )
    return [
        spec for i in range(2) for spec in [own[i]] + [part(g + 1, i) for g in range(len(rest))]
    ]


def feed(info, x, biases, up, down, rest, resid, cot, bias_down, gains, shifts, cols=512):
    rows, depth = x.shape
    groups, hidden = 1 + len(rest), up.shape[1]
    chunks = hidden // cols
    once = lambda shape: pl.BlockSpec(shape, lambda s, *_: (0, 0), pipeline_mode=pl.Buffered(1))
    anyspace = pl.BlockSpec(memory_space=pl.ANY)
    own = lambda g: (lambda s, *_: (0, jnp.clip(s - g * chunks, 0, chunks - 1)))
    return pl.pallas_call(
        functools.partial(feed_kernel, groups=groups, chunks=chunks, sub=min(512, rows)),
        grid_spec=pltpu.PrefetchScalarGridSpec(
            num_scalar_prefetch=1,
            grid=(groups * chunks,),
            in_specs=[
                once((rows, depth)),
                pl.BlockSpec((1, 1, cols), lambda s, *_: (s, 0, 0)),
                anyspace,
                anyspace,
                once((1, depth)),
                once(gains.shape),
                once(gains.shape),
            ]
            + feed_specs(depth, cols, chunks, rest),
            out_specs=[
                pl.BlockSpec((rows, cols), lambda s, *_: (0, s)),
                pl.BlockSpec((rows, cols), own(0)),
                once((rows, depth)),
                once((rows, depth)),
                once((8, depth)),
            ],
            scratch_shapes=[
                pltpu.VMEM((rows, depth), F32),
                pltpu.VMEM((rows, depth), F32),
                pltpu.VMEM((rows, depth), BF),
                pltpu.SemaphoreType.DMA((2,)),
            ],
        ),
        out_shape=[
            jax.ShapeDtypeStruct((rows, groups * hidden), BF),
            jax.ShapeDtypeStruct((rows, hidden), BF),
            jax.ShapeDtypeStruct((rows, depth), BF),
            jax.ShapeDtypeStruct((rows, depth), BF),
            jax.ShapeDtypeStruct((8, depth), F32),
        ],
        compiler_params=pltpu.CompilerParams(vmem_limit_bytes=60 * MIB),
        cost_estimate=pl.CostEstimate(flops=rows * depth, bytes_accessed=rows * depth, transcendentals=0),
        name="feed",
    )(info, x, biases.reshape(-1, 1, cols), resid, cot, bias_down, gains, shifts, up, *rest, down, *rest)


def feed_back_kernel(info_ref, *refs, groups, chunks, sub):
    gb_ref, slope_ref, resid_hbm, attn_hbm, cot_hbm, gain_ref = refs[:6]
    ups, downs = refs[6 : 6 + groups], refs[6 + groups : 6 + 2 * groups]
    gp_ref, gr_ref, ga_ref, sums_ref, acc, resid_ref, attn_ref, cot_ref, sems = refs[6 + 2 * groups :]
    step = pl.program_id(0)
    rows = gb_ref.shape[0]
    late = [
        pltpu.make_async_copy(src, dst, sems.at[i])
        for i, (src, dst) in enumerate(((resid_hbm, resid_ref), (attn_hbm, attn_ref), (cot_hbm, cot_ref)))
    ]

    @pl.when(step == 0)
    def _():
        for c in late:
            c.start()
        acc[...] = jnp.zeros_like(acc)

    for g in range(groups):

        @pl.when(step // chunks == g)
        def _():
            for r in range(0, rows, sub):
                grad = dotg(gb_ref[r : r + sub], downs[g][...], NT)
                low = (grad * slope_ref[r : r + sub].astype(F32)).astype(BF)
                if g == 0:
                    gp_ref[r : r + sub] = low
                acc[r : r + sub] += dotg(low, ups[g][...], NN if g else NT)

    @pl.when(step == groups * chunks - 1)
    def _():
        for c in late:
            c.wait()
        sums_ref[...] = jnp.zeros_like(sums_ref)
        blk = min(256, rows)

        def body(r):
            at = pl.ds(r, blk)
            g_out = valid_rows(info_ref, r, blk) * cot_ref[at].astype(F32)
            hat, scale = norm_parts(resid_ref[at])
            g_two = acc[at]
            g_resid = g_out + norm_back(g_two, hat, scale, gain_ref[2:3])
            gr_ref[at] = g_resid
            sums_ref[0:1] += column_sum(g_two * hat)
            sums_ref[1:2] += column_sum(g_two)
            hat, scale = norm_parts(attn_ref[at])
            ga_ref[at] = norm_back(g_resid, hat, scale, gain_ref[1:2]).astype(BF)
            sums_ref[2:3] += column_sum(g_resid * hat)
            sums_ref[3:4] += column_sum(g_resid)

        loop_rows(rows, blk, body)


def feed_back(info, gb, slope, up, down, rest, resid, attn_sum, cot, gains, cols=512):
    rows, depth = gb.shape
    groups, hidden = 1 + len(rest), up.shape[1]
    chunks = hidden // cols
    once = lambda shape: pl.BlockSpec(shape, lambda s, *_: (0, 0), pipeline_mode=pl.Buffered(1))
    anyspace = pl.BlockSpec(memory_space=pl.ANY)
    own = lambda g: (lambda s, *_: (0, jnp.clip(s - g * chunks, 0, chunks - 1)))
    return pl.pallas_call(
        functools.partial(feed_back_kernel, groups=groups, chunks=chunks, sub=min(512, rows)),
        grid_spec=pltpu.PrefetchScalarGridSpec(
            num_scalar_prefetch=1,
            grid=(groups * chunks,),
            in_specs=[
                once((rows, depth)),
                pl.BlockSpec((rows, cols), lambda s, *_: (0, s)),
                anyspace,
                anyspace,
                anyspace,
                once(gains.shape),
            ]
            + feed_specs(depth, cols, chunks, rest),
            out_specs=[
                pl.BlockSpec((rows, cols), own(0)),
                once((rows, depth)),
                once((rows, depth)),
                once((8, depth)),
            ],
            scratch_shapes=[
                pltpu.VMEM((rows, depth), F32),
                pltpu.VMEM((rows, depth), F32),
                pltpu.VMEM((rows, depth), F32),
                pltpu.VMEM((rows, depth), BF),
                pltpu.SemaphoreType.DMA((3,)),
            ],
        ),
        out_shape=[
            jax.ShapeDtypeStruct((rows, hidden), BF),
            jax.ShapeDtypeStruct((rows, depth), F32),
            jax.ShapeDtypeStruct((rows, depth), BF),
            jax.ShapeDtypeStruct((8, depth), F32),
        ],
        compiler_params=pltpu.CompilerParams(vmem_limit_bytes=60 * MIB),
        cost_estimate=pl.CostEstimate(flops=rows * depth, bytes_accessed=rows * depth, transcendentals=0),
        name="feed_back",
    )(info, gb, slope, resid, attn_sum, cot, gains, up, *rest, down, *rest)


def feed_grad_kernel(*refs, groups):
    up_ref, down_ref, bias_ref, act_ref, gp_ref = refs[:5]
    n2s, gbs = refs[5 : 5 + groups], refs[5 + groups : 5 + 2 * groups]
    grad_ref, sum_ref = refs[5 + 2 * groups :]
    act, gp = act_ref[...], gp_ref[...]
    dup = dotg(gp, n2s[0][...], TN)
    ddown = dotg(act, gbs[0][...], TN)
    sums = column_sum(gp.astype(F32))
    for g in range(1, groups):
        pre = dotg(n2s[g][...], up_ref[...]) + bias_ref[0]
        act, slope = gelu_both(pre)
        act = act.astype(BF)
        gp = (dotg(gbs[g][...], down_ref[...], NT) * slope).astype(BF)
        dup += dotg(gp, n2s[g][...], TN)
        ddown += dotg(act, gbs[g][...], TN)
        sums += column_sum(gp.astype(F32))
    grad_ref[0] = dup.astype(BF)
    grad_ref[1] = ddown.astype(BF)
    sum_ref[0] = sums


def feed_grad(up, down, bias, act, gp, n2s, gbs, cols=512):
    rows, depth = n2s[0].shape
    groups, hidden = len(n2s), up.shape[1]
    once = lambda shape: pl.BlockSpec(shape, lambda s: (0, 0), pipeline_mode=pl.Buffered(1))
    wide = lambda count: pl.BlockSpec((count, cols), lambda s: (0, s))
    tall = pl.BlockSpec((cols, depth), lambda s: (s, 0))
    flat = pl.BlockSpec((1, 1, cols), lambda s: (s, 0, 0))
    return pl.pallas_call(
        functools.partial(feed_grad_kernel, groups=groups),
        grid=(hidden // cols,),
        in_specs=[wide(depth), tall, flat, wide(rows), wide(rows)] + [once((rows, depth))] * (2 * groups),
        out_specs=[pl.BlockSpec((2, cols, depth), lambda s: (0, s, 0)), flat],
        out_shape=[
            jax.ShapeDtypeStruct((2, hidden, depth), BF),
            jax.ShapeDtypeStruct((hidden // cols, 1, cols), F32),
        ],
        compiler_params=pltpu.CompilerParams(vmem_limit_bytes=60 * MIB),
        cost_estimate=pl.CostEstimate(
            flops=(8 * groups - 4) * rows * depth * hidden, bytes_accessed=20 * rows * depth, transcendentals=0
        ),
        name="feed_grad",
    )(up, down, bias.reshape(-1, 1, cols), act, gp, *n2s, *gbs)


def norm_kernel(x_ref, gain_ref, shift_ref, o_ref):
    hat, _ = norm_parts(x_ref[...].astype(F32))
    o_ref[...] = (hat * gain_ref[0:1] + shift_ref[0:1]).astype(BF)


def first_norm(x, gains, shifts, blk=512):
    rows, depth = x.shape
    blk = min(blk, rows)
    whole = pl.BlockSpec(gains.shape, lambda i: (0, 0))
    block = pl.BlockSpec((blk, depth), lambda i: (i, 0))
    return pl.pallas_call(
        norm_kernel,
        grid=(rows // blk,),
        in_specs=[block, whole, whole],
        out_specs=block,
        out_shape=jax.ShapeDtypeStruct((rows, depth), BF),
        compiler_params=pltpu.CompilerParams(vmem_limit_bytes=60 * MIB),
        name="first_norm",
    )(x, gains, shifts)


def join_kernel(pick_ref, x_ref, gain_ref, shift_ref, *refs, blocks, each):
    parts, (attn_ref, resid_ref, low_ref) = refs[:-3], refs[-3:]
    block = pl.program_id(0) // each
    total = 0.0
    for g in range(len(parts) // blocks):
        wanted = pick_ref[g * blocks + block]
        part = parts[g * blocks][...]
        for b in range(1, blocks):
            part = jnp.where(wanted == b, parts[g * blocks + b][...], part)
        total = total + part.astype(F32)
    attn_ref[...] = total
    hat, _ = norm_parts(total)
    resid = x_ref[...].astype(F32) + hat * gain_ref[1:2] + shift_ref[1:2]
    resid_ref[...] = resid
    hat, _ = norm_parts(resid)
    low_ref[...] = (hat * gain_ref[2:3] + shift_ref[2:3]).astype(BF)


def join(x, gains, shifts, shares, picks, blk=256):
    rows, depth = x.shape
    blocks = len(shares[0])
    blk = min(blk, rows // blocks)
    each = rows // blocks // blk
    whole = pl.BlockSpec(gains.shape, lambda i, *_: (0, 0))
    block = pl.BlockSpec((blk, depth), lambda i, *_: (i, 0))
    part = lambda g, b: pl.BlockSpec(
        (blk, depth), lambda i, pick: (jnp.clip(i - pick[g * blocks + b] * each, 0, each - 1), 0)
    )
    return pl.pallas_call(
        functools.partial(join_kernel, blocks=blocks, each=each),
        grid_spec=pltpu.PrefetchScalarGridSpec(
            num_scalar_prefetch=1,
            grid=(rows // blk,),
            in_specs=[block, whole, whole] + [part(g, b) for g in range(len(shares)) for b in range(blocks)],
            out_specs=[block, block, block],
        ),
        out_shape=[
            jax.ShapeDtypeStruct((rows, depth), F32),
            jax.ShapeDtypeStruct((rows, depth), F32),
            jax.ShapeDtypeStruct((rows, depth), BF),
        ],
        compiler_params=pltpu.CompilerParams(vmem_limit_bytes=60 * MIB),
        name="join",
    )(picks, x, gains, shifts, *[v for share in shares for v in share])


def widen_kernel(up_ref, down_ref, dup_ref, ddown_ref):
    dup_ref[...] = jnp.transpose(up_ref[...]).astype(F32)
    ddown_ref[...] = down_ref[...].astype(F32)


def widen(grads, blk=512):
    hidden, depth = grads.shape[0] // 2, grads.shape[1]
    blk = min(blk, hidden)
    count = hidden // blk
    return pl.pallas_call(
        widen_kernel,
        grid=(count,),
        in_specs=[
            pl.BlockSpec((blk, depth), lambda i: (i, 0)),
            pl.BlockSpec((blk, depth), lambda i: (count + i, 0)),
        ],
        out_specs=[
            pl.BlockSpec((depth, blk), lambda i: (0, i)),
            pl.BlockSpec((blk, depth), lambda i: (i, 0)),
        ],
        out_shape=[
            jax.ShapeDtypeStruct((depth, hidden), F32),
            jax.ShapeDtypeStruct((hidden, depth), F32),
        ],
        compiler_params=pltpu.CompilerParams(vmem_limit_bytes=60 * MIB),
        name="widen",
    )(grads, grads)

MESH = pl.DeviceIdType.MESH


def exchange(src, dst, sems, slot, flipped):
    return pltpu.make_async_remote_copy(
        src_ref=src,
        dst_ref=dst,
        send_sem=sems[0].at[slot],
        recv_sem=sems[1].at[slot],
        device_id={"dp": lax.axis_index("dp") ^ flipped},
        device_id_type=MESH,
    )


def tail_kernel(
    gq_ref, gk_ref, gv_ref, mixed_ref, wq_ref, wk_ref, wv_ref, x_ref, gr_ref, gain_ref, vec_ref, *refs,
    bits, groups, steps,
):
    lefts, refs = refs[: 2 * groups], refs[2 * groups :]
    sum_ref, out_ref, total_ref = refs[:3]
    right, left, weight, x, g_resid, packed, acc, core_buf, buf, sent, came, own_share, vec_buf = refs[3:16]
    send, recv, vec_send, vec_recv, x_send, x_recv, local = refs[16:]
    sems = (send, recv)
    place, me = lax.axis_index("tensor"), lax.axis_index("dp")
    bit = lambda b: lax.rem(lax.div(me, 1 << b), 2)
    core = bit(0)
    outer = list(range(1, bits))
    order = [[b] for b in outer]
    rows, depth = x.shape
    width = weight.shape[2]
    half = 2 * depth
    base = pl.multiple_of(core * half, half)
    part = min(512, depth)
    chunks = half // part
    slots, fetched = iter(range(send.shape[0])), iter(range(local.shape[0]))

    def fetch(src, dst):
        c = pltpu.make_async_copy(src, dst, local.at[next(fetched)])
        c.start()
        return c

    def wait_all(copies):
        for c in copies:
            c.wait()

    second = [fetch(r, right.at[i]) for i, r in enumerate((gq_ref, gk_ref, gv_ref))]
    second += [fetch(r, weight.at[i]) for i, r in enumerate((wq_ref, wk_ref, wv_ref))]
    third = [fetch(r, left.at[i]) for i, r in enumerate(lefts)] + [fetch(mixed_ref, right.at[3])]
    fourth = [fetch(x_ref, x), fetch(gr_ref, g_resid)]

    flips = {1 << b for b in range(bits)}
    flips |= {sum(1 << b for b in some) for some in order}
    greeted = [{"dp": me ^ f} for f in sorted(flips)]
    greeted += [{"tensor": lax.rem(place + r, groups)} for r in range(1, groups)]
    for bits_of in steps:
        for mask in range(1, 1 << len(bits_of)):
            chosen = [bits_of[i] for i in range(len(bits_of)) if mask >> i & 1]
            flip = sum(1 << b for axis, b in chosen if axis == "dp")
            turn_by = sum(1 << b for axis, b in chosen if axis == "tensor")
            if flip and turn_by:
                greeted.append({"dp": me ^ flip, "tensor": place ^ turn_by})
            elif flip and flip not in flips:
                flips.add(flip)
                greeted.append({"dp": me ^ flip})
    barrier = pltpu.get_barrier_semaphore()
    for peer in greeted:
        pl.semaphore_signal(barrier, inc=1, device_id=peer, device_id_type=MESH)
    pl.semaphore_wait(barrier, len(greeted))

    def copy(src, dst, flipped):
        c = exchange(src, dst, sems, next(slots), flipped)
        c.start()
        return c

    def rank(some):
        return sum(bit(b) << i for i, b in enumerate(some))

    def other(mine, mask):
        for i in range(mask.bit_length()):
            if mask >> i & 1:
                mine = mine + (1 << i) * (1 - 2 * lax.rem(lax.div(mine, 1 << i), 2))
        return mine

    def peer(some, mask):
        return sum(1 << b for i, b in enumerate(some) if mask >> i & 1)

    forwards = []
    cores = {}

    def reduce(chunk):
        cores[chunk].wait()

        def join(i, _):
            at = pl.ds(pl.multiple_of(chunk * part + i * 64, 64), 64)
            own = packed[pl.ds(pl.multiple_of(base + chunk * part + i * 64, 64), 64)].astype(F32)
            acc[at] = (own + core_buf[at].astype(F32)).astype(BF)
            return 0

        lax.fori_loop(0, part // 64, join, 0)
        start, size = chunk * part, part
        landing = chunk * (part - part // (1 << (bits - 1)))
        for some in order:
            size //= 1 << len(some)
            mine = rank(some)
            copies = []
            for mask in range(1, 1 << len(some)):
                away = pl.multiple_of(start + other(mine, mask) * size, size)
                at = pl.ds(landing + (mask - 1) * size, size)
                copies.append(copy(acc.at[pl.ds(away, size)], buf.at[at], peer(some, mask)))
            start = start + mine * size
            yield
            wait_all(copies)
            step = min(size, 64)

            def body(i, _, start=start, landing=landing, step=step, size=size, count=len(copies)):
                at = pl.ds(pl.multiple_of(start + i * step, step), step)
                value = acc[at].astype(F32)
                for n in range(count):
                    value += buf[pl.ds(pl.multiple_of(landing + n * size + i * step, step), step)].astype(F32)
                acc[at] = value.astype(BF)
                return 0

            lax.fori_loop(0, size // step, body, 0)
            landing += len(copies) * size
        start = base + start
        sum_ref[pl.ds(pl.multiple_of(start, size), size)] = acc[pl.ds(pl.multiple_of(start - base, size), size)]
        for some in reversed(order):
            have = sum_ref.at[pl.ds(pl.multiple_of(start, size), size)]
            copies = [copy(have, have, peer(some, mask)) for mask in range(1, 1 << len(some))]
            yield
            wait_all(copies)
            start = start - rank(some) * size
            size *= 1 << len(some)
        have = sum_ref.at[pl.ds(pl.multiple_of(start, size), size)]
        forwards.append(copy(have, have, 1))

    quarter = rows // 4

    def share(r, piece):
        g = pl.ds(pl.multiple_of(lax.rem(place + r, groups) * rows + piece * quarter, quarter), quarter)
        value = dotg(right[0, g, :], weight[0], NT)
        value += dotg(right[1, g, :], weight[1], NT)
        value += dotg(right[2, g, :], weight[2], NT)
        return value

    shares = {}

    def share_away(r):
        def body(i, _):
            sent[r - 1, pl.ds(pl.multiple_of(i * quarter, quarter), quarter), :] = share(r, i).astype(BF)
            return 0

        for piece in range(4):
            lax.fori_loop(piece, piece + 1, body, 0)
            at, slot = pl.ds(piece * quarter, quarter), (r - 1) * 4 + piece
            c = pltpu.make_async_remote_copy(
                src_ref=sent.at[r - 1, at],
                dst_ref=came.at[r - 1, at],
                send_sem=x_send.at[slot],
                recv_sem=x_recv.at[slot],
                device_id={"tensor": lax.rem(place + r, groups)},
                device_id_type=MESH,
            )
            c.start()
            shares[r, piece] = c

    def share_own():
        def body(i, _):
            own_share[pl.ds(pl.multiple_of(i * quarter, quarter), quarter), :] = share(0, i)
            return 0

        lax.fori_loop(0, 4, body, 0)

    def weight_grad(side, some):
        cols = min(256, part)
        each = part // cols

        def body(i, _):
            first = pl.multiple_of(lax.rem(core + side, 2) * half + i * cols, cols)
            number = lax.div(first, depth)
            kind = lax.div(number, 3) * groups
            lanes = pl.ds(pl.multiple_of(lax.rem(first, depth), cols), cols)
            value = None
            for r in range(groups):
                at = pl.ds(pl.multiple_of(lax.rem(place + r, groups) * rows, rows), rows)
                term = dotg(left[kind + r, :, lanes], right[number, at, :], TN)
                value = term if value is None else value + term
            packed[pl.ds(first, cols), :] = value.astype(BF)
            return 0

        lax.fori_loop(some[0] * each, (some[-1] + 1) * each, body, 0)
        if side:
            for c in some:
                at = pl.ds(pl.multiple_of((1 - core) * half + c * part, part), part)
                cores[c] = copy(packed.at[at], core_buf.at[pl.ds(c * part, part)], 1)

    def last_norm(piece):
        wait_all([shares[r, piece] for r in range(1, groups)])
        blk = min(64, quarter)

        def body(i, _):
            at = pl.ds(pl.multiple_of(piece * quarter + i * blk, blk), blk)
            value = own_share[at, :]
            for r in range(groups - 1):
                value += came[r, at, :].astype(F32)
            hat, scale = norm_parts(x[at, :].astype(F32))
            out_ref[at, :] = (g_resid[at, :] + norm_back(value, hat, scale, gain_ref[0:1])).astype(BF)
            total_ref[0:1] += column_sum(value * hat)
            total_ref[1:2] += column_sum(value)
            return 0

        lax.fori_loop(0, quarter // blk, body, 0)

    def vectors():
        slot = 0
        for bits_of in steps:
            sends = []
            for mask in range(1, 1 << len(bits_of)):
                peer = {}
                for i, (axis, b) in enumerate(bits_of):
                    if mask >> i & 1:
                        peer[axis] = peer.get(axis, lax.axis_index(axis)) ^ (1 << b)
                sends.append(
                    pltpu.make_async_remote_copy(
                        src_ref=total_ref,
                        dst_ref=vec_buf.at[slot],
                        send_sem=vec_send.at[slot],
                        recv_sem=vec_recv.at[slot],
                        device_id=peer,
                        device_id_type=MESH,
                    )
                )
                sends[-1].start()
                slot += 1
            yield
            wait_all(sends)
            total = total_ref[...]
            for i in range(len(sends)):
                total += vec_buf[slot - len(sends) + i]
            total_ref[...] = total

    def turn(chains):
        still = []
        for chain in chains:
            try:
                next(chain)
                still.append(chain)
            except StopIteration:
                pass
        return still

    wait_all(second)
    for r in range(1, groups):
        share_away(r)
    wait_all(third)
    all_chunks = list(range(chunks))
    for some in (all_chunks[: chunks // 2], all_chunks[chunks // 2 :]):
        weight_grad(1, some)
    wait_all(fourth)
    total_ref[...] = vec_ref[...]
    reduces = []
    for i, chunk in enumerate(all_chunks):
        weight_grad(0, [chunk])
        reduces = turn(reduces + [reduce(chunk)])
    share_own()
    reduces = turn(reduces)
    last_norm(0)
    last_norm(1)
    reduces = turn(reduces)
    last_norm(2)
    reduces = turn(reduces)
    last_norm(3)
    chain = turn([vectors()])
    while reduces or chain:
        reduces, chain = turn(reduces), turn(chain)
    wait_all(forwards)


def tail(grads, mixed, weights, x, g_resid, gains, vectors, n1s, gas, bits, steps):
    (slots, width), (rows, depth), groups = mixed.shape, x.shape, len(n1s)
    half = 2 * depth
    landing = half - half // (1 << (bits - 1))
    count = half // min(512, depth) * (3 * bits + 2)
    vecs = sum((1 << len(b)) - 1 for b in steps)
    vmem = pl.BlockSpec(memory_space=pltpu.VMEM)
    anyspace = pl.BlockSpec(memory_space=pl.ANY)
    dma = pltpu.SemaphoreType.DMA
    peers = max(groups - 1, 1)
    return pl.pallas_call(
        functools.partial(tail_kernel, bits=bits, groups=groups, steps=steps),
        in_specs=[anyspace] * 9 + [vmem] * 2 + [anyspace] * (2 * groups),
        out_specs=[vmem, vmem, vmem],
        out_shape=[
            jax.ShapeDtypeStruct((4 * depth, width), BF),
            jax.ShapeDtypeStruct((rows, depth), BF),
            jax.ShapeDtypeStruct(vectors.shape, F32),
        ],
        scratch_shapes=[
            pltpu.VMEM((4, slots, width), BF),
            pltpu.VMEM((2 * groups, rows, depth), BF),
            pltpu.VMEM((3, depth, width), BF),
            pltpu.VMEM((rows, depth), BF),
            pltpu.VMEM((rows, depth), F32),
            pltpu.VMEM((4 * depth, width), BF),
            pltpu.VMEM((half, width), BF),
            pltpu.VMEM((half, width), BF),
            pltpu.VMEM((landing, width), BF),
            pltpu.VMEM((peers, rows, depth), BF),
            pltpu.VMEM((peers, rows, depth), BF),
            pltpu.VMEM((rows, depth), F32),
            pltpu.VMEM((vecs,) + vectors.shape, F32),
            dma((count,)),
            dma((count,)),
            dma((vecs,)),
            dma((vecs,)),
            dma((4 * peers,)),
            dma((4 * peers,)),
            dma((9 + 2 * groups,)),
        ],
        compiler_params=pltpu.CompilerParams(
            collective_id=1, has_side_effects=True, vmem_limit_bytes=60 * MIB
        ),
        cost_estimate=pl.CostEstimate(flops=rows * width, bytes_accessed=rows * width, transcendentals=0),
        name="tail",
    )(*grads, mixed, *weights, x, g_resid, gains, vectors, *n1s, *gas)


def mixed_back_kernel(at_ref, x_ref, w_ref, *refs):
    refs[-1][...] = dotg(x_ref[...], w_ref[...], NT).astype(BF)


def mixed_back(where, x, w_out, slots, held, blk=256):
    rows, depth = x.shape
    width = w_out.shape[0]
    blk = min(blk, rows)
    count = rows // blk
    return pl.pallas_call(
        mixed_back_kernel,
        grid_spec=pltpu.PrefetchScalarGridSpec(
            num_scalar_prefetch=1,
            grid=(count,),
            in_specs=[
                pl.BlockSpec((blk, depth), lambda i, at: (i, 0)),
                pl.BlockSpec((width, depth), lambda i, at: (0, 0)),
            ]
            + [pl.BlockSpec(memory_space=pl.ANY)] * len(held),
            out_specs=pl.BlockSpec((blk, width), lambda i, at: (at[0] * count + i, 0)),
        ),
        out_shape=jax.ShapeDtypeStruct((slots, width), BF),
        input_output_aliases={3: 0} if held else {},
        compiler_params=pltpu.CompilerParams(vmem_limit_bytes=60 * MIB),
        cost_estimate=pl.CostEstimate(flops=rows * depth, bytes_accessed=rows * depth, transcendentals=0),
        name="mixed_back",
    )(where, x, w_out, *held)


def shift(x, axis, count, step):
    return lax.ppermute(x, axis, [((i + step) % count, i) for i in range(count)])


def shards(
    tokens,
    lengths,
    cotangent,
    w_query,
    w_key,
    w_value,
    w_out,
    up_weight,
    bias_up,
    down_weight,
    bias_down,
    norm_gains,
    norm_shifts,
):
    rows, _, depth = tokens.shape
    groups, replicas = lax.axis_size("tensor"), lax.axis_size("dp")
    me, replica = lax.axis_index("tensor"), lax.axis_index("dp")
    slots = rows * groups
    width = w_query.shape[1]
    hidden = up_weight.shape[1]
    x = tokens.reshape(rows, depth)
    here = me.reshape(1).astype(jnp.int32)
    place = lambda r: (here + r) % groups

    def others(v):
        return [shift(v, "tensor", groups, r) for r in range(1, groups)]

    def to_owner(v, r):
        return shift(v, "tensor", groups, groups - r)

    count = hidden // replicas
    up_piece = lax.dynamic_slice_in_dim(up_weight, replica * count, count, 1)
    down_piece = lax.dynamic_slice_in_dim(down_weight, replica * count, count, 0)
    piece = jnp.stack([jnp.transpose(up_piece), down_piece])

    freqs = 10000.0 ** (-jnp.arange(HD // 2).astype(F32) * 2.0 / HD)
    angles = jnp.arange(slots).astype(F32)[:, None] * freqs[None, :]
    cosine, sine = jnp.cos(angles), jnp.sin(angles)
    cosine = jnp.concatenate([cosine] * 4, axis=1)
    sine = jnp.concatenate([-sine, sine] * 2, axis=1)
    x_rest = others(x)
    normed_one = first_norm(x, norm_gains, norm_shifts)
    weights = (w_query, w_key, w_value)
    joint = project(here, normed_one, *weights, cosine, sine)
    joint, x_rest, piece, bias = lax.optimization_barrier((joint, x_rest, piece, bias_up))
    pieces, bias_rest = others(piece), others(bias)
    normed_one_rest = [first_norm(v, norm_gains, norm_shifts) for v in x_rest]
    for r, n in enumerate(normed_one_rest):
        joint = project(place(r + 1), n, *weights, cosine, sine, joint)
    joint, pieces, bias_rest = lax.optimization_barrier((joint, pieces, bias_rest))
    blk = min(512, rows)
    each = rows // blk
    odd = lambda r: lax.rem(place(r), 2)
    ranks = lambda r, k: jnp.where(odd(r) == 1, each - 1 - k, k)
    held, shares, arrived = (), [], [[] for _ in range(1, groups)]
    for k in range(each):
        for r in range(1, groups):
            *held, share = attend(place(r) * each + ranks(0, k), lengths, joint, w_out, held, BF, blk)
            arrived[r - 1].append(to_owner(share, r))
        if k == each - 1 and k > 0:
            joint, arrived = lax.optimization_barrier((joint, [v[:k] for v in arrived])), arrived
            joint, early = joint
            arrived = [list(e) + v[k:] for e, v in zip(early, arrived)]
        *held, share = attend(here * each + ranks(0, k), lengths, joint, w_out, held, BF, blk)
        shares.append(share)
    mixed, lse = held
    shares = [shares] + arrived
    picks = jnp.concatenate([ranks(groups - r, k) for r in range(groups) for k in range(each)])
    rest = [lax.all_gather(p, "dp", axis=1, tiled=True) for p in pieces]
    biases = jnp.concatenate([bias_up] + bias_rest).astype(F32)

    info = jnp.stack([lengths[0], me * rows]).astype(jnp.int32)
    cot = cotangent.reshape(rows, depth)
    attn_sum, resid, normed_two = join(x, norm_gains, norm_shifts, shares, picks)
    normed_two_rest = others(normed_two)
    slope, act, layer_out, g_branch, sums3 = feed(
        info, normed_two, biases, up_weight, down_weight, rest, resid, cot,
        bias_down.reshape(1, depth), norm_gains, norm_shifts,
    )
    g_branch_rest = others(g_branch)
    g_pre, g_resid, g_attn, sums21 = feed_back(
        info, g_branch, slope, up_weight, down_weight, rest, resid, attn_sum, cot, norm_gains
    )
    g_attn_rest = others(g_attn)
    g_pre, normed_two_rest = lax.optimization_barrier((g_pre, normed_two_rest))
    g_mixed = mixed_back(here, g_attn, w_out, slots, [])
    g_pre, g_mixed = lax.optimization_barrier((g_pre, g_mixed))
    grad_feed, bias_up_sum = feed_grad(
        up_weight, down_weight, biases[:hidden], act, g_pre,
        [normed_two] + normed_two_rest, [g_branch] + g_branch_rest,
    )
    grad_feed = grad_feed.reshape(2 * hidden, depth)
    g_mixed, g_attn_rest, grad_feed = lax.optimization_barrier((g_mixed, g_attn_rest, grad_feed))
    grad_feed = lax.psum(grad_feed, "dp")
    for r, g in enumerate(g_attn_rest):
        g_mixed = mixed_back(place(r + 1), g, w_out, slots, [g_mixed])

    grads = attend_back(lengths, joint, mixed, g_mixed, lse, cosine, sine, width)
    placed = lax.dynamic_update_slice(
        jnp.zeros((groups * hidden,), F32), bias_up_sum.reshape(-1), (me * hidden,)
    ).reshape(-1, depth)
    bits = (replicas - 1).bit_length()
    steps = [("tensor", b) for b in range((groups - 1).bit_length())] + [("dp", b) for b in range(bits)]
    steps = [tuple(steps[i : i + 2]) for i in range(0, len(steps), 2)]
    vectors = jnp.concatenate([jnp.zeros((2, depth), F32), sums3[:3], sums21[:4], placed])
    vectors = jnp.pad(vectors, ((0, -len(vectors) % 8), (0, 0)))
    packed, grad_tokens, sums = tail(
        grads, mixed, weights, x, g_resid, norm_gains, vectors,
        [normed_one] + normed_one_rest, [g_attn] + g_attn_rest, bits, steps,
    )
    grad_up, grad_down = widen(grad_feed)
    grad_query, grad_key, grad_value = (packed[i * depth : (i + 1) * depth].astype(F32) for i in range(3))
    grad_out = jnp.transpose(packed[3 * depth :]).astype(F32)
    grad_gains = jnp.stack([sums[0], sums[7], sums[5], sums[2]])
    grad_shifts = jnp.stack([sums[1], sums[8], sums[6], sums[3]])
    grad_bias_up = lax.dynamic_slice_in_dim(sums[9 : 9 + groups * hidden // depth].reshape(-1), me * hidden, hidden, 0)
    whole = (rows, 1, depth)
    return (
        layer_out.reshape(whole),
        grad_tokens.reshape(whole),
        grad_query,
        grad_key,
        grad_value,
        grad_out,
        grad_up,
        grad_bias_up,
        grad_down,
        sums[4],
        grad_gains,
        grad_shifts,
    )


def solution(mesh):
    wide, tall = P(None, "tensor"), P("tensor", None)
    acts = P("tensor", "dp", None)
    return jax.shard_map(
        shards,
        mesh=mesh,
        in_specs=(acts, P("dp"), acts, wide, wide, wide, tall, wide, P("tensor"), tall, P(), P(), P()),
        out_specs=(acts, acts, wide, wide, wide, tall, wide, P("tensor"), tall, P(), P(), P()),
        check_vma=False,
    )
```

```python
import functools
import jax
import jax.numpy as jnp
from jax import lax
from jax.experimental import pallas as pl
from jax.experimental.pallas import tpu as pltpu
from jax.sharding import PartitionSpec as P

HD = 64
EPSILON = 1e-05
BF = jnp.bfloat16
F32 = jnp.float32
NT = (((1,), (1,)), ((), ()))
NN = (((1,), (0,)), ((), ()))
TN = (((0,), (0,)), ((), ()))
MIB = 1 << 20


def dotg(a, b, dims=NN):
    return lax.dot_general(a, b, dims, preferred_element_type=F32)


def rotate(x, cos, sin):
    first = lax.broadcasted_iota(jnp.int32, (x.shape[0], 128), 1) % HD < HD // 2
    parts = []
    for a in range(0, x.shape[1], 128):
        v = x[:, a : a + 128]
        swapped = jnp.where(first, pltpu.roll(v, 96, 1), pltpu.roll(v, 32, 1))
        parts.append(v * cos + swapped * sin)
    return jnp.concatenate(parts, axis=1) if len(parts) > 1 else parts[0]


def qkv_kernel(at_ref, x_ref, wq_ref, wk_ref, wv_ref, cos_ref, sin_ref, gain_ref, shift_ref, *refs):
    o_ref, normed_ref = refs[-2:]
    width = wq_ref.shape[1]
    hat, _ = norm_parts(x_ref[...].astype(F32))
    x = (hat * gain_ref[0:1] + shift_ref[0:1]).astype(BF)
    normed_ref[...] = x
    cos, sin = cos_ref[...], sin_ref[...]
    o_ref[:, :width] = rotate(dotg(x, wq_ref[...]), cos, sin).astype(BF)
    o_ref[:, width : 2 * width] = rotate(dotg(x, wk_ref[...]), cos, sin).astype(BF)
    o_ref[:, 2 * width :] = dotg(x, wv_ref[...]).astype(BF)


def project(where, x, gains, shifts, w_query, w_key, w_value, cos, sin, held, blk=512):
    rows, depth = x.shape
    width, slots = w_query.shape[1], cos.shape[0]
    blk = min(blk, rows)
    count = rows // blk
    once = lambda shape: pl.BlockSpec(shape, lambda i, at: (0, 0), pipeline_mode=pl.Buffered(1))
    angle = pl.BlockSpec((blk, 128), lambda i, at: (at[0] * count + i, 0))
    block = pl.BlockSpec((blk, depth), lambda i, at: (i, 0))
    return pl.pallas_call(
        qkv_kernel,
        grid_spec=pltpu.PrefetchScalarGridSpec(
            num_scalar_prefetch=1,
            grid=(count,),
            in_specs=[block] + [once((depth, width))] * 3 + [angle, angle, once(gains.shape), once(gains.shape)]
            + [pl.BlockSpec(memory_space=pl.ANY)] * len(held),
            out_specs=[pl.BlockSpec((blk, 3 * width), lambda i, at: (at[0] * count + i, 0)), block],
        ),
        out_shape=[
            jax.ShapeDtypeStruct((slots, 3 * width), BF),
            jax.ShapeDtypeStruct((rows, depth), BF),
        ],
        input_output_aliases={9: 0} if held else {},
        compiler_params=pltpu.CompilerParams(vmem_limit_bytes=60 * MIB),
        cost_estimate=pl.CostEstimate(flops=rows * depth, bytes_accessed=rows * depth, transcendentals=0),
        name="project",
    )(where, x, w_query, w_key, w_value, cos, sin, gains, shifts, *held)


def attend_kernel(at_ref, len_ref, q_ref, k_ref, v_ref, w_ref, *refs, blk):
    o_ref, lse_ref, share_ref, vt, low_ref = refs[-5:]
    pair = pl.program_id(0)
    i = at_ref[0]
    length = len_ref[0]
    def turn(j, _):
        part = pl.ds(pl.multiple_of(j * blk, blk), blk)
        vt[:, part] = jnp.transpose(v_ref[part, :])
        return 0

    lax.fori_loop(0, i + 1, turn, 0)
    lane = lax.broadcasted_iota(jnp.int32, (blk, 128), 1)
    q = q_ref[...] * jnp.asarray(0.125, BF)
    zero = jnp.zeros_like(q)
    qs = (jnp.where(lane < HD, q, zero), jnp.where(lane < HD, zero, q))

    def step(j, carry, diag):
        start = pl.multiple_of(j * blk, blk)
        kb = k_ref[pl.ds(start, blk), :]
        sub = min(256, blk)
        n = blk // sub
        if diag:
            key = lax.broadcasted_iota(jnp.int32, (sub, blk), 0)
            qry = lax.broadcasted_iota(jnp.int32, (sub, blk), 1)
        state = [carry[h] for h in range(2)]
        chains = [(h, t) for t in range(n) for h in range(2)]
        live = {}

        def first(c):
            h, t = chains[c]
            live[c] = dotg(kb[t * sub : t * sub + sub], qs[h], NT)

        def middle(c):
            h, t = chains[c]
            s = live[c]
            if diag:
                s = jnp.where((key + t * sub <= qry) & (key + t * sub + start < length), s, -1e30)
            m, l, acc = state[h]
            mn = jnp.maximum(m, jnp.max(s, axis=0, keepdims=True))
            p = jnp.exp(s - mn)
            al = jnp.exp(m - mn)
            state[h] = (mn, l * al + jnp.sum(p, axis=0, keepdims=True), acc)
            live[c] = (p.astype(BF), al)

        def last(c):
            h, t = chains[c]
            p, al = live.pop(c)
            m, l, acc = state[h]
            state[h] = (m, l, acc * al + dotg(vt[HD * h : HD * h + HD, pl.ds(start + t * sub, sub)], p))

        stages = (first, middle, last)
        for i in range(len(chains) + 4):
            for k in range(3):
                c = i - 2 * k
                if 0 <= c < len(chains):
                    stages[k](c)
        return tuple(state)

    init = tuple(
        (jnp.full((1, blk), -1e30, F32), jnp.zeros((1, blk), F32), jnp.zeros((HD, blk), F32))
        for _ in range(2)
    )
    c = lax.fori_loop(0, i, lambda j, c: step(j, c, False), init)
    c = step(i, c, True)
    ot = jnp.concatenate([c[h][2] / c[h][1] for h in range(2)], axis=0)
    low = jnp.transpose(ot).astype(BF)
    o_ref[...] = low
    lse_ref[0] = jnp.concatenate([c[h][0] + jnp.log(c[h][1]) for h in range(2)], axis=0)
    low_ref[pair] = low

    @pl.when(pair == pl.num_programs(0) - 1)
    def _():
        pairs = low_ref.shape[0]
        low = jnp.concatenate([low_ref[p] for p in range(pairs)], axis=1)
        share_ref[...] = dotg(low, w_ref[...]).astype(share_ref.dtype)


def attend(at, length, joint, w_out, held, kind, blk):
    rows, width, depth = joint.shape[0], w_out.shape[0], w_out.shape[1]
    pairs = width // 128
    return pl.pallas_call(
        functools.partial(attend_kernel, blk=blk),
        grid_spec=pltpu.PrefetchScalarGridSpec(
            num_scalar_prefetch=2,
            grid=(pairs,),
            in_specs=[
                pl.BlockSpec((blk, 128), lambda p, at, *_: (at[0], p)),
                pl.BlockSpec((rows, 128), lambda p, *_: (0, pairs + p)),
                pl.BlockSpec((rows, 128), lambda p, *_: (0, 2 * pairs + p)),
                pl.BlockSpec((width, depth), lambda p, *_: (0, 0), pipeline_mode=pl.Buffered(1)),
            ]
            + [pl.BlockSpec(memory_space=pl.ANY)] * len(held),
            out_specs=[
                pl.BlockSpec((blk, 128), lambda p, at, *_: (at[0], p)),
                pl.BlockSpec((1, 2, blk), lambda p, at, *_: (p, 0, at[0])),
                pl.BlockSpec((blk, depth), lambda p, *_: (0, 0)),
            ],
            scratch_shapes=[pltpu.VMEM((128, rows), BF), pltpu.VMEM((pairs, blk, 128), BF)],
        ),
        out_shape=[
            jax.ShapeDtypeStruct((rows, width), BF),
            jax.ShapeDtypeStruct((pairs, 2, rows), F32),
            jax.ShapeDtypeStruct((blk, depth), kind),
        ],
        input_output_aliases={6: 0, 7: 1} if held else {},
        compiler_params=pltpu.CompilerParams(vmem_limit_bytes=60 * MIB),
        cost_estimate=pl.CostEstimate(flops=rows * width, bytes_accessed=rows * width, transcendentals=0),
        name="attend",
    )(at, length, joint, joint, joint, w_out, *held)


def attend_back_kernel(
    len_ref, q_ref, k_ref, v_ref, o_ref, do_ref, lse_ref, cos_ref, sin_ref,
    dq_ref, dk_ref, dv_ref, kt, dlt, dqt, *, blk, blocks,
):
    length = len_ref[0]
    kt[...] = jnp.transpose(k_ref[...])
    dqt[...] = jnp.zeros_like(dqt)

    def products(i, _):
        at = pl.ds(pl.multiple_of(i * blk, blk), blk)
        both = jnp.transpose(do_ref[at, :].astype(F32) * o_ref[at, :].astype(F32))
        for h in range(2):
            dlt[h : h + 1, at] = jnp.sum(both[HD * h : HD * h + HD], axis=0, keepdims=True)
        return 0

    lax.fori_loop(0, blocks, products, 0)

    def keys(j, _):
        attend_back_keys(
            j, length, q_ref, k_ref, v_ref, do_ref, lse_ref, cos_ref, sin_ref, dk_ref, dv_ref, kt, dlt, dqt, blk, blocks
        )
        return 0

    lax.fori_loop(0, blocks, keys, 0)

    def turn(i, _):
        at = pl.ds(pl.multiple_of(i * blk, blk), blk)
        grad = jnp.transpose(dqt[:, at]) * 0.125
        dq_ref[at, :] = rotate(grad, cos_ref[at, :], -sin_ref[at, :]).astype(BF)
        return 0

    lax.fori_loop(0, blocks, turn, 0)


def attend_back_keys(
    j, length, q_ref, k_ref, v_ref, do_ref, lse_ref, cos_ref, sin_ref, dk_ref, dv_ref, kt, dlt, dqt, blk, blocks
):
    js = pl.multiple_of(j * blk, blk)
    lane = lax.broadcasted_iota(jnp.int32, (blk, 128), 1)
    kb = k_ref[pl.ds(js, blk), :] * jnp.asarray(0.125, BF)
    vb = v_ref[pl.ds(js, blk), :]
    zero = jnp.zeros_like(kb)
    ks = (jnp.where(lane < HD, kb, zero), jnp.where(lane < HD, zero, kb))
    vs = (jnp.where(lane < HD, vb, zero), jnp.where(lane < HD, zero, vb))

    def step(i, carry, diag):
        at = pl.ds(pl.multiple_of(i * blk, blk), blk)
        qb, dob = q_ref[at, :], do_ref[at, :]
        out = []
        for h in range(2):
            dk, dv = carry[h]
            s = dotg(ks[h], qb, NT)
            if diag:
                key = lax.broadcasted_iota(jnp.int32, (blk, blk), 0)
                qry = lax.broadcasted_iota(jnp.int32, (blk, blk), 1)
                s = jnp.where((key <= qry) & (key + js < length), s, -1e30)
            p = jnp.exp(s - lse_ref[0, h : h + 1, at])
            dp = dotg(vs[h], dob, NT)
            ds = (p * (dp - dlt[h : h + 1, at])).astype(BF)
            dv = dv + dotg(p.astype(BF), dob)
            dk = dk + dotg(ds, qb)
            dqt[HD * h : HD * h + HD, at] += dotg(kt[HD * h : HD * h + HD, pl.ds(js, blk)], ds)
            out.append((dk, dv))
        return tuple(out)

    z = jnp.zeros((blk, 128), F32)
    c = step(j, ((z, z), (z, z)), True)
    c = lax.fori_loop(j + 1, blocks, lambda i, c: step(i, c, False), c)
    grad = jnp.where(lane < HD, c[0][0], c[1][0]) * 0.125
    dk_ref[pl.ds(js, blk), :] = rotate(grad, cos_ref[pl.ds(js, blk), :], -sin_ref[pl.ds(js, blk), :]).astype(BF)
    dv_ref[pl.ds(js, blk), :] = jnp.where(lane < HD, c[0][1], c[1][1]).astype(BF)


def attend_back(length, joint, mixed, dmixed, lse, cos, sin, width, blk=512):
    rows = joint.shape[0]
    pairs, blocks = width // 128, rows // blk
    full = lambda off: pl.BlockSpec((rows, 128), lambda p, *_: (0, off * pairs + p))
    angle = pl.BlockSpec((rows, 128), lambda p, *_: (0, 0))
    return pl.pallas_call(
        functools.partial(attend_back_kernel, blk=blk, blocks=blocks),
        grid_spec=pltpu.PrefetchScalarGridSpec(
            num_scalar_prefetch=1,
            grid=(pairs,),
            in_specs=[full(0), full(1), full(2), full(0), full(0)]
            + [pl.BlockSpec((1, 2, rows), lambda p, *_: (p, 0, 0)), angle, angle],
            out_specs=[full(0)] * 3,
            scratch_shapes=[
                pltpu.VMEM((128, rows), BF),
                pltpu.VMEM((2, rows), F32),
                pltpu.VMEM((128, rows), F32),
            ],
        ),
        out_shape=[jax.ShapeDtypeStruct((rows, width), BF)] * 3,
        compiler_params=pltpu.CompilerParams(vmem_limit_bytes=60 * MIB),
        cost_estimate=pl.CostEstimate(
            flops=rows * width, bytes_accessed=rows * width, transcendentals=0
        ),
        name="attend_back",
    )(length, joint, joint, joint, mixed, dmixed, lse, cos, sin)


def gelu_parts(v):
    c = 0.7978845608028654
    return c, jnp.tanh(c * (v + 0.044715 * v * v * v))


def gelu_both(v):
    c, t = gelu_parts(v)
    half = 0.5 * (1.0 + t)
    return v * half, half + 0.5 * v * (1.0 - t * t) * c * (1.0 + 3 * 0.044715 * v * v)


def norm_parts(values):
    average = jnp.mean(values, axis=-1, keepdims=True)
    centred = values - average
    scale = lax.rsqrt(jnp.mean(centred * centred, axis=-1, keepdims=True) + EPSILON)
    return centred * scale, scale


def norm_back(grad, hat, scale, gain):
    g = grad * gain
    return scale * (
        g - jnp.mean(g, axis=-1, keepdims=True) - hat * jnp.mean(g * hat, axis=-1, keepdims=True)
    )


def column_sum(v):
    return jnp.sum(v, axis=0, keepdims=True)


def valid_rows(info_ref, start, count):
    at = info_ref[1] + start + lax.broadcasted_iota(jnp.int32, (count, 1), 0)
    return (at < info_ref[0]).astype(F32)


def loop_rows(rows, blk, body):
    def step(i, _):
        body(pl.multiple_of(i * blk, blk))
        return 0

    lax.fori_loop(0, rows // blk, step, 0)


def feed_kernel(info_ref, *refs, groups, chunks, sub):
    x_ref, bias_ref, resid_hbm, cot_hbm, bd_ref, gain_ref, shift_ref = refs[:7]
    ups, downs = refs[7 : 7 + groups], refs[7 + groups : 7 + 2 * groups]
    slope_ref, act_ref, out_ref, gb_ref, sums_ref, acc, resid_ref, cot_ref, sems = refs[7 + 2 * groups :]
    step = pl.program_id(0)
    rows = x_ref.shape[0]
    late = [
        pltpu.make_async_copy(resid_hbm, resid_ref, sems.at[0]),
        pltpu.make_async_copy(cot_hbm, cot_ref, sems.at[1]),
    ]

    @pl.when(step == 0)
    def _():
        for c in late:
            c.start()
        acc[...] = jnp.zeros_like(acc) + bd_ref[...].astype(F32)

    for g in range(groups):

        @pl.when(step // chunks == g)
        def _():
            for r in range(0, rows, sub):
                act, slope = gelu_both(dotg(x_ref[r : r + sub], ups[g][...], NT if g else NN) + bias_ref[0])
                slope_ref[r : r + sub] = slope.astype(BF)
                act = act.astype(BF)
                if g == 0:
                    act_ref[r : r + sub] = act
                acc[r : r + sub] += dotg(act, downs[g][...])

    @pl.when(step == groups * chunks - 1)
    def _():
        for c in late:
            c.wait()
        sums_ref[...] = jnp.zeros_like(sums_ref)
        gain, shift = gain_ref[3:4], shift_ref[3:4]
        blk = min(256, rows)

        def body(r):
            at = pl.ds(r, blk)
            valid = valid_rows(info_ref, r, blk)
            hat, scale = norm_parts(acc[at])
            out_ref[at] = (valid * (resid_ref[at] + hat * gain + shift)).astype(BF)
            g_out = valid * cot_ref[at].astype(F32)
            low = norm_back(g_out, hat, scale, gain).astype(BF)
            gb_ref[at] = low
            sums_ref[0:1] += column_sum(g_out * hat)
            sums_ref[1:2] += column_sum(g_out)
            sums_ref[2:3] += column_sum(low.astype(F32))

        loop_rows(rows, blk, body)


def feed_specs(depth, cols, chunks, rest):
    own = [
        pl.BlockSpec((depth, cols), lambda s, *_: (0, jnp.minimum(s, chunks - 1))),
        pl.BlockSpec((cols, depth), lambda s, *_: (jnp.minimum(s, chunks - 1), 0)),
    ]
    part = lambda g, i: pl.BlockSpec(
        (None, cols, depth), lambda s, *_: (i, jnp.clip(s - g * chunks, 0, chunks - 1), 0)
    )
    return [
        spec for i in range(2) for spec in [own[i]] + [part(g + 1, i) for g in range(len(rest))]
    ]


def feed(info, x, biases, up, down, rest, resid, cot, bias_down, gains, shifts, cols=1024):
    rows, depth = x.shape
    groups, hidden = 1 + len(rest), up.shape[1]
    cols = min(cols, hidden)
    chunks = hidden // cols
    once = lambda shape: pl.BlockSpec(shape, lambda s, *_: (0, 0), pipeline_mode=pl.Buffered(1))
    anyspace = pl.BlockSpec(memory_space=pl.ANY)
    own = lambda g: (lambda s, *_: (0, jnp.clip(s - g * chunks, 0, chunks - 1)))
    return pl.pallas_call(
        functools.partial(feed_kernel, groups=groups, chunks=chunks, sub=min(1024, rows)),
        grid_spec=pltpu.PrefetchScalarGridSpec(
            num_scalar_prefetch=1,
            grid=(groups * chunks,),
            in_specs=[
                once((rows, depth)),
                pl.BlockSpec((1, 1, cols), lambda s, *_: (s, 0, 0)),
                anyspace,
                anyspace,
                once((1, depth)),
                once(gains.shape),
                once(gains.shape),
            ]
            + feed_specs(depth, cols, chunks, rest),
            out_specs=[
                pl.BlockSpec((rows, cols), lambda s, *_: (0, s)),
                pl.BlockSpec((rows, cols), own(0)),
                once((rows, depth)),
                once((rows, depth)),
                once((8, depth)),
            ],
            scratch_shapes=[
                pltpu.VMEM((rows, depth), F32),
                pltpu.VMEM((rows, depth), F32),
                pltpu.VMEM((rows, depth), BF),
                pltpu.SemaphoreType.DMA((2,)),
            ],
        ),
        out_shape=[
            jax.ShapeDtypeStruct((rows, groups * hidden), BF),
            jax.ShapeDtypeStruct((rows, hidden), BF),
            jax.ShapeDtypeStruct((rows, depth), BF),
            jax.ShapeDtypeStruct((rows, depth), BF),
            jax.ShapeDtypeStruct((8, depth), F32),
        ],
        compiler_params=pltpu.CompilerParams(vmem_limit_bytes=60 * MIB),
        cost_estimate=pl.CostEstimate(flops=rows * depth, bytes_accessed=rows * depth, transcendentals=0),
        name="feed",
    )(info, x, biases.reshape(-1, 1, cols), resid, cot, bias_down, gains, shifts, up, *rest, down, *rest)


def feed_back_kernel(info_ref, *refs, groups, chunks, sub):
    gb_ref, slope_ref, resid_hbm, attn_hbm, cot_hbm, gain_ref = refs[:6]
    ups, downs = refs[6 : 6 + groups], refs[6 + groups : 6 + 2 * groups]
    gp_ref, gr_ref, ga_ref, sums_ref, acc, resid_ref, attn_ref, cot_ref, sems = refs[6 + 2 * groups :]
    step = pl.program_id(0)
    rows = gb_ref.shape[0]
    late = [
        pltpu.make_async_copy(src, dst, sems.at[i])
        for i, (src, dst) in enumerate(((resid_hbm, resid_ref), (attn_hbm, attn_ref), (cot_hbm, cot_ref)))
    ]

    @pl.when(step == 0)
    def _():
        for c in late:
            c.start()
        acc[...] = jnp.zeros_like(acc)

    for g in range(groups):

        @pl.when(step // chunks == g)
        def _():
            for r in range(0, rows, sub):
                grad = dotg(gb_ref[r : r + sub], downs[g][...], NT)
                low = (grad * slope_ref[r : r + sub].astype(F32)).astype(BF)
                if g == 0:
                    gp_ref[r : r + sub] = low
                acc[r : r + sub] += dotg(low, ups[g][...], NN if g else NT)

    @pl.when(step == groups * chunks - 1)
    def _():
        for c in late:
            c.wait()
        sums_ref[...] = jnp.zeros_like(sums_ref)
        blk = min(256, rows)

        def body(r):
            at = pl.ds(r, blk)
            g_out = valid_rows(info_ref, r, blk) * cot_ref[at].astype(F32)
            hat, scale = norm_parts(resid_ref[at])
            g_two = acc[at]
            g_resid = g_out + norm_back(g_two, hat, scale, gain_ref[2:3])
            gr_ref[at] = g_resid
            sums_ref[0:1] += column_sum(g_two * hat)
            sums_ref[1:2] += column_sum(g_two)
            hat, scale = norm_parts(attn_ref[at])
            ga_ref[at] = norm_back(g_resid, hat, scale, gain_ref[1:2]).astype(BF)
            sums_ref[2:3] += column_sum(g_resid * hat)
            sums_ref[3:4] += column_sum(g_resid)

        loop_rows(rows, blk, body)


def feed_back(info, gb, slope, up, down, rest, resid, attn_sum, cot, gains, cols=512):
    rows, depth = gb.shape
    groups, hidden = 1 + len(rest), up.shape[1]
    chunks = hidden // cols
    once = lambda shape: pl.BlockSpec(shape, lambda s, *_: (0, 0), pipeline_mode=pl.Buffered(1))
    anyspace = pl.BlockSpec(memory_space=pl.ANY)
    own = lambda g: (lambda s, *_: (0, jnp.clip(s - g * chunks, 0, chunks - 1)))
    return pl.pallas_call(
        functools.partial(feed_back_kernel, groups=groups, chunks=chunks, sub=min(1024, rows)),
        grid_spec=pltpu.PrefetchScalarGridSpec(
            num_scalar_prefetch=1,
            grid=(groups * chunks,),
            in_specs=[
                once((rows, depth)),
                pl.BlockSpec((rows, cols), lambda s, *_: (0, s)),
                anyspace,
                anyspace,
                anyspace,
                once(gains.shape),
            ]
            + feed_specs(depth, cols, chunks, rest),
            out_specs=[
                pl.BlockSpec((rows, cols), own(0)),
                once((rows, depth)),
                once((rows, depth)),
                once((8, depth)),
            ],
            scratch_shapes=[
                pltpu.VMEM((rows, depth), F32),
                pltpu.VMEM((rows, depth), F32),
                pltpu.VMEM((rows, depth), F32),
                pltpu.VMEM((rows, depth), BF),
                pltpu.SemaphoreType.DMA((3,)),
            ],
        ),
        out_shape=[
            jax.ShapeDtypeStruct((rows, hidden), BF),
            jax.ShapeDtypeStruct((rows, depth), F32),
            jax.ShapeDtypeStruct((rows, depth), BF),
            jax.ShapeDtypeStruct((8, depth), F32),
        ],
        compiler_params=pltpu.CompilerParams(vmem_limit_bytes=60 * MIB),
        cost_estimate=pl.CostEstimate(flops=rows * depth, bytes_accessed=rows * depth, transcendentals=0),
        name="feed_back",
    )(info, gb, slope, resid, attn_sum, cot, gains, up, *rest, down, *rest)


def feed_grad_kernel(*refs, groups):
    up_ref, down_ref, bias_ref, act_ref, gp_ref = refs[:5]
    n2s, gbs = refs[5 : 5 + groups], refs[5 + groups : 5 + 2 * groups]
    grad_ref, sum_ref = refs[5 + 2 * groups :]
    act, gp = act_ref[...], gp_ref[...]
    dup = dotg(gp, n2s[0][...], TN)
    ddown = dotg(act, gbs[0][...], TN)
    sums = column_sum(gp.astype(F32))
    for g in range(1, groups):
        pre = dotg(n2s[g][...], up_ref[...]) + bias_ref[0]
        act, slope = gelu_both(pre)
        act = act.astype(BF)
        gp = (dotg(gbs[g][...], down_ref[...], NT) * slope).astype(BF)
        dup += dotg(gp, n2s[g][...], TN)
        ddown += dotg(act, gbs[g][...], TN)
        sums += column_sum(gp.astype(F32))
    grad_ref[0] = dup.astype(BF)
    grad_ref[1] = ddown.astype(BF)
    sum_ref[0] = sums


def feed_grad(up, down, bias, act, gp, n2s, gbs, cols=512):
    rows, depth = n2s[0].shape
    groups, hidden = len(n2s), up.shape[1]
    once = lambda shape: pl.BlockSpec(shape, lambda s: (0, 0), pipeline_mode=pl.Buffered(1))
    wide = lambda count: pl.BlockSpec((count, cols), lambda s: (0, s))
    tall = pl.BlockSpec((cols, depth), lambda s: (s, 0))
    flat = pl.BlockSpec((1, 1, cols), lambda s: (s, 0, 0))
    return pl.pallas_call(
        functools.partial(feed_grad_kernel, groups=groups),
        grid=(hidden // cols,),
        in_specs=[wide(depth), tall, flat, wide(rows), wide(rows)] + [once((rows, depth))] * (2 * groups),
        out_specs=[pl.BlockSpec((2, cols, depth), lambda s: (0, s, 0)), flat],
        out_shape=[
            jax.ShapeDtypeStruct((2, hidden, depth), BF),
            jax.ShapeDtypeStruct((hidden // cols, 1, cols), F32),
        ],
        compiler_params=pltpu.CompilerParams(vmem_limit_bytes=60 * MIB),
        cost_estimate=pl.CostEstimate(
            flops=(8 * groups - 4) * rows * depth * hidden, bytes_accessed=20 * rows * depth, transcendentals=0
        ),
        name="feed_grad",
    )(up, down, bias.reshape(-1, 1, cols), act, gp, *n2s, *gbs)


def join_kernel(pick_ref, x_ref, gain_ref, shift_ref, *refs, blocks, each):
    parts, (attn_ref, resid_ref, low_ref) = refs[:-3], refs[-3:]
    block = pl.program_id(0) // each
    total = 0.0
    for g in range(len(parts) // blocks):
        wanted = pick_ref[g * blocks + block]
        part = parts[g * blocks][...]
        for b in range(1, blocks):
            part = jnp.where(wanted == b, parts[g * blocks + b][...], part)
        total = total + part.astype(F32)
    attn_ref[...] = total
    hat, _ = norm_parts(total)
    resid = x_ref[...].astype(F32) + hat * gain_ref[1:2] + shift_ref[1:2]
    resid_ref[...] = resid
    hat, _ = norm_parts(resid)
    low_ref[...] = (hat * gain_ref[2:3] + shift_ref[2:3]).astype(BF)


def join(x, gains, shifts, shares, picks, blk=256):
    rows, depth = x.shape
    blocks = len(shares[0])
    blk = min(blk, rows // blocks)
    each = rows // blocks // blk
    whole = pl.BlockSpec(gains.shape, lambda i, *_: (0, 0))
    block = pl.BlockSpec((blk, depth), lambda i, *_: (i, 0))
    part = lambda g, b: pl.BlockSpec(
        (blk, depth), lambda i, pick: (jnp.clip(i - pick[g * blocks + b] * each, 0, each - 1), 0)
    )
    return pl.pallas_call(
        functools.partial(join_kernel, blocks=blocks, each=each),
        grid_spec=pltpu.PrefetchScalarGridSpec(
            num_scalar_prefetch=1,
            grid=(rows // blk,),
            in_specs=[block, whole, whole] + [part(g, b) for g in range(len(shares)) for b in range(blocks)],
            out_specs=[block, block, block],
        ),
        out_shape=[
            jax.ShapeDtypeStruct((rows, depth), F32),
            jax.ShapeDtypeStruct((rows, depth), F32),
            jax.ShapeDtypeStruct((rows, depth), BF),
        ],
        compiler_params=pltpu.CompilerParams(vmem_limit_bytes=60 * MIB),
        name="join",
    )(picks, x, gains, shifts, *[v for share in shares for v in share])


def widen_kernel(up_ref, down_ref, dup_ref, ddown_ref):
    dup_ref[...] = jnp.transpose(up_ref[...]).astype(F32)
    ddown_ref[...] = down_ref[...].astype(F32)


def widen(grads, blk=512):
    hidden, depth = grads.shape[0] // 2, grads.shape[1]
    blk = min(blk, hidden)
    count = hidden // blk
    return pl.pallas_call(
        widen_kernel,
        grid=(count,),
        in_specs=[
            pl.BlockSpec((blk, depth), lambda i: (i, 0)),
            pl.BlockSpec((blk, depth), lambda i: (count + i, 0)),
        ],
        out_specs=[
            pl.BlockSpec((depth, blk), lambda i: (0, i)),
            pl.BlockSpec((blk, depth), lambda i: (i, 0)),
        ],
        out_shape=[
            jax.ShapeDtypeStruct((depth, hidden), F32),
            jax.ShapeDtypeStruct((hidden, depth), F32),
        ],
        compiler_params=pltpu.CompilerParams(vmem_limit_bytes=60 * MIB),
        name="widen",
    )(grads, grads)

MESH = pl.DeviceIdType.MESH


def exchange(src, dst, sems, slot, flipped):
    return pltpu.make_async_remote_copy(
        src_ref=src,
        dst_ref=dst,
        send_sem=sems[0].at[slot],
        recv_sem=sems[1].at[slot],
        device_id={"dp": lax.axis_index("dp") ^ flipped},
        device_id_type=MESH,
    )


def tail_kernel(
    gq_ref, gk_ref, gv_ref, mixed_ref, wq_ref, wk_ref, wv_ref, x_ref, gr_ref, gain_ref, vec_ref, *refs,
    bits, groups, steps,
):
    lefts, refs = refs[: 2 * groups], refs[2 * groups :]
    sum_ref, out_ref, total_ref = refs[:3]
    right, left, weight, x, g_resid, packed, acc, core_buf, buf, sent, came, own_share, vec_buf = refs[3:16]
    send, recv, vec_send, vec_recv, x_send, x_recv, local = refs[16:]
    sems = (send, recv)
    place, me = lax.axis_index("tensor"), lax.axis_index("dp")
    bit = lambda b: lax.rem(lax.div(me, 1 << b), 2)
    core = bit(0)
    outer = list(range(1, bits))
    order = [[b] for b in outer]
    rows, depth = x.shape
    width = weight.shape[2]
    half = 2 * depth
    base = pl.multiple_of(core * half, half)
    part = min(512, depth)
    chunks = half // part
    slots, fetched = iter(range(send.shape[0])), iter(range(local.shape[0]))

    def fetch(src, dst):
        c = pltpu.make_async_copy(src, dst, local.at[next(fetched)])
        c.start()
        return c

    def wait_all(copies):
        for c in copies:
            c.wait()

    second = [fetch(r, right.at[i]) for i, r in enumerate((gq_ref, gk_ref, gv_ref))]
    second += [fetch(r, weight.at[i]) for i, r in enumerate((wq_ref, wk_ref, wv_ref))]
    third = [fetch(r, left.at[i]) for i, r in enumerate(lefts)] + [fetch(mixed_ref, right.at[3])]
    fourth = [fetch(x_ref, x), fetch(gr_ref, g_resid)]

    flips = {1 << b for b in range(bits)}
    flips |= {sum(1 << b for b in some) for some in order}
    greeted = [{"dp": me ^ f} for f in sorted(flips)]
    greeted += [{"tensor": lax.rem(place + r, groups)} for r in range(1, groups)]
    for bits_of in steps:
        for mask in range(1, 1 << len(bits_of)):
            chosen = [bits_of[i] for i in range(len(bits_of)) if mask >> i & 1]
            flip = sum(1 << b for axis, b in chosen if axis == "dp")
            turn_by = sum(1 << b for axis, b in chosen if axis == "tensor")
            if flip and turn_by:
                greeted.append({"dp": me ^ flip, "tensor": place ^ turn_by})
            elif flip and flip not in flips:
                flips.add(flip)
                greeted.append({"dp": me ^ flip})
    barrier = pltpu.get_barrier_semaphore()
    for peer in greeted:
        pl.semaphore_signal(barrier, inc=1, device_id=peer, device_id_type=MESH)
    pl.semaphore_wait(barrier, len(greeted))

    def copy(src, dst, flipped):
        c = exchange(src, dst, sems, next(slots), flipped)
        c.start()
        return c

    def rank(some):
        return sum(bit(b) << i for i, b in enumerate(some))

    def other(mine, mask):
        for i in range(mask.bit_length()):
            if mask >> i & 1:
                mine = mine + (1 << i) * (1 - 2 * lax.rem(lax.div(mine, 1 << i), 2))
        return mine

    def peer(some, mask):
        return sum(1 << b for i, b in enumerate(some) if mask >> i & 1)

    forwards = []
    cores = {}

    def reduce(chunk):
        cores[chunk].wait()

        def join(i, _):
            at = pl.ds(pl.multiple_of(chunk * part + i * 64, 64), 64)
            own = packed[pl.ds(pl.multiple_of(base + chunk * part + i * 64, 64), 64)].astype(F32)
            acc[at] = (own + core_buf[at].astype(F32)).astype(BF)
            return 0

        lax.fori_loop(0, part // 64, join, 0)
        start, size = chunk * part, part
        landing = chunk * (part - part // (1 << (bits - 1)))
        for some in order:
            size //= 1 << len(some)
            mine = rank(some)
            copies = []
            for mask in range(1, 1 << len(some)):
                away = pl.multiple_of(start + other(mine, mask) * size, size)
                at = pl.ds(landing + (mask - 1) * size, size)
                copies.append(copy(acc.at[pl.ds(away, size)], buf.at[at], peer(some, mask)))
            start = start + mine * size
            yield
            wait_all(copies)
            step = min(size, 64)

            def body(i, _, start=start, landing=landing, step=step, size=size, count=len(copies)):
                at = pl.ds(pl.multiple_of(start + i * step, step), step)
                value = acc[at].astype(F32)
                for n in range(count):
                    value += buf[pl.ds(pl.multiple_of(landing + n * size + i * step, step), step)].astype(F32)
                acc[at] = value.astype(BF)
                return 0

            lax.fori_loop(0, size // step, body, 0)
            landing += len(copies) * size
        start = base + start
        sum_ref[pl.ds(pl.multiple_of(start, size), size)] = acc[pl.ds(pl.multiple_of(start - base, size), size)]
        for some in reversed(order):
            have = sum_ref.at[pl.ds(pl.multiple_of(start, size), size)]
            copies = [copy(have, have, peer(some, mask)) for mask in range(1, 1 << len(some))]
            yield
            wait_all(copies)
            start = start - rank(some) * size
            size *= 1 << len(some)
        have = sum_ref.at[pl.ds(pl.multiple_of(start, size), size)]
        forwards.append(copy(have, have, 1))

    quarter = rows // 4

    def share(r, piece):
        g = pl.ds(pl.multiple_of(lax.rem(place + r, groups) * rows + piece * quarter, quarter), quarter)
        value = dotg(right[0, g, :], weight[0], NT)
        value += dotg(right[1, g, :], weight[1], NT)
        value += dotg(right[2, g, :], weight[2], NT)
        return value

    shares = {}

    def share_away(r):
        def body(i, _):
            sent[r - 1, pl.ds(pl.multiple_of(i * quarter, quarter), quarter), :] = share(r, i).astype(BF)
            return 0

        for piece in range(4):
            lax.fori_loop(piece, piece + 1, body, 0)
            at, slot = pl.ds(piece * quarter, quarter), (r - 1) * 4 + piece
            c = pltpu.make_async_remote_copy(
                src_ref=sent.at[r - 1, at],
                dst_ref=came.at[r - 1, at],
                send_sem=x_send.at[slot],
                recv_sem=x_recv.at[slot],
                device_id={"tensor": lax.rem(place + r, groups)},
                device_id_type=MESH,
            )
            c.start()
            shares[r, piece] = c

    def share_own():
        def body(i, _):
            own_share[pl.ds(pl.multiple_of(i * quarter, quarter), quarter), :] = share(0, i)
            return 0

        lax.fori_loop(0, 4, body, 0)

    def weight_grad(side, some):
        cols = min(256, part)
        each = part // cols

        def body(i, _):
            first = pl.multiple_of(lax.rem(core + side, 2) * half + i * cols, cols)
            number = lax.div(first, depth)
            kind = lax.div(number, 3) * groups
            lanes = pl.ds(pl.multiple_of(lax.rem(first, depth), cols), cols)
            value = None
            for r in range(groups):
                at = pl.ds(pl.multiple_of(lax.rem(place + r, groups) * rows, rows), rows)
                term = dotg(left[kind + r, :, lanes], right[number, at, :], TN)
                value = term if value is None else value + term
            packed[pl.ds(first, cols), :] = value.astype(BF)
            return 0

        lax.fori_loop(some[0] * each, (some[-1] + 1) * each, body, 0)
        if side:
            for c in some:
                at = pl.ds(pl.multiple_of((1 - core) * half + c * part, part), part)
                cores[c] = copy(packed.at[at], core_buf.at[pl.ds(c * part, part)], 1)

    def last_norm(piece):
        wait_all([shares[r, piece] for r in range(1, groups)])
        blk = min(64, quarter)

        def body(i, _):
            at = pl.ds(pl.multiple_of(piece * quarter + i * blk, blk), blk)
            value = own_share[at, :]
            for r in range(groups - 1):
                value += came[r, at, :].astype(F32)
            hat, scale = norm_parts(x[at, :].astype(F32))
            out_ref[at, :] = (g_resid[at, :] + norm_back(value, hat, scale, gain_ref[0:1])).astype(BF)
            total_ref[0:1] += column_sum(value * hat)
            total_ref[1:2] += column_sum(value)
            return 0

        lax.fori_loop(0, quarter // blk, body, 0)

    def vectors():
        slot = 0
        for bits_of in steps:
            sends = []
            for mask in range(1, 1 << len(bits_of)):
                peer = {}
                for i, (axis, b) in enumerate(bits_of):
                    if mask >> i & 1:
                        peer[axis] = peer.get(axis, lax.axis_index(axis)) ^ (1 << b)
                sends.append(
                    pltpu.make_async_remote_copy(
                        src_ref=total_ref,
                        dst_ref=vec_buf.at[slot],
                        send_sem=vec_send.at[slot],
                        recv_sem=vec_recv.at[slot],
                        device_id=peer,
                        device_id_type=MESH,
                    )
                )
                sends[-1].start()
                slot += 1
            yield
            wait_all(sends)
            total = total_ref[...]
            for i in range(len(sends)):
                total += vec_buf[slot - len(sends) + i]
            total_ref[...] = total

    def turn(chains):
        still = []
        for chain in chains:
            try:
                next(chain)
                still.append(chain)
            except StopIteration:
                pass
        return still

    wait_all(second)
    for r in range(1, groups):
        share_away(r)
    wait_all(third)
    all_chunks = list(range(chunks))
    for some in (all_chunks[: chunks // 2], all_chunks[chunks // 2 :]):
        weight_grad(1, some)
    wait_all(fourth)
    total_ref[...] = vec_ref[...]
    reduces = []
    for i, chunk in enumerate(all_chunks):
        weight_grad(0, [chunk])
        reduces = turn(reduces + [reduce(chunk)])
    share_own()
    reduces = turn(reduces)
    last_norm(0)
    last_norm(1)
    reduces = turn(reduces)
    last_norm(2)
    reduces = turn(reduces)
    last_norm(3)
    chain = turn([vectors()])
    while reduces or chain:
        reduces, chain = turn(reduces), turn(chain)
    wait_all(forwards)


def tail(grads, mixed, weights, x, g_resid, gains, vectors, n1s, gas, bits, steps):
    (slots, width), (rows, depth), groups = mixed.shape, x.shape, len(n1s)
    half = 2 * depth
    landing = half - half // (1 << (bits - 1))
    count = half // min(512, depth) * (3 * bits + 2)
    vecs = sum((1 << len(b)) - 1 for b in steps)
    vmem = pl.BlockSpec(memory_space=pltpu.VMEM)
    anyspace = pl.BlockSpec(memory_space=pl.ANY)
    dma = pltpu.SemaphoreType.DMA
    peers = max(groups - 1, 1)
    return pl.pallas_call(
        functools.partial(tail_kernel, bits=bits, groups=groups, steps=steps),
        in_specs=[anyspace] * 9 + [vmem] * 2 + [anyspace] * (2 * groups),
        out_specs=[vmem, vmem, vmem],
        out_shape=[
            jax.ShapeDtypeStruct((4 * depth, width), BF),
            jax.ShapeDtypeStruct((rows, depth), BF),
            jax.ShapeDtypeStruct(vectors.shape, F32),
        ],
        scratch_shapes=[
            pltpu.VMEM((4, slots, width), BF),
            pltpu.VMEM((2 * groups, rows, depth), BF),
            pltpu.VMEM((3, depth, width), BF),
            pltpu.VMEM((rows, depth), BF),
            pltpu.VMEM((rows, depth), F32),
            pltpu.VMEM((4 * depth, width), BF),
            pltpu.VMEM((half, width), BF),
            pltpu.VMEM((half, width), BF),
            pltpu.VMEM((landing, width), BF),
            pltpu.VMEM((peers, rows, depth), BF),
            pltpu.VMEM((peers, rows, depth), BF),
            pltpu.VMEM((rows, depth), F32),
            pltpu.VMEM((vecs,) + vectors.shape, F32),
            dma((count,)),
            dma((count,)),
            dma((vecs,)),
            dma((vecs,)),
            dma((4 * peers,)),
            dma((4 * peers,)),
            dma((9 + 2 * groups,)),
        ],
        compiler_params=pltpu.CompilerParams(
            collective_id=1, has_side_effects=True, vmem_limit_bytes=60 * MIB
        ),
        cost_estimate=pl.CostEstimate(flops=rows * width, bytes_accessed=rows * width, transcendentals=0),
        name="tail",
    )(*grads, mixed, *weights, x, g_resid, gains, vectors, *n1s, *gas)


def mixed_back_kernel(at_ref, x_ref, w_ref, *refs):
    refs[-1][...] = dotg(x_ref[...], w_ref[...], NT).astype(BF)


def mixed_back(where, x, w_out, slots, held, blk=512):
    rows, depth = x.shape
    width = w_out.shape[0]
    blk = min(blk, rows)
    count = rows // blk
    return pl.pallas_call(
        mixed_back_kernel,
        grid_spec=pltpu.PrefetchScalarGridSpec(
            num_scalar_prefetch=1,
            grid=(count,),
            in_specs=[
                pl.BlockSpec((blk, depth), lambda i, at: (i, 0)),
                pl.BlockSpec((width, depth), lambda i, at: (0, 0)),
            ]
            + [pl.BlockSpec(memory_space=pl.ANY)] * len(held),
            out_specs=pl.BlockSpec((blk, width), lambda i, at: (at[0] * count + i, 0)),
        ),
        out_shape=jax.ShapeDtypeStruct((slots, width), BF),
        input_output_aliases={3: 0} if held else {},
        compiler_params=pltpu.CompilerParams(vmem_limit_bytes=60 * MIB),
        cost_estimate=pl.CostEstimate(flops=rows * depth, bytes_accessed=rows * depth, transcendentals=0),
        name="mixed_back",
    )(where, x, w_out, *held)


def shift(x, axis, count, step):
    return lax.ppermute(x, axis, [((i + step) % count, i) for i in range(count)])


def shards(
    tokens,
    lengths,
    cotangent,
    w_query,
    w_key,
    w_value,
    w_out,
    up_weight,
    bias_up,
    down_weight,
    bias_down,
    norm_gains,
    norm_shifts,
):
    rows, _, depth = tokens.shape
    groups, replicas = lax.axis_size("tensor"), lax.axis_size("dp")
    me, replica = lax.axis_index("tensor"), lax.axis_index("dp")
    slots = rows * groups
    width = w_query.shape[1]
    hidden = up_weight.shape[1]
    x = tokens.reshape(rows, depth)
    here = me.reshape(1).astype(jnp.int32)
    place = lambda r: (here + r) % groups

    def others(v):
        return [shift(v, "tensor", groups, r) for r in range(1, groups)]

    def to_owner(v, r):
        return shift(v, "tensor", groups, groups - r)

    count = hidden // replicas
    up_piece = lax.dynamic_slice_in_dim(up_weight, replica * count, count, 1)
    down_piece = lax.dynamic_slice_in_dim(down_weight, replica * count, count, 0)
    piece = jnp.stack([jnp.transpose(up_piece), down_piece])

    freqs = 10000.0 ** (-jnp.arange(HD // 2).astype(F32) * 2.0 / HD)
    angles = jnp.arange(slots).astype(F32)[:, None] * freqs[None, :]
    cosine, sine = jnp.cos(angles), jnp.sin(angles)
    cosine = jnp.concatenate([cosine] * 4, axis=1)
    sine = jnp.concatenate([-sine, sine] * 2, axis=1)
    x_rest = others(x)
    weights = (w_query, w_key, w_value)
    joint, normed_one = project(here, x, norm_gains, norm_shifts, *weights, cosine, sine, [])
    joint, x_rest, piece, bias = lax.optimization_barrier((joint, x_rest, piece, bias_up))
    pieces, bias_rest = others(piece), others(bias)
    normed_one_rest = []
    for r, v in enumerate(x_rest):
        joint, n = project(place(r + 1), v, norm_gains, norm_shifts, *weights, cosine, sine, [joint])
        normed_one_rest.append(n)
    joint, pieces, bias_rest = lax.optimization_barrier((joint, pieces, bias_rest))
    blk = min(512, rows)
    each = rows // blk
    odd = lambda r: lax.rem(place(r), 2)
    ranks = lambda r, k: jnp.where(odd(r) == 1, each - 1 - k, k)
    held, shares, arrived = (), [], [[] for _ in range(1, groups)]
    for k in range(each):
        for r in range(1, groups):
            *held, share = attend(place(r) * each + ranks(0, k), lengths, joint, w_out, held, BF, blk)
            arrived[r - 1].append(to_owner(share, r))
        if k == each - 1 and k > 0:
            joint, arrived = lax.optimization_barrier((joint, [v[:k] for v in arrived])), arrived
            joint, early = joint
            arrived = [list(e) + v[k:] for e, v in zip(early, arrived)]
        *held, share = attend(here * each + ranks(0, k), lengths, joint, w_out, held, BF, blk)
        shares.append(share)
    mixed, lse = held
    shares = [shares] + arrived
    picks = jnp.concatenate([ranks(groups - r, k) for r in range(groups) for k in range(each)])
    rest = [lax.all_gather(p, "dp", axis=1, tiled=True) for p in pieces]
    biases = jnp.concatenate([bias_up] + bias_rest).astype(F32)

    info = jnp.stack([lengths[0], me * rows]).astype(jnp.int32)
    cot = cotangent.reshape(rows, depth)
    attn_sum, resid, normed_two = join(x, norm_gains, norm_shifts, shares, picks)
    normed_two_rest = others(normed_two)
    slope, act, layer_out, g_branch, sums3 = feed(
        info, normed_two, biases, up_weight, down_weight, rest, resid, cot,
        bias_down.reshape(1, depth), norm_gains, norm_shifts,
    )
    g_branch_rest = others(g_branch)
    g_pre, g_resid, g_attn, sums21 = feed_back(
        info, g_branch, slope, up_weight, down_weight, rest, resid, attn_sum, cot, norm_gains
    )
    g_attn_rest = others(g_attn)
    g_pre, normed_two_rest = lax.optimization_barrier((g_pre, normed_two_rest))
    g_mixed = mixed_back(here, g_attn, w_out, slots, [])
    g_pre, g_mixed = lax.optimization_barrier((g_pre, g_mixed))
    grad_feed, bias_up_sum = feed_grad(
        up_weight, down_weight, biases[:hidden], act, g_pre,
        [normed_two] + normed_two_rest, [g_branch] + g_branch_rest,
    )
    grad_feed = grad_feed.reshape(2 * hidden, depth)
    g_mixed, g_attn_rest, grad_feed = lax.optimization_barrier((g_mixed, g_attn_rest, grad_feed))
    grad_feed = lax.psum(grad_feed, "dp")
    for r, g in enumerate(g_attn_rest):
        g_mixed = mixed_back(place(r + 1), g, w_out, slots, [g_mixed])

    grads = attend_back(lengths, joint, mixed, g_mixed, lse, cosine, sine, width)
    placed = lax.dynamic_update_slice(
        jnp.zeros((groups * hidden,), F32), bias_up_sum.reshape(-1), (me * hidden,)
    ).reshape(-1, depth)
    bits = (replicas - 1).bit_length()
    steps = [("tensor", b) for b in range((groups - 1).bit_length())] + [("dp", b) for b in range(bits)]
    steps = [tuple(steps[i : i + 2]) for i in range(0, len(steps), 2)]
    vectors = jnp.concatenate([jnp.zeros((2, depth), F32), sums3[:3], sums21[:4], placed])
    vectors = jnp.pad(vectors, ((0, -len(vectors) % 8), (0, 0)))
    packed, grad_tokens, sums = tail(
        grads, mixed, weights, x, g_resid, norm_gains, vectors,
        [normed_one] + normed_one_rest, [g_attn] + g_attn_rest, bits, steps,
    )
    grad_up, grad_down = widen(grad_feed)
    grad_query, grad_key, grad_value = (packed[i * depth : (i + 1) * depth].astype(F32) for i in range(3))
    grad_out = jnp.transpose(packed[3 * depth :]).astype(F32)
    grad_gains = jnp.stack([sums[0], sums[7], sums[5], sums[2]])
    grad_shifts = jnp.stack([sums[1], sums[8], sums[6], sums[3]])
    grad_bias_up = lax.dynamic_slice_in_dim(sums[9 : 9 + groups * hidden // depth].reshape(-1), me * hidden, hidden, 0)
    whole = (rows, 1, depth)
    return (
        layer_out.reshape(whole),
        grad_tokens.reshape(whole),
        grad_query,
        grad_key,
        grad_value,
        grad_out,
        grad_up,
        grad_bias_up,
        grad_down,
        sums[4],
        grad_gains,
        grad_shifts,
    )


def solution(mesh):
    wide, tall = P(None, "tensor"), P("tensor", None)
    acts = P("tensor", "dp", None)
    return jax.shard_map(
        shards,
        mesh=mesh,
        in_specs=(acts, P("dp"), acts, wide, wide, wide, tall, wide, P("tensor"), tall, P(), P(), P()),
        out_specs=(acts, acts, wide, wide, wide, tall, wide, P("tensor"), tall, P(), P(), P()),
        check_vma=False,
    )
```

```python
import functools
import jax
import jax.numpy as jnp
from jax import lax
from jax.experimental import pallas as pl
from jax.experimental.pallas import tpu as pltpu
from jax.sharding import PartitionSpec as P

HD = 64
EPSILON = 1e-05
BF = jnp.bfloat16
F32 = jnp.float32
NT = (((1,), (1,)), ((), ()))
NN = (((1,), (0,)), ((), ()))
TN = (((0,), (0,)), ((), ()))
MIB = 1 << 20


def dotg(a, b, dims=NN):
    return lax.dot_general(a, b, dims, preferred_element_type=F32)


def rotate(x, cos, sin):
    first = lax.broadcasted_iota(jnp.int32, (x.shape[0], 128), 1) % HD < HD // 2
    parts = []
    for a in range(0, x.shape[1], 128):
        v = x[:, a : a + 128]
        swapped = jnp.where(first, pltpu.roll(v, 96, 1), pltpu.roll(v, 32, 1))
        parts.append(v * cos + swapped * sin)
    return jnp.concatenate(parts, axis=1) if len(parts) > 1 else parts[0]


def qkv_kernel(at_ref, x_ref, wq_ref, wk_ref, wv_ref, cos_ref, sin_ref, gain_ref, shift_ref, *refs):
    o_ref, normed_ref = refs[-2:]
    width = wq_ref.shape[1]
    hat, _ = norm_parts(x_ref[...].astype(F32))
    x = (hat * gain_ref[0:1] + shift_ref[0:1]).astype(BF)
    normed_ref[...] = x
    cos, sin = cos_ref[...], sin_ref[...]
    o_ref[:, :width] = rotate(dotg(x, wq_ref[...]), cos, sin).astype(BF)
    o_ref[:, width : 2 * width] = rotate(dotg(x, wk_ref[...]), cos, sin).astype(BF)
    o_ref[:, 2 * width :] = dotg(x, wv_ref[...]).astype(BF)


def project(where, x, gains, shifts, w_query, w_key, w_value, cos, sin, held, blk=512):
    rows, depth = x.shape
    width, slots = w_query.shape[1], cos.shape[0]
    blk = min(blk, rows)
    count = rows // blk
    once = lambda shape: pl.BlockSpec(shape, lambda i, at: (0, 0), pipeline_mode=pl.Buffered(1))
    angle = pl.BlockSpec((blk, 128), lambda i, at: (at[0] * count + i, 0))
    block = pl.BlockSpec((blk, depth), lambda i, at: (i, 0))
    return pl.pallas_call(
        qkv_kernel,
        grid_spec=pltpu.PrefetchScalarGridSpec(
            num_scalar_prefetch=1,
            grid=(count,),
            in_specs=[block] + [once((depth, width))] * 3 + [angle, angle, once(gains.shape), once(gains.shape)]
            + [pl.BlockSpec(memory_space=pl.ANY)] * len(held),
            out_specs=[pl.BlockSpec((blk, 3 * width), lambda i, at: (at[0] * count + i, 0)), block],
        ),
        out_shape=[
            jax.ShapeDtypeStruct((slots, 3 * width), BF),
            jax.ShapeDtypeStruct((rows, depth), BF),
        ],
        input_output_aliases={9: 0} if held else {},
        compiler_params=pltpu.CompilerParams(vmem_limit_bytes=60 * MIB),
        cost_estimate=pl.CostEstimate(flops=rows * depth, bytes_accessed=rows * depth, transcendentals=0),
        name="project",
    )(where, x, w_query, w_key, w_value, cos, sin, gains, shifts, *held)


def attend_kernel(at_ref, len_ref, q_ref, k_ref, v_ref, w_ref, *refs, blk):
    o_ref, lse_ref, share_ref, vt, low_ref = refs[-5:]
    pair = pl.program_id(0)
    i = at_ref[0]
    length = len_ref[0]
    def turn(j, _):
        part = pl.ds(pl.multiple_of(j * blk, blk), blk)
        vt[:, part] = jnp.transpose(v_ref[part, :])
        return 0

    lax.fori_loop(0, i + 1, turn, 0)
    lane = lax.broadcasted_iota(jnp.int32, (blk, 128), 1)
    q = q_ref[...] * jnp.asarray(0.125, BF)
    zero = jnp.zeros_like(q)
    qs = (jnp.where(lane < HD, q, zero), jnp.where(lane < HD, zero, q))

    def step(j, carry, diag):
        start = pl.multiple_of(j * blk, blk)
        kb = k_ref[pl.ds(start, blk), :]
        sub = min(256, blk)
        n = blk // sub
        if diag:
            key = lax.broadcasted_iota(jnp.int32, (sub, blk), 0)
            qry = lax.broadcasted_iota(jnp.int32, (sub, blk), 1)
        state = [carry[h] for h in range(2)]
        chains = [(h, t) for t in range(n) for h in range(2)]
        live = {}

        def first(c):
            h, t = chains[c]
            live[c] = dotg(kb[t * sub : t * sub + sub], qs[h], NT)

        def middle(c):
            h, t = chains[c]
            s = live[c]
            if diag:
                s = jnp.where((key + t * sub <= qry) & (key + t * sub + start < length), s, -1e30)
            m, l, acc = state[h]
            mn = jnp.maximum(m, jnp.max(s, axis=0, keepdims=True))
            p = jnp.exp(s - mn)
            al = jnp.exp(m - mn)
            state[h] = (mn, l * al + jnp.sum(p, axis=0, keepdims=True), acc)
            live[c] = (p.astype(BF), al)

        def last(c):
            h, t = chains[c]
            p, al = live.pop(c)
            m, l, acc = state[h]
            state[h] = (m, l, acc * al + dotg(vt[HD * h : HD * h + HD, pl.ds(start + t * sub, sub)], p))

        stages = (first, middle, last)
        for i in range(len(chains) + 4):
            for k in range(3):
                c = i - 2 * k
                if 0 <= c < len(chains):
                    stages[k](c)
        return tuple(state)

    init = tuple(
        (jnp.full((1, blk), -1e30, F32), jnp.zeros((1, blk), F32), jnp.zeros((HD, blk), F32))
        for _ in range(2)
    )
    c = lax.fori_loop(0, i, lambda j, c: step(j, c, False), init)
    c = step(i, c, True)
    ot = jnp.concatenate([c[h][2] / c[h][1] for h in range(2)], axis=0)
    low = jnp.transpose(ot).astype(BF)
    o_ref[...] = low
    lse_ref[0] = jnp.concatenate([c[h][0] + jnp.log(c[h][1]) for h in range(2)], axis=0)
    low_ref[pair] = low

    @pl.when(pair == pl.num_programs(0) - 1)
    def _():
        pairs = low_ref.shape[0]
        low = jnp.concatenate([low_ref[p] for p in range(pairs)], axis=1)
        share_ref[...] = dotg(low, w_ref[...]).astype(share_ref.dtype)


def attend(at, length, joint, w_out, held, kind, blk):
    rows, width, depth = joint.shape[0], w_out.shape[0], w_out.shape[1]
    pairs = width // 128
    return pl.pallas_call(
        functools.partial(attend_kernel, blk=blk),
        grid_spec=pltpu.PrefetchScalarGridSpec(
            num_scalar_prefetch=2,
            grid=(pairs,),
            in_specs=[
                pl.BlockSpec((blk, 128), lambda p, at, *_: (at[0], p)),
                pl.BlockSpec((rows, 128), lambda p, *_: (0, pairs + p)),
                pl.BlockSpec((rows, 128), lambda p, *_: (0, 2 * pairs + p)),
                pl.BlockSpec((width, depth), lambda p, *_: (0, 0), pipeline_mode=pl.Buffered(1)),
            ]
            + [pl.BlockSpec(memory_space=pl.ANY)] * len(held),
            out_specs=[
                pl.BlockSpec((blk, 128), lambda p, at, *_: (at[0], p)),
                pl.BlockSpec((1, 2, blk), lambda p, at, *_: (p, 0, at[0])),
                pl.BlockSpec((blk, depth), lambda p, *_: (0, 0)),
            ],
            scratch_shapes=[pltpu.VMEM((128, rows), BF), pltpu.VMEM((pairs, blk, 128), BF)],
        ),
        out_shape=[
            jax.ShapeDtypeStruct((rows, width), BF),
            jax.ShapeDtypeStruct((pairs, 2, rows), F32),
            jax.ShapeDtypeStruct((blk, depth), kind),
        ],
        input_output_aliases={6: 0, 7: 1} if held else {},
        compiler_params=pltpu.CompilerParams(vmem_limit_bytes=60 * MIB),
        cost_estimate=pl.CostEstimate(flops=rows * width, bytes_accessed=rows * width, transcendentals=0),
        name="attend",
    )(at, length, joint, joint, joint, w_out, *held)


def attend_back_kernel(
    len_ref, q_ref, k_ref, v_ref, o_ref, do_ref, lse_ref, cos_ref, sin_ref,
    dq_ref, dk_ref, dv_ref, kt, dlt, dqt, *, blk, blocks,
):
    length = len_ref[0]
    kt[...] = jnp.transpose(k_ref[...])
    dqt[...] = jnp.zeros_like(dqt)

    def products(i, _):
        at = pl.ds(pl.multiple_of(i * blk, blk), blk)
        both = jnp.transpose(do_ref[at, :].astype(F32) * o_ref[at, :].astype(F32))
        for h in range(2):
            dlt[h : h + 1, at] = jnp.sum(both[HD * h : HD * h + HD], axis=0, keepdims=True)
        return 0

    lax.fori_loop(0, blocks, products, 0)

    def keys(j, _):
        attend_back_keys(
            j, length, q_ref, k_ref, v_ref, do_ref, lse_ref, cos_ref, sin_ref, dk_ref, dv_ref, kt, dlt, dqt, blk, blocks
        )
        return 0

    lax.fori_loop(0, blocks, keys, 0)

    def turn(i, _):
        at = pl.ds(pl.multiple_of(i * blk, blk), blk)
        grad = jnp.transpose(dqt[:, at]) * 0.125
        dq_ref[at, :] = rotate(grad, cos_ref[at, :], -sin_ref[at, :]).astype(BF)
        return 0

    lax.fori_loop(0, blocks, turn, 0)


def attend_back_keys(
    j, length, q_ref, k_ref, v_ref, do_ref, lse_ref, cos_ref, sin_ref, dk_ref, dv_ref, kt, dlt, dqt, blk, blocks
):
    js = pl.multiple_of(j * blk, blk)
    lane = lax.broadcasted_iota(jnp.int32, (blk, 128), 1)
    kb = k_ref[pl.ds(js, blk), :] * jnp.asarray(0.125, BF)
    vb = v_ref[pl.ds(js, blk), :]
    zero = jnp.zeros_like(kb)
    ks = (jnp.where(lane < HD, kb, zero), jnp.where(lane < HD, zero, kb))
    vs = (jnp.where(lane < HD, vb, zero), jnp.where(lane < HD, zero, vb))

    def step(i, carry, diag):
        at = pl.ds(pl.multiple_of(i * blk, blk), blk)
        qb, dob = q_ref[at, :], do_ref[at, :]
        out = []
        for h in range(2):
            dk, dv = carry[h]
            s = dotg(ks[h], qb, NT)
            if diag:
                key = lax.broadcasted_iota(jnp.int32, (blk, blk), 0)
                qry = lax.broadcasted_iota(jnp.int32, (blk, blk), 1)
                s = jnp.where((key <= qry) & (key + js < length), s, -1e30)
            p = jnp.exp(s - lse_ref[0, h : h + 1, at])
            dp = dotg(vs[h], dob, NT)
            ds = (p * (dp - dlt[h : h + 1, at])).astype(BF)
            dv = dv + dotg(p.astype(BF), dob)
            dk = dk + dotg(ds, qb)
            dqt[HD * h : HD * h + HD, at] += dotg(kt[HD * h : HD * h + HD, pl.ds(js, blk)], ds)
            out.append((dk, dv))
        return tuple(out)

    z = jnp.zeros((blk, 128), F32)
    c = step(j, ((z, z), (z, z)), True)
    c = lax.fori_loop(j + 1, blocks, lambda i, c: step(i, c, False), c)
    grad = jnp.where(lane < HD, c[0][0], c[1][0]) * 0.125
    dk_ref[pl.ds(js, blk), :] = rotate(grad, cos_ref[pl.ds(js, blk), :], -sin_ref[pl.ds(js, blk), :]).astype(BF)
    dv_ref[pl.ds(js, blk), :] = jnp.where(lane < HD, c[0][1], c[1][1]).astype(BF)


def attend_back(length, joint, mixed, dmixed, lse, cos, sin, width, blk=512):
    rows = joint.shape[0]
    pairs, blocks = width // 128, rows // blk
    full = lambda off: pl.BlockSpec((rows, 128), lambda p, *_: (0, off * pairs + p))
    angle = pl.BlockSpec((rows, 128), lambda p, *_: (0, 0))
    return pl.pallas_call(
        functools.partial(attend_back_kernel, blk=blk, blocks=blocks),
        grid_spec=pltpu.PrefetchScalarGridSpec(
            num_scalar_prefetch=1,
            grid=(pairs,),
            in_specs=[full(0), full(1), full(2), full(0), full(0)]
            + [pl.BlockSpec((1, 2, rows), lambda p, *_: (p, 0, 0)), angle, angle],
            out_specs=[full(0)] * 3,
            scratch_shapes=[
                pltpu.VMEM((128, rows), BF),
                pltpu.VMEM((2, rows), F32),
                pltpu.VMEM((128, rows), F32),
            ],
        ),
        out_shape=[jax.ShapeDtypeStruct((rows, width), BF)] * 3,
        compiler_params=pltpu.CompilerParams(vmem_limit_bytes=60 * MIB),
        cost_estimate=pl.CostEstimate(
            flops=rows * width, bytes_accessed=rows * width, transcendentals=0
        ),
        name="attend_back",
    )(length, joint, joint, joint, mixed, dmixed, lse, cos, sin)


def gelu_parts(v):
    c = 0.7978845608028654
    return c, jnp.tanh(c * (v + 0.044715 * v * v * v))


def gelu_both(v):
    c, t = gelu_parts(v)
    half = 0.5 * (1.0 + t)
    return v * half, half + 0.5 * v * (1.0 - t * t) * c * (1.0 + 3 * 0.044715 * v * v)


def norm_parts(values):
    average = jnp.mean(values, axis=-1, keepdims=True)
    centred = values - average
    scale = lax.rsqrt(jnp.mean(centred * centred, axis=-1, keepdims=True) + EPSILON)
    return centred * scale, scale


def norm_back(grad, hat, scale, gain):
    g = grad * gain
    return scale * (
        g - jnp.mean(g, axis=-1, keepdims=True) - hat * jnp.mean(g * hat, axis=-1, keepdims=True)
    )


def column_sum(v):
    return jnp.sum(v, axis=0, keepdims=True)


def valid_rows(info_ref, start, count):
    at = info_ref[1] + start + lax.broadcasted_iota(jnp.int32, (count, 1), 0)
    return (at < info_ref[0]).astype(F32)


def loop_rows(rows, blk, body):
    def step(i, _):
        body(pl.multiple_of(i * blk, blk))
        return 0

    lax.fori_loop(0, rows // blk, step, 0)


def feed_kernel(info_ref, *refs, groups, chunks, sub):
    x_ref, bias_ref, resid_hbm, cot_hbm, bd_ref, gain_ref, shift_ref = refs[:7]
    ups, downs = refs[7 : 7 + groups], refs[7 + groups : 7 + 2 * groups]
    slope_ref, act_ref, out_ref, gb_ref, sums_ref, acc, resid_ref, cot_ref, sems = refs[7 + 2 * groups :]
    step = pl.program_id(0)
    rows = x_ref.shape[0]
    late = [
        pltpu.make_async_copy(resid_hbm, resid_ref, sems.at[0]),
        pltpu.make_async_copy(cot_hbm, cot_ref, sems.at[1]),
    ]

    @pl.when(step == 0)
    def _():
        for c in late:
            c.start()
        acc[...] = jnp.zeros_like(acc) + bd_ref[...].astype(F32)

    for g in range(groups):

        @pl.when(step // chunks == g)
        def _():
            for r in range(0, rows, sub):
                act, slope = gelu_both(dotg(x_ref[r : r + sub], ups[g][...], NT if g else NN) + bias_ref[0])
                slope_ref[r : r + sub] = slope.astype(BF)
                act = act.astype(BF)
                if g == 0:
                    act_ref[r : r + sub] = act
                acc[r : r + sub] += dotg(act, downs[g][...])

    @pl.when(step == groups * chunks - 1)
    def _():
        for c in late:
            c.wait()
        sums_ref[...] = jnp.zeros_like(sums_ref)
        gain, shift = gain_ref[3:4], shift_ref[3:4]
        blk = min(256, rows)

        def body(r):
            at = pl.ds(r, blk)
            valid = valid_rows(info_ref, r, blk)
            hat, scale = norm_parts(acc[at])
            out_ref[at] = (valid * (resid_ref[at] + hat * gain + shift)).astype(BF)
            g_out = valid * cot_ref[at].astype(F32)
            low = norm_back(g_out, hat, scale, gain).astype(BF)
            gb_ref[at] = low
            sums_ref[0:1] += column_sum(g_out * hat)
            sums_ref[1:2] += column_sum(g_out)
            sums_ref[2:3] += column_sum(low.astype(F32))

        loop_rows(rows, blk, body)


def feed_specs(depth, cols, chunks, rest):
    own = [
        pl.BlockSpec((depth, cols), lambda s, *_: (0, jnp.minimum(s, chunks - 1))),
        pl.BlockSpec((cols, depth), lambda s, *_: (jnp.minimum(s, chunks - 1), 0)),
    ]
    part = lambda g, i: pl.BlockSpec(
        (None, cols, depth), lambda s, *_: (i, jnp.clip(s - g * chunks, 0, chunks - 1), 0)
    )
    return [
        spec for i in range(2) for spec in [own[i]] + [part(g + 1, i) for g in range(len(rest))]
    ]


def feed(info, x, biases, up, down, rest, resid, cot, bias_down, gains, shifts, cols=1024):
    rows, depth = x.shape
    groups, hidden = 1 + len(rest), up.shape[1]
    cols = min(cols, hidden)
    chunks = hidden // cols
    once = lambda shape: pl.BlockSpec(shape, lambda s, *_: (0, 0), pipeline_mode=pl.Buffered(1))
    anyspace = pl.BlockSpec(memory_space=pl.ANY)
    own = lambda g: (lambda s, *_: (0, jnp.clip(s - g * chunks, 0, chunks - 1)))
    return pl.pallas_call(
        functools.partial(feed_kernel, groups=groups, chunks=chunks, sub=min(1024, rows)),
        grid_spec=pltpu.PrefetchScalarGridSpec(
            num_scalar_prefetch=1,
            grid=(groups * chunks,),
            in_specs=[
                once((rows, depth)),
                pl.BlockSpec((1, 1, cols), lambda s, *_: (s, 0, 0)),
                anyspace,
                anyspace,
                once((1, depth)),
                once(gains.shape),
                once(gains.shape),
            ]
            + feed_specs(depth, cols, chunks, rest),
            out_specs=[
                pl.BlockSpec((rows, cols), lambda s, *_: (0, s)),
                pl.BlockSpec((rows, cols), own(0)),
                once((rows, depth)),
                once((rows, depth)),
                once((8, depth)),
            ],
            scratch_shapes=[
                pltpu.VMEM((rows, depth), F32),
                pltpu.VMEM((rows, depth), F32),
                pltpu.VMEM((rows, depth), BF),
                pltpu.SemaphoreType.DMA((2,)),
            ],
        ),
        out_shape=[
            jax.ShapeDtypeStruct((rows, groups * hidden), BF),
            jax.ShapeDtypeStruct((rows, hidden), BF),
            jax.ShapeDtypeStruct((rows, depth), BF),
            jax.ShapeDtypeStruct((rows, depth), BF),
            jax.ShapeDtypeStruct((8, depth), F32),
        ],
        compiler_params=pltpu.CompilerParams(vmem_limit_bytes=60 * MIB),
        cost_estimate=pl.CostEstimate(flops=rows * depth, bytes_accessed=rows * depth, transcendentals=0),
        name="feed",
    )(info, x, biases.reshape(-1, 1, cols), resid, cot, bias_down, gains, shifts, up, *rest, down, *rest)


def feed_back_kernel(info_ref, *refs, groups, chunks, sub):
    gb_ref, slope_ref, resid_hbm, attn_hbm, cot_hbm, gain_ref = refs[:6]
    ups, downs = refs[6 : 6 + groups], refs[6 + groups : 6 + 2 * groups]
    gp_ref, gr_ref, ga_ref, sums_ref, acc, resid_ref, attn_ref, cot_ref, sems = refs[6 + 2 * groups :]
    step = pl.program_id(0)
    rows = gb_ref.shape[0]
    late = [
        pltpu.make_async_copy(src, dst, sems.at[i])
        for i, (src, dst) in enumerate(((resid_hbm, resid_ref), (attn_hbm, attn_ref), (cot_hbm, cot_ref)))
    ]

    @pl.when(step == 0)
    def _():
        for c in late:
            c.start()
        acc[...] = jnp.zeros_like(acc)

    for g in range(groups):

        @pl.when(step // chunks == g)
        def _():
            for r in range(0, rows, sub):
                grad = dotg(gb_ref[r : r + sub], downs[g][...], NT)
                low = (grad * slope_ref[r : r + sub].astype(F32)).astype(BF)
                if g == 0:
                    gp_ref[r : r + sub] = low
                acc[r : r + sub] += dotg(low, ups[g][...], NN if g else NT)

    @pl.when(step == groups * chunks - 1)
    def _():
        for c in late:
            c.wait()
        sums_ref[...] = jnp.zeros_like(sums_ref)
        blk = min(256, rows)

        def body(r):
            at = pl.ds(r, blk)
            g_out = valid_rows(info_ref, r, blk) * cot_ref[at].astype(F32)
            hat, scale = norm_parts(resid_ref[at])
            g_two = acc[at]
            g_resid = g_out + norm_back(g_two, hat, scale, gain_ref[2:3])
            gr_ref[at] = g_resid
            sums_ref[0:1] += column_sum(g_two * hat)
            sums_ref[1:2] += column_sum(g_two)
            hat, scale = norm_parts(attn_ref[at])
            ga_ref[at] = norm_back(g_resid, hat, scale, gain_ref[1:2]).astype(BF)
            sums_ref[2:3] += column_sum(g_resid * hat)
            sums_ref[3:4] += column_sum(g_resid)

        loop_rows(rows, blk, body)


def feed_back(info, gb, slope, up, down, rest, resid, attn_sum, cot, gains, cols=512):
    rows, depth = gb.shape
    groups, hidden = 1 + len(rest), up.shape[1]
    chunks = hidden // cols
    once = lambda shape: pl.BlockSpec(shape, lambda s, *_: (0, 0), pipeline_mode=pl.Buffered(1))
    anyspace = pl.BlockSpec(memory_space=pl.ANY)
    own = lambda g: (lambda s, *_: (0, jnp.clip(s - g * chunks, 0, chunks - 1)))
    return pl.pallas_call(
        functools.partial(feed_back_kernel, groups=groups, chunks=chunks, sub=min(1024, rows)),
        grid_spec=pltpu.PrefetchScalarGridSpec(
            num_scalar_prefetch=1,
            grid=(groups * chunks,),
            in_specs=[
                once((rows, depth)),
                pl.BlockSpec((rows, cols), lambda s, *_: (0, s)),
                anyspace,
                anyspace,
                anyspace,
                once(gains.shape),
            ]
            + feed_specs(depth, cols, chunks, rest),
            out_specs=[
                pl.BlockSpec((rows, cols), own(0)),
                once((rows, depth)),
                once((rows, depth)),
                once((8, depth)),
            ],
            scratch_shapes=[
                pltpu.VMEM((rows, depth), F32),
                pltpu.VMEM((rows, depth), F32),
                pltpu.VMEM((rows, depth), F32),
                pltpu.VMEM((rows, depth), BF),
                pltpu.SemaphoreType.DMA((3,)),
            ],
        ),
        out_shape=[
            jax.ShapeDtypeStruct((rows, hidden), BF),
            jax.ShapeDtypeStruct((rows, depth), F32),
            jax.ShapeDtypeStruct((rows, depth), BF),
            jax.ShapeDtypeStruct((8, depth), F32),
        ],
        compiler_params=pltpu.CompilerParams(vmem_limit_bytes=60 * MIB),
        cost_estimate=pl.CostEstimate(flops=rows * depth, bytes_accessed=rows * depth, transcendentals=0),
        name="feed_back",
    )(info, gb, slope, resid, attn_sum, cot, gains, up, *rest, down, *rest)


def feed_grad_kernel(*refs, groups):
    up_ref, down_ref, bias_ref, act_ref, gp_ref = refs[:5]
    n2s, gbs = refs[5 : 5 + groups], refs[5 + groups : 5 + 2 * groups]
    grad_ref, sum_ref = refs[5 + 2 * groups :]
    act, gp = act_ref[...], gp_ref[...]
    dup = dotg(gp, n2s[0][...], TN)
    ddown = dotg(act, gbs[0][...], TN)
    sums = column_sum(gp.astype(F32))
    for g in range(1, groups):
        pre = dotg(n2s[g][...], up_ref[...]) + bias_ref[0]
        act, slope = gelu_both(pre)
        act = act.astype(BF)
        gp = (dotg(gbs[g][...], down_ref[...], NT) * slope).astype(BF)
        dup += dotg(gp, n2s[g][...], TN)
        ddown += dotg(act, gbs[g][...], TN)
        sums += column_sum(gp.astype(F32))
    grad_ref[0] = dup.astype(BF)
    grad_ref[1] = ddown.astype(BF)
    sum_ref[0] = sums


def feed_grad(up, down, bias, act, gp, n2s, gbs, cols=512):
    rows, depth = n2s[0].shape
    groups, hidden = len(n2s), up.shape[1]
    once = lambda shape: pl.BlockSpec(shape, lambda s: (0, 0), pipeline_mode=pl.Buffered(1))
    wide = lambda count: pl.BlockSpec((count, cols), lambda s: (0, s))
    tall = pl.BlockSpec((cols, depth), lambda s: (s, 0))
    flat = pl.BlockSpec((1, 1, cols), lambda s: (s, 0, 0))
    return pl.pallas_call(
        functools.partial(feed_grad_kernel, groups=groups),
        grid=(hidden // cols,),
        in_specs=[wide(depth), tall, flat, wide(rows), wide(rows)] + [once((rows, depth))] * (2 * groups),
        out_specs=[pl.BlockSpec((2, cols, depth), lambda s: (0, s, 0)), flat],
        out_shape=[
            jax.ShapeDtypeStruct((2, hidden, depth), BF),
            jax.ShapeDtypeStruct((hidden // cols, 1, cols), F32),
        ],
        compiler_params=pltpu.CompilerParams(vmem_limit_bytes=60 * MIB),
        cost_estimate=pl.CostEstimate(
            flops=(8 * groups - 4) * rows * depth * hidden, bytes_accessed=20 * rows * depth, transcendentals=0
        ),
        name="feed_grad",
    )(up, down, bias.reshape(-1, 1, cols), act, gp, *n2s, *gbs)


def join_kernel(pick_ref, x_ref, gain_ref, shift_ref, *refs, blocks, each):
    parts, (attn_ref, resid_ref, low_ref) = refs[:-3], refs[-3:]
    block = pl.program_id(0) // each
    total = 0.0
    for g in range(len(parts) // blocks):
        wanted = pick_ref[g * blocks + block]
        part = parts[g * blocks][...]
        for b in range(1, blocks):
            part = jnp.where(wanted == b, parts[g * blocks + b][...], part)
        total = total + part.astype(F32)
    attn_ref[...] = total
    hat, _ = norm_parts(total)
    resid = x_ref[...].astype(F32) + hat * gain_ref[1:2] + shift_ref[1:2]
    resid_ref[...] = resid
    hat, _ = norm_parts(resid)
    low_ref[...] = (hat * gain_ref[2:3] + shift_ref[2:3]).astype(BF)


def join(x, gains, shifts, shares, picks, blk=256):
    rows, depth = x.shape
    blocks = len(shares[0])
    blk = min(blk, rows // blocks)
    each = rows // blocks // blk
    whole = pl.BlockSpec(gains.shape, lambda i, *_: (0, 0))
    block = pl.BlockSpec((blk, depth), lambda i, *_: (i, 0))
    part = lambda g, b: pl.BlockSpec(
        (blk, depth), lambda i, pick: (jnp.clip(i - pick[g * blocks + b] * each, 0, each - 1), 0)
    )
    return pl.pallas_call(
        functools.partial(join_kernel, blocks=blocks, each=each),
        grid_spec=pltpu.PrefetchScalarGridSpec(
            num_scalar_prefetch=1,
            grid=(rows // blk,),
            in_specs=[block, whole, whole] + [part(g, b) for g in range(len(shares)) for b in range(blocks)],
            out_specs=[block, block, block],
        ),
        out_shape=[
            jax.ShapeDtypeStruct((rows, depth), F32),
            jax.ShapeDtypeStruct((rows, depth), F32),
            jax.ShapeDtypeStruct((rows, depth), BF),
        ],
        compiler_params=pltpu.CompilerParams(vmem_limit_bytes=60 * MIB),
        name="join",
    )(picks, x, gains, shifts, *[v for share in shares for v in share])


def widen_kernel(up_ref, down_ref, dup_ref, ddown_ref):
    dup_ref[...] = jnp.transpose(up_ref[...]).astype(F32)
    ddown_ref[...] = down_ref[...].astype(F32)


def widen(grads, blk=512):
    hidden, depth = grads.shape[0] // 2, grads.shape[1]
    blk = min(blk, hidden)
    count = hidden // blk
    return pl.pallas_call(
        widen_kernel,
        grid=(count,),
        in_specs=[
            pl.BlockSpec((blk, depth), lambda i: (i, 0)),
            pl.BlockSpec((blk, depth), lambda i: (count + i, 0)),
        ],
        out_specs=[
            pl.BlockSpec((depth, blk), lambda i: (0, i)),
            pl.BlockSpec((blk, depth), lambda i: (i, 0)),
        ],
        out_shape=[
            jax.ShapeDtypeStruct((depth, hidden), F32),
            jax.ShapeDtypeStruct((hidden, depth), F32),
        ],
        compiler_params=pltpu.CompilerParams(vmem_limit_bytes=60 * MIB),
        name="widen",
    )(grads, grads)

MESH = pl.DeviceIdType.MESH


def exchange(src, dst, sems, slot, flipped):
    return pltpu.make_async_remote_copy(
        src_ref=src,
        dst_ref=dst,
        send_sem=sems[0].at[slot],
        recv_sem=sems[1].at[slot],
        device_id={"dp": lax.axis_index("dp") ^ flipped},
        device_id_type=MESH,
    )


def tail_kernel(
    gq_ref, gk_ref, gv_ref, mixed_ref, wq_ref, wk_ref, wv_ref, x_ref, gr_ref, gain_ref, vec_ref, *refs,
    bits, groups, steps,
):
    lefts, refs = refs[: 2 * groups], refs[2 * groups :]
    sum_ref, out_ref, total_ref = refs[:3]
    right, left, weight, x, g_resid, packed, acc, core_buf, buf, sent, came, own_share, vec_buf = refs[3:16]
    send, recv, vec_send, vec_recv, x_send, x_recv, local = refs[16:]
    sems = (send, recv)
    place, me = lax.axis_index("tensor"), lax.axis_index("dp")
    bit = lambda b: lax.rem(lax.div(me, 1 << b), 2)
    core = bit(0)
    outer = list(range(1, bits))
    order = [[b] for b in outer]
    rows, depth = x.shape
    width = weight.shape[2]
    half = 2 * depth
    base = pl.multiple_of(core * half, half)
    part = min(512, depth)
    chunks = half // part
    slots, fetched = iter(range(send.shape[0])), iter(range(local.shape[0]))

    def fetch(src, dst):
        c = pltpu.make_async_copy(src, dst, local.at[next(fetched)])
        c.start()
        return c

    def wait_all(copies):
        for c in copies:
            c.wait()

    second = [fetch(r, right.at[i]) for i, r in enumerate((gq_ref, gk_ref, gv_ref))]
    second += [fetch(r, weight.at[i]) for i, r in enumerate((wq_ref, wk_ref, wv_ref))]
    third = [fetch(r, left.at[i]) for i, r in enumerate(lefts)] + [fetch(mixed_ref, right.at[3])]
    fourth = [fetch(x_ref, x), fetch(gr_ref, g_resid)]

    flips = {1 << b for b in range(bits)}
    flips |= {sum(1 << b for b in some) for some in order}
    greeted = [{"dp": me ^ f} for f in sorted(flips)]
    greeted += [{"tensor": lax.rem(place + r, groups)} for r in range(1, groups)]
    for bits_of in steps:
        for mask in range(1, 1 << len(bits_of)):
            chosen = [bits_of[i] for i in range(len(bits_of)) if mask >> i & 1]
            flip = sum(1 << b for axis, b in chosen if axis == "dp")
            turn_by = sum(1 << b for axis, b in chosen if axis == "tensor")
            if flip and turn_by:
                greeted.append({"dp": me ^ flip, "tensor": place ^ turn_by})
            elif flip and flip not in flips:
                flips.add(flip)
                greeted.append({"dp": me ^ flip})
    barrier = pltpu.get_barrier_semaphore()
    for peer in greeted:
        pl.semaphore_signal(barrier, inc=1, device_id=peer, device_id_type=MESH)
    pl.semaphore_wait(barrier, len(greeted))

    def copy(src, dst, flipped):
        c = exchange(src, dst, sems, next(slots), flipped)
        c.start()
        return c

    def rank(some):
        return sum(bit(b) << i for i, b in enumerate(some))

    def other(mine, mask):
        for i in range(mask.bit_length()):
            if mask >> i & 1:
                mine = mine + (1 << i) * (1 - 2 * lax.rem(lax.div(mine, 1 << i), 2))
        return mine

    def peer(some, mask):
        return sum(1 << b for i, b in enumerate(some) if mask >> i & 1)

    forwards = []
    cores = {}

    def reduce(chunk):
        cores[chunk].wait()

        def join(i, _):
            at = pl.ds(pl.multiple_of(chunk * part + i * 64, 64), 64)
            own = packed[pl.ds(pl.multiple_of(base + chunk * part + i * 64, 64), 64)].astype(F32)
            acc[at] = (own + core_buf[at].astype(F32)).astype(BF)
            return 0

        lax.fori_loop(0, part // 64, join, 0)
        start, size = chunk * part, part
        landing = chunk * (part - part // (1 << (bits - 1)))
        for some in order:
            size //= 1 << len(some)
            mine = rank(some)
            copies = []
            for mask in range(1, 1 << len(some)):
                away = pl.multiple_of(start + other(mine, mask) * size, size)
                at = pl.ds(landing + (mask - 1) * size, size)
                copies.append(copy(acc.at[pl.ds(away, size)], buf.at[at], peer(some, mask)))
            start = start + mine * size
            yield
            wait_all(copies)
            step = min(size, 64)

            def body(i, _, start=start, landing=landing, step=step, size=size, count=len(copies)):
                at = pl.ds(pl.multiple_of(start + i * step, step), step)
                value = acc[at].astype(F32)
                for n in range(count):
                    value += buf[pl.ds(pl.multiple_of(landing + n * size + i * step, step), step)].astype(F32)
                acc[at] = value.astype(BF)
                return 0

            lax.fori_loop(0, size // step, body, 0)
            landing += len(copies) * size
        start = base + start
        sum_ref[pl.ds(pl.multiple_of(start, size), size)] = acc[pl.ds(pl.multiple_of(start - base, size), size)]
        for some in reversed(order):
            have = sum_ref.at[pl.ds(pl.multiple_of(start, size), size)]
            copies = [copy(have, have, peer(some, mask)) for mask in range(1, 1 << len(some))]
            yield
            wait_all(copies)
            start = start - rank(some) * size
            size *= 1 << len(some)
        have = sum_ref.at[pl.ds(pl.multiple_of(start, size), size)]
        forwards.append(copy(have, have, 1))

    quarter = rows // 4

    def share(r, piece):
        g = pl.ds(pl.multiple_of(lax.rem(place + r, groups) * rows + piece * quarter, quarter), quarter)
        value = dotg(right[0, g, :], weight[0], NT)
        value += dotg(right[1, g, :], weight[1], NT)
        value += dotg(right[2, g, :], weight[2], NT)
        return value

    shares = {}

    def share_away(r):
        def body(i, _):
            sent[r - 1, pl.ds(pl.multiple_of(i * quarter, quarter), quarter), :] = share(r, i).astype(BF)
            return 0

        for piece in range(4):
            lax.fori_loop(piece, piece + 1, body, 0)
            at, slot = pl.ds(piece * quarter, quarter), (r - 1) * 4 + piece
            c = pltpu.make_async_remote_copy(
                src_ref=sent.at[r - 1, at],
                dst_ref=came.at[r - 1, at],
                send_sem=x_send.at[slot],
                recv_sem=x_recv.at[slot],
                device_id={"tensor": lax.rem(place + r, groups)},
                device_id_type=MESH,
            )
            c.start()
            shares[r, piece] = c

    def share_own():
        def body(i, _):
            own_share[pl.ds(pl.multiple_of(i * quarter, quarter), quarter), :] = share(0, i)
            return 0

        lax.fori_loop(0, 4, body, 0)

    def weight_grad(side, some):
        cols = min(256, part)
        each = part // cols

        def body(i, _):
            first = pl.multiple_of(lax.rem(core + side, 2) * half + i * cols, cols)
            number = lax.div(first, depth)
            kind = lax.div(number, 3) * groups
            lanes = pl.ds(pl.multiple_of(lax.rem(first, depth), cols), cols)
            value = None
            for r in range(groups):
                at = pl.ds(pl.multiple_of(lax.rem(place + r, groups) * rows, rows), rows)
                term = dotg(left[kind + r, :, lanes], right[number, at, :], TN)
                value = term if value is None else value + term
            packed[pl.ds(first, cols), :] = value.astype(BF)
            return 0

        lax.fori_loop(some[0] * each, (some[-1] + 1) * each, body, 0)
        if side:
            for c in some:
                at = pl.ds(pl.multiple_of((1 - core) * half + c * part, part), part)
                cores[c] = copy(packed.at[at], core_buf.at[pl.ds(c * part, part)], 1)

    def last_norm(piece):
        wait_all([shares[r, piece] for r in range(1, groups)])
        blk = min(64, quarter)

        def body(i, _):
            at = pl.ds(pl.multiple_of(piece * quarter + i * blk, blk), blk)
            value = own_share[at, :]
            for r in range(groups - 1):
                value += came[r, at, :].astype(F32)
            hat, scale = norm_parts(x[at, :].astype(F32))
            out_ref[at, :] = (g_resid[at, :] + norm_back(value, hat, scale, gain_ref[0:1])).astype(BF)
            total_ref[0:1] += column_sum(value * hat)
            total_ref[1:2] += column_sum(value)
            return 0

        lax.fori_loop(0, quarter // blk, body, 0)

    def vectors():
        slot = 0
        for bits_of in steps:
            sends = []
            for mask in range(1, 1 << len(bits_of)):
                peer = {}
                for i, (axis, b) in enumerate(bits_of):
                    if mask >> i & 1:
                        peer[axis] = peer.get(axis, lax.axis_index(axis)) ^ (1 << b)
                sends.append(
                    pltpu.make_async_remote_copy(
                        src_ref=total_ref,
                        dst_ref=vec_buf.at[slot],
                        send_sem=vec_send.at[slot],
                        recv_sem=vec_recv.at[slot],
                        device_id=peer,
                        device_id_type=MESH,
                    )
                )
                sends[-1].start()
                slot += 1
            yield
            wait_all(sends)
            total = total_ref[...]
            for i in range(len(sends)):
                total += vec_buf[slot - len(sends) + i]
            total_ref[...] = total

    def turn(chains):
        still = []
        for chain in chains:
            try:
                next(chain)
                still.append(chain)
            except StopIteration:
                pass
        return still

    wait_all(second)
    for r in range(1, groups):
        share_away(r)
    wait_all(third)
    all_chunks = list(range(chunks))
    for some in (all_chunks[: chunks // 2], all_chunks[chunks // 2 :]):
        weight_grad(1, some)
    wait_all(fourth)
    total_ref[...] = vec_ref[...]
    reduces = []
    for i, chunk in enumerate(all_chunks):
        weight_grad(0, [chunk])
        reduces = turn(reduces + [reduce(chunk)])
    share_own()
    reduces = turn(reduces)
    last_norm(0)
    last_norm(1)
    reduces = turn(reduces)
    last_norm(2)
    reduces = turn(reduces)
    last_norm(3)
    chain = turn([vectors()])
    while reduces or chain:
        reduces, chain = turn(reduces), turn(chain)
    wait_all(forwards)


def tail(grads, mixed, weights, x, g_resid, gains, vectors, n1s, gas, bits, steps):
    (slots, width), (rows, depth), groups = mixed.shape, x.shape, len(n1s)
    half = 2 * depth
    landing = half - half // (1 << (bits - 1))
    count = half // min(512, depth) * (3 * bits + 2)
    vecs = sum((1 << len(b)) - 1 for b in steps)
    vmem = pl.BlockSpec(memory_space=pltpu.VMEM)
    anyspace = pl.BlockSpec(memory_space=pl.ANY)
    dma = pltpu.SemaphoreType.DMA
    peers = max(groups - 1, 1)
    return pl.pallas_call(
        functools.partial(tail_kernel, bits=bits, groups=groups, steps=steps),
        in_specs=[anyspace] * 9 + [vmem] * 2 + [anyspace] * (2 * groups),
        out_specs=[vmem, vmem, vmem],
        out_shape=[
            jax.ShapeDtypeStruct((4 * depth, width), BF),
            jax.ShapeDtypeStruct((rows, depth), BF),
            jax.ShapeDtypeStruct(vectors.shape, F32),
        ],
        scratch_shapes=[
            pltpu.VMEM((4, slots, width), BF),
            pltpu.VMEM((2 * groups, rows, depth), BF),
            pltpu.VMEM((3, depth, width), BF),
            pltpu.VMEM((rows, depth), BF),
            pltpu.VMEM((rows, depth), F32),
            pltpu.VMEM((4 * depth, width), BF),
            pltpu.VMEM((half, width), BF),
            pltpu.VMEM((half, width), BF),
            pltpu.VMEM((landing, width), BF),
            pltpu.VMEM((peers, rows, depth), BF),
            pltpu.VMEM((peers, rows, depth), BF),
            pltpu.VMEM((rows, depth), F32),
            pltpu.VMEM((vecs,) + vectors.shape, F32),
            dma((count,)),
            dma((count,)),
            dma((vecs,)),
            dma((vecs,)),
            dma((4 * peers,)),
            dma((4 * peers,)),
            dma((9 + 2 * groups,)),
        ],
        compiler_params=pltpu.CompilerParams(
            collective_id=1, has_side_effects=True, vmem_limit_bytes=60 * MIB
        ),
        cost_estimate=pl.CostEstimate(flops=rows * width, bytes_accessed=rows * width, transcendentals=0),
        name="tail",
    )(*grads, mixed, *weights, x, g_resid, gains, vectors, *n1s, *gas)


def mixed_back_kernel(at_ref, x_ref, w_ref, *refs):
    refs[-1][...] = dotg(x_ref[...], w_ref[...], NT).astype(BF)


def mixed_back(where, x, w_out, slots, held, flops, blk=512):
    rows, depth = x.shape
    width = w_out.shape[0]
    blk = min(blk, rows)
    count = rows // blk
    return pl.pallas_call(
        mixed_back_kernel,
        grid_spec=pltpu.PrefetchScalarGridSpec(
            num_scalar_prefetch=1,
            grid=(count,),
            in_specs=[
                pl.BlockSpec((blk, depth), lambda i, at: (i, 0)),
                pl.BlockSpec((width, depth), lambda i, at: (0, 0)),
            ]
            + [pl.BlockSpec(memory_space=pl.ANY)] * len(held),
            out_specs=pl.BlockSpec((blk, width), lambda i, at: (at[0] * count + i, 0)),
        ),
        out_shape=jax.ShapeDtypeStruct((slots, width), BF),
        input_output_aliases={3: 0} if held else {},
        compiler_params=pltpu.CompilerParams(vmem_limit_bytes=60 * MIB),
        cost_estimate=pl.CostEstimate(flops=flops, bytes_accessed=rows * depth, transcendentals=0),
        name="mixed_back",
    )(where, x, w_out, *held)


def shift(x, axis, count, step):
    return lax.ppermute(x, axis, [((i + step) % count, i) for i in range(count)])


def shards(
    tokens,
    lengths,
    cotangent,
    w_query,
    w_key,
    w_value,
    w_out,
    up_weight,
    bias_up,
    down_weight,
    bias_down,
    norm_gains,
    norm_shifts,
):
    rows, _, depth = tokens.shape
    groups, replicas = lax.axis_size("tensor"), lax.axis_size("dp")
    me, replica = lax.axis_index("tensor"), lax.axis_index("dp")
    slots = rows * groups
    width = w_query.shape[1]
    hidden = up_weight.shape[1]
    x = tokens.reshape(rows, depth)
    here = me.reshape(1).astype(jnp.int32)
    place = lambda r: (here + r) % groups

    def others(v):
        return [shift(v, "tensor", groups, r) for r in range(1, groups)]

    def to_owner(v, r):
        return shift(v, "tensor", groups, groups - r)

    count = hidden // replicas
    up_piece = lax.dynamic_slice_in_dim(up_weight, replica * count, count, 1)
    down_piece = lax.dynamic_slice_in_dim(down_weight, replica * count, count, 0)
    piece = jnp.stack([jnp.transpose(up_piece), down_piece])

    freqs = 10000.0 ** (-jnp.arange(HD // 2).astype(F32) * 2.0 / HD)
    angles = jnp.arange(slots).astype(F32)[:, None] * freqs[None, :]
    cosine, sine = jnp.cos(angles), jnp.sin(angles)
    cosine = jnp.concatenate([cosine] * 4, axis=1)
    sine = jnp.concatenate([-sine, sine] * 2, axis=1)
    x_rest = others(x)
    weights = (w_query, w_key, w_value)
    joint, normed_one = project(here, x, norm_gains, norm_shifts, *weights, cosine, sine, [])
    joint, x_rest, piece, bias = lax.optimization_barrier((joint, x_rest, piece, bias_up))
    pieces, bias_rest = others(piece), others(bias)
    normed_one_rest = []
    for r, v in enumerate(x_rest):
        joint, n = project(place(r + 1), v, norm_gains, norm_shifts, *weights, cosine, sine, [joint])
        normed_one_rest.append(n)
    joint, pieces, bias_rest = lax.optimization_barrier((joint, pieces, bias_rest))
    blk = min(512, rows)
    each = rows // blk
    odd = lambda r: lax.rem(place(r), 2)
    ranks = lambda r, k: jnp.where(odd(r) == 1, each - 1 - k, k)
    held, shares, arrived = (), [], [[] for _ in range(1, groups)]
    for k in range(each):
        for r in range(1, groups):
            *held, share = attend(place(r) * each + ranks(0, k), lengths, joint, w_out, held, BF, blk)
            arrived[r - 1].append(to_owner(share, r))
        if k == each - 1 and k > 0:
            joint, arrived = lax.optimization_barrier((joint, [v[:k] for v in arrived])), arrived
            joint, early = joint
            arrived = [list(e) + v[k:] for e, v in zip(early, arrived)]
        *held, share = attend(here * each + ranks(0, k), lengths, joint, w_out, held, BF, blk)
        shares.append(share)
    mixed, lse = held
    shares = [shares] + arrived
    picks = jnp.concatenate([ranks(groups - r, k) for r in range(groups) for k in range(each)])
    rest = [lax.all_gather(p, "dp", axis=1, tiled=True) for p in pieces]
    biases = jnp.concatenate([bias_up] + bias_rest).astype(F32)

    info = jnp.stack([lengths[0], me * rows]).astype(jnp.int32)
    cot = cotangent.reshape(rows, depth)
    attn_sum, resid, normed_two = join(x, norm_gains, norm_shifts, shares, picks)
    normed_two_rest = others(normed_two)
    slope, act, layer_out, g_branch, sums3 = feed(
        info, normed_two, biases, up_weight, down_weight, rest, resid, cot,
        bias_down.reshape(1, depth), norm_gains, norm_shifts,
    )
    g_branch_rest = others(g_branch)
    g_pre, g_resid, g_attn, sums21 = feed_back(
        info, g_branch, slope, up_weight, down_weight, rest, resid, attn_sum, cot, norm_gains
    )
    g_attn_rest = others(g_attn)
    g_pre, normed_two_rest = lax.optimization_barrier((g_pre, normed_two_rest))
    g_mixed = mixed_back(here, g_attn, w_out, slots, [], rows * depth)
    g_pre, g_mixed = lax.optimization_barrier((g_pre, g_mixed))
    grad_feed, bias_up_sum = feed_grad(
        up_weight, down_weight, biases[:hidden], act, g_pre,
        [normed_two] + normed_two_rest, [g_branch] + g_branch_rest,
    )
    grad_feed = grad_feed.reshape(2 * hidden, depth)
    grad_feed = lax.psum(grad_feed, "dp")
    g_mixed, g_attn_rest, bias_up_sum = lax.optimization_barrier((g_mixed, g_attn_rest, bias_up_sum))
    for r, g in enumerate(g_attn_rest):
        g_mixed = mixed_back(place(r + 1), g, w_out, slots, [g_mixed], 50 * rows * depth * width)

    grads = attend_back(lengths, joint, mixed, g_mixed, lse, cosine, sine, width)
    placed = lax.dynamic_update_slice(
        jnp.zeros((groups * hidden,), F32), bias_up_sum.reshape(-1), (me * hidden,)
    ).reshape(-1, depth)
    bits = (replicas - 1).bit_length()
    steps = [("tensor", b) for b in range((groups - 1).bit_length())] + [("dp", b) for b in range(bits)]
    steps = [tuple(steps[i : i + 2]) for i in range(0, len(steps), 2)]
    vectors = jnp.concatenate([jnp.zeros((2, depth), F32), sums3[:3], sums21[:4], placed])
    vectors = jnp.pad(vectors, ((0, -len(vectors) % 8), (0, 0)))
    packed, grad_tokens, sums = tail(
        grads, mixed, weights, x, g_resid, norm_gains, vectors,
        [normed_one] + normed_one_rest, [g_attn] + g_attn_rest, bits, steps,
    )
    grad_up, grad_down = widen(grad_feed)
    grad_query, grad_key, grad_value = (packed[i * depth : (i + 1) * depth].astype(F32) for i in range(3))
    grad_out = jnp.transpose(packed[3 * depth :]).astype(F32)
    grad_gains = jnp.stack([sums[0], sums[7], sums[5], sums[2]])
    grad_shifts = jnp.stack([sums[1], sums[8], sums[6], sums[3]])
    grad_bias_up = lax.dynamic_slice_in_dim(sums[9 : 9 + groups * hidden // depth].reshape(-1), me * hidden, hidden, 0)
    whole = (rows, 1, depth)
    return (
        layer_out.reshape(whole),
        grad_tokens.reshape(whole),
        grad_query,
        grad_key,
        grad_value,
        grad_out,
        grad_up,
        grad_bias_up,
        grad_down,
        sums[4],
        grad_gains,
        grad_shifts,
    )


def solution(mesh):
    wide, tall = P(None, "tensor"), P("tensor", None)
    acts = P("tensor", "dp", None)
    return jax.shard_map(
        shards,
        mesh=mesh,
        in_specs=(acts, P("dp"), acts, wide, wide, wide, tall, wide, P("tensor"), tall, P(), P(), P()),
        out_specs=(acts, acts, wide, wide, wide, tall, wide, P("tensor"), tall, P(), P(), P()),
        check_vma=False,
    )
```

```python
import functools
import jax
import jax.numpy as jnp
from jax import lax
from jax.experimental import pallas as pl
from jax.experimental.pallas import tpu as pltpu
from jax.sharding import PartitionSpec as P

HD = 64
EPSILON = 1e-05
BF = jnp.bfloat16
F32 = jnp.float32
NT = (((1,), (1,)), ((), ()))
NN = (((1,), (0,)), ((), ()))
TN = (((0,), (0,)), ((), ()))
MIB = 1 << 20


def dotg(a, b, dims=NN):
    return lax.dot_general(a, b, dims, preferred_element_type=F32)


def rotate(x, cos, sin):
    first = lax.broadcasted_iota(jnp.int32, (x.shape[0], 128), 1) % HD < HD // 2
    parts = []
    for a in range(0, x.shape[1], 128):
        v = x[:, a : a + 128]
        swapped = jnp.where(first, pltpu.roll(v, 96, 1), pltpu.roll(v, 32, 1))
        parts.append(v * cos + swapped * sin)
    return jnp.concatenate(parts, axis=1) if len(parts) > 1 else parts[0]


def qkv_kernel(at_ref, x_ref, wq_ref, wk_ref, wv_ref, cos_ref, sin_ref, gain_ref, shift_ref, *refs):
    o_ref, normed_ref = refs[-2:]
    width = wq_ref.shape[1]
    hat, _ = norm_parts(x_ref[...].astype(F32))
    x = (hat * gain_ref[0:1] + shift_ref[0:1]).astype(BF)
    normed_ref[...] = x
    cos, sin = cos_ref[...], sin_ref[...]
    o_ref[:, :width] = rotate(dotg(x, wq_ref[...]), cos, sin).astype(BF)
    o_ref[:, width : 2 * width] = rotate(dotg(x, wk_ref[...]), cos, sin).astype(BF)
    o_ref[:, 2 * width :] = dotg(x, wv_ref[...]).astype(BF)


def project(where, x, gains, shifts, w_query, w_key, w_value, cos, sin, held, blk=512):
    rows, depth = x.shape
    width, slots = w_query.shape[1], cos.shape[0]
    blk = min(blk, rows)
    count = rows // blk
    once = lambda shape: pl.BlockSpec(shape, lambda i, at: (0, 0), pipeline_mode=pl.Buffered(1))
    angle = pl.BlockSpec((blk, 128), lambda i, at: (at[0] * count + i, 0))
    block = pl.BlockSpec((blk, depth), lambda i, at: (i, 0))
    return pl.pallas_call(
        qkv_kernel,
        grid_spec=pltpu.PrefetchScalarGridSpec(
            num_scalar_prefetch=1,
            grid=(count,),
            in_specs=[block] + [once((depth, width))] * 3 + [angle, angle, once(gains.shape), once(gains.shape)]
            + [pl.BlockSpec(memory_space=pl.ANY)] * len(held),
            out_specs=[pl.BlockSpec((blk, 3 * width), lambda i, at: (at[0] * count + i, 0)), block],
        ),
        out_shape=[
            jax.ShapeDtypeStruct((slots, 3 * width), BF),
            jax.ShapeDtypeStruct((rows, depth), BF),
        ],
        input_output_aliases={9: 0} if held else {},
        compiler_params=pltpu.CompilerParams(vmem_limit_bytes=60 * MIB),
        cost_estimate=pl.CostEstimate(flops=rows * depth, bytes_accessed=rows * depth, transcendentals=0),
        name="project",
    )(where, x, w_query, w_key, w_value, cos, sin, gains, shifts, *held)


def attend_kernel(at_ref, len_ref, q_ref, k_ref, v_ref, w_ref, *refs, blk):
    o_ref, lse_ref, share_ref, vt, low_ref = refs[-5:]
    pair = pl.program_id(0)
    i = at_ref[0]
    length = len_ref[0]
    def turn(j, _):
        part = pl.ds(pl.multiple_of(j * blk, blk), blk)
        vt[:, part] = jnp.transpose(v_ref[part, :])
        return 0

    lax.fori_loop(0, i + 1, turn, 0)
    lane = lax.broadcasted_iota(jnp.int32, (blk, 128), 1)
    q = q_ref[...] * jnp.asarray(0.125, BF)
    zero = jnp.zeros_like(q)
    qs = (jnp.where(lane < HD, q, zero), jnp.where(lane < HD, zero, q))

    def step(j, carry, diag):
        start = pl.multiple_of(j * blk, blk)
        kb = k_ref[pl.ds(start, blk), :]
        sub = min(256, blk)
        n = blk // sub
        if diag:
            key = lax.broadcasted_iota(jnp.int32, (sub, blk), 0)
            qry = lax.broadcasted_iota(jnp.int32, (sub, blk), 1)
        state = [carry[h] for h in range(2)]
        chains = [(h, t) for t in range(n) for h in range(2)]
        live = {}

        def first(c):
            h, t = chains[c]
            live[c] = dotg(kb[t * sub : t * sub + sub], qs[h], NT)

        def middle(c):
            h, t = chains[c]
            s = live[c]
            if diag:
                s = jnp.where((key + t * sub <= qry) & (key + t * sub + start < length), s, -1e30)
            m, l, acc = state[h]
            mn = jnp.maximum(m, jnp.max(s, axis=0, keepdims=True))
            p = jnp.exp(s - mn)
            al = jnp.exp(m - mn)
            state[h] = (mn, l * al + jnp.sum(p, axis=0, keepdims=True), acc)
            live[c] = (p.astype(BF), al)

        def last(c):
            h, t = chains[c]
            p, al = live.pop(c)
            m, l, acc = state[h]
            state[h] = (m, l, acc * al + dotg(vt[HD * h : HD * h + HD, pl.ds(start + t * sub, sub)], p))

        stages = (first, middle, last)
        for i in range(len(chains) + 4):
            for k in range(3):
                c = i - 2 * k
                if 0 <= c < len(chains):
                    stages[k](c)
        return tuple(state)

    init = tuple(
        (jnp.full((1, blk), -1e30, F32), jnp.zeros((1, blk), F32), jnp.zeros((HD, blk), F32))
        for _ in range(2)
    )
    c = lax.fori_loop(0, i, lambda j, c: step(j, c, False), init)
    c = step(i, c, True)
    ot = jnp.concatenate([c[h][2] / c[h][1] for h in range(2)], axis=0)
    low = jnp.transpose(ot).astype(BF)
    o_ref[...] = low
    lse_ref[0] = jnp.concatenate([c[h][0] + jnp.log(c[h][1]) for h in range(2)], axis=0)
    low_ref[pair] = low

    @pl.when(pair == pl.num_programs(0) - 1)
    def _():
        pairs = low_ref.shape[0]
        low = jnp.concatenate([low_ref[p] for p in range(pairs)], axis=1)
        share_ref[...] = dotg(low, w_ref[...]).astype(share_ref.dtype)


def attend(at, length, joint, w_out, held, kind, blk):
    rows, width, depth = joint.shape[0], w_out.shape[0], w_out.shape[1]
    pairs = width // 128
    return pl.pallas_call(
        functools.partial(attend_kernel, blk=blk),
        grid_spec=pltpu.PrefetchScalarGridSpec(
            num_scalar_prefetch=2,
            grid=(pairs,),
            in_specs=[
                pl.BlockSpec((blk, 128), lambda p, at, *_: (at[0], p)),
                pl.BlockSpec((rows, 128), lambda p, *_: (0, pairs + p)),
                pl.BlockSpec((rows, 128), lambda p, *_: (0, 2 * pairs + p)),
                pl.BlockSpec((width, depth), lambda p, *_: (0, 0), pipeline_mode=pl.Buffered(1)),
            ]
            + [pl.BlockSpec(memory_space=pl.ANY)] * len(held),
            out_specs=[
                pl.BlockSpec((blk, 128), lambda p, at, *_: (at[0], p)),
                pl.BlockSpec((1, 2, blk), lambda p, at, *_: (p, 0, at[0])),
                pl.BlockSpec((blk, depth), lambda p, *_: (0, 0)),
            ],
            scratch_shapes=[pltpu.VMEM((128, rows), BF), pltpu.VMEM((pairs, blk, 128), BF)],
        ),
        out_shape=[
            jax.ShapeDtypeStruct((rows, width), BF),
            jax.ShapeDtypeStruct((pairs, 2, rows), F32),
            jax.ShapeDtypeStruct((blk, depth), kind),
        ],
        input_output_aliases={6: 0, 7: 1} if held else {},
        compiler_params=pltpu.CompilerParams(vmem_limit_bytes=60 * MIB),
        cost_estimate=pl.CostEstimate(flops=rows * width, bytes_accessed=rows * width, transcendentals=0),
        name="attend",
    )(at, length, joint, joint, joint, w_out, *held)


def attend_back_kernel(
    len_ref, q_ref, k_ref, v_ref, o_ref, do_ref, lse_ref, cos_ref, sin_ref,
    dq_ref, dk_ref, dv_ref, kt, dlt, dqt, *, blk, blocks,
):
    length = len_ref[0]
    kt[...] = jnp.transpose(k_ref[...])
    dqt[...] = jnp.zeros_like(dqt)

    def products(i, _):
        at = pl.ds(pl.multiple_of(i * blk, blk), blk)
        both = jnp.transpose(do_ref[at, :].astype(F32) * o_ref[at, :].astype(F32))
        for h in range(2):
            dlt[h : h + 1, at] = jnp.sum(both[HD * h : HD * h + HD], axis=0, keepdims=True)
        return 0

    lax.fori_loop(0, blocks, products, 0)

    def keys(j, _):
        attend_back_keys(
            j, length, q_ref, k_ref, v_ref, do_ref, lse_ref, cos_ref, sin_ref, dk_ref, dv_ref, kt, dlt, dqt, blk, blocks
        )
        return 0

    lax.fori_loop(0, blocks, keys, 0)

    def turn(i, _):
        at = pl.ds(pl.multiple_of(i * blk, blk), blk)
        grad = jnp.transpose(dqt[:, at]) * 0.125
        dq_ref[at, :] = rotate(grad, cos_ref[at, :], -sin_ref[at, :]).astype(BF)
        return 0

    lax.fori_loop(0, blocks, turn, 0)


def attend_back_keys(
    j, length, q_ref, k_ref, v_ref, do_ref, lse_ref, cos_ref, sin_ref, dk_ref, dv_ref, kt, dlt, dqt, blk, blocks
):
    js = pl.multiple_of(j * blk, blk)
    lane = lax.broadcasted_iota(jnp.int32, (blk, 128), 1)
    kb = k_ref[pl.ds(js, blk), :] * jnp.asarray(0.125, BF)
    vb = v_ref[pl.ds(js, blk), :]
    zero = jnp.zeros_like(kb)
    ks = (jnp.where(lane < HD, kb, zero), jnp.where(lane < HD, zero, kb))
    vs = (jnp.where(lane < HD, vb, zero), jnp.where(lane < HD, zero, vb))

    def step(i, carry, diag):
        at = pl.ds(pl.multiple_of(i * blk, blk), blk)
        qb, dob = q_ref[at, :], do_ref[at, :]
        out = []
        for h in range(2):
            dk, dv = carry[h]
            s = dotg(ks[h], qb, NT)
            if diag:
                key = lax.broadcasted_iota(jnp.int32, (blk, blk), 0)
                qry = lax.broadcasted_iota(jnp.int32, (blk, blk), 1)
                s = jnp.where((key <= qry) & (key + js < length), s, -1e30)
            p = jnp.exp(s - lse_ref[0, h : h + 1, at])
            dp = dotg(vs[h], dob, NT)
            ds = (p * (dp - dlt[h : h + 1, at])).astype(BF)
            dv = dv + dotg(p.astype(BF), dob)
            dk = dk + dotg(ds, qb)
            dqt[HD * h : HD * h + HD, at] += dotg(kt[HD * h : HD * h + HD, pl.ds(js, blk)], ds)
            out.append((dk, dv))
        return tuple(out)

    z = jnp.zeros((blk, 128), F32)
    c = step(j, ((z, z), (z, z)), True)
    c = lax.fori_loop(j + 1, blocks, lambda i, c: step(i, c, False), c)
    grad = jnp.where(lane < HD, c[0][0], c[1][0]) * 0.125
    dk_ref[pl.ds(js, blk), :] = rotate(grad, cos_ref[pl.ds(js, blk), :], -sin_ref[pl.ds(js, blk), :]).astype(BF)
    dv_ref[pl.ds(js, blk), :] = jnp.where(lane < HD, c[0][1], c[1][1]).astype(BF)


def attend_back(length, joint, mixed, dmixed, lse, cos, sin, width, blk=512):
    rows = joint.shape[0]
    pairs, blocks = width // 128, rows // blk
    full = lambda off: pl.BlockSpec((rows, 128), lambda p, *_: (0, off * pairs + p))
    angle = pl.BlockSpec((rows, 128), lambda p, *_: (0, 0))
    return pl.pallas_call(
        functools.partial(attend_back_kernel, blk=blk, blocks=blocks),
        grid_spec=pltpu.PrefetchScalarGridSpec(
            num_scalar_prefetch=1,
            grid=(pairs,),
            in_specs=[full(0), full(1), full(2), full(0), full(0)]
            + [pl.BlockSpec((1, 2, rows), lambda p, *_: (p, 0, 0)), angle, angle],
            out_specs=[full(0)] * 3,
            scratch_shapes=[
                pltpu.VMEM((128, rows), BF),
                pltpu.VMEM((2, rows), F32),
                pltpu.VMEM((128, rows), F32),
            ],
        ),
        out_shape=[jax.ShapeDtypeStruct((rows, width), BF)] * 3,
        compiler_params=pltpu.CompilerParams(vmem_limit_bytes=60 * MIB),
        cost_estimate=pl.CostEstimate(
            flops=rows * width, bytes_accessed=rows * width, transcendentals=0
        ),
        name="attend_back",
    )(length, joint, joint, joint, mixed, dmixed, lse, cos, sin)


def gelu_parts(v):
    c = 0.7978845608028654
    return c, jnp.tanh(c * (v + 0.044715 * v * v * v))


def gelu_both(v):
    c, t = gelu_parts(v)
    half = 0.5 * (1.0 + t)
    return v * half, half + 0.5 * v * (1.0 - t * t) * c * (1.0 + 3 * 0.044715 * v * v)


def norm_parts(values):
    average = jnp.mean(values, axis=-1, keepdims=True)
    centred = values - average
    scale = lax.rsqrt(jnp.mean(centred * centred, axis=-1, keepdims=True) + EPSILON)
    return centred * scale, scale


def norm_back(grad, hat, scale, gain):
    g = grad * gain
    return scale * (
        g - jnp.mean(g, axis=-1, keepdims=True) - hat * jnp.mean(g * hat, axis=-1, keepdims=True)
    )


def column_sum(v):
    return jnp.sum(v, axis=0, keepdims=True)


def valid_rows(info_ref, start, count):
    at = info_ref[1] + start + lax.broadcasted_iota(jnp.int32, (count, 1), 0)
    return (at < info_ref[0]).astype(F32)


def loop_rows(rows, blk, body):
    def step(i, _):
        body(pl.multiple_of(i * blk, blk))
        return 0

    lax.fori_loop(0, rows // blk, step, 0)


def feed_kernel(info_ref, *refs, groups, chunks, sub):
    x_ref, bias_ref, resid_hbm, cot_hbm, bd_ref, gain_ref, shift_ref = refs[:7]
    ups, downs = refs[7 : 7 + groups], refs[7 + groups : 7 + 2 * groups]
    slope_ref, act_ref, out_ref, gb_ref, sums_ref, acc, resid_ref, cot_ref, sems = refs[7 + 2 * groups :]
    step = pl.program_id(0)
    rows = x_ref.shape[0]
    late = [
        pltpu.make_async_copy(resid_hbm, resid_ref, sems.at[0]),
        pltpu.make_async_copy(cot_hbm, cot_ref, sems.at[1]),
    ]

    @pl.when(step == 0)
    def _():
        for c in late:
            c.start()
        acc[...] = jnp.zeros_like(acc) + bd_ref[...].astype(F32)

    for g in range(groups):

        @pl.when(step // chunks == g)
        def _():
            for r in range(0, rows, sub):
                act, slope = gelu_both(dotg(x_ref[r : r + sub], ups[g][...], NT if g else NN) + bias_ref[0])
                slope_ref[r : r + sub] = slope.astype(BF)
                act = act.astype(BF)
                if g == 0:
                    act_ref[r : r + sub] = act
                acc[r : r + sub] += dotg(act, downs[g][...])

    @pl.when(step == groups * chunks - 1)
    def _():
        for c in late:
            c.wait()
        sums_ref[...] = jnp.zeros_like(sums_ref)
        gain, shift = gain_ref[3:4], shift_ref[3:4]
        blk = min(256, rows)

        def body(r):
            at = pl.ds(r, blk)
            valid = valid_rows(info_ref, r, blk)
            hat, scale = norm_parts(acc[at])
            out_ref[at] = (valid * (resid_ref[at] + hat * gain + shift)).astype(BF)
            g_out = valid * cot_ref[at].astype(F32)
            low = norm_back(g_out, hat, scale, gain).astype(BF)
            gb_ref[at] = low
            sums_ref[0:1] += column_sum(g_out * hat)
            sums_ref[1:2] += column_sum(g_out)
            sums_ref[2:3] += column_sum(low.astype(F32))

        loop_rows(rows, blk, body)


def feed_specs(depth, cols, chunks, rest):
    own = [
        pl.BlockSpec((depth, cols), lambda s, *_: (0, jnp.minimum(s, chunks - 1))),
        pl.BlockSpec((cols, depth), lambda s, *_: (jnp.minimum(s, chunks - 1), 0)),
    ]
    part = lambda g, i: pl.BlockSpec(
        (None, cols, depth), lambda s, *_: (i, jnp.clip(s - g * chunks, 0, chunks - 1), 0)
    )
    return [
        spec for i in range(2) for spec in [own[i]] + [part(g + 1, i) for g in range(len(rest))]
    ]


def feed(info, x, biases, up, down, rest, resid, cot, bias_down, gains, shifts, cols=1024):
    rows, depth = x.shape
    groups, hidden = 1 + len(rest), up.shape[1]
    cols = min(cols, hidden)
    chunks = hidden // cols
    once = lambda shape: pl.BlockSpec(shape, lambda s, *_: (0, 0), pipeline_mode=pl.Buffered(1))
    anyspace = pl.BlockSpec(memory_space=pl.ANY)
    own = lambda g: (lambda s, *_: (0, jnp.clip(s - g * chunks, 0, chunks - 1)))
    return pl.pallas_call(
        functools.partial(feed_kernel, groups=groups, chunks=chunks, sub=min(1024, rows)),
        grid_spec=pltpu.PrefetchScalarGridSpec(
            num_scalar_prefetch=1,
            grid=(groups * chunks,),
            in_specs=[
                once((rows, depth)),
                pl.BlockSpec((1, 1, cols), lambda s, *_: (s, 0, 0)),
                anyspace,
                anyspace,
                once((1, depth)),
                once(gains.shape),
                once(gains.shape),
            ]
            + feed_specs(depth, cols, chunks, rest),
            out_specs=[
                pl.BlockSpec((rows, cols), lambda s, *_: (0, s)),
                pl.BlockSpec((rows, cols), own(0)),
                once((rows, depth)),
                once((rows, depth)),
                once((8, depth)),
            ],
            scratch_shapes=[
                pltpu.VMEM((rows, depth), F32),
                pltpu.VMEM((rows, depth), F32),
                pltpu.VMEM((rows, depth), BF),
                pltpu.SemaphoreType.DMA((2,)),
            ],
        ),
        out_shape=[
            jax.ShapeDtypeStruct((rows, groups * hidden), BF),
            jax.ShapeDtypeStruct((rows, hidden), BF),
            jax.ShapeDtypeStruct((rows, depth), BF),
            jax.ShapeDtypeStruct((rows, depth), BF),
            jax.ShapeDtypeStruct((8, depth), F32),
        ],
        compiler_params=pltpu.CompilerParams(vmem_limit_bytes=60 * MIB),
        cost_estimate=pl.CostEstimate(flops=rows * depth, bytes_accessed=rows * depth, transcendentals=0),
        name="feed",
    )(info, x, biases.reshape(-1, 1, cols), resid, cot, bias_down, gains, shifts, up, *rest, down, *rest)


def feed_back_kernel(info_ref, *refs, groups, chunks, sub):
    gb_ref, slope_ref, resid_hbm, attn_hbm, cot_hbm, gain_ref = refs[:6]
    ups, downs = refs[6 : 6 + groups], refs[6 + groups : 6 + 2 * groups]
    gp_ref, gr_ref, ga_ref, sums_ref, acc, resid_ref, attn_ref, cot_ref, sems = refs[6 + 2 * groups :]
    step = pl.program_id(0)
    rows = gb_ref.shape[0]
    late = [
        pltpu.make_async_copy(src, dst, sems.at[i])
        for i, (src, dst) in enumerate(((resid_hbm, resid_ref), (attn_hbm, attn_ref), (cot_hbm, cot_ref)))
    ]

    @pl.when(step == 0)
    def _():
        for c in late:
            c.start()
        acc[...] = jnp.zeros_like(acc)

    for g in range(groups):

        @pl.when(step // chunks == g)
        def _():
            for r in range(0, rows, sub):
                grad = dotg(gb_ref[r : r + sub], downs[g][...], NT)
                low = (grad * slope_ref[r : r + sub].astype(F32)).astype(BF)
                if g == 0:
                    gp_ref[r : r + sub] = low
                acc[r : r + sub] += dotg(low, ups[g][...], NN if g else NT)

    @pl.when(step == groups * chunks - 1)
    def _():
        for c in late:
            c.wait()
        sums_ref[...] = jnp.zeros_like(sums_ref)
        blk = min(256, rows)

        def body(r):
            at = pl.ds(r, blk)
            g_out = valid_rows(info_ref, r, blk) * cot_ref[at].astype(F32)
            hat, scale = norm_parts(resid_ref[at])
            g_two = acc[at]
            g_resid = g_out + norm_back(g_two, hat, scale, gain_ref[2:3])
            gr_ref[at] = g_resid
            sums_ref[0:1] += column_sum(g_two * hat)
            sums_ref[1:2] += column_sum(g_two)
            hat, scale = norm_parts(attn_ref[at])
            ga_ref[at] = norm_back(g_resid, hat, scale, gain_ref[1:2]).astype(BF)
            sums_ref[2:3] += column_sum(g_resid * hat)
            sums_ref[3:4] += column_sum(g_resid)

        loop_rows(rows, blk, body)


def feed_back(info, gb, slope, up, down, rest, resid, attn_sum, cot, gains, cols=512):
    rows, depth = gb.shape
    groups, hidden = 1 + len(rest), up.shape[1]
    chunks = hidden // cols
    once = lambda shape: pl.BlockSpec(shape, lambda s, *_: (0, 0), pipeline_mode=pl.Buffered(1))
    anyspace = pl.BlockSpec(memory_space=pl.ANY)
    own = lambda g: (lambda s, *_: (0, jnp.clip(s - g * chunks, 0, chunks - 1)))
    return pl.pallas_call(
        functools.partial(feed_back_kernel, groups=groups, chunks=chunks, sub=min(1024, rows)),
        grid_spec=pltpu.PrefetchScalarGridSpec(
            num_scalar_prefetch=1,
            grid=(groups * chunks,),
            in_specs=[
                once((rows, depth)),
                pl.BlockSpec((rows, cols), lambda s, *_: (0, s)),
                anyspace,
                anyspace,
                anyspace,
                once(gains.shape),
            ]
            + feed_specs(depth, cols, chunks, rest),
            out_specs=[
                pl.BlockSpec((rows, cols), own(0)),
                once((rows, depth)),
                once((rows, depth)),
                once((8, depth)),
            ],
            scratch_shapes=[
                pltpu.VMEM((rows, depth), F32),
                pltpu.VMEM((rows, depth), F32),
                pltpu.VMEM((rows, depth), F32),
                pltpu.VMEM((rows, depth), BF),
                pltpu.SemaphoreType.DMA((3,)),
            ],
        ),
        out_shape=[
            jax.ShapeDtypeStruct((rows, hidden), BF),
            jax.ShapeDtypeStruct((rows, depth), F32),
            jax.ShapeDtypeStruct((rows, depth), BF),
            jax.ShapeDtypeStruct((8, depth), F32),
        ],
        compiler_params=pltpu.CompilerParams(vmem_limit_bytes=60 * MIB),
        cost_estimate=pl.CostEstimate(flops=rows * depth, bytes_accessed=rows * depth, transcendentals=0),
        name="feed_back",
    )(info, gb, slope, resid, attn_sum, cot, gains, up, *rest, down, *rest)


def feed_grad_kernel(*refs, groups):
    up_ref, down_ref, bias_ref, act_ref, gp_ref = refs[:5]
    n2s, gbs = refs[5 : 5 + groups], refs[5 + groups : 5 + 2 * groups]
    grad_ref, sum_ref = refs[5 + 2 * groups :]
    act, gp = act_ref[...], gp_ref[...]
    dup = dotg(gp, n2s[0][...], TN)
    ddown = dotg(act, gbs[0][...], TN)
    sums = column_sum(gp.astype(F32))
    for g in range(1, groups):
        pre = dotg(n2s[g][...], up_ref[...]) + bias_ref[0]
        act, slope = gelu_both(pre)
        act = act.astype(BF)
        gp = (dotg(gbs[g][...], down_ref[...], NT) * slope).astype(BF)
        dup += dotg(gp, n2s[g][...], TN)
        ddown += dotg(act, gbs[g][...], TN)
        sums += column_sum(gp.astype(F32))
    grad_ref[0] = dup.astype(BF)
    grad_ref[1] = ddown.astype(BF)
    sum_ref[0] = sums


def feed_grad(up, down, bias, act, gp, n2s, gbs, cols=512):
    rows, depth = n2s[0].shape
    groups, hidden = len(n2s), up.shape[1]
    once = lambda shape: pl.BlockSpec(shape, lambda s: (0, 0), pipeline_mode=pl.Buffered(1))
    wide = lambda count: pl.BlockSpec((count, cols), lambda s: (0, s))
    tall = pl.BlockSpec((cols, depth), lambda s: (s, 0))
    flat = pl.BlockSpec((1, 1, cols), lambda s: (s, 0, 0))
    return pl.pallas_call(
        functools.partial(feed_grad_kernel, groups=groups),
        grid=(hidden // cols,),
        in_specs=[wide(depth), tall, flat, wide(rows), wide(rows)] + [once((rows, depth))] * (2 * groups),
        out_specs=[pl.BlockSpec((2, cols, depth), lambda s: (0, s, 0)), flat],
        out_shape=[
            jax.ShapeDtypeStruct((2, hidden, depth), BF),
            jax.ShapeDtypeStruct((hidden // cols, 1, cols), F32),
        ],
        compiler_params=pltpu.CompilerParams(vmem_limit_bytes=60 * MIB),
        cost_estimate=pl.CostEstimate(
            flops=(8 * groups - 4) * rows * depth * hidden, bytes_accessed=20 * rows * depth, transcendentals=0
        ),
        name="feed_grad",
    )(up, down, bias.reshape(-1, 1, cols), act, gp, *n2s, *gbs)


def join_kernel(pick_ref, x_ref, gain_ref, shift_ref, *refs, blocks, each):
    parts, (attn_ref, resid_ref, low_ref) = refs[:-3], refs[-3:]
    block = pl.program_id(0) // each
    total = 0.0
    for g in range(len(parts) // blocks):
        wanted = pick_ref[g * blocks + block]
        part = parts[g * blocks][...]
        for b in range(1, blocks):
            part = jnp.where(wanted == b, parts[g * blocks + b][...], part)
        total = total + part.astype(F32)
    attn_ref[...] = total
    hat, _ = norm_parts(total)
    resid = x_ref[...].astype(F32) + hat * gain_ref[1:2] + shift_ref[1:2]
    resid_ref[...] = resid
    hat, _ = norm_parts(resid)
    low_ref[...] = (hat * gain_ref[2:3] + shift_ref[2:3]).astype(BF)


def join(x, gains, shifts, shares, picks, blk=256):
    rows, depth = x.shape
    blocks = len(shares[0])
    blk = min(blk, rows // blocks)
    each = rows // blocks // blk
    whole = pl.BlockSpec(gains.shape, lambda i, *_: (0, 0))
    block = pl.BlockSpec((blk, depth), lambda i, *_: (i, 0))
    part = lambda g, b: pl.BlockSpec(
        (blk, depth), lambda i, pick: (jnp.clip(i - pick[g * blocks + b] * each, 0, each - 1), 0)
    )
    return pl.pallas_call(
        functools.partial(join_kernel, blocks=blocks, each=each),
        grid_spec=pltpu.PrefetchScalarGridSpec(
            num_scalar_prefetch=1,
            grid=(rows // blk,),
            in_specs=[block, whole, whole] + [part(g, b) for g in range(len(shares)) for b in range(blocks)],
            out_specs=[block, block, block],
        ),
        out_shape=[
            jax.ShapeDtypeStruct((rows, depth), F32),
            jax.ShapeDtypeStruct((rows, depth), F32),
            jax.ShapeDtypeStruct((rows, depth), BF),
        ],
        compiler_params=pltpu.CompilerParams(vmem_limit_bytes=60 * MIB),
        name="join",
    )(picks, x, gains, shifts, *[v for share in shares for v in share])


def widen_kernel(up_ref, down_ref, dup_ref, ddown_ref):
    dup_ref[...] = jnp.transpose(up_ref[...]).astype(F32)
    ddown_ref[...] = down_ref[...].astype(F32)


def widen(grads, blk=512):
    hidden, depth = grads.shape[0] // 2, grads.shape[1]
    blk = min(blk, hidden)
    count = hidden // blk
    return pl.pallas_call(
        widen_kernel,
        grid=(count,),
        in_specs=[
            pl.BlockSpec((blk, depth), lambda i: (i, 0)),
            pl.BlockSpec((blk, depth), lambda i: (count + i, 0)),
        ],
        out_specs=[
            pl.BlockSpec((depth, blk), lambda i: (0, i)),
            pl.BlockSpec((blk, depth), lambda i: (i, 0)),
        ],
        out_shape=[
            jax.ShapeDtypeStruct((depth, hidden), F32),
            jax.ShapeDtypeStruct((hidden, depth), F32),
        ],
        compiler_params=pltpu.CompilerParams(vmem_limit_bytes=60 * MIB),
        name="widen",
    )(grads, grads)

MESH = pl.DeviceIdType.MESH


def exchange(src, dst, sems, slot, flipped):
    return pltpu.make_async_remote_copy(
        src_ref=src,
        dst_ref=dst,
        send_sem=sems[0].at[slot],
        recv_sem=sems[1].at[slot],
        device_id={"dp": lax.axis_index("dp") ^ flipped},
        device_id_type=MESH,
    )


def tail_kernel(
    gq_ref, gk_ref, gv_ref, mixed_ref, wq_ref, wk_ref, wv_ref, x_ref, gr_ref, gain_ref, vec_ref, *refs,
    bits, groups, steps,
):
    lefts, refs = refs[: 2 * groups], refs[2 * groups :]
    sum_ref, out_ref, total_ref = refs[:3]
    right, left, weight, x, g_resid, packed, acc, core_buf, buf, sent, came, own_share, vec_buf = refs[3:16]
    send, recv, vec_send, vec_recv, x_send, x_recv, local = refs[16:]
    sems = (send, recv)
    place, me = lax.axis_index("tensor"), lax.axis_index("dp")
    bit = lambda b: lax.rem(lax.div(me, 1 << b), 2)
    core = bit(0)
    outer = list(range(1, bits))
    order = [[b] for b in outer]
    rows, depth = x.shape
    width = weight.shape[2]
    half = 2 * depth
    base = pl.multiple_of(core * half, half)
    part = min(512, depth)
    chunks = half // part
    slots, fetched = iter(range(send.shape[0])), iter(range(local.shape[0]))

    def fetch(src, dst):
        c = pltpu.make_async_copy(src, dst, local.at[next(fetched)])
        c.start()
        return c

    def wait_all(copies):
        for c in copies:
            c.wait()

    second = [fetch(r, right.at[i]) for i, r in enumerate((gq_ref, gk_ref, gv_ref))]
    second += [fetch(r, weight.at[i]) for i, r in enumerate((wq_ref, wk_ref, wv_ref))]
    third = [fetch(r, left.at[i]) for i, r in enumerate(lefts)] + [fetch(mixed_ref, right.at[3])]
    fourth = [fetch(x_ref, x), fetch(gr_ref, g_resid)]

    flips = {1 << b for b in range(bits)}
    flips |= {sum(1 << b for b in some) for some in order}
    greeted = [{"dp": me ^ f} for f in sorted(flips)]
    greeted += [{"tensor": lax.rem(place + r, groups)} for r in range(1, groups)]
    for bits_of in steps:
        for mask in range(1, 1 << len(bits_of)):
            chosen = [bits_of[i] for i in range(len(bits_of)) if mask >> i & 1]
            flip = sum(1 << b for axis, b in chosen if axis == "dp")
            turn_by = sum(1 << b for axis, b in chosen if axis == "tensor")
            if flip and turn_by:
                greeted.append({"dp": me ^ flip, "tensor": place ^ turn_by})
            elif flip and flip not in flips:
                flips.add(flip)
                greeted.append({"dp": me ^ flip})
    barrier = pltpu.get_barrier_semaphore()
    for peer in greeted:
        pl.semaphore_signal(barrier, inc=1, device_id=peer, device_id_type=MESH)
    pl.semaphore_wait(barrier, len(greeted))

    def copy(src, dst, flipped):
        c = exchange(src, dst, sems, next(slots), flipped)
        c.start()
        return c

    def rank(some):
        return sum(bit(b) << i for i, b in enumerate(some))

    def other(mine, mask):
        for i in range(mask.bit_length()):
            if mask >> i & 1:
                mine = mine + (1 << i) * (1 - 2 * lax.rem(lax.div(mine, 1 << i), 2))
        return mine

    def peer(some, mask):
        return sum(1 << b for i, b in enumerate(some) if mask >> i & 1)

    forwards = []
    cores = {}

    def reduce(chunk):
        cores[chunk].wait()

        def join(i, _):
            at = pl.ds(pl.multiple_of(chunk * part + i * 64, 64), 64)
            own = packed[pl.ds(pl.multiple_of(base + chunk * part + i * 64, 64), 64)].astype(F32)
            acc[at] = (own + core_buf[at].astype(F32)).astype(BF)
            return 0

        lax.fori_loop(0, part // 64, join, 0)
        start, size = chunk * part, part
        landing = chunk * (part - part // (1 << (bits - 1)))
        for some in order:
            size //= 1 << len(some)
            mine = rank(some)
            copies = []
            for mask in range(1, 1 << len(some)):
                away = pl.multiple_of(start + other(mine, mask) * size, size)
                at = pl.ds(landing + (mask - 1) * size, size)
                copies.append(copy(acc.at[pl.ds(away, size)], buf.at[at], peer(some, mask)))
            start = start + mine * size
            yield
            wait_all(copies)
            step = min(size, 64)

            def body(i, _, start=start, landing=landing, step=step, size=size, count=len(copies)):
                at = pl.ds(pl.multiple_of(start + i * step, step), step)
                value = acc[at].astype(F32)
                for n in range(count):
                    value += buf[pl.ds(pl.multiple_of(landing + n * size + i * step, step), step)].astype(F32)
                acc[at] = value.astype(BF)
                return 0

            lax.fori_loop(0, size // step, body, 0)
            landing += len(copies) * size
        start = base + start
        sum_ref[pl.ds(pl.multiple_of(start, size), size)] = acc[pl.ds(pl.multiple_of(start - base, size), size)]
        for some in reversed(order):
            have = sum_ref.at[pl.ds(pl.multiple_of(start, size), size)]
            copies = [copy(have, have, peer(some, mask)) for mask in range(1, 1 << len(some))]
            yield
            wait_all(copies)
            start = start - rank(some) * size
            size *= 1 << len(some)
        have = sum_ref.at[pl.ds(pl.multiple_of(start, size), size)]
        forwards.append(copy(have, have, 1))

    quarter = rows // 4

    def share(r, piece):
        g = pl.ds(pl.multiple_of(lax.rem(place + r, groups) * rows + piece * quarter, quarter), quarter)
        value = dotg(right[0, g, :], weight[0], NT)
        value += dotg(right[1, g, :], weight[1], NT)
        value += dotg(right[2, g, :], weight[2], NT)
        return value

    shares = {}

    def share_away(r):
        def body(i, _):
            sent[r - 1, pl.ds(pl.multiple_of(i * quarter, quarter), quarter), :] = share(r, i).astype(BF)
            return 0

        for piece in range(4):
            lax.fori_loop(piece, piece + 1, body, 0)
            at, slot = pl.ds(piece * quarter, quarter), (r - 1) * 4 + piece
            c = pltpu.make_async_remote_copy(
                src_ref=sent.at[r - 1, at],
                dst_ref=came.at[r - 1, at],
                send_sem=x_send.at[slot],
                recv_sem=x_recv.at[slot],
                device_id={"tensor": lax.rem(place + r, groups)},
                device_id_type=MESH,
            )
            c.start()
            shares[r, piece] = c

    def share_own():
        def body(i, _):
            own_share[pl.ds(pl.multiple_of(i * quarter, quarter), quarter), :] = share(0, i)
            return 0

        lax.fori_loop(0, 4, body, 0)

    def weight_grad(side, some):
        cols = min(256, part)
        each = part // cols

        def body(i, _):
            first = pl.multiple_of(lax.rem(core + side, 2) * half + i * cols, cols)
            number = lax.div(first, depth)
            kind = lax.div(number, 3) * groups
            lanes = pl.ds(pl.multiple_of(lax.rem(first, depth), cols), cols)
            value = None
            for r in range(groups):
                at = pl.ds(pl.multiple_of(lax.rem(place + r, groups) * rows, rows), rows)
                term = dotg(left[kind + r, :, lanes], right[number, at, :], TN)
                value = term if value is None else value + term
            packed[pl.ds(first, cols), :] = value.astype(BF)
            return 0

        lax.fori_loop(some[0] * each, (some[-1] + 1) * each, body, 0)
        if side:
            for c in some:
                at = pl.ds(pl.multiple_of((1 - core) * half + c * part, part), part)
                cores[c] = copy(packed.at[at], core_buf.at[pl.ds(c * part, part)], 1)

    def last_norm(piece):
        wait_all([shares[r, piece] for r in range(1, groups)])
        blk = min(128, quarter)

        def body(i, _):
            at = pl.ds(pl.multiple_of(piece * quarter + i * blk, blk), blk)
            value = own_share[at, :]
            for r in range(groups - 1):
                value += came[r, at, :].astype(F32)
            hat, scale = norm_parts(x[at, :].astype(F32))
            out_ref[at, :] = (g_resid[at, :] + norm_back(value, hat, scale, gain_ref[0:1])).astype(BF)
            total_ref[0:1] += column_sum(value * hat)
            total_ref[1:2] += column_sum(value)
            return 0

        lax.fori_loop(0, quarter // blk, body, 0)

    def vectors():
        slot = 0
        for bits_of in steps:
            sends = []
            for mask in range(1, 1 << len(bits_of)):
                peer = {}
                for i, (axis, b) in enumerate(bits_of):
                    if mask >> i & 1:
                        peer[axis] = peer.get(axis, lax.axis_index(axis)) ^ (1 << b)
                sends.append(
                    pltpu.make_async_remote_copy(
                        src_ref=total_ref,
                        dst_ref=vec_buf.at[slot],
                        send_sem=vec_send.at[slot],
                        recv_sem=vec_recv.at[slot],
                        device_id=peer,
                        device_id_type=MESH,
                    )
                )
                sends[-1].start()
                slot += 1
            yield
            wait_all(sends)
            total = total_ref[...]
            for i in range(len(sends)):
                total += vec_buf[slot - len(sends) + i]
            total_ref[...] = total

    def turn(chains):
        still = []
        for chain in chains:
            try:
                next(chain)
                still.append(chain)
            except StopIteration:
                pass
        return still

    wait_all(second)
    for r in range(1, groups):
        share_away(r)
    wait_all(third)
    all_chunks = list(range(chunks))
    for some in (all_chunks[: chunks // 2], all_chunks[chunks // 2 :]):
        weight_grad(1, some)
    wait_all(fourth)
    total_ref[...] = vec_ref[...]
    reduces = []
    for i, chunk in enumerate(all_chunks):
        weight_grad(0, [chunk])
        reduces = turn(reduces + [reduce(chunk)])
    share_own()
    reduces = turn(reduces)
    last_norm(0)
    last_norm(1)
    reduces = turn(reduces)
    last_norm(2)
    reduces = turn(reduces)
    last_norm(3)
    chain = turn([vectors()])
    while reduces or chain:
        reduces, chain = turn(reduces), turn(chain)
    wait_all(forwards)


def tail(grads, mixed, weights, x, g_resid, gains, vectors, n1s, gas, bits, steps):
    (slots, width), (rows, depth), groups = mixed.shape, x.shape, len(n1s)
    half = 2 * depth
    landing = half - half // (1 << (bits - 1))
    count = half // min(512, depth) * (3 * bits + 2)
    vecs = sum((1 << len(b)) - 1 for b in steps)
    vmem = pl.BlockSpec(memory_space=pltpu.VMEM)
    anyspace = pl.BlockSpec(memory_space=pl.ANY)
    dma = pltpu.SemaphoreType.DMA
    peers = max(groups - 1, 1)
    return pl.pallas_call(
        functools.partial(tail_kernel, bits=bits, groups=groups, steps=steps),
        in_specs=[anyspace] * 9 + [vmem] * 2 + [anyspace] * (2 * groups),
        out_specs=[vmem, vmem, vmem],
        out_shape=[
            jax.ShapeDtypeStruct((4 * depth, width), BF),
            jax.ShapeDtypeStruct((rows, depth), BF),
            jax.ShapeDtypeStruct(vectors.shape, F32),
        ],
        scratch_shapes=[
            pltpu.VMEM((4, slots, width), BF),
            pltpu.VMEM((2 * groups, rows, depth), BF),
            pltpu.VMEM((3, depth, width), BF),
            pltpu.VMEM((rows, depth), BF),
            pltpu.VMEM((rows, depth), F32),
            pltpu.VMEM((4 * depth, width), BF),
            pltpu.VMEM((half, width), BF),
            pltpu.VMEM((half, width), BF),
            pltpu.VMEM((landing, width), BF),
            pltpu.VMEM((peers, rows, depth), BF),
            pltpu.VMEM((peers, rows, depth), BF),
            pltpu.VMEM((rows, depth), F32),
            pltpu.VMEM((vecs,) + vectors.shape, F32),
            dma((count,)),
            dma((count,)),
            dma((vecs,)),
            dma((vecs,)),
            dma((4 * peers,)),
            dma((4 * peers,)),
            dma((9 + 2 * groups,)),
        ],
        compiler_params=pltpu.CompilerParams(
            collective_id=1, has_side_effects=True, vmem_limit_bytes=60 * MIB
        ),
        cost_estimate=pl.CostEstimate(flops=rows * width, bytes_accessed=rows * width, transcendentals=0),
        name="tail",
    )(*grads, mixed, *weights, x, g_resid, gains, vectors, *n1s, *gas)


def mixed_back_kernel(at_ref, x_ref, w_ref, *refs):
    refs[-1][...] = dotg(x_ref[...], w_ref[...], NT).astype(BF)


def mixed_back(where, x, w_out, slots, held, blk=512):
    rows, depth = x.shape
    width = w_out.shape[0]
    blk = min(blk, rows)
    count = rows // blk
    return pl.pallas_call(
        mixed_back_kernel,
        grid_spec=pltpu.PrefetchScalarGridSpec(
            num_scalar_prefetch=1,
            grid=(count,),
            in_specs=[
                pl.BlockSpec((blk, depth), lambda i, at: (i, 0)),
                pl.BlockSpec((width, depth), lambda i, at: (0, 0)),
            ]
            + [pl.BlockSpec(memory_space=pl.ANY)] * len(held),
            out_specs=pl.BlockSpec((blk, width), lambda i, at: (at[0] * count + i, 0)),
        ),
        out_shape=jax.ShapeDtypeStruct((slots, width), BF),
        input_output_aliases={3: 0} if held else {},
        compiler_params=pltpu.CompilerParams(vmem_limit_bytes=60 * MIB),
        cost_estimate=pl.CostEstimate(flops=rows * depth, bytes_accessed=rows * depth, transcendentals=0),
        name="mixed_back",
    )(where, x, w_out, *held)


def shift(x, axis, count, step):
    return lax.ppermute(x, axis, [((i + step) % count, i) for i in range(count)])


def shards(
    tokens,
    lengths,
    cotangent,
    w_query,
    w_key,
    w_value,
    w_out,
    up_weight,
    bias_up,
    down_weight,
    bias_down,
    norm_gains,
    norm_shifts,
):
    rows, _, depth = tokens.shape
    groups, replicas = lax.axis_size("tensor"), lax.axis_size("dp")
    me, replica = lax.axis_index("tensor"), lax.axis_index("dp")
    slots = rows * groups
    width = w_query.shape[1]
    hidden = up_weight.shape[1]
    x = tokens.reshape(rows, depth)
    here = me.reshape(1).astype(jnp.int32)
    place = lambda r: (here + r) % groups

    def others(v):
        return [shift(v, "tensor", groups, r) for r in range(1, groups)]

    def to_owner(v, r):
        return shift(v, "tensor", groups, groups - r)

    count = hidden // replicas
    up_piece = lax.dynamic_slice_in_dim(up_weight, replica * count, count, 1)
    down_piece = lax.dynamic_slice_in_dim(down_weight, replica * count, count, 0)
    piece = jnp.stack([jnp.transpose(up_piece), down_piece])

    freqs = 10000.0 ** (-jnp.arange(HD // 2).astype(F32) * 2.0 / HD)
    angles = jnp.arange(slots).astype(F32)[:, None] * freqs[None, :]
    cosine, sine = jnp.cos(angles), jnp.sin(angles)
    cosine = jnp.concatenate([cosine] * 4, axis=1)
    sine = jnp.concatenate([-sine, sine] * 2, axis=1)
    x_rest = others(x)
    weights = (w_query, w_key, w_value)
    joint, normed_one = project(here, x, norm_gains, norm_shifts, *weights, cosine, sine, [])
    joint, x_rest, piece, bias = lax.optimization_barrier((joint, x_rest, piece, bias_up))
    pieces, bias_rest = others(piece), others(bias)
    normed_one_rest = []
    for r, v in enumerate(x_rest):
        joint, n = project(place(r + 1), v, norm_gains, norm_shifts, *weights, cosine, sine, [joint])
        normed_one_rest.append(n)
    joint, pieces, bias_rest = lax.optimization_barrier((joint, pieces, bias_rest))
    blk = min(512, rows)
    each = rows // blk
    odd = lambda r: lax.rem(place(r), 2)
    ranks = lambda r, k: jnp.where(odd(r) == 1, each - 1 - k, k)
    held, shares, arrived = (), [], [[] for _ in range(1, groups)]
    for k in range(each):
        for r in range(1, groups):
            *held, share = attend(place(r) * each + ranks(0, k), lengths, joint, w_out, held, BF, blk)
            arrived[r - 1].append(to_owner(share, r))
        if k == each - 1 and k > 0:
            joint, arrived = lax.optimization_barrier((joint, [v[:k] for v in arrived])), arrived
            joint, early = joint
            arrived = [list(e) + v[k:] for e, v in zip(early, arrived)]
        *held, share = attend(here * each + ranks(0, k), lengths, joint, w_out, held, BF, blk)
        shares.append(share)
    mixed, lse = held
    shares = [shares] + arrived
    picks = jnp.concatenate([ranks(groups - r, k) for r in range(groups) for k in range(each)])
    rest = [lax.all_gather(p, "dp", axis=1, tiled=True) for p in pieces]
    biases = jnp.concatenate([bias_up] + bias_rest).astype(F32)

    info = jnp.stack([lengths[0], me * rows]).astype(jnp.int32)
    cot = cotangent.reshape(rows, depth)
    attn_sum, resid, normed_two = join(x, norm_gains, norm_shifts, shares, picks)
    normed_two_rest = others(normed_two)
    slope, act, layer_out, g_branch, sums3 = feed(
        info, normed_two, biases, up_weight, down_weight, rest, resid, cot,
        bias_down.reshape(1, depth), norm_gains, norm_shifts,
    )
    g_branch_rest = others(g_branch)
    g_pre, g_resid, g_attn, sums21 = feed_back(
        info, g_branch, slope, up_weight, down_weight, rest, resid, attn_sum, cot, norm_gains
    )
    g_attn_rest = others(g_attn)
    g_pre, normed_two_rest = lax.optimization_barrier((g_pre, normed_two_rest))
    g_mixed = mixed_back(here, g_attn, w_out, slots, [])
    g_pre, g_mixed = lax.optimization_barrier((g_pre, g_mixed))
    grad_feed, bias_up_sum = feed_grad(
        up_weight, down_weight, biases[:hidden], act, g_pre,
        [normed_two] + normed_two_rest, [g_branch] + g_branch_rest,
    )
    grad_feed = grad_feed.reshape(2 * hidden, depth)
    g_mixed, g_attn_rest, grad_feed = lax.optimization_barrier((g_mixed, g_attn_rest, grad_feed))
    grad_feed = lax.psum(grad_feed, "dp")
    for r, g in enumerate(g_attn_rest):
        g_mixed = mixed_back(place(r + 1), g, w_out, slots, [g_mixed])

    grads = attend_back(lengths, joint, mixed, g_mixed, lse, cosine, sine, width)
    placed = lax.dynamic_update_slice(
        jnp.zeros((groups * hidden,), F32), bias_up_sum.reshape(-1), (me * hidden,)
    ).reshape(-1, depth)
    bits = (replicas - 1).bit_length()
    steps = [("tensor", b) for b in range((groups - 1).bit_length())] + [("dp", b) for b in range(bits)]
    steps = [tuple(steps[i : i + 2]) for i in range(0, len(steps), 2)]
    vectors = jnp.concatenate([jnp.zeros((2, depth), F32), sums3[:3], sums21[:4], placed])
    vectors = jnp.pad(vectors, ((0, -len(vectors) % 8), (0, 0)))
    packed, grad_tokens, sums = tail(
        grads, mixed, weights, x, g_resid, norm_gains, vectors,
        [normed_one] + normed_one_rest, [g_attn] + g_attn_rest, bits, steps,
    )
    grad_up, grad_down = widen(grad_feed)
    grad_query, grad_key, grad_value = (packed[i * depth : (i + 1) * depth].astype(F32) for i in range(3))
    grad_out = jnp.transpose(packed[3 * depth :]).astype(F32)
    grad_gains = jnp.stack([sums[0], sums[7], sums[5], sums[2]])
    grad_shifts = jnp.stack([sums[1], sums[8], sums[6], sums[3]])
    grad_bias_up = lax.dynamic_slice_in_dim(sums[9 : 9 + groups * hidden // depth].reshape(-1), me * hidden, hidden, 0)
    whole = (rows, 1, depth)
    return (
        layer_out.reshape(whole),
        grad_tokens.reshape(whole),
        grad_query,
        grad_key,
        grad_value,
        grad_out,
        grad_up,
        grad_bias_up,
        grad_down,
        sums[4],
        grad_gains,
        grad_shifts,
    )


def solution(mesh):
    wide, tall = P(None, "tensor"), P("tensor", None)
    acts = P("tensor", "dp", None)
    return jax.shard_map(
        shards,
        mesh=mesh,
        in_specs=(acts, P("dp"), acts, wide, wide, wide, tall, wide, P("tensor"), tall, P(), P(), P()),
        out_specs=(acts, acts, wide, wide, wide, tall, wide, P("tensor"), tall, P(), P(), P()),
        check_vma=False,
    )
```
